32 devices in a mesh: dp: 2 (over x), seq: 4 (over y, core), mp: 4 (over z).
Axes of the slice: x: 2, y: 2, z: 4, core: 2. Of those that a mesh axis runs over, the one named last changes fastest.
Arguments:
- source: bfloat16 [4, 1024, 1024], P('dp', ('seq', 'mp')), may hold values from -6 to 6
- target: bfloat16 [4, 1024, 1024], P('dp', ('seq', 'mp')), may hold values from -6 to 6
- cotangent: bfloat16 [4, 1024, 1024], P('dp', ('seq', 'mp')), may hold values from -6 to 6
- source_len: int32 [4], P('dp'), may hold values from 512 to 1024, as said below
- target_len: int32 [4], P('dp'), may hold values from 512 to 1024, as said below
- source_seg: int32 [4, 1024], P('dp'), may hold values from 0 to 7, as said below
- target_seg: int32 [4, 1024], P('dp'), may hold values from 0 to 7, as said below
- enc_qkv: bfloat16 [3, 1024, 1024], P(None, ('dp', 'seq'), 'mp'), may hold values from -0.1875 to 0.1875
- enc_proj: bfloat16 [1024, 1024], P('mp', ('dp', 'seq')), may hold values from -0.75 to 0.75
- enc_up: bfloat16 [1024, 4096], P(('dp', 'seq'), 'mp'), may hold values from -0.1875 to 0.1875
- enc_down: bfloat16 [4096, 1024], P('mp', ('dp', 'seq')), may hold values from -0.125 to 0.125
- enc_gain: float32 [3, 1024], P(None, ('dp', 'seq', 'mp')), may hold values from 0.1 to 1.9
- enc_shift: float32 [3, 1024], P(None, ('dp', 'seq', 'mp')), may hold values from -1.8 to 1.8
- dec_qkv: bfloat16 [3, 1024, 1024], P(None, ('dp', 'seq'), 'mp'), may hold values from -0.1875 to 0.1875
- dec_proj: bfloat16 [1024, 1024], P('mp', ('dp', 'seq')), may hold values from -0.75 to 0.75
- cross_qkv: bfloat16 [3, 1024, 1024], P(None, ('dp', 'seq'), 'mp'), may hold values from -0.1875 to 0.1875
- cross_proj: bfloat16 [1024, 1024], P('mp', ('dp', 'seq')), may hold values from -0.75 to 0.75
- dec_up: bfloat16 [1024, 4096], P(('dp', 'seq'), 'mp'), may hold values from -0.1875 to 0.1875
- dec_down: bfloat16 [4096, 1024], P('mp', ('dp', 'seq')), may hold values from -0.125 to 0.125
- dec_gain: float32 [4, 1024], P(None, ('dp', 'seq', 'mp')), may hold values from 0.1 to 1.9
- dec_shift: float32 [4, 1024], P(None, ('dp', 'seq', 'mp')), may hold values from -1.8 to 1.8
Outputs:
- decoded: bfloat16 [4, 1024, 1024], P('dp', ('seq', 'mp'))
- source_grad: float32 [4, 1024, 1024], P('dp', ('seq', 'mp'))
- target_grad: float32 [4, 1024, 1024], P('dp', ('seq', 'mp'))
- grad_enc_qkv: float32 [3, 1024, 1024], P(None, ('dp', 'seq'), 'mp')
- grad_enc_proj: float32 [1024, 1024], P('mp', ('dp', 'seq'))
- grad_enc_up: float32 [1024, 4096], P(('dp', 'seq'), 'mp')
- grad_enc_down: float32 [4096, 1024], P('mp', ('dp', 'seq'))
- grad_enc_gain: float32 [3, 1024], P(None, ('dp', 'seq', 'mp'))
- grad_enc_shift: float32 [3, 1024], P(None, ('dp', 'seq', 'mp'))
- grad_dec_qkv: float32 [3, 1024, 1024], P(None, ('dp', 'seq'), 'mp')
- grad_dec_proj: float32 [1024, 1024], P('mp', ('dp', 'seq'))
- grad_cross_qkv: float32 [3, 1024, 1024], P(None, ('dp', 'seq'), 'mp')
- grad_cross_proj: float32 [1024, 1024], P('mp', ('dp', 'seq'))
- grad_dec_up: float32 [1024, 4096], P(('dp', 'seq'), 'mp')
- grad_dec_down: float32 [4096, 1024], P('mp', ('dp', 'seq'))
- grad_dec_gain: float32 [4, 1024], P(None, ('dp', 'seq', 'mp'))
- grad_dec_shift: float32 [4, 1024], P(None, ('dp', 'seq', 'mp'))
The draws below stay inside these ranges and needn't reach their ends.
Inputs may be any that keep to these rules, and one draw needn't show every extreme that they name: `source_len`: rows of a slot from its length on are padding; some slot of every draw has 1024 live rows. `target_len`: rows of a slot from its length on are padding; some slot of every draw has 1024 live rows. `source_seg`: ids never fall along a slot. A slot holds one pair (id 0 throughout) or 8 pairs, each with live rows; padding rows carry the last id. A slot's source and target hold the same number of pairs, and some slot of every draw holds 8. `target_seg`: ids never fall along a slot. A slot holds one pair (id 0 throughout) or 8 pairs, each with live rows; padding rows carry the last id. A slot's source and target hold the same number of pairs, and some slot of every draw holds 8.
All inputs are finite; a program needn't handle non-finite values.
Results may differ from the reference program's by a relative error of at most 0.035.
Values may be sent and summed in bfloat16 or wider, within the bound.
A program may use at most 192 MiB of HBM per device.

```python
import jax
import jax.numpy as jnp
from jax import lax

D = 1024
HEADS = 16
HEAD_DIM = 64
FF = 4096
L = 1024
PAIRS = 8
SLOTS = 4


def slot_layout(key, offset_tag):
    kind_key = jax.random.fold_in(key, 11)
    slot_ids = jnp.arange(SLOTS)
    packed = jax.random.randint(jax.random.fold_in(kind_key, 1), (SLOTS,), 0, 2)
    forced = jax.random.randint(jax.random.fold_in(kind_key, 2), (), 0, SLOTS)
    packed = jnp.where(slot_ids == forced, 1, packed)
    own_key = jax.random.fold_in(key, offset_tag)
    length = jax.random.randint(jax.random.fold_in(own_key, 1), (SLOTS,), L // 2, L + 1)
    longest = jax.random.randint(jax.random.fold_in(own_key, 2), (), 0, SLOTS)
    length = jnp.where(slot_ids == longest, L, length)
    wobble = L // 64
    jitter = jax.random.randint(jax.random.fold_in(own_key, 3), (SLOTS, PAIRS - 1), -wobble, wobble + 1)
    cut_rows = jnp.arange(1, PAIRS)[None, :] * length[:, None] // PAIRS + jitter
    row_ids = jnp.arange(L)
    segment = jnp.sum((row_ids[None, :, None] >= cut_rows[:, None, :]).astype(jnp.int32), -1) * packed[:, None]
    return (length.astype(jnp.int32), segment.astype(jnp.int32))


def draw_source_len(key, part):
    return slot_layout(key, 21)[0]


def draw_target_len(key, part):
    return slot_layout(key, 22)[0]


def draw_source_seg(key, part):
    return slot_layout(key, 21)[1]


def draw_target_seg(key, part):
    return slot_layout(key, 22)[1]


def levels(key, dims, shards, low, top_value):
    def one(dim, parts):
        steps = jax.random.uniform(jax.random.fold_in(jax.random.fold_in(key, 6), dim), (parts,), jnp.float32, low / len(shards), top_value / len(shards))
        return jnp.repeat(jnp.exp(steps), dims[dim] // parts).reshape((-1,) + (1,) * (len(dims) - dim - 1))

    loudness = one(*shards[0])
    for cut in shards[1:]:
        loudness = loudness * one(*cut)
    return loudness


def scatter_about(key, shape, width, reach, shards=(), dtype=jnp.bfloat16):
    gain = levels(key, shape, shards, -0.22, 0.18) if shards else 1.0
    values = jax.random.normal(key, shape, jnp.float32) * width * gain
    return jnp.minimum(jnp.maximum(values, -reach), reach).astype(dtype)


def setup_inputs(seed: int = 0) -> dict:
    splits = jax.random.split(jax.random.key(seed), 22)
    return {
        "source": scatter_about(splits[0], (SLOTS, L, D), 1.0, 6.0, ((0, 2), (1, 16))),
        "target": scatter_about(splits[1], (SLOTS, L, D), 1.0, 6.0, ((0, 2), (1, 16))),
        "cotangent": scatter_about(splits[2], (SLOTS, L, D), 1.0, 6.0, ((0, 2), (1, 16))),
        "source_len": draw_source_len(jax.random.fold_in(splits[21], 71), 0),
        "target_len": draw_target_len(jax.random.fold_in(splits[21], 71), 0),
        "source_seg": draw_source_seg(jax.random.fold_in(splits[21], 71), 0),
        "target_seg": draw_target_seg(jax.random.fold_in(splits[21], 71), 0),
        "enc_qkv": scatter_about(splits[7], (3, D, D), D ** -0.5, 0.1875, ((1, 8), (2, 4))),
        "enc_proj": scatter_about(splits[8], (D, D), (D // 16) ** -0.5, 0.75, ((0, 4), (1, 8))),
        "enc_up": scatter_about(splits[9], (D, FF), D ** -0.5, 0.1875, ((0, 8), (1, 4))),
        "enc_down": scatter_about(splits[10], (FF, D), (FF // 2) ** -0.5, 0.125, ((0, 4), (1, 8))),
        "enc_gain": jnp.clip(1.0 + 0.18 * jax.random.normal(splits[11], (3, D), jnp.float32), 0.1, 1.9),
        "enc_shift": scatter_about(splits[12], (3, D), 0.3, 1.8, ((1, 32),), jnp.float32),
        "dec_qkv": scatter_about(splits[13], (3, D, D), D ** -0.5, 0.1875, ((1, 8), (2, 4))),
        "dec_proj": scatter_about(splits[14], (D, D), (D // 16) ** -0.5, 0.75, ((0, 4), (1, 8))),
        "cross_qkv": scatter_about(splits[15], (3, D, D), D ** -0.5, 0.1875, ((1, 8), (2, 4))),
        "cross_proj": scatter_about(splits[16], (D, D), (D // 16) ** -0.5, 0.75, ((0, 4), (1, 8))),
        "dec_up": scatter_about(splits[17], (D, FF), D ** -0.5, 0.1875, ((0, 8), (1, 4))),
        "dec_down": scatter_about(splits[18], (FF, D), (FF // 2) ** -0.5, 0.125, ((0, 4), (1, 8))),
        "dec_gain": jnp.clip(1.0 + 0.18 * jax.random.normal(splits[19], (4, D), jnp.float32), 0.1, 1.9),
        "dec_shift": scatter_about(splits[20], (4, D), 0.3, 1.8, ((1, 32),), jnp.float32),
    }


EPSILON = 1e-05
MASKED = -1000000000.0

@jax.custom_vjp
def low(v):
    return lax.optimization_barrier(v.astype(jnp.bfloat16)).astype(jnp.float32)

@jax.custom_vjp
def low_back(v):
    return v

def low_keep(v):
    return (low(v), None)

def low_pass(kept, grad):
    return (grad,)

def back_keep(v):
    return (v, None)

def back_low(kept, grad):
    return (low(grad),)
low.defvjp(low_keep, low_pass)
low_back.defvjp(back_keep, back_low)

def layer_norm(stream, norm_gain, norm_shift):
    average = lax.optimization_barrier(jnp.mean(stream, -1, keepdims=True))
    centred = stream - average
    spread = lax.optimization_barrier(jnp.mean(centred * centred, -1, keepdims=True))
    return centred * lax.rsqrt(spread + EPSILON) * norm_gain + norm_shift

def matmul(left, right):
    return jnp.dot(left, right, precision=lax.Precision.HIGHEST, preferred_element_type=jnp.float32)

def attend(rows_query, rows_key, w_query, w_key, w_value, w_out, allowed):
    count_query = rows_query.shape[0]
    count_key = rows_key.shape[0]
    queries = low_back(low(matmul(rows_query, w_query))).reshape(count_query, HEADS, HEAD_DIM)
    keys_all = low_back(low(matmul(rows_key, w_key))).reshape(count_key, HEADS, HEAD_DIM)
    values_all = low_back(low(matmul(rows_key, w_value))).reshape(count_key, HEADS, HEAD_DIM)
    raw = low_back(jnp.einsum('qhd,khd->hqk', queries, keys_all, precision=lax.Precision.HIGHEST))
    scores = jnp.where(allowed[None], raw * HEAD_DIM ** (-0.5), MASKED)
    attn_probs = low(jax.nn.softmax(scores, axis=-1))
    mixed_heads = jnp.einsum('hqk,khd->qhd', attn_probs, values_all, precision=lax.Precision.HIGHEST)
    mixed_heads = low_back(low(mixed_heads.reshape(count_query, D)))
    return low_back(matmul(mixed_heads, w_out))

def feed(normed, w_up, w_down):
    activation = low_back(matmul(normed, w_up))
    hidden = low(jax.nn.gelu(activation, approximate=False))
    return low_back(matmul(hidden, w_down))

def slot_forward(params, stream_in, target_in, enc_allowed, self_allowed, cross_allowed):
    enc_qkv, enc_proj, enc_up, enc_down, enc_gain, enc_shift, dec_qkv, dec_proj, cross_qkv, cross_proj, dec_up, dec_down, dec_gain, dec_shift = params
    normed_a = low(layer_norm(stream_in, enc_gain[0], enc_shift[0]))
    stream_mid = stream_in + attend(normed_a, normed_a, enc_qkv[0], enc_qkv[1], enc_qkv[2], enc_proj, enc_allowed)
    normed_b = low(layer_norm(stream_mid, enc_gain[1], enc_shift[1]))
    stream_end = stream_mid + feed(normed_b, enc_up, enc_down)
    memory = low(layer_norm(stream_end, enc_gain[2], enc_shift[2]))
    normed_c = low(layer_norm(target_in, dec_gain[0], dec_shift[0]))
    target_mid = target_in + attend(normed_c, normed_c, dec_qkv[0], dec_qkv[1], dec_qkv[2], dec_proj, self_allowed)
    normed_d = low(layer_norm(target_mid, dec_gain[1], dec_shift[1]))
    target_late = target_mid + attend(normed_d, memory, cross_qkv[0], cross_qkv[1], cross_qkv[2], cross_proj, cross_allowed)
    normed_e = low(layer_norm(target_late, dec_gain[2], dec_shift[2]))
    target_end = target_late + feed(normed_e, dec_up, dec_down)
    return layer_norm(target_end, dec_gain[3], dec_shift[3])

def slot_masks(src_length, tgt_length, src_segment, tgt_segment):
    positions = jnp.arange(src_segment.shape[0])
    source_live = positions[None, :] < src_length
    target_live = positions[None, :] < tgt_length
    enc_allowed = (src_segment[:, None] == src_segment[None, :]) & source_live
    self_allowed = (tgt_segment[:, None] == tgt_segment[None, :]) & target_live & (positions[None, :] <= positions[:, None])
    cross_allowed = (tgt_segment[:, None] == src_segment[None, :]) & source_live
    return (enc_allowed, self_allowed, cross_allowed)

def reference(source, target, cotangent, source_len, target_len, source_seg, target_seg, enc_qkv, enc_proj, enc_up, enc_down, enc_gain, enc_shift, dec_qkv, dec_proj, cross_qkv, cross_proj, dec_up, dec_down, dec_gain, dec_shift):
    params = tuple((weight_arg.astype(jnp.float32) for weight_arg in (enc_qkv, enc_proj, enc_up, enc_down, enc_gain, enc_shift, dec_qkv, dec_proj, cross_qkv, cross_proj, dec_up, dec_down, dec_gain, dec_shift)))
    zeros_tree = jax.tree.map(jnp.zeros_like, params)

    def one_slot(totals, slot_data):
        source_rows, target_rows, grad_out, src_length, tgt_length, src_segment, tgt_segment = slot_data
        enc_allowed, self_allowed, cross_allowed = slot_masks(src_length, tgt_length, src_segment, tgt_segment)

        def forward(weights, stream_in, target_in):
            return slot_forward(weights, stream_in, target_in, enc_allowed, self_allowed, cross_allowed)
        decoded, pullback = jax.vjp(forward, params, source_rows.astype(jnp.float32), target_rows.astype(jnp.float32))
        grad_params, grad_source, grad_target = pullback(grad_out.astype(jnp.float32))
        totals = jax.tree.map(jnp.add, totals, grad_params)
        return (totals, (decoded.astype(jnp.bfloat16), grad_source, grad_target))
    totals, outputs = lax.scan(one_slot, zeros_tree, (source, target, cotangent, source_len, target_len, source_seg, target_seg))
    return (outputs[0], outputs[1], outputs[2], totals[0], totals[1], totals[2], totals[3], totals[4], totals[5], totals[6], totals[7], totals[8], totals[9], totals[10], totals[11], totals[12], totals[13])
```

```python
import jax
import jax.numpy as jnp
from jax import lax
from jax.experimental import pallas as pl
from jax.experimental.pallas import tpu as pltpu
from jax.sharding import Mesh, PartitionSpec as P

HEAD_DIM = 64
EPSILON = 1e-05
MASKED = -1000000000.0
AXES = ("hi", "k", "y", "c", "mp")
MESH_ID = pl.DeviceIdType.MESH
F32 = jnp.float32
BF16 = jnp.bfloat16
SWAP = [(0, 1), (1, 0)]


def plane_place():
    hi, k, y, c, z = (lax.axis_index(name) for name in AXES)
    partners = ((1 - hi, k, 1 - y, c, z), (1 - hi, k, y, c, z), (hi, k, 1 - y, c, z))
    blocks = ((1 - y) * 2 + 1 - hi, y * 2 + 1 - hi, (1 - y) * 2 + hi)
    return partners, blocks, y * 2 + hi


def greet(partners):
    barrier = pltpu.get_barrier_semaphore()
    for partner in partners:
        pl.semaphore_signal(barrier, inc=1, device_id=partner, device_id_type=MESH_ID)
    pl.semaphore_wait(barrier, len(partners))


def gather_kernel(h_ref, out_ref, send_sem, recv_sem):
    partners, unused, mine = plane_place()
    greet(partners)
    copies = []
    for i, partner in enumerate(partners):
        copy = pltpu.make_async_remote_copy(
            src_ref=h_ref,
            dst_ref=out_ref.at[mine],
            send_sem=send_sem.at[i],
            recv_sem=recv_sem.at[i],
            device_id=partner,
            device_id_type=MESH_ID,
        )
        copy.start()
        copies.append(copy)
    out_ref[mine] = h_ref[...]
    for copy in copies:
        copy.wait()


def gather_rows(own):
    rows, width = own.shape
    out = pl.pallas_call(
        gather_kernel,
        out_shape=jax.ShapeDtypeStruct((4, rows, width), own.dtype),
        in_specs=[pl.BlockSpec(memory_space=pltpu.VMEM)],
        out_specs=pl.BlockSpec(memory_space=pltpu.VMEM),
        scratch_shapes=[pltpu.SemaphoreType.DMA((3,)), pltpu.SemaphoreType.DMA((3,))],
        compiler_params=pltpu.CompilerParams(collective_id=0, has_side_effects=True),
        name="gather_rows",
    )(own)
    return out.reshape(4 * rows, width)


def scatter_kernel(p_ref, out_ref, landed, send_sem, recv_sem):
    partners, blocks, mine = plane_place()
    greet(partners)
    copies = []
    for i, partner in enumerate(partners):
        copy = pltpu.make_async_remote_copy(
            src_ref=p_ref.at[blocks[i]],
            dst_ref=landed.at[i],
            send_sem=send_sem.at[i],
            recv_sem=recv_sem.at[i],
            device_id=partner,
            device_id_type=MESH_ID,
        )
        copy.start()
        copies.append(copy)
    for copy in copies:
        copy.wait()
    total = p_ref[mine].astype(F32) + landed[0].astype(F32)
    out_ref[...] = total + landed[1].astype(F32) + landed[2].astype(F32)


def sum_rows(partial):
    rows, width = partial.shape[0] // 4, partial.shape[1]
    return pl.pallas_call(
        scatter_kernel,
        out_shape=jax.ShapeDtypeStruct((rows, width), F32),
        in_specs=[pl.BlockSpec(memory_space=pltpu.VMEM)],
        out_specs=pl.BlockSpec(memory_space=pltpu.VMEM),
        scratch_shapes=[
            pltpu.VMEM((3, rows, width), BF16),
            pltpu.SemaphoreType.DMA((3,)),
            pltpu.SemaphoreType.DMA((3,)),
        ],
        compiler_params=pltpu.CompilerParams(collective_id=1, has_side_effects=True),
        name="sum_rows",
    )(partial.astype(BF16).reshape(4, rows, width))


def norm_forward(stream, gain, shift):
    average = jnp.mean(stream, -1, keepdims=True)
    centred = stream - average
    scale = lax.rsqrt(jnp.mean(centred * centred, -1, keepdims=True) + EPSILON)
    unit = centred * scale
    return unit * gain + shift, (unit, scale)


def norm_back(kept, gain, upstream):
    unit, scale = kept
    inner = upstream * gain
    grad = scale * (
        inner - jnp.mean(inner, -1, keepdims=True) - unit * jnp.mean(inner * unit, -1, keepdims=True)
    )
    return grad, jnp.sum(upstream * unit, 0), jnp.sum(upstream, 0)


def nt(left, right):
    return lax.dot_general(left, right, (((1,), (1,)), ((), ())), preferred_element_type=F32)


def nn(left, right):
    return lax.dot_general(left, right, (((1,), (0,)), ((), ())), preferred_element_type=F32)


def tn(left, right):
    return lax.dot_general(left, right, (((0,), (0,)), ((), ())), preferred_element_type=F32)


def heads(values):
    return values.reshape(values.shape[0], values.shape[1] // HEAD_DIM, HEAD_DIM)


def swap_core(values):
    return lax.ppermute(values, "c", SWAP)


def whole_keys(own):
    return jnp.concatenate([own, swap_core(own)], 0)


def own_keys(partial):
    half = partial.shape[0] // 2
    partial = partial.astype(BF16)
    return (partial[:half].astype(F32) + swap_core(partial[half:]).astype(F32)).astype(BF16)


def attend(queries, keys, values, allowed):
    raw = jnp.einsum("qhd,khd->hqk", heads(queries), heads(keys), preferred_element_type=F32)
    scores = jnp.where(allowed[None], raw * HEAD_DIM ** (-0.5), MASKED)
    row_max = jnp.max(scores, -1, keepdims=True)
    raised = jnp.exp(scores - row_max)
    total = jnp.sum(raised, -1, keepdims=True)
    probs = raised / total
    mixed = jnp.einsum(
        "hqk,khd->qhd", probs.astype(BF16), heads(values), preferred_element_type=F32
    )
    mixed = mixed.reshape(queries.shape).astype(BF16)
    return mixed, (queries, keys, values, row_max + jnp.log(total))


def attend_back(kept, grad_mixed, allowed):
    queries, keys, values, log_total = kept
    raw = jnp.einsum("qhd,khd->hqk", heads(queries), heads(keys), preferred_element_type=F32)
    scores = jnp.where(allowed[None], raw * HEAD_DIM ** (-0.5), MASKED)
    probs = jnp.exp(scores - log_total)
    grad_mixed = heads(grad_mixed)
    grad_values = jnp.einsum(
        "hqk,qhd->khd", probs.astype(BF16), grad_mixed, preferred_element_type=F32
    )
    grad_probs = jnp.einsum(
        "qhd,khd->hqk", grad_mixed, heads(values), preferred_element_type=F32
    )
    weighted = probs * grad_probs
    grad_scores = weighted - probs * jnp.sum(weighted, -1, keepdims=True)
    grad_raw = (grad_scores * HEAD_DIM ** (-0.5)).astype(BF16)
    grad_queries = jnp.einsum("hqk,khd->qhd", grad_raw, heads(keys), preferred_element_type=F32)
    grad_keys = jnp.einsum("hqk,qhd->khd", grad_raw, heads(queries), preferred_element_type=F32)
    return (
        grad_queries.reshape(queries.shape).astype(BF16),
        own_keys(grad_keys.reshape(keys.shape)),
        own_keys(grad_values.reshape(values.shape)),
    )


def gelu(values):
    return jax.nn.gelu(values, approximate=False)


def gelu_back(activation, upstream):
    unused, pullback = jax.vjp(gelu, activation)
    return pullback(upstream)[0]


def pack_attend(qkv, proj):
    stacked = jnp.concatenate([jnp.swapaxes(qkv, 1, 2), proj[None]], 0)
    count, units, width = stacked.shape
    return jnp.swapaxes(stacked.reshape(count, 4, units // 4, width), 0, 1).reshape(4, -1, width)


def pack_feed(up, down):
    stacked = jnp.stack([up.T, down])
    count, units, width = stacked.shape
    return jnp.swapaxes(stacked.reshape(count, 4, units // 4, width), 0, 1).reshape(4, -1, width)


def unpack(packed, count):
    parts, rows, width = packed.shape
    unpacked = packed.reshape(parts, count, rows // count, width)
    return jnp.swapaxes(unpacked, 0, 1).reshape(count, parts * rows // count, width)


def gather_weights(packed, count):
    rows, width = packed.shape[1:]
    copies = lax.axis_size("k")
    if copies > 1:
        packed = lax.all_gather(packed, "k", axis=2, tiled=True)
    packed = lax.all_to_all(packed, ("hi", "y"), 0, 0, tiled=True)
    packed = lax.all_gather(lax.all_gather(packed, "mp"), "c")
    packed = packed.reshape(2, 4, 2, 2, rows, copies, width)
    packed = packed.transpose(1, 4, 2, 5, 3, 0, 6).reshape(4, rows, 8 * copies * width)
    return unpack(packed, count)


def scatter_weights(grads):
    parts, rows, total = grads.shape
    copies = lax.axis_size("k")
    width = total // (8 * copies)
    grads = grads.astype(BF16).reshape(4, rows, 2, copies, 2, 2, width)
    grads = grads.transpose(5, 0, 2, 4, 1, 3, 6).reshape(2, 4, 4, rows, copies * width)
    grads = lax.psum_scatter(grads, "c", scatter_dimension=0)
    grads = lax.psum_scatter(grads, "mp", scatter_dimension=0)
    grads = lax.all_to_all(grads, ("hi", "y"), 0, 0, tiled=True).astype(F32)
    if copies > 1:
        grads = lax.psum_scatter(grads, "k", scatter_dimension=2, tiled=True)
    return grads


def by_z(stacked):
    count, units, width = stacked.shape
    return jnp.swapaxes(stacked.reshape(count, 4, units // 4, width), 0, 1).reshape(4, -1, width)


def slot_perm(step):
    copies = lax.axis_size("k")
    sizes = (2, copies, 2, 2, 4)

    def flat(hi, k, y, c, z):
        return (((hi * sizes[1] + k) * 2 + y) * 2 + c) * 4 + z

    pairs = []
    for hi in range(2):
        for k in range(copies):
            for y in range(2):
                for c in range(2):
                    for z in range(4):
                        pairs.append(
                            (flat(hi, k, y, c, z), flat(z // 2, k, y, c, 2 * hi + (z % 2 ^ step)))
                        )
    return pairs


def to_slot(rows):
    odd = lax.axis_index("mp") % 2
    first, second = (
        lax.ppermute(jnp.where(odd == step, rows[0], rows[1]), AXES, slot_perm(step))
        for step in range(2)
    )
    return jnp.concatenate(
        [jnp.where(odd == 0, first, second), jnp.where(odd == 0, second, first)], 0
    )


def from_slot(rows):
    half = rows.shape[0] // 2
    odd = lax.axis_index("mp") % 2
    first, second = (
        lax.ppermute(jnp.where(odd == step, rows[:half], rows[half:]), AXES, slot_perm(step))
        for step in range(2)
    )
    return jnp.stack([jnp.where(odd == 0, first, second), jnp.where(odd == 0, second, first)])


def slot_facts(lengths, segments):
    packed = jnp.concatenate([segments, jnp.broadcast_to(lengths[:, None], (2, 128))], 1)
    z = lax.axis_index("mp")
    other = lax.ppermute(packed, "hi", SWAP)
    chosen = jnp.where(lax.axis_index("hi") == z // 2, packed, other)
    chosen = jnp.where(z % 2 == 0, chosen[0], chosen[1])
    length = segments.shape[1]
    return chosen[length], chosen[:length]


def row_order(values):
    c = lax.axis_index("c")
    split = values.reshape(2, 2, values.shape[0] // 4)
    own = jnp.where(c == 0, split[:, 0], split[:, 1]).reshape(-1)
    other = jnp.where(c == 0, split[:, 1], split[:, 0]).reshape(-1)
    return own, jnp.concatenate([own, other])


def local(
    source,
    target,
    cotangent,
    source_len,
    target_len,
    source_seg,
    target_seg,
    enc_qkv,
    enc_proj,
    enc_up,
    enc_down,
    enc_gain,
    enc_shift,
    dec_qkv,
    dec_proj,
    cross_qkv,
    cross_proj,
    dec_up,
    dec_down,
    dec_gain,
    dec_shift,
):
    vectors = jnp.concatenate([enc_gain, enc_shift, dec_gain, dec_shift], 0)
    for name in ("mp", "c", "y", "k", "hi"):
        if lax.axis_size(name) > 1:
            vectors = lax.all_gather(vectors, name, axis=1, tiled=True)
    enc_g, enc_b, dec_g, dec_b = vectors[:3], vectors[3:6], vectors[6:10], vectors[10:]

    enc_w = gather_weights(pack_attend(enc_qkv, enc_proj), 4)
    self_w = gather_weights(pack_attend(dec_qkv, dec_proj), 4)
    enc_f = gather_weights(pack_feed(enc_up, enc_down), 2)
    cross_w = gather_weights(pack_attend(cross_qkv, cross_proj), 4)
    dec_f = gather_weights(pack_feed(dec_up, dec_down), 2)

    source_length, source_ids = slot_facts(source_len, source_seg)
    target_length, target_ids = slot_facts(target_len, target_seg)
    place, key_place = row_order(jnp.arange(source_ids.shape[0]))
    source_query, source_key = row_order(source_ids)
    target_query, target_key = row_order(target_ids)
    source_live = key_place[None] < source_length
    enc_allowed = (source_query[:, None] == source_key[None]) & source_live
    self_allowed = (
        (target_query[:, None] == target_key[None])
        & (key_place[None] < target_length)
        & (key_place[None] <= place[:, None])
    )
    cross_allowed = (target_query[:, None] == source_key[None]) & source_live

    stream_in = to_slot(source).astype(F32)
    target_in = to_slot(target).astype(F32)
    grad_out = to_slot(cotangent).astype(F32)

    def projections(rows, weights, keys_only=False):
        made = nt(rows, weights).astype(BF16)
        return made

    normed, kept_a = norm_forward(stream_in, enc_g[0], enc_b[0])
    rows_a = gather_rows(normed.astype(BF16))
    normed, kept_c = norm_forward(target_in, dec_g[0], dec_b[0])
    rows_c = gather_rows(normed.astype(BF16))
    width = enc_w.shape[1]

    def self_attend(rows, weights, allowed):
        made = nt(rows, weights[:3].reshape(3 * width, -1)).astype(BF16)
        key_value = whole_keys(made[:, width:])
        mixed, kept = attend(made[:, :width], key_value[:, :width], key_value[:, width:], allowed)
        return sum_rows(nn(mixed, weights[3])), (mixed, kept)

    branch, enc_kept = self_attend(rows_a, enc_w, enc_allowed)
    stream_mid = stream_in + branch
    normed, kept_b = norm_forward(stream_mid, enc_g[1], enc_b[1])
    rows_b = gather_rows(normed.astype(BF16))
    enc_act = nt(rows_b, enc_f[0])
    enc_hidden = gelu(enc_act).astype(BF16)
    stream_end = stream_mid + sum_rows(nn(enc_hidden, enc_f[1]))
    normed, kept_m = norm_forward(stream_end, enc_g[2], enc_b[2])
    memory = gather_rows(normed.astype(BF16))

    branch, self_kept = self_attend(rows_c, self_w, self_allowed)
    target_mid = target_in + branch
    normed, kept_d = norm_forward(target_mid, dec_g[1], dec_b[1])
    rows_d = gather_rows(normed.astype(BF16))
    cross_q = nt(rows_d, cross_w[0]).astype(BF16)
    cross_kv = whole_keys(nt(memory, cross_w[1:3].reshape(2 * width, -1)).astype(BF16))
    cross_mixed, cross_kept = attend(
        cross_q, cross_kv[:, :width], cross_kv[:, width:], cross_allowed
    )
    target_late = target_mid + sum_rows(nn(cross_mixed, cross_w[3]))
    normed, kept_e = norm_forward(target_late, dec_g[2], dec_b[2])
    rows_e = gather_rows(normed.astype(BF16))
    dec_act = nt(rows_e, dec_f[0])
    dec_hidden = gelu(dec_act).astype(BF16)
    target_end = target_late + sum_rows(nn(dec_hidden, dec_f[1]))
    normed, kept_o = norm_forward(target_end, dec_g[3], dec_b[3])
    decoded = normed.astype(BF16)

    def feed_back(grad, act, hidden, rows, weights):
        grad_rows = gather_rows(grad.astype(BF16))
        grad_act = gelu_back(act, nt(grad_rows, weights[1])).astype(BF16)
        shares = jnp.stack([tn(grad_act, rows), tn(hidden, grad_rows)])
        return sum_rows(nn(grad_act, weights[0])), shares

    def attend_grads(grad, kept, allowed, query_rows, key_rows, weights):
        mixed, kept = kept
        grad_rows = gather_rows(grad.astype(BF16))
        grad_mixed = nt(grad_rows, weights[3]).astype(BF16)
        grad_q, grad_k, grad_v = attend_back(kept, grad_mixed, allowed)
        shares = jnp.stack(
            [tn(grad_q, query_rows), tn(grad_k, key_rows), tn(grad_v, key_rows), tn(mixed, grad_rows)]
        )
        return grad_q, jnp.concatenate([grad_k, grad_v], 1), shares

    grad_end, gain_3, shift_3 = norm_back(kept_o, dec_g[3], grad_out)
    grad_normed, dec_f_share = feed_back(grad_end, dec_act, dec_hidden, rows_e, dec_f)
    dec_f_grad = scatter_weights(by_z(dec_f_share))
    piece, gain_2, shift_2 = norm_back(kept_e, dec_g[2], grad_normed)
    grad_late = grad_end + piece
    grad_q, grad_kv, cross_share = attend_grads(
        grad_late, (cross_mixed, cross_kept), cross_allowed, rows_d, memory, cross_w
    )
    cross_grad = scatter_weights(by_z(cross_share))
    grad_memory = sum_rows(nn(grad_kv, cross_w[1:3].reshape(2 * width, -1)))
    piece, gain_1, shift_1 = norm_back(kept_d, dec_g[1], sum_rows(nn(grad_q, cross_w[0])))
    grad_mid = grad_late + piece

    grad_stream, enc_gain_2, enc_shift_2 = norm_back(kept_m, enc_g[2], grad_memory)
    grad_normed, enc_f_share = feed_back(grad_stream, enc_act, enc_hidden, rows_b, enc_f)
    enc_f_grad = scatter_weights(by_z(enc_f_share))

    grad_q, grad_kv, self_share = attend_grads(
        grad_mid, self_kept, self_allowed, rows_c, rows_c, self_w
    )
    self_grad = scatter_weights(by_z(self_share))
    piece, gain_0, shift_0 = norm_back(
        kept_c,
        dec_g[0],
        sum_rows(nn(jnp.concatenate([grad_q, grad_kv], 1), self_w[:3].reshape(3 * width, -1))),
    )
    target_grad = grad_mid + piece

    piece, enc_gain_1, enc_shift_1 = norm_back(kept_b, enc_g[1], grad_normed)
    grad_stream = grad_stream + piece
    grad_q, grad_kv, enc_share = attend_grads(
        grad_stream, enc_kept, enc_allowed, rows_a, rows_a, enc_w
    )
    piece, enc_gain_0, enc_shift_0 = norm_back(
        kept_a,
        enc_g[0],
        sum_rows(nn(jnp.concatenate([grad_q, grad_kv], 1), enc_w[:3].reshape(3 * width, -1))),
    )
    source_grad = grad_stream + piece

    norm_share = jnp.stack(
        [enc_gain_0, enc_gain_1, enc_gain_2, enc_shift_0, enc_shift_1, enc_shift_2]
        + [gain_0, gain_1, gain_2, gain_3, shift_0, shift_1, shift_2, shift_3]
    )
    norm_share = jnp.concatenate([norm_share, jnp.zeros_like(norm_share[:2])], 0)
    enc_grad = scatter_weights(by_z(enc_share))
    norm_grad = scatter_weights(jnp.broadcast_to(norm_share[None], (4, 16, norm_share.shape[1])))
    norm_grad = jnp.sum(norm_grad, 0)
    part = norm_grad.shape[1] // 4
    norm_grad = lax.dynamic_slice_in_dim(norm_grad, lax.axis_index("mp") * part, part, 1)

    def attend_shares(grads):
        grads = unpack(grads, 4)
        return jnp.swapaxes(grads[:3], 1, 2), grads[3]

    def feed_shares(grads):
        grads = unpack(grads, 2)
        return grads[0].T, grads[1]

    enc_a, enc_o = attend_shares(enc_grad)
    self_a, self_o = attend_shares(self_grad)
    cross_a, cross_o = attend_shares(cross_grad)
    enc_u, enc_d = feed_shares(enc_f_grad)
    dec_u, dec_d = feed_shares(dec_f_grad)
    return (
        from_slot(decoded),
        from_slot(source_grad),
        from_slot(target_grad),
        enc_a,
        enc_o,
        enc_u,
        enc_d,
        norm_grad[:3],
        norm_grad[3:6],
        self_a,
        self_o,
        cross_a,
        cross_o,
        dec_u,
        dec_d,
        norm_grad[6:10],
        norm_grad[10:14],
    )


def solution(mesh):
    dp, seq, mp = (mesh.shape[name] for name in ("dp", "seq", "mp"))
    assert dp % 2 == 0 and seq == 4 and mp == 4
    fine = Mesh(mesh.devices.reshape(2, dp // 2, 2, 2, 4), AXES)
    d, s = ("hi", "k"), ("y", "c")
    rows = P(d, s + ("mp",), None)
    three, flat = P(None, d + s, "mp"), P("mp", d + s)
    up, vector = P(d + s, "mp"), P(None, d + s + ("mp",))
    attention, feeding = (three, flat), (up, flat)
    return jax.shard_map(
        local,
        mesh=fine,
        in_specs=(rows,) * 3
        + (P(d), P(d), P(d, None), P(d, None))
        + attention
        + feeding
        + (vector, vector)
        + attention * 2
        + feeding
        + (vector, vector),
        out_specs=(rows,) * 3
        + attention
        + feeding
        + (vector, vector)
        + attention * 2
        + feeding
        + (vector, vector),
        check_vma=False,
    )
```

```python
import jax
import jax.numpy as jnp
from jax import lax
from jax.experimental import pallas as pl
from jax.experimental.pallas import tpu as pltpu
from jax.sharding import Mesh, PartitionSpec as P

HEAD_DIM = 64
EPSILON = 1e-05
MASKED = -1000000000.0
AXES = ("hi", "k", "y", "c", "mp")
MESH_ID = pl.DeviceIdType.MESH
F32 = jnp.float32
BF16 = jnp.bfloat16


class Call:
    def __init__(self):
        self.arrays, self.specs = [], []
        self.shapes, self.scratch = [], []

    def take(self, array, space=pltpu.VMEM):
        for i, known in enumerate(self.arrays):
            if known is array:
                return ("in", i)
        self.arrays.append(array)
        self.specs.append(pl.BlockSpec(memory_space=space))
        return ("in", len(self.arrays) - 1)

    def give(self, shape, dtype):
        self.shapes.append(jax.ShapeDtypeStruct(shape, dtype))
        return ("out", len(self.shapes) - 1)

    def hold(self, shape, dtype):
        self.scratch.append(pltpu.VMEM(shape, dtype))
        return ("tmp", len(self.scratch) - 1)

    def sems(self, count):
        self.scratch.append(pltpu.SemaphoreType.DMA((count,)))
        return ("tmp", len(self.scratch) - 1)

    def run(self, body, name, collective=None, flops=0):
        ins, outs = len(self.arrays), len(self.shapes)

        def kernel(*refs):
            parts = {"in": refs[:ins], "out": refs[ins : ins + outs], "tmp": refs[ins + outs :]}
            body(lambda handle: parts[handle[0]][handle[1]])

        return pl.pallas_call(
            kernel,
            out_shape=tuple(self.shapes),
            in_specs=self.specs,
            out_specs=tuple(pl.BlockSpec(memory_space=pltpu.VMEM) for _ in self.shapes),
            scratch_shapes=self.scratch,
            compiler_params=pltpu.CompilerParams(
                collective_id=collective,
                has_side_effects=collective is not None,
                vmem_limit_bytes=48 << 20,
            ),
            cost_estimate=pl.CostEstimate(flops=flops, bytes_accessed=0, transcendentals=0),
            name=name,
        )(*self.arrays)


MICROSECOND = 1_000_000_000


def nt(left, right):
    return lax.dot_general(left, right, (((1,), (1,)), ((), ())), preferred_element_type=F32)


def nn(left, right):
    return lax.dot_general(left, right, (((1,), (0,)), ((), ())), preferred_element_type=F32)


def tn(left, right):
    return lax.dot_general(left, right, (((0,), (0,)), ((), ())), preferred_element_type=F32)


def unit_of(stream):
    average = jnp.mean(stream, -1, keepdims=True)
    centred = stream - average
    scale = lax.rsqrt(jnp.mean(centred * centred, -1, keepdims=True) + EPSILON)
    return centred * scale, scale


def norm_back(stream, gain, upstream):
    unit, scale = unit_of(stream)
    inner = upstream * gain
    grad = scale * (
        inner - jnp.mean(inner, -1, keepdims=True) - unit * jnp.mean(inner * unit, -1, keepdims=True)
    )
    shares = jnp.concatenate(
        [jnp.sum(upstream * unit, 0, keepdims=True), jnp.sum(upstream, 0, keepdims=True)], 0
    )
    return grad, shares


def gelu_pair(act):
    bell = 0.5 + 0.5 * lax.erf(act * 0.7071067811865476)
    slope = bell + act * (jnp.exp(act * act * -0.5) * 0.3989422804014327)
    return act * bell, slope


def place():
    hi, k, y, c, z = (lax.axis_index(name) for name in AXES)
    return {
        "x": (1 - hi, k, y, c, z),
        "y": (hi, k, 1 - y, c, z),
        "d": (1 - hi, k, 1 - y, c, z),
        "core": (hi, k, y, 1 - c, z),
        "mesh": (hi, k, y, c, z),
        "own_row": y * 2 + hi,
        "x_row": y * 2 + 1 - hi,
        "y_row": (1 - y) * 2 + hi,
        "d_row": (1 - y) * 2 + 1 - hi,
    }


def greet(partners):
    barrier = pltpu.get_barrier_semaphore()
    for partner in partners:
        pl.semaphore_signal(barrier, inc=1, device_id=partner, device_id_type=MESH_ID)
    pl.semaphore_wait(barrier, len(partners))


class Weight:
    def __init__(self, call, packed, first, count):
        self.source = call.take(packed, pl.ANY)
        self.room = call.hold((4, count, 1024), BF16)
        self.sem = call.sems(1)
        self.first, self.count = first, count

    def start(self, get):
        source, room, sem = get(self.source), get(self.room), get(self.sem)
        for q in range(4):
            for c in range(2):
                pltpu.make_async_copy(
                    source.at[c, :, q, pl.ds(self.first, self.count), :],
                    room.at[:, :, pl.ds((q * 2 + c) * 128, 128)],
                    sem.at[0],
                ).start()

    def wait(self, get):
        room = get(self.room)
        pltpu.make_async_copy(room, room, get(self.sem).at[0]).wait()

    def matrix(self, get, first, count):
        return get(self.room)[:, first : first + count, :].reshape(4 * count, 1024)


class Job:
    def __init__(self, call, left, mid, right):
        self.left, self.mid, self.right = left, mid, right
        if left is not None:
            self.rows_in = call.take(left[0])
            self.out_first = call.hold((2, 128, 1024), BF16)
            self.out_edge = call.hold((2, 64, 1024), BF16)
            self.out_late = call.hold((2, 64, 1024), BF16)
            self.keep = call.hold((2, 64, 1024), F32)
            self.own = call.hold((128, 1024), F32)
            self.landed = call.hold((6, 64, 1024), BF16)
            self.sum_send, self.sum_recv = call.sems(6), call.sems(6)
        self.gathered = None
        if right is not None:
            self.gathered = call.give((4, 128, 1024), BF16)
            self.row_send, self.row_recv = call.sems(6), call.sems(6)

    def part(self, get, row, half=None):
        unused, weight, picks = self.left
        total, column = None, 0
        for first, count in picks:
            width = 4 * count
            left = get(self.rows_in)[row, :, column : column + width]
            term = nn(left, weight.matrix(get, first, count))
            total = term if total is None else total + term
            column += width
        return total

    def send(self, get, i, source, target, partner):
        copy = pltpu.make_async_remote_copy(
            src_ref=source,
            dst_ref=target,
            send_sem=get(self.sum_send).at[i],
            recv_sem=get(self.sum_recv).at[i],
            device_id=partner,
            device_id_type=MESH_ID,
        )
        copy.start()
        return copy

    def sum_start(self, get, at):
        first, edge, landed = get(self.out_first), get(self.out_edge), get(self.landed)
        keep = get(self.keep)
        self.copies = [None] * 6
        first[0] = self.part(get, at["d_row"]).astype(BF16)
        self.copies[0] = self.send(
            get, 0, first.at[0, pl.ds(0, 64)], landed.at[0], at["x"]
        )
        self.copies[1] = self.send(
            get, 1, first.at[0, pl.ds(64, 64)], landed.at[1], at["y"]
        )
        part = self.part(get, at["x_row"])
        edge[0] = part[:64].astype(BF16)
        keep[0] = part[64:]
        self.copies[2] = self.send(get, 2, edge.at[0], landed.at[2], at["x"])
        part = self.part(get, at["y_row"])
        edge[1] = part[64:].astype(BF16)
        keep[1] = part[:64]
        self.copies[3] = self.send(get, 3, edge.at[1], landed.at[3], at["y"])
        get(self.own)[...] = self.part(get, at["own_row"])

    def sum_forward(self, get, at):
        late, landed, keep = get(self.out_late), get(self.landed), get(self.keep)
        self.copies[0].wait_recv()
        late[1] = (keep[1] + landed[0].astype(F32)).astype(BF16)
        self.copies[4] = self.send(get, 4, late.at[1], landed.at[4], at["y"])
        self.copies[1].wait_recv()
        late[0] = (keep[0] + landed[1].astype(F32)).astype(BF16)
        self.copies[5] = self.send(get, 5, late.at[0], landed.at[5], at["x"])

    def sum_end(self, get):
        landed, own = get(self.landed), get(self.own)
        for i in (2, 3, 4, 5):
            self.copies[i].wait_recv()
        upper = own[:64] + landed[2].astype(F32) + landed[4].astype(F32)
        lower = own[64:] + landed[5].astype(F32) + landed[3].astype(F32)
        return jnp.concatenate([upper, lower], 0)

    def row_copy(self, get, i, row, half, partner):
        block = get(self.gathered).at[row, pl.ds(half * 64, 64)]
        copy = pltpu.make_async_remote_copy(
            src_ref=block,
            dst_ref=block,
            send_sem=get(self.row_send).at[i],
            recv_sem=get(self.row_recv).at[i],
            device_id=partner,
            device_id_type=MESH_ID,
        )
        copy.start()
        return copy

    def rows_start(self, get, at, normed):
        get(self.gathered)[at["own_row"]] = normed
        self.moves = [
            self.row_copy(get, 0, at["own_row"], 0, at["y"]),
            self.row_copy(get, 1, at["own_row"], 1, at["x"]),
            self.row_copy(get, 2, at["own_row"], 1, at["y"]),
            self.row_copy(get, 3, at["own_row"], 0, at["x"]),
        ]

    def rows_forward(self, get, at):
        self.moves[0].wait_recv()
        self.moves.append(self.row_copy(get, 4, at["y_row"], 0, at["x"]))
        self.moves[1].wait_recv()
        self.moves.append(self.row_copy(get, 5, at["x_row"], 1, at["y"]))

    def product(self, get, at, row):
        weight, picks, store = self.right
        rows = get(self.gathered)[row]
        column = 0
        for first, count in picks:
            store(get, at, row, column, nt(rows, weight.matrix(get, first, count)))
            column += 4 * count

    def drain(self):
        if self.left is not None:
            for copy in self.copies:
                copy.wait_send()
        if self.right is not None:
            for copy in self.moves:
                copy.wait_send()


def run_stage(call, jobs, weights, name, collective, finish=None, flops=0, core=False, more=None):
    def body(get):
        at = place()
        for weight in weights:
            weight.start(get)
        greet(
            [at["x"], at["y"]]
            + ([at["core"]] if core else [])
            + ([at["d"]] if more is not None else [])
        )
        lefts = [job for job in jobs if job.left is not None]
        rights = [job for job in jobs if job.right is not None and job.right[0] is not None]
        waited = []

        def ready(weight):
            if weight not in waited:
                weight.wait(get)
                waited.append(weight)

        for job in lefts:
            ready(job.left[1])
            job.sum_start(get, at)
        for job in lefts:
            job.sum_forward(get, at)
        for job in jobs:
            normed = job.mid(get, job.sum_end(get) if job.left is not None else None)
            if job.right is not None:
                job.rows_start(get, at, normed)
        if more is not None:
            more.start(get, at)
        for weight in weights:
            ready(weight)
        for job in rights:
            job.product(get, at, at["own_row"])
        for job in jobs:
            if job.right is not None:
                job.rows_forward(get, at)
        for job in jobs:
            if job.right is not None:
                job.moves[3].wait_recv()
                if job in rights:
                    job.product(get, at, at["x_row"])
                job.moves[2].wait_recv()
                if job in rights:
                    job.product(get, at, at["y_row"])
        for job in jobs:
            if job.right is not None:
                job.moves[4].wait_recv()
                job.moves[5].wait_recv()
                if job in rights:
                    job.product(get, at, at["d_row"])
        for job in jobs:
            job.drain()
        if finish is not None:
            finish(get)
        if more is not None:
            more.finish()

    return call.run(body, name, collective, flops)


class Plain:
    def __init__(self, call, width):
        self.out = call.give((4, 128, width), BF16)

    def store(self, get, at, row, column, value):
        get(self.out)[row, :, column : column + value.shape[1]] = value.astype(BF16)


class Shared:
    def __init__(self, call, width, skip=0):
        self.out = call.give((2, 4, 128, width), BF16)
        self.send_sem, self.recv_sem = call.sems(4), call.sems(4)
        self.width, self.skip, self.copies, self.blocks = width, skip, [], 0

    def store(self, get, at, row, column, value):
        out = get(self.out)
        column = column - self.skip
        out[0, row, :, column : column + value.shape[1]] = value.astype(BF16)
        if column + value.shape[1] == self.width:
            i = len(self.copies)
            copy = pltpu.make_async_remote_copy(
                src_ref=out.at[0, row],
                dst_ref=out.at[1, row],
                send_sem=get(self.send_sem).at[i],
                recv_sem=get(self.recv_sem).at[i],
                device_id=at["core"],
                device_id_type=MESH_ID,
            )
            copy.start()
            self.copies.append(copy)

    def finish(self, get):
        for copy in self.copies:
            copy.wait()


def query_and_shared(call, width):
    query, shared = Plain(call, width), Shared(call, 2 * width, skip=width)

    def store(get, at, row, column, value):
        if column < width:
            query.store(get, at, row, column, value)
        else:
            shared.store(get, at, row, column, value)

    return store, shared.finish


def lanes_of(head, rows):
    lane = lax.broadcasted_iota(jnp.int32, (rows, 128), 1)
    return lane // HEAD_DIM == head


def allowed_bias(facts_ref, keys_ref, causal):
    key = keys_ref[...]
    query = facts_ref[...]
    allowed = (key[:, 0:1] == query[0:1, :]) & (key[:, 2:3] > 0)
    if causal:
        allowed = allowed & (key[:, 1:2] <= query[1:2, :])
    return jnp.where(allowed, 0.0, MASKED)


def attend_kernel(causal, q_ref, kv_ref, facts_ref, keys_ref, mixed_ref, total_ref, bias):
    bias[...] = allowed_bias(facts_ref, keys_ref, causal)
    rows = q_ref.shape[0]
    half = rows // 2

    def pair_step(pair, carry):
        lanes = pl.ds(pl.multiple_of(pair * 128, 128), 128)
        value_lanes = pl.ds(pl.multiple_of(256 + pair * 128, 128), 128)
        keys, values = kv_ref[:, lanes], kv_ref[:, value_lanes]
        for block in range(2):
            queries = q_ref[pl.ds(block * half, half), lanes]
            mixed = []
            for head in range(2):
                picked = jnp.where(lanes_of(head, half), queries * 0.125, 0.0).astype(BF16)
                scores = nt(keys, picked) + bias[:, block * half : (block + 1) * half]
                top = jnp.max(scores, 0, keepdims=True)
                raised = jnp.exp(scores - top)
                total = jnp.sum(raised, 0, keepdims=True)
                probs = (raised * (1.0 / total)).astype(BF16)
                mixed.append(tn(values, probs)[head * HEAD_DIM : (head + 1) * HEAD_DIM])
                total_ref[pl.ds(pair * 2 + head, 1), block * half : (block + 1) * half] = (
                    top + jnp.log(total)
                )
            mixed = jnp.concatenate(mixed, 0).T
            mixed_ref[pl.ds(block * half, half), lanes] = mixed.astype(BF16)
        return carry

    lax.fori_loop(0, 2, pair_step, 0)


def attend(queries, key_value, facts, keys, causal):
    rows, width = 512, queries.shape[-1]

    def kernel(*refs):
        attend_kernel(causal, *refs)

    mixed, total = pl.pallas_call(
        kernel,
        out_shape=(
            jax.ShapeDtypeStruct((rows, width), BF16),
            jax.ShapeDtypeStruct((8, rows), F32),
        ),
        in_specs=[pl.BlockSpec(memory_space=pltpu.VMEM)] * 4,
        out_specs=(pl.BlockSpec(memory_space=pltpu.VMEM),) * 2,
        scratch_shapes=[pltpu.VMEM((1024, rows), F32)],
        compiler_params=pltpu.CompilerParams(vmem_limit_bytes=48 << 20),
        cost_estimate=pl.CostEstimate(flops=8 * MICROSECOND, bytes_accessed=0, transcendentals=0),
        name="attend",
    )(queries.reshape(rows, width), key_value.reshape(1024, 2 * width), facts, keys)
    return mixed.reshape(4, 128, width), total


def attend_back(
    queries, key_value, grad_mixed, total, facts, keys, causal, collective, done=()
):
    rows, width = 512, queries.shape[-1]
    half = rows // 2
    call = Call()
    q_in, kv_in = call.take(queries.reshape(rows, width)), call.take(key_value.reshape(1024, 2 * width))
    grad_in, total_in = call.take(grad_mixed.reshape(rows, width)), call.take(total)
    facts_in, keys_in = call.take(facts), call.take(keys)
    for array in done:
        call.take(array, pl.ANY)
    grad_out = call.give((rows, 3 * width), BF16)
    bias = call.hold((1024, rows), F32)
    gathered = call.hold((1024, 4 * 128), F32)
    outgoing, landed = call.hold((2, 512, 256), BF16), call.hold((2, 512, 256), BF16)
    send_sem, recv_sem = call.sems(2), call.sems(2)

    def body(get):
        at = place()
        q_ref, kv_ref, grad_ref, total_ref = get(q_in), get(kv_in), get(grad_in), get(total_in)
        out, mask, sums = get(grad_out), get(bias), get(gathered)
        away, here = get(outgoing), get(landed)
        mask[...] = allowed_bias(get(facts_in), get(keys_in), causal)
        greet([at["core"]])
        copies = []
        for pair in range(2):
            lanes = slice(pair * 128, pair * 128 + 128)
            keys_pair = kv_ref[:, lanes]
            values_pair = kv_ref[:, 256 + pair * 128 : 256 + pair * 128 + 128]
            key_sum = slice(pair * 256, pair * 256 + 128)
            value_sum = slice(pair * 256 + 128, pair * 256 + 256)
            for block in range(2):
                span = slice(block * half, (block + 1) * half)
                q_block, g_block = q_ref[span, lanes], grad_ref[span, lanes]
                grad_query = []
                for head in range(2):
                    inside = lanes_of(head, half)
                    picked = jnp.where(inside, q_block * 1.0, 0.0).astype(BF16)
                    grads = jnp.where(inside, g_block * 1.0, 0.0).astype(BF16)
                    scores = nt(keys_pair, picked) * 0.125 + mask[:, span]
                    probs = jnp.exp(scores - total_ref[pair * 2 + head : pair * 2 + head + 1, span])
                    weighted = probs * nt(values_pair, grads)
                    inner = jnp.sum(weighted, 0, keepdims=True)
                    grad_raw = ((weighted - probs * inner) * 0.125).astype(BF16)
                    value_term = nn(probs.astype(BF16), grads)
                    key_term = nn(grad_raw, picked)
                    if block == 0 and head == 0:
                        sums[:, key_sum] = key_term
                        sums[:, value_sum] = value_term
                    else:
                        sums[:, key_sum] += key_term
                        sums[:, value_sum] += value_term
                    grad_query.append(tn(keys_pair, grad_raw)[head * HEAD_DIM : (head + 1) * HEAD_DIM])
                out[span, lanes] = jnp.concatenate(grad_query, 0).T.astype(BF16)
            away[pair] = sums[512:, pair * 256 : pair * 256 + 256].astype(BF16)
            copy = pltpu.make_async_remote_copy(
                src_ref=away.at[pair],
                dst_ref=here.at[pair],
                send_sem=get(send_sem).at[pair],
                recv_sem=get(recv_sem).at[pair],
                device_id=at["core"],
                device_id_type=MESH_ID,
            )
            copy.start()
            copies.append(copy)
        for pair in range(2):
            copies[pair].wait()
            both = sums[:512, pair * 256 : pair * 256 + 256] + here[pair].astype(F32)
            out[:, width + pair * 128 : width + pair * 128 + 128] = both[:, :128].astype(BF16)
            out[:, 2 * width + pair * 128 : 2 * width + pair * 128 + 128] = both[:, 128:].astype(BF16)

    (grads,) = call.run(body, "attend_back", collective, 16 * MICROSECOND)
    return grads.reshape(4, 128, 3 * width)


def weight_shares(groups, collective):
    call = Call()
    plans = []
    for pairs in groups:
        count = 256 // len(pairs)
        handles = [
            (call.take(left.reshape(512, -1)), column, call.take(right.reshape(512, 1024)))
            for left, column, right in pairs
        ]
        made, landed = call.hold((2, 4, 4, 256, 128), BF16), call.hold((4, 4, 256, 128), BF16)
        send_sem, recv_sem = call.sems(4), call.sems(4)
        shares = call.give((4, 4, 256, 128), BF16)
        plans.append((count, handles, made, landed, send_sem, recv_sem, shares))

    def body(get):
        at = place()
        core = lax.axis_index("c")
        greet([at["core"]])
        copies = []

        def send(plan, i, part):
            made, landed, send_sem, recv_sem = (get(handle) for handle in plan[2:6])
            copy = pltpu.make_async_remote_copy(
                src_ref=made.at[(1 - core,) + part],
                dst_ref=landed.at[part],
                send_sem=send_sem.at[i],
                recv_sem=recv_sem.at[i],
                device_id=at["core"],
                device_id_type=MESH_ID,
            )
            copy.start()
            copies.append((plan, part, copy))

        for plan in plans:
            count, handles, made = plan[0], plan[1], get(plan[2])
            for m, (left, column, right) in enumerate(handles):
                left, right = get(left), get(right)
                for first in range(0, 4 * count, 256):
                    product = tn(left[:, column + first : column + first + 256], right[...])
                    for inner in range(0, 256, count):
                        z = (first + inner) // count
                        for d in range(8):
                            made[d % 2, z, d // 2, m * count : (m + 1) * count, :] = product[
                                inner : inner + count, d * 128 : d * 128 + 128
                            ].astype(BF16)
                    if count == 256:
                        send(plan, z, (z,))
                if count < 256:
                    every = slice(None)
                    send(plan, m, (every, every, pl.ds(m * count, count)))
        for plan, part, copy in copies:
            copy.wait()
            made, landed, shares = get(plan[2]), get(plan[3]), get(plan[6])
            own = made[(core,) + part].astype(F32)
            shares[part] = (own + landed[part].astype(F32)).astype(BF16)

    return call.run(body, "weight_shares", collective, 4 * len(groups) * MICROSECOND)


class Swap:
    def __init__(self, call, packs):
        self.packs = [call.take(pack) for pack in packs]
        self.outs = [call.give(pack.shape, pack.dtype) for pack in packs]
        self.send_sem, self.recv_sem = call.sems(3 * len(packs)), call.sems(3 * len(packs))

    def start(self, get, at):
        hi, k, y, c, z = at["mesh"]
        own = hi * 2 + y
        self.copies = []
        for pack, out in zip(self.packs, self.outs, strict=True):
            pack, out = get(pack), get(out)
            for name, q in (
                ("d", (1 - hi) * 2 + 1 - y),
                ("x", (1 - hi) * 2 + y),
                ("y", hi * 2 + 1 - y),
            ):
                i = len(self.copies)
                copy = pltpu.make_async_remote_copy(
                    src_ref=pack.at[q],
                    dst_ref=out.at[own],
                    send_sem=get(self.send_sem).at[i],
                    recv_sem=get(self.recv_sem).at[i],
                    device_id=at[name],
                    device_id_type=MESH_ID,
                )
                copy.start()
                self.copies.append(copy)
            out[own] = pack[own]

    def finish(self):
        for copy in self.copies:
            copy.wait()


class Slots:
    def __init__(self, call, arrays, inward):
        self.inward = inward
        self.arrays = [call.take(array) for array in arrays]
        shape = (128, 1024) if inward else (2, 64, 1024)
        self.outs = [call.give(shape, array.dtype) for array in arrays]
        self.send_sem, self.recv_sem = call.sems(2 * len(arrays)), call.sems(2 * len(arrays))

    def ends(self, get, at, j, step):
        z = at["mesh"][4]
        odd = lax.rem(z, 2)
        other = odd if step == 0 else 1 - odd
        array, out = get(self.arrays[j]), get(self.outs[j])
        if self.inward:
            return array.at[other], out.at[pl.ds(pl.multiple_of(odd * 64, 64), 64)]
        return array.at[pl.ds(pl.multiple_of(other * 64, 64), 64)], out.at[odd]

    def copy(self, get, at, j, step):
        hi, k, y, c, z = at["mesh"]
        odd = lax.rem(z, 2)
        source, target = self.ends(get, at, j, step)
        return pltpu.make_async_remote_copy(
            src_ref=source,
            dst_ref=target,
            send_sem=get(self.send_sem).at[2 * j + step],
            recv_sem=get(self.recv_sem).at[2 * j + step],
            device_id=(lax.div(z, 2), k, y, c, 2 * hi + (odd if step == 0 else 1 - odd)),
            device_id_type=MESH_ID,
        )

    def start(self, get, at):
        hi, z = at["mesh"][0], at["mesh"][4]
        stays = lax.div(z, 2) == hi
        for j in range(len(self.arrays)):
            self.copy(get, at, j, 1).start()

        @pl.when(jnp.logical_not(stays))
        def _():
            for j in range(len(self.arrays)):
                self.copy(get, at, j, 0).start()

        @pl.when(stays)
        def _():
            for j in range(len(self.arrays)):
                source, target = self.ends(get, at, j, 0)
                target[...] = source[...]

    def finish(self, get, at):
        hi, z = at["mesh"][0], at["mesh"][4]
        for j in range(len(self.arrays)):
            self.copy(get, at, j, 1).wait()

        @pl.when(lax.div(z, 2) != hi)
        def _():
            for j in range(len(self.arrays)):
                self.copy(get, at, j, 0).wait()


def all_partners(at):
    hi, k, y, c, z = at["mesh"]
    plane = [
        ((hi + i) % 2, k, (y + j) % 2, (c + n) % 2, z)
        for i in range(2)
        for j in range(2)
        for n in range(2)
        if i + j + n > 0
    ]
    ways = [((hi + i) % 2, k, y, c, (z + n) % 4) for i in range(2) for n in range(1, 4)]
    return plane, ways


def meet(at):
    plane, ways = all_partners(at)
    greet(plane + ways)
    return plane


def open_program(rows, vectors, facts, packs):
    call = Call()
    slots, swap = Slots(call, rows, True), Swap(call, packs)
    vec_in, fact_in = call.take(vectors), call.take(facts)
    vec_out, fact_out = call.give((16, 1024), F32), call.give((2,) + facts.shape, facts.dtype)
    landed, whole = call.hold((3, 16, 128), F32), call.hold((16, 128), F32)
    vec_send, vec_recv = call.sems(11), call.sems(11)

    def body(get):
        at = place()
        plane = meet(at)
        hi, k, y, c, z = at["mesh"]
        send, recv = get(vec_send), get(vec_recv)

        def push(i, source, target, partner):
            copy = pltpu.make_async_remote_copy(
                src_ref=source,
                dst_ref=target,
                send_sem=send.at[i],
                recv_sem=recv.at[i],
                device_id=partner,
                device_id_type=MESH_ID,
            )
            copy.start()
            return copy

        first = [
            push(n - 1, get(vec_in), get(landed).at[n - 1], (hi, k, y, c, (z + n) % 4))
            for n in range(1, 4)
        ]
        fact_copy = push(10, get(fact_in), get(fact_out).at[1], at["x"])
        slots.start(get, at)
        swap.start(get, at)
        get(fact_out)[0] = get(fact_in)[...]
        for copy in first:
            copy.wait()
        parts = get(landed)
        get(whole)[...] = get(vec_in)[...] + parts[0] + parts[1] + parts[2]
        block = pl.ds(pl.multiple_of(((hi * 2 + y) * 2 + c) * 128, 128), 128)
        second = [
            push(3 + i, get(whole), get(vec_out).at[:, block], partner)
            for i, partner in enumerate(plane)
        ]
        get(vec_out)[:, block] = get(whole)[...]
        for copy in second:
            copy.wait()
        fact_copy.wait()
        slots.finish(get, at)
        swap.finish()

    outs = call.run(body, "open_program", 13, 12 * MICROSECOND)
    n, m = len(rows), len(packs)
    return outs[:n], outs[n : n + m], outs[n + m], outs[n + m + 1]


def close_program(rows, vectors, packs):
    call = Call()
    slots, swap = Slots(call, rows, False), Swap(call, packs)
    vec_in = call.take(vectors)
    vec_out = call.give((16, 128), F32)
    landed, block_sum = call.hold((7, 16, 128), F32), call.hold((16, 128), F32)
    blocks, along = call.hold((8, 16, 128), F32), call.hold((3, 16, 128), F32)
    vec_send, vec_recv = call.sems(10), call.sems(10)

    def body(get):
        at = place()
        plane = meet(at)
        hi, k, y, c, z = at["mesh"]
        send, recv = get(vec_send), get(vec_recv)
        split = get(blocks)
        for d in range(8):
            split[d] = get(vec_in)[:, d * 128 : d * 128 + 128]

        def push(i, source, target, partner):
            copy = pltpu.make_async_remote_copy(
                src_ref=source,
                dst_ref=target,
                send_sem=send.at[i],
                recv_sem=recv.at[i],
                device_id=partner,
                device_id_type=MESH_ID,
            )
            copy.start()
            return copy

        first = [
            push(
                i,
                split.at[(partner[0] * 2 + partner[2]) * 2 + partner[3]],
                get(landed).at[i],
                partner,
            )
            for i, partner in enumerate(plane)
        ]
        slots.start(get, at)
        swap.start(get, at)
        for copy in first:
            copy.wait()
        total = split[(hi * 2 + y) * 2 + c]
        for i in range(7):
            total = total + get(landed)[i]
        get(block_sum)[...] = total
        second = [
            push(6 + n, get(block_sum), get(along).at[n - 1], (hi, k, y, c, (z + n) % 4))
            for n in range(1, 4)
        ]
        for copy in second:
            copy.wait()
        get(vec_out)[...] = get(block_sum)[...] + get(along)[0] + get(along)[1] + get(along)[2]
        slots.finish(get, at)
        swap.finish()

    outs = call.run(body, "close_program", 14, 16 * MICROSECOND)
    n, m = len(rows), len(packs)
    return outs[:n], outs[n : n + m], outs[n + m]


def swap_packs(packs, collective):
    call = Call()
    swap = Swap(call, packs)

    def body(get):
        at = place()
        greet([at["x"], at["y"], at["d"]])
        swap.start(get, at)
        swap.finish()

    return call.run(body, "swap_packs", collective, 5 * MICROSECOND)


def transposed(qkv):
    return [qkv[i].T for i in range(3)]


def pack_rows(matrices):
    stacked = jnp.stack(matrices)
    count, units, width = stacked.shape
    return jnp.swapaxes(stacked.reshape(count, 4, units // 4, width), 0, 1).reshape(4, -1, width)


def over_slots(shares):
    return lax.psum_scatter(shares, "mp", scatter_dimension=0)


def widen(packed):
    return packed if lax.axis_size("k") == 1 else lax.all_gather(packed, "k", axis=2, tiled=True)


def gather_weights(packed):
    copies = lax.axis_size("k")
    rows, width = packed.shape[1], 128 // copies
    packed = lax.all_gather(packed, ("c", "mp")).reshape(2, 4, 4, rows, 128)
    if copies > 1:
        packed = packed.reshape(2, 4, 2, 2, rows, copies, width)
        packed = packed.transpose(1, 4, 2, 5, 3, 0, 6).reshape(4, rows, 4, 2, 128)
        packed = packed.transpose(3, 0, 2, 1, 4)
    return packed


def by_owner(rights):
    copies = lax.axis_size("k")
    if copies == 1:
        return rights
    shape = rights.shape
    rights = rights.reshape(-1, 2, copies, 2, 2, 128 // copies).transpose(0, 1, 3, 4, 2, 5)
    return rights.reshape(shape)


def narrow(shares):
    shares = shares.astype(F32)
    if lax.axis_size("k") > 1:
        shares = lax.psum_scatter(shares, "k", scatter_dimension=2, tiled=True)
    return shares


def unpack(packed, count):
    parts, rows, width = packed.shape
    unpacked = packed.reshape(parts, count, rows // count, width)
    return jnp.swapaxes(unpacked, 0, 1).reshape(count, parts * rows // count, width)


def row_order(values):
    c = lax.axis_index("c")
    split = values.reshape(2, 2, values.shape[0] // 4)
    own = jnp.where(c == 0, split[:, 0], split[:, 1]).reshape(-1)
    other = jnp.where(c == 0, split[:, 1], split[:, 0]).reshape(-1)
    return own, jnp.concatenate([own, other])


def local(
    source,
    target,
    cotangent,
    source_len,
    target_len,
    source_seg,
    target_seg,
    enc_qkv,
    enc_proj,
    enc_up,
    enc_down,
    enc_gain,
    enc_shift,
    dec_qkv,
    dec_proj,
    cross_qkv,
    cross_proj,
    dec_up,
    dec_down,
    dec_gain,
    dec_shift,
):
    copies, z = lax.axis_size("k"), lax.axis_index("mp")
    vectors = jnp.concatenate([enc_gain, enc_shift, dec_gain, dec_shift, dec_shift[:2]], 0)
    if copies > 1:
        vectors = lax.all_gather(vectors, "k", axis=1, tiled=True)
    lane = jnp.arange(128)[None]
    vectors = jnp.where(lane // 32 == z, jnp.tile(vectors, (1, 4)), 0.0)
    facts = jnp.concatenate(
        [
            jnp.concatenate([segments, jnp.broadcast_to(lengths[:, None], (2, 128))], 1)
            for lengths, segments in ((source_len, source_seg), (target_len, target_seg))
        ],
        0,
    )
    facts = jnp.concatenate([facts.reshape(-1, 128), jnp.zeros((4, 128), jnp.int32)], 0)
    enc_p = widen(pack_rows([*transposed(enc_qkv), enc_proj]))
    self_p = widen(pack_rows([*transposed(dec_qkv), dec_proj]))
    cross_p = widen(pack_rows([*transposed(cross_qkv), cross_proj]))
    enc_up_p, enc_down_p = widen(pack_rows([enc_up.T])), widen(pack_rows([enc_down]))
    dec_up_p, dec_down_p = widen(pack_rows([dec_up.T])), widen(pack_rows([dec_down]))

    (stream_in, target_in, grad_out), (enc_p, self_p), vectors, facts = open_program(
        [source, target, cotangent], vectors, facts, [enc_p, self_p]
    )
    if copies > 1:
        vectors = vectors.reshape(16, 2, 2, 2, 4, copies, 32 // copies)
        vectors = vectors.transpose(0, 1, 5, 2, 3, 4, 6).reshape(16, 1024)
    enc_w, self_w = gather_weights(enc_p), gather_weights(self_p)
    near = jnp.where(lax.axis_index("hi") == z // 2, facts[0], facts[1])[:36].reshape(2, 2, 1152)
    near = jnp.where(z % 2 == 0, near[:, 0], near[:, 1])
    source_length, source_ids = near[0, 1024], near[0, :1024]
    target_length, target_ids = near[1, 1024], near[1, :1024]
    place_own, place_all = row_order(jnp.arange(source_ids.shape[0]))
    source_own, source_all = row_order(source_ids)
    target_own, target_all = row_order(target_ids)
    zero = jnp.zeros_like(place_own)
    source_facts = jnp.stack([source_own, place_own] + [zero] * 6)
    target_facts = jnp.stack([target_own, place_own] + [zero] * 6)

    def key_facts(ids, length):
        live = (place_all < length).astype(jnp.int32)
        blank = jnp.zeros_like(live)
        return jnp.stack([ids, place_all, live] + [blank] * 5, 1)

    source_keys = key_facts(source_all, source_length)
    target_keys = key_facts(target_all, target_length)

    ENC_G, ENC_B, DEC_G, DEC_B = 0, 3, 6, 10
    Q, K, V, O = (0, 64), (64, 64), (128, 64), (192, 64)
    ALL = (0, 256)

    def forward_mid(call, residual, gain, shift):
        vec, res = call.take(vectors), call.take(residual)
        kept = call.give((128, 1024), F32)

        def mid(get, total):
            stream = get(res)[...].astype(F32) + total
            get(kept)[...] = stream
            unit, scale = unit_of(stream)
            return (unit * get(vec)[gain : gain + 1] + get(vec)[shift : shift + 1]).astype(BF16)

        return mid

    def backward_mid(call, stream, gain, residual=None):
        vec, kept = call.take(vectors), call.take(stream)
        res = None if residual is None else call.take(residual)
        grad_out, share_out = call.give((128, 1024), F32), call.give((2, 1024), F32)

        def mid(get, total):
            grad, shares = norm_back(get(kept)[...].astype(F32), get(vec)[gain : gain + 1], total)
            if res is not None:
                grad = grad + get(res)[...]
            get(grad_out)[...] = grad
            get(share_out)[...] = shares
            return grad.astype(BF16)

        return mid

    def activated(call):
        hidden = call.give((4, 128, 1024), BF16)
        slope = call.give((4, 128, 1024), F32)

        def store(get, at, row, column, value):
            made, slopes = gelu_pair(value)
            get(hidden)[row, :, column : column + value.shape[1]] = made.astype(BF16)
            get(slope)[row, :, column : column + value.shape[1]] = slopes

        return store

    def deactivated(call, slope):
        kept, out = call.take(slope), call.give((4, 128, 1024), BF16)

        def store(get, at, row, column, value):
            span = slice(column, column + value.shape[1])
            get(out)[row, :, span] = (value * get(kept)[row, :, span]).astype(BF16)

        return store

    call = Call()

    def first_mid(stream, gain, shift):
        vec, res = call.take(vectors), call.take(stream)

        def mid(get, total):
            unit, scale = unit_of(get(res)[...].astype(F32))
            return (unit * get(vec)[gain : gain + 1] + get(vec)[shift : shift + 1]).astype(BF16)

        return mid

    jobs = []
    for stream, gain, shift in ((stream_in, ENC_G, ENC_B), (target_in, DEC_G, DEC_B)):
        jobs.append(Job(call, None, first_mid(stream, gain, shift), (None, None, None)))
    swap = Swap(call, [enc_up_p, cross_p, enc_down_p, dec_up_p, dec_down_p])
    outs = run_stage(call, jobs, [], "first_rows", 0, flops=30 * MICROSECOND, more=swap)
    rows_a, rows_c = outs[:2]
    enc_up_w, cross_w, enc_down_w, dec_up_w, dec_down_w = (
        gather_weights(packed) for packed in outs[2:]
    )

    call = Call()
    made, finishes, plans = [], [], []
    for rows, packed in ((rows_a, enc_w), (rows_c, self_w)):
        weight = Weight(call, packed, 0, 192)
        store, finish = query_and_shared(call, 256)
        plans.append((call.take(rows), weight, store))
        finishes.append(finish)

    def project(get):
        at = place()
        for unused, weight, unused2 in plans:
            weight.start(get)
        greet([at["core"]])
        for rows, weight, store in plans:
            weight.wait(get)
            for row in range(4):
                for m in range(3):
                    store(
                        get, at, row, m * 256, nt(get(rows)[row], weight.matrix(get, m * 64, 64))
                    )
        for finish in finishes:
            finish(get)

    enc_q, enc_kv, self_q, self_kv = call.run(project, "project", 1, 6 * MICROSECOND)

    enc_mixed, enc_total = attend(enc_q, enc_kv, source_facts, source_keys, False)
    self_mixed, self_total = attend(self_q, self_kv, target_facts, target_keys, True)

    call = Call()
    enc_o, enc_u = Weight(call, enc_w, *O), Weight(call, enc_up_w, *ALL)
    self_o, cross_a = Weight(call, self_w, *O), Weight(call, cross_w, *Q)
    mid_b = forward_mid(call, stream_in, ENC_G + 1, ENC_B + 1)
    job_b = Job(call, (enc_mixed, enc_o, [(0, 64)]), mid_b, (enc_u, [(0, 256)], activated(call)))
    mid_d = forward_mid(call, target_in, DEC_G + 1, DEC_B + 1)
    job_d = Job(call, (self_mixed, self_o, [(0, 64)]), mid_d, (cross_a, [(0, 64)], None))
    query = Plain(call, 256)
    job_d.right = (cross_a, [(0, 64)], query.store)
    (
        stream_mid,
        enc_hidden,
        enc_slope,
        rows_b,
        target_mid,
        rows_d,
        cross_q,
    ) = run_stage(
        call,
        [job_b, job_d],
        [enc_o, self_o, enc_u, cross_a],
        "after_self",
        2,
        flops=32 * MICROSECOND,
    )

    call = Call()
    enc_d, cross_b = Weight(call, enc_down_w, *ALL), Weight(call, cross_w, 64, 128)
    mid_m = forward_mid(call, stream_mid, ENC_G + 2, ENC_B + 2)
    shared = Shared(call, 512)
    job = Job(
        call, (enc_hidden, enc_d, [(0, 256)]), mid_m, (cross_b, [(0, 64), (64, 64)], shared.store)
    )
    stream_end, cross_kv, memory = run_stage(
        call, [job], [enc_d, cross_b], "memory", 3, shared.finish, 20 * MICROSECOND, core=True
    )

    cross_mixed, cross_total = attend(cross_q, cross_kv, target_facts, source_keys, False)

    call = Call()
    cross_o, dec_u = Weight(call, cross_w, *O), Weight(call, dec_up_w, *ALL)
    mid_e = forward_mid(call, target_mid, DEC_G + 2, DEC_B + 2)
    job = Job(call, (cross_mixed, cross_o, [(0, 64)]), mid_e, (dec_u, [(0, 256)], activated(call)))
    target_late, dec_hidden, dec_slope, rows_e = run_stage(
        call, [job], [cross_o, dec_u], "after_cross", 4, flops=20 * MICROSECOND
    )

    call = Call()
    dec_d = Weight(call, dec_down_w, *ALL)
    vec, res, cot = call.take(vectors), call.take(target_late), call.take(grad_out)
    decoded_out, grad_end_out = call.give((128, 1024), BF16), call.give((128, 1024), F32)
    share_out = call.give((2, 1024), F32)

    def last_mid(get, total):
        stream = get(res)[...] + total
        gain, shift = get(vec)[DEC_G + 3 : DEC_G + 4], get(vec)[DEC_B + 3 : DEC_B + 4]
        unit, unused = unit_of(stream)
        get(decoded_out)[...] = (unit * gain + shift).astype(BF16)
        grad, shares = norm_back(stream, gain, get(cot)[...].astype(F32))
        get(grad_end_out)[...] = grad
        get(share_out)[...] = shares
        return grad.astype(BF16)

    job = Job(
        call,
        (dec_hidden, dec_d, [(0, 256)]),
        last_mid,
        (dec_d, [(0, 256)], deactivated(call, dec_slope)),
    )
    decoded, grad_end, norm_3, dec_grad_act, grad_rows_e = run_stage(
        call, [job], [dec_d], "turn", 5, flops=20 * MICROSECOND
    )
    dec_up_s, dec_down_s = weight_shares(
        [[(dec_grad_act, 0, by_owner(rows_e))], [(dec_hidden, 0, by_owner(grad_rows_e))]], 15
    )
    dec_up_g, dec_down_g = over_slots(dec_up_s), over_slots(dec_down_s)

    call = Call()
    call.take(dec_up_s, pl.ANY)
    call.take(dec_down_s, pl.ANY)
    dec_u, cross_o = Weight(call, dec_up_w, *ALL), Weight(call, cross_w, *O)
    mid = backward_mid(call, target_late, DEC_G + 2, grad_end)
    query = Plain(call, 256)
    job = Job(call, (dec_grad_act, dec_u, [(0, 256)]), mid, (cross_o, [(0, 64)], query.store))
    grad_late, norm_2, cross_grad_mixed, grad_rows_d = run_stage(
        call, [job], [dec_u, cross_o], "back_cross", 6, flops=20 * MICROSECOND
    )

    cross_grads = attend_back(
        cross_q, cross_kv, cross_grad_mixed, cross_total, target_facts, source_keys, False, 7
    )
    memory_o, rows_o = by_owner(memory), by_owner(rows_d)
    (cross_s,) = weight_shares(
        [
            [
                (cross_grads, 0, rows_o),
                (cross_grads, 256, memory_o),
                (cross_grads, 512, memory_o),
                (cross_mixed, 0, by_owner(grad_rows_d)),
            ]
        ],
        16,
    )
    cross_g = over_slots(cross_s)

    call = Call()
    call.take(cross_s, pl.ANY)
    cross_a, cross_b = Weight(call, cross_w, *Q), Weight(call, cross_w, 64, 128)
    self_o, enc_d = Weight(call, self_w, *O), Weight(call, enc_down_w, *ALL)
    mid = backward_mid(call, target_mid, DEC_G + 1, grad_late)
    query = Plain(call, 256)
    job_t = Job(
        call, (cross_grads[:, :, :256], cross_a, [(0, 64)]), mid, (self_o, [(0, 64)], query.store)
    )
    mid = backward_mid(call, stream_end, ENC_G + 2)
    job_s = Job(
        call,
        (cross_grads[:, :, 256:], cross_b, [(0, 64), (64, 64)]),
        mid,
        (enc_d, [(0, 256)], deactivated(call, enc_slope)),
    )
    (
        grad_mid,
        norm_1,
        self_grad_mixed,
        grad_rows_c,
        grad_stream,
        enc_norm_2,
        enc_grad_act,
        grad_rows_b,
    ) = run_stage(
        call,
        [job_t, job_s],
        [cross_a, cross_b, self_o, enc_d],
        "back_both",
        8,
        flops=32 * MICROSECOND,
    )
    enc_up_s, enc_down_s = weight_shares(
        [[(enc_grad_act, 0, by_owner(rows_b))], [(enc_hidden, 0, by_owner(grad_rows_b))]], 17
    )
    enc_up_g, enc_down_g = over_slots(enc_up_s), over_slots(enc_down_s)

    self_grads = attend_back(
        self_q, self_kv, self_grad_mixed, self_total, target_facts, target_keys, True, 9, [enc_up_s, enc_down_s]
    )
    rows_o = by_owner(rows_c)
    (self_s,) = weight_shares(
        [
            [
                (self_grads, 0, rows_o),
                (self_grads, 256, rows_o),
                (self_grads, 512, rows_o),
                (self_mixed, 0, by_owner(grad_rows_c)),
            ]
        ],
        18,
    )
    self_g = over_slots(self_s)

    call = Call()
    for done in (self_s, dec_up_g, dec_down_g):
        call.take(done, pl.ANY)
    enc_u, enc_o, self_a = Weight(call, enc_up_w, *ALL), Weight(call, enc_w, *O), Weight(call, self_w, 0, 192)
    mid = backward_mid(call, stream_mid, ENC_G + 1, grad_stream)
    query = Plain(call, 256)
    job_s = Job(call, (enc_grad_act, enc_u, [(0, 256)]), mid, (enc_o, [(0, 64)], query.store))
    mid = backward_mid(call, target_in, DEC_G, grad_mid)
    job_t = Job(call, (self_grads, self_a, [(0, 64), (64, 64), (128, 64)]), mid, None)
    (
        grad_stream,
        enc_norm_1,
        enc_grad_mixed,
        grad_rows_a,
        target_grad,
        norm_0,
    ) = run_stage(
        call, [job_s, job_t], [enc_u, self_a, enc_o], "back_self", 10, flops=28 * MICROSECOND
    )

    enc_grads = attend_back(
        enc_q, enc_kv, enc_grad_mixed, enc_total, source_facts, source_keys, False, 11, [cross_g]
    )
    rows_o = by_owner(rows_a)
    (enc_s,) = weight_shares(
        [
            [
                (enc_grads, 0, rows_o),
                (enc_grads, 256, rows_o),
                (enc_grads, 512, rows_o),
                (enc_mixed, 0, by_owner(grad_rows_a)),
            ]
        ],
        19,
    )
    enc_g = over_slots(enc_s)

    call = Call()
    for done in (enc_s, enc_up_g, enc_down_g):
        call.take(done, pl.ANY)
    enc_a = Weight(call, enc_w, 0, 192)
    mid = backward_mid(call, stream_in, ENC_G, grad_stream)
    job = Job(call, (enc_grads, enc_a, [(0, 64), (64, 64), (128, 64)]), mid, None)
    source_grad, enc_norm_0 = run_stage(
        call, [job], [enc_a], "back_first", 12, flops=12 * MICROSECOND
    )

    norm_share = jnp.stack(
        [enc_norm_0, enc_norm_1, enc_norm_2], 1
    ).reshape(6, 1024)
    norm_share = jnp.concatenate(
        [
            norm_share,
            jnp.stack([norm_0, norm_1, norm_2, norm_3], 1).reshape(8, 1024),
            jnp.zeros((2, 1024), F32),
        ],
        0,
    )
    (decoded, source_grad, target_grad), swapped, norm_grad = close_program(
        [decoded, source_grad.astype(BF16), target_grad.astype(BF16)],
        by_owner(norm_share),
        [dec_up_g, dec_down_g, cross_g, enc_up_g, enc_down_g, self_g],
    )
    norm_grad = norm_grad.reshape(16, copies, 4, 32 // copies)
    if copies > 1:
        norm_grad = lax.psum_scatter(norm_grad, "k", scatter_dimension=1)
    norm_grad = norm_grad.reshape(16, 4, -1)
    norm_grad = lax.dynamic_index_in_dim(norm_grad, z, 1, False)
    (enc_g,) = swap_packs([enc_g], 20)

    def attend_shares(packed):
        grads = unpack(narrow(packed), 4)
        return jnp.swapaxes(grads[:3], 1, 2), grads[3]

    def feed_share(packed):
        return unpack(narrow(packed), 1)[0]

    dec_u, dec_d, enc_u, enc_d = (feed_share(swapped[i]) for i in (0, 1, 3, 4))
    dec_u, enc_u = dec_u.T, enc_u.T
    enc_a, enc_o = attend_shares(enc_g)
    cross_a, cross_o = attend_shares(swapped[2])
    self_a, self_o = attend_shares(swapped[5])
    return (
        decoded,
        source_grad.astype(F32),
        target_grad.astype(F32),
        enc_a,
        enc_o,
        enc_u,
        enc_d,
        norm_grad[:3],
        norm_grad[3:6],
        self_a,
        self_o,
        cross_a,
        cross_o,
        dec_u,
        dec_d,
        norm_grad[6:10],
        norm_grad[10:14],
    )


def solution(mesh):
    dp, seq, mp = (mesh.shape[name] for name in ("dp", "seq", "mp"))
    assert dp % 2 == 0 and seq == 4 and mp == 4
    fine = Mesh(mesh.devices.reshape(2, dp // 2, 2, 2, 4), AXES)
    d, s = ("hi", "k"), ("y", "c")
    rows = P(d, s + ("mp",), None)
    three, flat = P(None, d + s, "mp"), P("mp", d + s)
    up, vector = P(d + s, "mp"), P(None, d + s + ("mp",))
    attention, feeding = (three, flat), (up, flat)
    return jax.shard_map(
        local,
        mesh=fine,
        in_specs=(rows,) * 3
        + (P(d), P(d), P(d, None), P(d, None))
        + attention
        + feeding
        + (vector, vector)
        + attention * 2
        + feeding
        + (vector, vector),
        out_specs=(rows,) * 3
        + attention
        + feeding
        + (vector, vector)
        + attention * 2
        + feeding
        + (vector, vector),
        check_vma=False,
    )
```

```python
import math

import jax
import jax.numpy as jnp
from jax import lax
from jax.experimental import pallas as pl
from jax.experimental.pallas import tpu as pltpu
from jax.sharding import Mesh, PartitionSpec as P

HEAD_DIM = 64
EPSILON = 1e-05
MASKED = -1000000000.0
AXES = ("hi", "k", "y", "c", "mp")
MESH_ID = pl.DeviceIdType.MESH
F32 = jnp.float32
BF16 = jnp.bfloat16


class Call:
    def __init__(self):
        self.known, self.arrays, self.specs = [], [], []
        self.shapes, self.places, self.scratch = [], [], []
        self.fetched, self.kept = [], []

    def take(self, array, space=pltpu.VMEM):
        for i, known in enumerate(self.known):
            if known is array and self.specs[i].memory_space == space:
                return ("in", i)
        self.known.append(array)
        if space == pltpu.HBM:
            array = pltpu.with_memory_space_constraint(array, pltpu.HBM)
        self.arrays.append(array)
        self.specs.append(pl.BlockSpec(memory_space=space))
        return ("in", len(self.arrays) - 1)

    def fetch(self, array):
        source = self.take(array, pltpu.HBM)
        for i, (known, room, sem) in enumerate(self.fetched):
            if known == source:
                return ("fetch", i)
        self.fetched.append((source, self.hold(array.shape, array.dtype), self.sems(1)))
        return ("fetch", len(self.fetched) - 1)

    def give(self, shape, dtype, space=pltpu.VMEM):
        if space == pltpu.HBM:
            self.shapes.append(pltpu.HBM(shape, dtype))
        else:
            self.shapes.append(jax.ShapeDtypeStruct(shape, dtype))
        self.places.append(pl.BlockSpec(memory_space=space))
        return ("out", len(self.shapes) - 1)

    def keep(self, shape, dtype, parts=1):
        target = self.give(shape, dtype, pltpu.HBM)
        self.kept.append((target, self.hold(shape, dtype), self.sems(parts)))
        return ("keep", len(self.kept) - 1)

    def hold(self, shape, dtype):
        self.scratch.append(pltpu.VMEM(shape, dtype))
        return ("tmp", len(self.scratch) - 1)

    def sems(self, count):
        self.scratch.append(pltpu.SemaphoreType.DMA((count,)))
        return ("tmp", len(self.scratch) - 1)

    def save(self, get, handle, row=None):
        target, room, sems = (get(part) for part in self.kept[handle[1]])
        if row is not None:
            target, room = target.at[row], room.at[row]
        count = sum(1 for known, unused in self.saves if known == handle)
        copy = pltpu.make_async_copy(room, target, sems.at[count])
        copy.start()
        self.saves.append((handle, copy))

    def run(self, body, name, collective=None, flops=0):
        ins, outs = len(self.arrays), len(self.shapes)

        def kernel(*refs):
            parts = {"in": refs[:ins], "out": refs[ins : ins + outs], "tmp": refs[ins + outs :]}
            here, self.saves = set(), []

            def get(handle):
                kind, i = handle
                if kind == "keep":
                    return get(self.kept[i][1])
                if kind != "fetch":
                    return parts[kind][i]
                source, room, sem = (get(part) for part in self.fetched[i])
                if i not in here:
                    here.add(i)
                    pltpu.make_async_copy(source, room, sem.at[0]).wait()
                return room

            for source, room, sem in self.fetched:
                pltpu.make_async_copy(get(source), get(room), get(sem).at[0]).start()
            body(get)
            for i in range(len(self.fetched)):
                get(("fetch", i))
            for handle, copy in self.saves:
                copy.wait()

        held = [a for a, spec in zip(self.arrays, self.specs) if spec.memory_space == pltpu.VMEM]
        held += [a for a, spec in zip(self.shapes, self.places) if spec.memory_space == pltpu.VMEM]
        held += [x for x in self.scratch if x.dtype in (BF16, F32)]
        room = sum(math.prod(x.shape) * jnp.dtype(x.dtype).itemsize for x in held)
        return pl.pallas_call(
            kernel,
            out_shape=tuple(self.shapes),
            in_specs=self.specs,
            out_specs=tuple(self.places),
            scratch_shapes=self.scratch,
            compiler_params=pltpu.CompilerParams(
                collective_id=collective,
                has_side_effects=collective is not None,
                vmem_limit_bytes=room + (8 << 20),
            ),
            cost_estimate=pl.CostEstimate(flops=flops, bytes_accessed=0, transcendentals=0),
            name=name,
        )(*self.arrays)


MICROSECOND = 1_000_000_000


def nt(left, right):
    return lax.dot_general(left, right, (((1,), (1,)), ((), ())), preferred_element_type=F32)


def nn(left, right):
    return lax.dot_general(left, right, (((1,), (0,)), ((), ())), preferred_element_type=F32)


def tn(left, right):
    return lax.dot_general(left, right, (((0,), (0,)), ((), ())), preferred_element_type=F32)


def unit_of(stream):
    average = jnp.mean(stream, -1, keepdims=True)
    centred = stream - average
    scale = lax.rsqrt(jnp.mean(centred * centred, -1, keepdims=True) + EPSILON)
    return centred * scale, scale


def norm_back(stream, gain, upstream):
    unit, scale = unit_of(stream)
    inner = upstream * gain
    grad = scale * (
        inner - jnp.mean(inner, -1, keepdims=True) - unit * jnp.mean(inner * unit, -1, keepdims=True)
    )
    shares = jnp.concatenate(
        [jnp.sum(upstream * unit, 0, keepdims=True), jnp.sum(upstream, 0, keepdims=True)], 0
    )
    return grad, shares


def gelu_pair(act):
    bell = 0.5 + 0.5 * lax.erf(act * 0.7071067811865476)
    slope = bell + act * (jnp.exp(act * act * -0.5) * 0.3989422804014327)
    return act * bell, slope


def place():
    hi, k, y, c, z = (lax.axis_index(name) for name in AXES)
    return {
        "x": (1 - hi, k, y, c, z),
        "y": (hi, k, 1 - y, c, z),
        "d": (1 - hi, k, 1 - y, c, z),
        "core": (hi, k, y, 1 - c, z),
        "mesh": (hi, k, y, c, z),
        "own_row": y * 2 + hi,
        "x_row": y * 2 + 1 - hi,
        "y_row": (1 - y) * 2 + hi,
        "d_row": (1 - y) * 2 + 1 - hi,
    }


def greet(partners):
    barrier = pltpu.get_barrier_semaphore()
    for partner in partners:
        pl.semaphore_signal(barrier, inc=1, device_id=partner, device_id_type=MESH_ID)
    pl.semaphore_wait(barrier, len(partners))


class Weight:
    def __init__(self, call, packed, first, count):
        self.source = call.take(packed, pltpu.HBM)
        self.room = call.hold((4, count, 1024), BF16)
        self.sem = call.sems(1)
        self.first, self.count = first, count

    def start(self, get):
        source, room, sem = get(self.source), get(self.room), get(self.sem)
        for q in range(4):
            for c in range(2):
                pltpu.make_async_copy(
                    source.at[c, :, q, pl.ds(self.first, self.count), :],
                    room.at[:, :, pl.ds((q * 2 + c) * 128, 128)],
                    sem.at[0],
                ).start()

    def wait(self, get):
        room = get(self.room)
        pltpu.make_async_copy(room, room, get(self.sem).at[0]).wait()

    def matrix(self, get, first, count):
        return get(self.room)[:, first : first + count, :].reshape(4 * count, 1024)


class Feed:
    def __init__(self, call, rows, up, down):
        self.call, self.rows, self.weights = call, call.fetch(rows), [up, down]
        self.hidden = call.keep((4, 128, 1024), BF16, 4)
        self.slope = call.keep((4, 128, 1024), F32, 4)

    def part(self, get, row):
        up, down = self.weights
        made, slope = gelu_pair(nt(get(self.rows)[row], up.matrix(get, 0, 256)))
        made = made.astype(BF16)
        get(self.hidden)[row] = made
        get(self.slope)[row] = slope
        self.call.save(get, self.hidden, row)
        self.call.save(get, self.slope, row)
        return nn(made, down.matrix(get, 0, 256))


class Job:
    def __init__(self, call, left, mid, right):
        self.call, self.left, self.mid, self.right = call, left, mid, right
        if left is not None:
            self.rows_in = None if isinstance(left, Feed) else call.fetch(left[0])
            self.out_first = call.hold((2, 128, 1024), BF16)
            self.out_edge = call.hold((2, 64, 1024), BF16)
            self.out_late = call.hold((2, 64, 1024), BF16)
            self.keep = call.hold((2, 64, 1024), F32)
            self.own = call.hold((128, 1024), F32)
            self.landed = call.hold((6, 64, 1024), BF16)
            self.sum_send, self.sum_recv = call.sems(6), call.sems(6)
        self.gathered = None
        if right is not None:
            self.gathered = call.keep((4, 128, 1024), BF16, 4)
            self.row_send, self.row_recv = call.sems(6), call.sems(6)

    def lefts(self):
        return self.left.weights if isinstance(self.left, Feed) else [self.left[1]]

    def part(self, get, row):
        if isinstance(self.left, Feed):
            return self.left.part(get, row)
        unused, weight, picks, column = self.left
        total = None
        for first, count in picks:
            width = 4 * count
            left = get(self.rows_in)[row, :, column : column + width]
            term = nn(left, weight.matrix(get, first, count))
            total = term if total is None else total + term
            column += width
        return total

    def send(self, get, i, source, target, partner):
        copy = pltpu.make_async_remote_copy(
            src_ref=source,
            dst_ref=target,
            send_sem=get(self.sum_send).at[i],
            recv_sem=get(self.sum_recv).at[i],
            device_id=partner,
            device_id_type=MESH_ID,
        )
        copy.start()
        return copy

    def sum_start(self, get, at):
        first, edge, landed = get(self.out_first), get(self.out_edge), get(self.landed)
        keep = get(self.keep)
        self.copies = [None] * 6
        first[0] = self.part(get, at["d_row"]).astype(BF16)
        self.copies[0] = self.send(
            get, 0, first.at[0, pl.ds(0, 64)], landed.at[0], at["x"]
        )
        self.copies[1] = self.send(
            get, 1, first.at[0, pl.ds(64, 64)], landed.at[1], at["y"]
        )
        part = self.part(get, at["x_row"])
        edge[0] = part[:64].astype(BF16)
        keep[0] = part[64:]
        self.copies[2] = self.send(get, 2, edge.at[0], landed.at[2], at["x"])
        part = self.part(get, at["y_row"])
        edge[1] = part[64:].astype(BF16)
        keep[1] = part[:64]
        self.copies[3] = self.send(get, 3, edge.at[1], landed.at[3], at["y"])
        get(self.own)[...] = self.part(get, at["own_row"])

    def sum_forward(self, get, at):
        late, landed, keep = get(self.out_late), get(self.landed), get(self.keep)
        self.copies[0].wait_recv()
        late[1] = (keep[1] + landed[0].astype(F32)).astype(BF16)
        self.copies[4] = self.send(get, 4, late.at[1], landed.at[4], at["y"])
        self.copies[1].wait_recv()
        late[0] = (keep[0] + landed[1].astype(F32)).astype(BF16)
        self.copies[5] = self.send(get, 5, late.at[0], landed.at[5], at["x"])

    def sum_end(self, get):
        landed, own = get(self.landed), get(self.own)
        for i in (2, 3, 4, 5):
            self.copies[i].wait_recv()
        upper = own[:64] + landed[2].astype(F32) + landed[4].astype(F32)
        lower = own[64:] + landed[5].astype(F32) + landed[3].astype(F32)
        return jnp.concatenate([upper, lower], 0)

    def row_copy(self, get, i, row, half, partner):
        block = get(self.gathered).at[row, pl.ds(half * 64, 64)]
        copy = pltpu.make_async_remote_copy(
            src_ref=block,
            dst_ref=block,
            send_sem=get(self.row_send).at[i],
            recv_sem=get(self.row_recv).at[i],
            device_id=partner,
            device_id_type=MESH_ID,
        )
        copy.start()
        return copy

    def rows_start(self, get, at, normed):
        get(self.gathered)[at["own_row"]] = normed
        self.call.save(get, self.gathered, at["own_row"])
        self.moves = [
            self.row_copy(get, 0, at["own_row"], 0, at["y"]),
            self.row_copy(get, 1, at["own_row"], 1, at["x"]),
            self.row_copy(get, 2, at["own_row"], 1, at["y"]),
            self.row_copy(get, 3, at["own_row"], 0, at["x"]),
        ]

    def rows_forward(self, get, at):
        self.moves[0].wait_recv()
        self.moves.append(self.row_copy(get, 4, at["y_row"], 0, at["x"]))
        self.moves[1].wait_recv()
        self.moves.append(self.row_copy(get, 5, at["x_row"], 1, at["y"]))

    def product(self, get, at, row):
        weight, picks, store = self.right
        rows = get(self.gathered)[row]
        column = 0
        for first, count in picks:
            store(get, at, row, column, nt(rows, weight.matrix(get, first, count)))
            column += 4 * count

    def drain(self):
        if self.left is not None:
            for copy in self.copies:
                copy.wait_send()
        if self.right is not None:
            for copy in self.moves:
                copy.wait_send()


class Extra:
    def partners(self, at):
        return []

    def start(self, get, at):
        return None

    def middle(self, get, at):
        return None

    def late(self, get, at):
        return None

    def finish(self, get, at):
        return None


def run_stage(call, jobs, weights, name, collective, finish=None, flops=0, core=False, more=()):
    def body(get):
        at = place()
        for weight in weights:
            weight.start(get)
        partners = [at["x"], at["y"]] + ([at["core"]] if core else [])
        for extra in more:
            partners += [p for p in extra.partners(at) if all(p is not q for q in partners)]
        greet(partners)
        lefts = [job for job in jobs if job.left is not None]
        movers = [job for job in jobs if job.right is not None]
        rights = [job for job in movers if job.right[0] is not None]
        waited = []

        def ready(weight):
            if weight not in waited:
                weight.wait(get)
                waited.append(weight)

        def arrived(job, row):
            call.save(get, job.gathered, row)
            if job in rights:
                job.product(get, at, row)

        for job in lefts:
            for weight in job.lefts():
                ready(weight)
            job.sum_start(get, at)
        for job in lefts:
            job.sum_forward(get, at)
        for extra in more:
            extra.middle(get, at)
        for job in jobs:
            normed = job.mid(get, job.sum_end(get) if job.left is not None else None)
            if job.right is not None:
                job.rows_start(get, at, normed)
        for extra in more:
            extra.start(get, at)
        for weight in weights:
            ready(weight)
        for extra in more:
            extra.late(get, at)
        for job in rights:
            job.product(get, at, at["own_row"])
        for job in movers:
            job.rows_forward(get, at)
        for job in movers:
            job.moves[3].wait_recv()
            arrived(job, at["x_row"])
            job.moves[2].wait_recv()
            arrived(job, at["y_row"])
        for job in movers:
            job.moves[4].wait_recv()
            job.moves[5].wait_recv()
            arrived(job, at["d_row"])
        for job in jobs:
            job.drain()
        if finish is not None:
            finish(get)
        for extra in more:
            extra.finish(get, at)

    return call.run(body, name, collective, flops)


class Plain:
    def __init__(self, call, width):
        self.call, self.width = call, width
        self.out = call.keep((4, 128, width), BF16, 4)

    def store(self, get, at, row, column, value):
        get(self.out)[row, :, column : column + value.shape[1]] = value.astype(BF16)
        if column + value.shape[1] == self.width:
            self.call.save(get, self.out, row)


class Shared:
    def __init__(self, call, width, skip=0):
        self.call, self.out = call, call.keep((2, 4, 128, width), BF16, 2)
        self.send_sem, self.recv_sem = call.sems(4), call.sems(4)
        self.width, self.skip, self.copies, self.blocks = width, skip, [], 0

    def store(self, get, at, row, column, value):
        out = get(self.out)
        column = column - self.skip
        out[0, row, :, column : column + value.shape[1]] = value.astype(BF16)
        if column + value.shape[1] == self.width:
            i = len(self.copies)
            copy = pltpu.make_async_remote_copy(
                src_ref=out.at[0, row],
                dst_ref=out.at[1, row],
                send_sem=get(self.send_sem).at[i],
                recv_sem=get(self.recv_sem).at[i],
                device_id=at["core"],
                device_id_type=MESH_ID,
            )
            copy.start()
            self.copies.append(copy)

    def finish(self, get):
        self.call.save(get, self.out, 0)
        for copy in self.copies:
            copy.wait()
        self.call.save(get, self.out, 1)


def query_and_shared(call, width):
    query, shared = Plain(call, width), Shared(call, 2 * width, skip=width)

    def store(get, at, row, column, value):
        if column < width:
            query.store(get, at, row, column, value)
        else:
            shared.store(get, at, row, column, value)

    return store, shared.finish


def lanes_of(head, rows):
    lane = lax.broadcasted_iota(jnp.int32, (rows, 128), 1)
    return lane // HEAD_DIM == head


def allowed_bias(facts_ref, keys_ref, causal):
    key = keys_ref[...]
    query = facts_ref[...]
    allowed = (key[:, 0:1] == query[0:1, :]) & (key[:, 2:3] > 0)
    if causal:
        allowed = allowed & (key[:, 1:2] <= query[1:2, :])
    return jnp.where(allowed, 0.0, MASKED)


def attend(queries, key_value, facts, keys, causal):
    rows, width = 512, queries.shape[-1]
    half = rows // 2
    call = Call()
    q_in = call.fetch(queries.reshape(rows, width))
    kv_in = call.fetch(key_value.reshape(1024, 2 * width))
    facts_in, keys_in = call.take(facts), call.take(keys)
    mixed_out, total_out = call.keep((rows, width), BF16, 2), call.give((8, rows), F32)
    bias = call.hold((1024, rows), F32)

    def body(get):
        mask = get(bias)
        mask[...] = allowed_bias(get(facts_in), get(keys_in), causal)
        q_ref, kv_ref, mixed_ref, total_ref = get(q_in), get(kv_in), get(mixed_out), get(total_out)

        def pair_step(pair, carry):
            lanes = pl.ds(pl.multiple_of(pair * 128, 128), 128)
            value_lanes = pl.ds(pl.multiple_of(256 + pair * 128, 128), 128)
            keys, values = kv_ref[:, lanes], kv_ref[:, value_lanes]
            for block in range(2):
                span = slice(block * half, (block + 1) * half)
                queries = q_ref[span, lanes]
                mixed = []
                for head in range(2):
                    picked = jnp.where(lanes_of(head, half), queries * 0.125, 0.0).astype(BF16)
                    scores = nt(keys, picked) + mask[:, span]
                    top = jnp.max(scores, 0, keepdims=True)
                    raised = jnp.exp(scores - top)
                    total = jnp.sum(raised, 0, keepdims=True)
                    probs = (raised * (1.0 / total)).astype(BF16)
                    mixed.append(tn(values, probs)[head * HEAD_DIM : (head + 1) * HEAD_DIM])
                    total_ref[pl.ds(pair * 2 + head, 1), span] = top + jnp.log(total)
                mixed_ref[span, lanes] = jnp.concatenate(mixed, 0).T.astype(BF16)
            return carry

        lax.fori_loop(0, 2, pair_step, 0)
        call.save(get, mixed_out)

    mixed, total = call.run(body, "attend", None, 8 * MICROSECOND)
    return mixed.reshape(4, 128, width), total


def attend_back(
    queries, key_value, grad_mixed, total, facts, keys, causal, collective, done=()
):
    rows, width = 512, queries.shape[-1]
    half = rows // 2
    call = Call()
    q_in = call.fetch(queries.reshape(rows, width))
    kv_in = call.fetch(key_value.reshape(1024, 2 * width))
    grad_in, total_in = call.fetch(grad_mixed.reshape(rows, width)), call.take(total)
    facts_in, keys_in = call.take(facts), call.take(keys)
    for array in done:
        call.take(array, pltpu.HBM)
    grad_out = call.keep((rows, 3 * width), BF16)
    bias = call.hold((1024, rows), F32)
    gathered = call.hold((1024, 4 * 128), F32)
    outgoing, landed = call.hold((2, 512, 256), BF16), call.hold((2, 512, 256), BF16)
    send_sem, recv_sem = call.sems(2), call.sems(2)

    def body(get):
        at = place()
        out, mask, sums = get(grad_out), get(bias), get(gathered)
        away, here = get(outgoing), get(landed)
        mask[...] = allowed_bias(get(facts_in), get(keys_in), causal)
        greet([at["core"]])
        q_ref, kv_ref, grad_ref, total_ref = get(q_in), get(kv_in), get(grad_in), get(total_in)
        copies = []
        for pair in range(2):
            lanes = slice(pair * 128, pair * 128 + 128)
            keys_pair = kv_ref[:, lanes]
            values_pair = kv_ref[:, 256 + pair * 128 : 256 + pair * 128 + 128]
            key_sum = slice(pair * 256, pair * 256 + 128)
            value_sum = slice(pair * 256 + 128, pair * 256 + 256)
            for block in range(2):
                span = slice(block * half, (block + 1) * half)
                q_block, g_block = q_ref[span, lanes], grad_ref[span, lanes]
                grad_query = []
                for head in range(2):
                    inside = lanes_of(head, half)
                    picked = jnp.where(inside, q_block * 1.0, 0.0).astype(BF16)
                    grads = jnp.where(inside, g_block * 1.0, 0.0).astype(BF16)
                    scores = nt(keys_pair, picked) * 0.125 + mask[:, span]
                    probs = jnp.exp(scores - total_ref[pair * 2 + head : pair * 2 + head + 1, span])
                    weighted = probs * nt(values_pair, grads)
                    inner = jnp.sum(weighted, 0, keepdims=True)
                    grad_raw = ((weighted - probs * inner) * 0.125).astype(BF16)
                    value_term = nn(probs.astype(BF16), grads)
                    key_term = nn(grad_raw, picked)
                    if block == 0 and head == 0:
                        sums[:, key_sum] = key_term
                        sums[:, value_sum] = value_term
                    else:
                        sums[:, key_sum] += key_term
                        sums[:, value_sum] += value_term
                    grad_query.append(tn(keys_pair, grad_raw)[head * HEAD_DIM : (head + 1) * HEAD_DIM])
                out[span, lanes] = jnp.concatenate(grad_query, 0).T.astype(BF16)
            away[pair] = sums[512:, pair * 256 : pair * 256 + 256].astype(BF16)
            copy = pltpu.make_async_remote_copy(
                src_ref=away.at[pair],
                dst_ref=here.at[pair],
                send_sem=get(send_sem).at[pair],
                recv_sem=get(recv_sem).at[pair],
                device_id=at["core"],
                device_id_type=MESH_ID,
            )
            copy.start()
            copies.append(copy)
        for pair in range(2):
            copies[pair].wait()
            both = sums[:512, pair * 256 : pair * 256 + 256] + here[pair].astype(F32)
            out[:, width + pair * 128 : width + pair * 128 + 128] = both[:, :128].astype(BF16)
            out[:, 2 * width + pair * 128 : 2 * width + pair * 128 + 128] = both[:, 128:].astype(BF16)
        call.save(get, grad_out)

    (grads,) = call.run(body, "attend_back", collective, 16 * MICROSECOND)
    return grads.reshape(4, 128, 3 * width)


class Shares(Extra):
    def __init__(self, call, pairs, count):
        self.call, self.count = call, count
        self.handles = [
            (call.fetch(left.reshape(512, -1)), column, call.fetch(by_owner(right).reshape(512, 1024)))
            for left, column, right in pairs
        ]
        shape = (4, 4, len(pairs) * count, 128)
        sends = len(pairs) * max(1, count // 64)
        self.made, self.landed = call.hold((2,) + shape, BF16), call.hold(shape, BF16)
        self.send_sem, self.recv_sem = call.sems(sends), call.sems(sends)
        self.out = call.keep(shape, BF16)

    def partners(self, at):
        return [at["core"]]

    def send(self, get, at, part):
        i = len(self.copies)
        copy = pltpu.make_async_remote_copy(
            src_ref=get(self.made).at[(1 - lax.axis_index("c"),) + part],
            dst_ref=get(self.landed).at[part],
            send_sem=get(self.send_sem).at[i],
            recv_sem=get(self.recv_sem).at[i],
            device_id=at["core"],
            device_id_type=MESH_ID,
        )
        copy.start()
        self.copies.append((part, copy))

    def middle(self, get, at):
        self.copies, every, count = [], slice(None), self.count
        made = get(self.made)
        for m, (left, column, right) in enumerate(self.handles):
            left, right = get(left), get(right)
            span = slice(m * count, (m + 1) * count)
            for first in range(0, 4 * count, 256):
                product = tn(left[:, column + first : column + first + 256], right[...])
                for inner in range(0, 256, count):
                    z = (first + inner) // count
                    for d in range(8):
                        made[d % 2, z, d // 2, span, :] = product[
                            inner : inner + count, d * 128 : d * 128 + 128
                        ].astype(BF16)
                if count == 256:
                    self.send(get, at, (first // 256, every, pl.ds(m * count, count)))
            if count < 256:
                self.send(get, at, (every, every, pl.ds(m * count, count)))

    def finish(self, get, at):
        core = lax.axis_index("c")
        for part, copy in self.copies:
            copy.wait()
            own = get(self.made)[(core,) + part].astype(F32)
            get(self.out)[part] = (own + get(self.landed)[part].astype(F32)).astype(BF16)
        self.call.save(get, self.out)


def weight_shares(pairs, count, collective):
    call = Call()
    shares = Shares(call, pairs, count)

    def body(get):
        at = place()
        greet([at["core"]])
        shares.middle(get, at)
        shares.finish(get, at)

    (made,) = call.run(body, "weight_shares", collective, len(pairs) * count // 64 * MICROSECOND)
    return made


class Swap(Extra):
    def __init__(self, call, packs):
        self.packs = [call.take(pack) for pack in packs]
        self.outs = [call.give(pack.shape, pack.dtype) for pack in packs]
        self.send_sem, self.recv_sem = call.sems(3 * len(packs)), call.sems(3 * len(packs))

    def start(self, get, at):
        hi, k, y, c, z = at["mesh"]
        own = hi * 2 + y
        self.copies = []
        for pack, out in zip(self.packs, self.outs, strict=True):
            pack, out = get(pack), get(out)
            for name, q in (
                ("d", (1 - hi) * 2 + 1 - y),
                ("x", (1 - hi) * 2 + y),
                ("y", hi * 2 + 1 - y),
            ):
                i = len(self.copies)
                copy = pltpu.make_async_remote_copy(
                    src_ref=pack.at[q],
                    dst_ref=out.at[own],
                    send_sem=get(self.send_sem).at[i],
                    recv_sem=get(self.recv_sem).at[i],
                    device_id=at[name],
                    device_id_type=MESH_ID,
                )
                copy.start()
                self.copies.append(copy)
            out[own] = pack[own]

    def partners(self, at):
        return [at["x"], at["y"], at["d"]]

    def finish(self, get, at):
        for copy in self.copies:
            copy.wait()


class Local(Extra):
    def __init__(self, work):
        self.late = work


class Slots(Extra):
    def __init__(self, call, arrays, inward):
        self.inward = inward
        self.arrays = [call.take(array) for array in arrays]
        shape = (128, 1024) if inward else (2, 64, 1024)
        self.outs = [call.give(shape, array.dtype) for array in arrays]
        self.send_sem, self.recv_sem = call.sems(2 * len(arrays)), call.sems(2 * len(arrays))

    def ends(self, get, at, j, step):
        z = at["mesh"][4]
        low = lax.div(z, 2)
        other = low if step == 0 else 1 - low
        array, out = get(self.arrays[j]), get(self.outs[j])
        if self.inward:
            return array.at[other], out.at[pl.ds(pl.multiple_of(low * 64, 64), 64)]
        return array.at[pl.ds(pl.multiple_of(other * 64, 64), 64)], out.at[low]

    def partners(self, at):
        return all_partners(at)[1]

    def stays(self, at):
        hi, z = at["mesh"][0], at["mesh"][4]
        return lax.rem(z, 2) == hi

    def copy(self, get, at, j, step):
        hi, k, y, c, z = at["mesh"]
        low = lax.div(z, 2)
        partner = (lax.rem(z, 2), k, y, c, 2 * (low if step == 0 else 1 - low) + hi)
        source, target = self.ends(get, at, j, step)
        return pltpu.make_async_remote_copy(
            src_ref=source,
            dst_ref=target,
            send_sem=get(self.send_sem).at[2 * j + step],
            recv_sem=get(self.recv_sem).at[2 * j + step],
            device_id=partner,
            device_id_type=MESH_ID,
        )

    def start(self, get, at):
        stays = self.stays(at)
        for j in range(len(self.arrays)):
            self.copy(get, at, j, 1).start()

        @pl.when(jnp.logical_not(stays))
        def _():
            for j in range(len(self.arrays)):
                self.copy(get, at, j, 0).start()

        @pl.when(stays)
        def _():
            for j in range(len(self.arrays)):
                source, target = self.ends(get, at, j, 0)
                target[...] = source[...]

    def finish(self, get, at):
        for j in range(len(self.arrays)):
            self.copy(get, at, j, 1).wait()

        @pl.when(jnp.logical_not(self.stays(at)))
        def _():
            for j in range(len(self.arrays)):
                self.copy(get, at, j, 0).wait()


def all_partners(at):
    hi, k, y, c, z = at["mesh"]
    plane = [
        ((hi + i) % 2, k, (y + j) % 2, (c + n) % 2, z)
        for i in range(2)
        for j in range(2)
        for n in range(2)
        if i + j + n > 0
    ]
    ways = [((hi + i) % 2, k, y, c, (z + n) % 4) for i in range(2) for n in range(1, 4)]
    return plane, ways


def meet(at):
    plane, ways = all_partners(at)
    greet(plane + ways)
    return plane


def open_program(rows, vectors, facts, packs):
    call = Call()
    slots, swap = Slots(call, rows, True), Swap(call, packs)
    vec_in, fact_in = call.take(vectors), call.take(facts)
    vec_out, fact_out = call.give((16, 1024), F32), call.give((2,) + facts.shape, facts.dtype)
    landed, whole = call.hold((3, 16, 128), F32), call.hold((16, 128), F32)
    vec_send, vec_recv = call.sems(11), call.sems(11)

    def body(get):
        at = place()
        plane = meet(at)
        hi, k, y, c, z = at["mesh"]
        send, recv = get(vec_send), get(vec_recv)

        def push(i, source, target, partner):
            copy = pltpu.make_async_remote_copy(
                src_ref=source,
                dst_ref=target,
                send_sem=send.at[i],
                recv_sem=recv.at[i],
                device_id=partner,
                device_id_type=MESH_ID,
            )
            copy.start()
            return copy

        first = [
            push(n - 1, get(vec_in), get(landed).at[n - 1], (hi, k, y, c, (z + n) % 4))
            for n in range(1, 4)
        ]
        fact_copy = push(10, get(fact_in), get(fact_out).at[1], at["x"])
        slots.start(get, at)
        swap.start(get, at)
        get(fact_out)[0] = get(fact_in)[...]
        for copy in first:
            copy.wait()
        parts = get(landed)
        get(whole)[...] = get(vec_in)[...] + parts[0] + parts[1] + parts[2]
        block = pl.ds(pl.multiple_of(((hi * 2 + y) * 2 + c) * 128, 128), 128)
        second = [
            push(3 + i, get(whole), get(vec_out).at[:, block], partner)
            for i, partner in enumerate(plane)
        ]
        get(vec_out)[:, block] = get(whole)[...]
        for copy in second:
            copy.wait()
        fact_copy.wait()
        slots.finish(get, at)
        swap.finish(get, at)

    outs = call.run(body, "open_program", 13, 12 * MICROSECOND)
    n, m = len(rows), len(packs)
    return outs[:n], outs[n : n + m], outs[n + m], outs[n + m + 1]


def close_program(rows, vectors, packs):
    call = Call()
    slots, swap = Slots(call, rows, False), Swap(call, packs)
    vec_in = call.take(vectors)
    vec_out = call.give((16, 128), F32)
    landed, block_sum = call.hold((7, 16, 128), F32), call.hold((16, 128), F32)
    blocks, along = call.hold((8, 16, 128), F32), call.hold((3, 16, 128), F32)
    vec_send, vec_recv = call.sems(10), call.sems(10)

    def body(get):
        at = place()
        plane = meet(at)
        hi, k, y, c, z = at["mesh"]
        send, recv = get(vec_send), get(vec_recv)
        split = get(blocks)
        for d in range(8):
            split[d] = get(vec_in)[:, d * 128 : d * 128 + 128]

        def push(i, source, target, partner):
            copy = pltpu.make_async_remote_copy(
                src_ref=source,
                dst_ref=target,
                send_sem=send.at[i],
                recv_sem=recv.at[i],
                device_id=partner,
                device_id_type=MESH_ID,
            )
            copy.start()
            return copy

        first = [
            push(
                i,
                split.at[(partner[0] * 2 + partner[2]) * 2 + partner[3]],
                get(landed).at[i],
                partner,
            )
            for i, partner in enumerate(plane)
        ]
        slots.start(get, at)
        swap.start(get, at)
        for copy in first:
            copy.wait()
        total = split[(hi * 2 + y) * 2 + c]
        for i in range(7):
            total = total + get(landed)[i]
        get(block_sum)[...] = total
        second = [
            push(6 + n, get(block_sum), get(along).at[n - 1], (hi, k, y, c, (z + n) % 4))
            for n in range(1, 4)
        ]
        for copy in second:
            copy.wait()
        get(vec_out)[...] = get(block_sum)[...] + get(along)[0] + get(along)[1] + get(along)[2]
        slots.finish(get, at)
        swap.finish(get, at)

    outs = call.run(body, "close_program", 14, 16 * MICROSECOND)
    n, m = len(rows), len(packs)
    return outs[:n], outs[n : n + m], outs[n + m]


def swap_packs(packs, collective):
    call = Call()
    swap = Swap(call, packs)

    def body(get):
        at = place()
        greet([at["x"], at["y"], at["d"]])
        swap.start(get, at)
        swap.finish(get, at)

    return call.run(body, "swap_packs", collective, 5 * MICROSECOND)


def transposed(qkv):
    return [qkv[i].T for i in range(3)]


def pack_rows(matrices):
    stacked = jnp.stack(matrices)
    count, units, width = stacked.shape
    return jnp.swapaxes(stacked.reshape(count, 4, units // 4, width), 0, 1).reshape(4, -1, width)


def over_slots(shares):
    return lax.psum_scatter(shares, "mp", scatter_dimension=0)


def widen(packed):
    return packed if lax.axis_size("k") == 1 else lax.all_gather(packed, "k", axis=2, tiled=True)


def gather_weights(packed):
    copies = lax.axis_size("k")
    rows, width = packed.shape[1], 128 // copies
    packed = lax.all_gather(packed, ("c", "mp")).reshape(2, 4, 4, rows, 128)
    if copies > 1:
        packed = packed.reshape(2, 4, 2, 2, rows, copies, width)
        packed = packed.transpose(1, 4, 2, 5, 3, 0, 6).reshape(4, rows, 4, 2, 128)
        packed = packed.transpose(3, 0, 2, 1, 4)
    return packed


def by_owner(rights):
    copies = lax.axis_size("k")
    if copies == 1:
        return rights
    shape = rights.shape
    rights = rights.reshape(-1, 2, copies, 2, 2, 128 // copies).transpose(0, 1, 3, 4, 2, 5)
    return rights.reshape(shape)


def narrow(shares):
    shares = shares.astype(F32)
    if lax.axis_size("k") > 1:
        shares = lax.psum_scatter(shares, "k", scatter_dimension=2, tiled=True)
    return shares


def unpack(packed, count):
    parts, rows, width = packed.shape
    unpacked = packed.reshape(parts, count, rows // count, width)
    return jnp.swapaxes(unpacked, 0, 1).reshape(count, parts * rows // count, width)


def row_order(values):
    c = lax.axis_index("c")
    split = values.reshape(2, 2, 2, 2, values.shape[0] // 16).swapaxes(2, 3)
    own = jnp.where(c == 0, split[:, 0], split[:, 1]).reshape(-1)
    other = jnp.where(c == 0, split[:, 1], split[:, 0]).reshape(-1)
    return own, jnp.concatenate([own, other])


def local(
    source,
    target,
    cotangent,
    source_len,
    target_len,
    source_seg,
    target_seg,
    enc_qkv,
    enc_proj,
    enc_up,
    enc_down,
    enc_gain,
    enc_shift,
    dec_qkv,
    dec_proj,
    cross_qkv,
    cross_proj,
    dec_up,
    dec_down,
    dec_gain,
    dec_shift,
):
    copies, z = lax.axis_size("k"), lax.axis_index("mp")
    vectors = jnp.concatenate([enc_gain, enc_shift, dec_gain, dec_shift, dec_shift[:2]], 0)
    if copies > 1:
        vectors = lax.all_gather(vectors, "k", axis=1, tiled=True)
    lane = jnp.arange(128)[None]
    vectors = jnp.where(lane // 32 == z, jnp.tile(vectors, (1, 4)), 0.0)
    facts = jnp.concatenate(
        [
            jnp.concatenate([segments, jnp.broadcast_to(lengths[:, None], (2, 128))], 1)
            for lengths, segments in ((source_len, source_seg), (target_len, target_seg))
        ],
        0,
    )
    facts = jnp.concatenate([facts.reshape(-1, 128), jnp.zeros((4, 128), jnp.int32)], 0)
    first_p = widen(
        pack_rows([*transposed(enc_qkv), enc_proj, *transposed(dec_qkv), dec_proj])
    )
    second_p = jnp.concatenate(
        [pack_rows([*transposed(cross_qkv), cross_proj]), pack_rows([enc_up.T, enc_down])], 1
    )
    second_p, third_p = widen(second_p), widen(pack_rows([dec_up.T, dec_down]))

    (stream_in, target_in), (first_p,), vectors, facts = open_program(
        [source, target], vectors, facts, [first_p]
    )
    if copies > 1:
        vectors = vectors.reshape(16, 2, 2, 2, 4, copies, 32 // copies)
        vectors = vectors.transpose(0, 1, 5, 2, 3, 4, 6).reshape(16, 1024)
    first_w = gather_weights(first_p)
    near = jnp.where(lax.axis_index("hi") == z % 2, facts[0], facts[1])[:36].reshape(2, 2, 1152)
    near = jnp.where(z < 2, near[:, 0], near[:, 1])
    source_length, source_ids = near[0, 1024], near[0, :1024]
    target_length, target_ids = near[1, 1024], near[1, :1024]
    place_own, place_all = row_order(jnp.arange(source_ids.shape[0]))
    source_own, source_all = row_order(source_ids)
    target_own, target_all = row_order(target_ids)
    zero = jnp.zeros_like(place_own)
    source_facts = jnp.stack([source_own, place_own] + [zero] * 6)
    target_facts = jnp.stack([target_own, place_own] + [zero] * 6)

    def key_facts(ids, length):
        live = (place_all < length).astype(jnp.int32)
        blank = jnp.zeros_like(live)
        return jnp.stack([ids, place_all, live] + [blank] * 5, 1)

    source_keys = key_facts(source_all, source_length)
    target_keys = key_facts(target_all, target_length)

    ENC_G, ENC_B, DEC_G, DEC_B = 0, 3, 6, 10
    SELF, CROSS = 256, 0
    Q, QKV, KV, O = (0, 64), (0, 192), (64, 128), (192, 64)
    ENC_UP, ENC_DOWN, DEC_UP, DEC_DOWN = (256, 256), (512, 256), (0, 256), (256, 256)

    def pick(call, packed, span, base=0):
        return Weight(call, packed, base + span[0], span[1])

    def forward_mid(call, residual, gain, shift):
        vec, res = call.take(vectors), call.fetch(residual)
        kept = call.keep((128, 1024), F32)

        def mid(get, total):
            stream = get(res)[...].astype(F32) + total
            get(kept)[...] = stream
            call.save(get, kept)
            unit, scale = unit_of(stream)
            return (unit * get(vec)[gain : gain + 1] + get(vec)[shift : shift + 1]).astype(BF16)

        return mid

    def backward_mid(call, stream, gain, residual=None):
        vec, kept = call.take(vectors), call.fetch(stream)
        res = None if residual is None else call.fetch(residual)
        grad_out, share_out = call.keep((128, 1024), F32), call.give((2, 1024), F32)

        def mid(get, total):
            grad, shares = norm_back(get(kept)[...].astype(F32), get(vec)[gain : gain + 1], total)
            if res is not None:
                grad = grad + get(res)[...]
            get(grad_out)[...] = grad
            call.save(get, grad_out)
            get(share_out)[...] = shares
            return grad.astype(BF16)

        return mid

    def deactivated(call, slope):
        out = call.keep((4, 128, 1024), BF16, 4)

        def store(get, at, row, column, value):
            get(out)[row] = (value * get(slope)[row]).astype(BF16)
            call.save(get, out, row)

        return store

    call = Call()

    def first_mid(stream, gain, shift):
        vec, res = call.take(vectors), call.fetch(stream)

        def mid(get, total):
            unit, scale = unit_of(get(res)[...].astype(F32))
            return (unit * get(vec)[gain : gain + 1] + get(vec)[shift : shift + 1]).astype(BF16)

        return mid

    jobs = []
    for stream, gain, shift in ((stream_in, ENC_G, ENC_B), (target_in, DEC_G, DEC_B)):
        jobs.append(Job(call, None, first_mid(stream, gain, shift), (None, None, None)))
    swap = Swap(call, [second_p])
    rows_a, rows_c, second_p = run_stage(
        call, jobs, [], "first_rows", 0, flops=24 * MICROSECOND, more=[swap]
    )
    second_w = gather_weights(second_p)

    call = Call()
    made, finishes, plans = [], [], []
    swap = Swap(call, [third_p])
    for rows, base in ((rows_a, 0), (rows_c, SELF)):
        weight = pick(call, first_w, QKV, base)
        store, finish = query_and_shared(call, 256)
        plans.append((call.fetch(rows), weight, store))
        finishes.append(finish)

    def project(get):
        at = place()
        for unused, weight, unused2 in plans:
            weight.start(get)
        greet([at["core"]] + swap.partners(at))
        swap.start(get, at)
        for rows, weight, store in plans:
            weight.wait(get)
            for row in range(4):
                for m in range(3):
                    store(
                        get, at, row, m * 256, nt(get(rows)[row], weight.matrix(get, m * 64, 64))
                    )
        for finish in finishes:
            finish(get)
        swap.finish(get, at)

    third_p, enc_q, enc_kv, self_q, self_kv = call.run(project, "project", 1, 8 * MICROSECOND)
    third_w = gather_weights(third_p)

    enc_mixed, enc_total = attend(enc_q, enc_kv, source_facts, source_keys, False)
    self_mixed, self_total = attend(self_q, self_kv, target_facts, target_keys, True)

    call = Call()
    enc_o, self_o = pick(call, first_w, O), pick(call, first_w, O, SELF)
    mid = forward_mid(call, stream_in, ENC_G + 1, ENC_B + 1)
    job_b = Job(call, (enc_mixed, enc_o, [(0, 64)], 0), mid, (None, None, None))
    mid = forward_mid(call, target_in, DEC_G + 1, DEC_B + 1)
    job_d = Job(call, (self_mixed, self_o, [(0, 64)], 0), mid, (None, None, None))
    stream_mid, rows_b, target_mid, rows_d = run_stage(
        call, [job_b, job_d], [enc_o, self_o], "after_self", 2, flops=34 * MICROSECOND
    )

    call = Call()
    enc_u, enc_d = pick(call, second_w, ENC_UP), pick(call, second_w, ENC_DOWN)
    cross_a, cross_b = pick(call, second_w, Q), pick(call, second_w, KV)
    feed = Feed(call, rows_b, enc_u, enc_d)
    mid = forward_mid(call, stream_mid, ENC_G + 2, ENC_B + 2)
    shared, query, rows_in = Shared(call, 512), Plain(call, 256), call.fetch(rows_d)
    job = Job(call, feed, mid, (cross_b, [(0, 64), (64, 64)], shared.store))

    def queries(get, at):
        for row in range(4):
            query.store(get, at, row, 0, nt(get(rows_in)[row], cross_a.matrix(get, 0, 64)))

    enc_hidden, enc_slope, stream_end, cross_kv, cross_q, memory = run_stage(
        call,
        [job],
        [enc_u, enc_d, cross_a, cross_b],
        "memory",
        3,
        shared.finish,
        24 * MICROSECOND,
        core=True,
        more=[Local(queries)],
    )

    cross_mixed, cross_total = attend(cross_q, cross_kv, target_facts, source_keys, False)

    call = Call()
    cross_o = pick(call, second_w, O)
    mid = forward_mid(call, target_mid, DEC_G + 2, DEC_B + 2)
    slots = Slots(call, [cotangent], True)
    job = Job(call, (cross_mixed, cross_o, [(0, 64)], 0), mid, (None, None, None))
    target_late, grad_out, rows_e = run_stage(
        call, [job], [cross_o], "after_cross", 4, flops=20 * MICROSECOND, more=[slots]
    )

    call = Call()
    dec_u, dec_d = pick(call, third_w, DEC_UP), pick(call, third_w, DEC_DOWN)
    feed = Feed(call, rows_e, dec_u, dec_d)
    vec, res, cot = call.take(vectors), call.fetch(target_late), call.fetch(grad_out)
    decoded_out, grad_end_out = call.keep((128, 1024), BF16), call.keep((128, 1024), F32)
    share_out = call.give((2, 1024), F32)

    def last_mid(get, total):
        stream = get(res)[...] + total
        gain, shift = get(vec)[DEC_G + 3 : DEC_G + 4], get(vec)[DEC_B + 3 : DEC_B + 4]
        unit, unused = unit_of(stream)
        get(decoded_out)[...] = (unit * gain + shift).astype(BF16)
        grad, shares = norm_back(stream, gain, get(cot)[...].astype(F32))
        get(grad_end_out)[...] = grad
        get(share_out)[...] = shares
        call.save(get, decoded_out)
        call.save(get, grad_end_out)
        return grad.astype(BF16)

    job = Job(call, feed, last_mid, (dec_d, [(0, 256)], deactivated(call, feed.slope)))
    dec_hidden, dec_slope, decoded, grad_end, norm_3, dec_grad_act, grad_rows_e = run_stage(
        call, [job], [dec_u, dec_d], "turn", 5, flops=24 * MICROSECOND
    )
    dec_s = weight_shares(
        [(dec_grad_act, 0, rows_e), (dec_hidden, 0, grad_rows_e)], 256, 15
    )
    dec_g = over_slots(dec_s)

    call = Call()
    call.take(dec_s, pltpu.HBM)
    dec_u, cross_o = pick(call, third_w, DEC_UP), pick(call, second_w, O)
    mid = backward_mid(call, target_late, DEC_G + 2, grad_end)
    query = Plain(call, 256)
    job = Job(call, (dec_grad_act, dec_u, [(0, 256)], 0), mid, (cross_o, [(0, 64)], query.store))
    grad_late, norm_2, cross_grad_mixed, grad_rows_d = run_stage(
        call, [job], [dec_u, cross_o], "back_cross", 6, flops=20 * MICROSECOND
    )

    cross_grads = attend_back(
        cross_q, cross_kv, cross_grad_mixed, cross_total, target_facts, source_keys, False, 7
    )
    cross_s = weight_shares(
        [
            (cross_grads, 0, rows_d),
            (cross_grads, 256, memory),
            (cross_grads, 512, memory),
            (cross_mixed, 0, grad_rows_d),
        ],
        64,
        16,
    )
    cross_g = over_slots(cross_s)

    call = Call()
    call.take(cross_s, pltpu.HBM)
    cross_a, cross_b = pick(call, second_w, Q), pick(call, second_w, KV)
    self_o, enc_d = pick(call, first_w, O, SELF), pick(call, second_w, ENC_DOWN)
    slots = Slots(call, [decoded], False)
    mid = backward_mid(call, target_mid, DEC_G + 1, grad_late)
    query = Plain(call, 256)
    job_t = Job(
        call, (cross_grads, cross_a, [(0, 64)], 0), mid, (self_o, [(0, 64)], query.store)
    )
    mid = backward_mid(call, stream_end, ENC_G + 2)
    job_s = Job(
        call,
        (cross_grads, cross_b, [(0, 64), (64, 64)], 256),
        mid,
        (enc_d, [(0, 256)], deactivated(call, call.fetch(enc_slope))),
    )
    (
        decoded,
        grad_mid,
        norm_1,
        self_grad_mixed,
        grad_rows_c,
        grad_stream,
        enc_norm_2,
        enc_grad_act,
        grad_rows_b,
    ) = run_stage(
        call,
        [job_t, job_s],
        [cross_a, cross_b, self_o, enc_d],
        "back_both",
        8,
        flops=38 * MICROSECOND,
        more=[slots],
    )
    feed_s = weight_shares(
        [(enc_grad_act, 0, rows_b), (enc_hidden, 0, grad_rows_b)], 256, 17
    )
    feed_g = over_slots(feed_s)

    self_grads = attend_back(
        self_q, self_kv, self_grad_mixed, self_total, target_facts, target_keys, True, 9, [feed_s]
    )
    call = Call()
    call.take(dec_g, pltpu.HBM)
    shares = Shares(
        call,
        [
            (self_grads, 0, rows_c),
            (self_grads, 256, rows_c),
            (self_grads, 512, rows_c),
            (self_mixed, 0, grad_rows_c),
        ],
        64,
    )
    enc_u, enc_o = pick(call, second_w, ENC_UP), pick(call, first_w, O)
    self_a = pick(call, first_w, QKV, SELF)
    mid = backward_mid(call, stream_mid, ENC_G + 1, grad_stream)
    query = Plain(call, 256)
    job_s = Job(call, (enc_grad_act, enc_u, [(0, 256)], 0), mid, (enc_o, [(0, 64)], query.store))
    mid = backward_mid(call, target_in, DEC_G, grad_mid)
    job_t = Job(call, (self_grads, self_a, [(0, 64), (64, 64), (128, 64)], 0), mid, None)
    (
        self_s,
        grad_stream,
        enc_norm_1,
        enc_grad_mixed,
        grad_rows_a,
        target_grad,
        norm_0,
    ) = run_stage(
        call,
        [job_s, job_t],
        [enc_u, self_a, enc_o],
        "back_self",
        10,
        flops=28 * MICROSECOND,
        more=[shares],
    )
    self_g = over_slots(self_s)

    enc_grads = attend_back(
        enc_q, enc_kv, enc_grad_mixed, enc_total, source_facts, source_keys, False, 11, [cross_g]
    )
    enc_s = weight_shares(
        [
            (enc_grads, 0, rows_a),
            (enc_grads, 256, rows_a),
            (enc_grads, 512, rows_a),
            (enc_mixed, 0, grad_rows_a),
        ],
        64,
        19,
    )
    enc_g = over_slots(enc_s)

    call = Call()
    for done in (enc_s, feed_g):
        call.take(done, pltpu.HBM)
    enc_a = pick(call, first_w, QKV)
    mid = backward_mid(call, stream_in, ENC_G, grad_stream)
    job = Job(call, (enc_grads, enc_a, [(0, 64), (64, 64), (128, 64)], 0), mid, None)
    source_grad, enc_norm_0 = run_stage(
        call, [job], [enc_a], "back_first", 12, flops=12 * MICROSECOND
    )

    norm_share = jnp.stack(
        [enc_norm_0, enc_norm_1, enc_norm_2], 1
    ).reshape(6, 1024)
    norm_share = jnp.concatenate(
        [
            norm_share,
            jnp.stack([norm_0, norm_1, norm_2, norm_3], 1).reshape(8, 1024),
            jnp.zeros((2, 1024), F32),
        ],
        0,
    )
    (source_grad, target_grad), swapped, norm_grad = close_program(
        [source_grad.astype(BF16), target_grad.astype(BF16)],
        by_owner(norm_share),
        [dec_g, cross_g, feed_g, self_g],
    )
    norm_grad = norm_grad.reshape(16, copies, 4, 32 // copies)
    if copies > 1:
        norm_grad = lax.psum_scatter(norm_grad, "k", scatter_dimension=1)
    norm_grad = norm_grad.reshape(16, 4, -1)
    norm_grad = lax.dynamic_index_in_dim(norm_grad, z, 1, False)
    (enc_g,) = swap_packs([enc_g], 20)

    def attend_shares(packed):
        grads = unpack(narrow(packed), 4)
        return jnp.swapaxes(grads[:3], 1, 2), grads[3]

    def feed_shares(packed):
        grads = unpack(narrow(packed), 2)
        return grads[0].T, grads[1]

    dec_u, dec_d = feed_shares(swapped[0])
    enc_u, enc_d = feed_shares(swapped[2])
    enc_a, enc_o = attend_shares(enc_g)
    cross_a, cross_o = attend_shares(swapped[1])
    self_a, self_o = attend_shares(swapped[3])
    return (
        decoded,
        source_grad.astype(F32),
        target_grad.astype(F32),
        enc_a,
        enc_o,
        enc_u,
        enc_d,
        norm_grad[:3],
        norm_grad[3:6],
        self_a,
        self_o,
        cross_a,
        cross_o,
        dec_u,
        dec_d,
        norm_grad[6:10],
        norm_grad[10:14],
    )


def solution(mesh):
    dp, seq, mp = (mesh.shape[name] for name in ("dp", "seq", "mp"))
    assert dp % 2 == 0 and seq == 4 and mp == 4
    fine = Mesh(mesh.devices.reshape(2, dp // 2, 2, 2, 4), AXES)
    d, s = ("hi", "k"), ("y", "c")
    rows = P(d, s + ("mp",), None)
    three, flat = P(None, d + s, "mp"), P("mp", d + s)
    up, vector = P(d + s, "mp"), P(None, d + s + ("mp",))
    attention, feeding = (three, flat), (up, flat)
    return jax.shard_map(
        local,
        mesh=fine,
        in_specs=(rows,) * 3
        + (P(d), P(d), P(d, None), P(d, None))
        + attention
        + feeding
        + (vector, vector)
        + attention * 2
        + feeding
        + (vector, vector),
        out_specs=(rows,) * 3
        + attention
        + feeding
        + (vector, vector)
        + attention * 2
        + feeding
        + (vector, vector),
        check_vma=False,
    )
```

```python
import math

import jax
import jax.numpy as jnp
from jax import lax
from jax.experimental import pallas as pl
from jax.experimental.pallas import tpu as pltpu
from jax.sharding import Mesh, PartitionSpec as P

HEAD_DIM = 64
EPSILON = 1e-05
MASKED = -1000000000.0
AXES = ("hi", "k", "y", "c", "mp")
MESH_ID = pl.DeviceIdType.MESH
F32 = jnp.float32
BF16 = jnp.bfloat16


class Call:
    def __init__(self):
        self.known, self.arrays, self.specs = [], [], []
        self.shapes, self.places, self.scratch = [], [], []
        self.fetched, self.kept = [], []

    def take(self, array, space=pltpu.VMEM):
        if isinstance(array, tuple):
            return array
        for i, known in enumerate(self.known):
            if known is array and self.specs[i].memory_space == space:
                return ("in", i)
        self.known.append(array)
        if space == pltpu.HBM:
            array = pltpu.with_memory_space_constraint(array, pltpu.HBM)
        self.arrays.append(array)
        self.specs.append(pl.BlockSpec(memory_space=space))
        return ("in", len(self.arrays) - 1)

    def fetch(self, array):
        if isinstance(array, tuple):
            return array
        source = self.take(array, pltpu.HBM)
        for i, (known, room, sem) in enumerate(self.fetched):
            if known == source:
                return ("fetch", i)
        self.fetched.append((source, self.hold(array.shape, array.dtype), self.sems(1)))
        return ("fetch", len(self.fetched) - 1)

    def give(self, shape, dtype, space=pltpu.VMEM):
        if space == pltpu.HBM:
            self.shapes.append(pltpu.HBM(shape, dtype))
        else:
            self.shapes.append(jax.ShapeDtypeStruct(shape, dtype))
        self.places.append(pl.BlockSpec(memory_space=space))
        return ("out", len(self.shapes) - 1)

    def keep(self, shape, dtype, parts=1):
        target = self.give(shape, dtype, pltpu.HBM)
        self.kept.append((target, self.hold(shape, dtype), self.sems(parts)))
        return ("keep", len(self.kept) - 1)

    def hold(self, shape, dtype):
        self.scratch.append(pltpu.VMEM(shape, dtype))
        return ("tmp", len(self.scratch) - 1)

    def sems(self, count):
        self.scratch.append(pltpu.SemaphoreType.DMA((count,)))
        return ("tmp", len(self.scratch) - 1)

    def save(self, get, handle, row=None):
        target, room, sems = (get(part) for part in self.kept[handle[1]])
        if row is not None:
            target, room = target.at[row], room.at[row]
        count = sum(1 for known, unused in self.saves if known == handle)
        copy = pltpu.make_async_copy(room, target, sems.at[count])
        copy.start()
        self.saves.append((handle, copy))

    def run(self, body, name, collective=None, flops=0):
        ins, outs = len(self.arrays), len(self.shapes)

        def kernel(*refs):
            parts = {"in": refs[:ins], "out": refs[ins : ins + outs], "tmp": refs[ins + outs :]}
            here, self.saves, self.waited = set(), [], []

            def get(handle):
                kind, i = handle
                if kind == "keep":
                    return get(self.kept[i][1])
                if kind != "fetch":
                    return parts[kind][i]
                source, room, sem = (get(part) for part in self.fetched[i])
                if i not in here:
                    here.add(i)
                    pltpu.make_async_copy(source, room, sem.at[0]).wait()
                return room

            for source, room, sem in self.fetched:
                pltpu.make_async_copy(get(source), get(room), get(sem).at[0]).start()
            body(get)
            for i in range(len(self.fetched)):
                get(("fetch", i))
            for handle, copy in self.saves:
                copy.wait()

        held = [a for a, spec in zip(self.arrays, self.specs) if spec.memory_space == pltpu.VMEM]
        held += [a for a, spec in zip(self.shapes, self.places) if spec.memory_space == pltpu.VMEM]
        held += [x for x in self.scratch if x.dtype in (BF16, F32)]
        room = sum(math.prod(x.shape) * jnp.dtype(x.dtype).itemsize for x in held)
        return pl.pallas_call(
            kernel,
            out_shape=tuple(self.shapes),
            in_specs=self.specs,
            out_specs=tuple(self.places),
            scratch_shapes=self.scratch,
            compiler_params=pltpu.CompilerParams(
                collective_id=collective,
                has_side_effects=collective is not None,
                vmem_limit_bytes=room + (8 << 20),
            ),
            cost_estimate=pl.CostEstimate(flops=flops, bytes_accessed=0, transcendentals=0),
            name=name,
        )(*self.arrays)


MICROSECOND = 1_000_000_000


def nt(left, right):
    return lax.dot_general(left, right, (((1,), (1,)), ((), ())), preferred_element_type=F32)


def nn(left, right):
    return lax.dot_general(left, right, (((1,), (0,)), ((), ())), preferred_element_type=F32)


def tn(left, right):
    return lax.dot_general(left, right, (((0,), (0,)), ((), ())), preferred_element_type=F32)


def unit_of(stream):
    average = jnp.mean(stream, -1, keepdims=True)
    centred = stream - average
    scale = lax.rsqrt(jnp.mean(centred * centred, -1, keepdims=True) + EPSILON)
    return centred * scale, scale


def norm_back(stream, gain, upstream):
    unit, scale = unit_of(stream)
    inner = upstream * gain
    grad = scale * (
        inner - jnp.mean(inner, -1, keepdims=True) - unit * jnp.mean(inner * unit, -1, keepdims=True)
    )
    shares = jnp.concatenate(
        [jnp.sum(upstream * unit, 0, keepdims=True), jnp.sum(upstream, 0, keepdims=True)], 0
    )
    return grad, shares


def gelu_pair(act):
    bell = 0.5 + 0.5 * lax.erf(act * 0.7071067811865476)
    slope = bell + act * (jnp.exp(act * act * -0.5) * 0.3989422804014327)
    return act * bell, slope


def place():
    hi, k, y, c, z = (lax.axis_index(name) for name in AXES)
    return {
        "x": (1 - hi, k, y, c, z),
        "y": (hi, k, 1 - y, c, z),
        "d": (1 - hi, k, 1 - y, c, z),
        "core": (hi, k, y, 1 - c, z),
        "mesh": (hi, k, y, c, z),
        "own_row": y * 2 + hi,
        "x_row": y * 2 + 1 - hi,
        "y_row": (1 - y) * 2 + hi,
        "d_row": (1 - y) * 2 + 1 - hi,
    }


def greet(partners):
    barrier = pltpu.get_barrier_semaphore()
    for partner in partners:
        pl.semaphore_signal(barrier, inc=1, device_id=partner, device_id_type=MESH_ID)
    pl.semaphore_wait(barrier, len(partners))


class Weight:
    def __init__(self, call, packed, first, count):
        self.source = call.take(packed, pltpu.HBM)
        self.room = call.hold((4, count, 1024), BF16)
        self.sem = call.sems(1)
        self.first, self.count = first, count

    def start(self, get):
        source, room, sem = get(self.source), get(self.room), get(self.sem)
        for q in range(4):
            for c in range(2):
                pltpu.make_async_copy(
                    source.at[c, :, q, pl.ds(self.first, self.count), :],
                    room.at[:, :, pl.ds((q * 2 + c) * 128, 128)],
                    sem.at[0],
                ).start()

    def wait(self, get):
        room = get(self.room)
        pltpu.make_async_copy(room, room, get(self.sem).at[0]).wait()

    def matrix(self, get, first, count):
        return get(self.room)[:, first : first + count, :].reshape(4 * count, 1024)


def stack(blocks):
    return blocks[0] if len(blocks) == 1 else jnp.concatenate(blocks, 0)


class Feed:
    def __init__(self, call, rows, up, down):
        self.call, self.rows, self.weights = call, call.fetch(rows), [up, down]
        self.hidden = call.keep((4, 128, 1024), BF16, 4)
        self.slope = call.keep((4, 128, 1024), F32, 4)

    def part(self, get, *rows):
        up, down = self.weights
        whole = stack([get(self.rows)[row] for row in rows])
        made, slope = gelu_pair(nt(whole, up.matrix(get, 0, 256)))
        made = made.astype(BF16)
        for i, row in enumerate(rows):
            get(self.hidden)[row] = made[i * 128 : (i + 1) * 128]
            get(self.slope)[row] = slope[i * 128 : (i + 1) * 128]
            self.call.save(get, self.hidden, row)
            self.call.save(get, self.slope, row)
        return nn(made, down.matrix(get, 0, 256))


class Job:
    def __init__(self, call, left, mid, right):
        self.call, self.left, self.mid, self.right = call, left, mid, right
        if left is not None:
            self.rows_in = None if isinstance(left, Feed) else call.fetch(left[0])
            self.out_first = call.hold((2, 128, 1024), BF16)
            self.out_edge = call.hold((2, 64, 1024), BF16)
            self.out_late = call.hold((2, 64, 1024), BF16)
            self.keep = call.hold((2, 64, 1024), F32)
            self.own = call.hold((128, 1024), F32)
            self.landed = call.hold((6, 64, 1024), BF16)
            self.sum_send, self.sum_recv = call.sems(6), call.sems(6)
        self.gathered = None
        if right is not None:
            self.gathered = call.keep((4, 128, 1024), BF16, 4)
            self.row_send, self.row_recv = call.sems(6), call.sems(6)

    def lefts(self):
        return self.left.weights if isinstance(self.left, Feed) else [self.left[1]]

    def part(self, get, *rows):
        if isinstance(self.left, Feed):
            return self.left.part(get, *rows)
        unused, weight, picks, column = self.left
        total = None
        for first, count in picks:
            width = 4 * count
            left = stack([get(self.rows_in)[row, :, column : column + width] for row in rows])
            term = nn(left, weight.matrix(get, first, count))
            total = term if total is None else total + term
            column += width
        return total

    def send(self, get, i, source, target, partner):
        copy = pltpu.make_async_remote_copy(
            src_ref=source,
            dst_ref=target,
            send_sem=get(self.sum_send).at[i],
            recv_sem=get(self.sum_recv).at[i],
            device_id=partner,
            device_id_type=MESH_ID,
        )
        copy.start()
        return copy

    def sum_start(self, get, at):
        first, edge, landed = get(self.out_first), get(self.out_edge), get(self.landed)
        keep = get(self.keep)
        self.copies = [None] * 6
        first[0] = self.part(get, at["d_row"]).astype(BF16)
        self.copies[0] = self.send(
            get, 0, first.at[0, pl.ds(0, 64)], landed.at[0], at["x"]
        )
        self.copies[1] = self.send(
            get, 1, first.at[0, pl.ds(64, 64)], landed.at[1], at["y"]
        )
        part = self.part(get, at["x_row"], at["y_row"])
        edge[0] = part[:64].astype(BF16)
        keep[0] = part[64:128]
        self.copies[2] = self.send(get, 2, edge.at[0], landed.at[2], at["x"])
        edge[1] = part[192:].astype(BF16)
        keep[1] = part[128:192]
        self.copies[3] = self.send(get, 3, edge.at[1], landed.at[3], at["y"])

    def sum_forward(self, get, at):
        late, landed, keep = get(self.out_late), get(self.landed), get(self.keep)
        self.copies[0].wait_recv()
        late[1] = (keep[1] + landed[0].astype(F32)).astype(BF16)
        self.copies[4] = self.send(get, 4, late.at[1], landed.at[4], at["y"])
        self.copies[1].wait_recv()
        late[0] = (keep[0] + landed[1].astype(F32)).astype(BF16)
        self.copies[5] = self.send(get, 5, late.at[0], landed.at[5], at["x"])

    def sum_own(self, get, at):
        get(self.own)[...] = self.part(get, at["own_row"])

    def sum_end(self, get):
        landed, own = get(self.landed), get(self.own)
        for i in (2, 3, 4, 5):
            self.copies[i].wait_recv()
        upper = own[:64] + landed[2].astype(F32) + landed[4].astype(F32)
        lower = own[64:] + landed[5].astype(F32) + landed[3].astype(F32)
        return jnp.concatenate([upper, lower], 0)

    def row_copy(self, get, i, row, half, partner):
        block = get(self.gathered).at[row, pl.ds(half * 64, 64)]
        copy = pltpu.make_async_remote_copy(
            src_ref=block,
            dst_ref=block,
            send_sem=get(self.row_send).at[i],
            recv_sem=get(self.row_recv).at[i],
            device_id=partner,
            device_id_type=MESH_ID,
        )
        copy.start()
        return copy

    def rows_start(self, get, at, normed):
        get(self.gathered)[at["own_row"]] = normed
        self.call.save(get, self.gathered, at["own_row"])
        self.moves = [
            self.row_copy(get, 0, at["own_row"], 0, at["y"]),
            self.row_copy(get, 1, at["own_row"], 1, at["x"]),
            self.row_copy(get, 2, at["own_row"], 1, at["y"]),
            self.row_copy(get, 3, at["own_row"], 0, at["x"]),
        ]

    def rows_forward(self, get, at):
        self.moves[0].wait_recv()
        self.moves.append(self.row_copy(get, 4, at["y_row"], 0, at["x"]))
        self.moves[1].wait_recv()
        self.moves.append(self.row_copy(get, 5, at["x_row"], 1, at["y"]))

    def product(self, get, at, row):
        weight, picks, store = self.right
        rows = get(self.gathered)[row]
        column = 0
        for first, count in picks:
            store(get, at, row, column, nt(rows, weight.matrix(get, first, count)))
            column += 4 * count

    def drain(self):
        if self.left is not None:
            for copy in self.copies:
                copy.wait_send()
        if self.right is not None:
            for copy in self.moves:
                copy.wait_send()


class Extra:
    def partners(self, at):
        return []

    def start(self, get, at):
        return None

    def middle(self, get, at):
        return None

    def late(self, get, at):
        return None

    def finish(self, get, at):
        return None

    def begin(self, get):
        return None

    def run(self, get, at):
        self.middle(get, at)
        self.start(get, at)
        self.late(get, at)
        self.finish(get, at)


class Stage(Extra):
    def __init__(self, call, jobs, weights=(), finish=None, core=False, more=()):
        self.call, self.jobs, self.weights = call, jobs, weights
        self.end, self.core, self.more = finish, core, more

    def partners(self, at):
        found = [at["x"], at["y"]] + ([at["core"]] if self.core else [])
        for extra in self.more:
            found += extra.partners(at)
        return found

    def begin(self, get):
        for weight in self.weights:
            weight.start(get)

    def run(self, get, at):
        call, jobs, more = self.call, self.jobs, self.more
        lefts = [job for job in jobs if job.left is not None]
        movers = [job for job in jobs if job.right is not None]
        rights = [job for job in movers if job.right[0] is not None]

        def ready(weight):
            if weight not in call.waited:
                weight.wait(get)
                call.waited.append(weight)

        def arrived(job, row):
            call.save(get, job.gathered, row)
            if job in rights:
                job.product(get, at, row)

        for job in lefts:
            for weight in job.lefts():
                ready(weight)
            job.sum_start(get, at)
        for job in lefts:
            job.sum_forward(get, at)
        for job in lefts:
            job.sum_own(get, at)
        for extra in more:
            extra.middle(get, at)
        for job in jobs:
            normed = job.mid(get, job.sum_end(get) if job.left is not None else None)
            if job.right is not None:
                job.rows_start(get, at, normed)
        for extra in more:
            extra.start(get, at)
        for weight in self.weights:
            ready(weight)
        for extra in more:
            extra.late(get, at)
        for job in rights:
            job.product(get, at, at["own_row"])
        for job in movers:
            job.rows_forward(get, at)
        for job in movers:
            job.moves[3].wait_recv()
            arrived(job, at["x_row"])
            job.moves[2].wait_recv()
            arrived(job, at["y_row"])
        for job in movers:
            job.moves[4].wait_recv()
            job.moves[5].wait_recv()
            arrived(job, at["d_row"])
        for job in jobs:
            job.drain()
        if self.end is not None:
            self.end(get)
        for extra in more:
            extra.finish(get, at)


def run_steps(call, steps, name, collective, flops=0):
    def body(get):
        at = place()
        for step in steps:
            step.begin(get)
        partners = []
        for step in steps:
            for partner in step.partners(at):
                if all(partner is not known for known in partners):
                    partners.append(partner)
        greet(partners)
        for step in steps:
            step.run(get, at)

    return call.run(body, name, collective, flops)


def run_stage(call, jobs, weights, name, collective, finish=None, flops=0, core=False, more=()):
    return run_steps(call, [Stage(call, jobs, weights, finish, core, more)], name, collective, flops)


class Kept:
    def __init__(self, out, store):
        self.out, self.store = out, store


class Plain:
    def __init__(self, call, width):
        self.call, self.width = call, width
        self.out = call.keep((4, 128, width), BF16, 4)

    def store(self, get, at, row, column, value):
        get(self.out)[row, :, column : column + value.shape[1]] = value.astype(BF16)
        if column + value.shape[1] == self.width:
            self.call.save(get, self.out, row)


class Shared:
    def __init__(self, call, width, skip=0):
        self.call, self.out = call, call.keep((2, 4, 128, width), BF16, 2)
        self.send_sem, self.recv_sem = call.sems(4), call.sems(4)
        self.width, self.skip, self.copies, self.blocks = width, skip, [], 0

    def store(self, get, at, row, column, value):
        out = get(self.out)
        column = column - self.skip
        out[0, row, :, column : column + value.shape[1]] = value.astype(BF16)
        if column + value.shape[1] == self.width:
            i = len(self.copies)
            copy = pltpu.make_async_remote_copy(
                src_ref=out.at[0, row],
                dst_ref=out.at[1, row],
                send_sem=get(self.send_sem).at[i],
                recv_sem=get(self.recv_sem).at[i],
                device_id=at["core"],
                device_id_type=MESH_ID,
            )
            copy.start()
            self.copies.append(copy)

    def finish(self, get):
        self.call.save(get, self.out, 0)
        for copy in self.copies:
            copy.wait()
        self.call.save(get, self.out, 1)


def query_and_shared(call, width):
    query, shared = Plain(call, width), Shared(call, 2 * width, skip=width)

    def store(get, at, row, column, value):
        if column < width:
            query.store(get, at, row, column, value)
        else:
            shared.store(get, at, row, column, value)

    return store, shared.finish


def lanes_of(head, rows):
    lane = lax.broadcasted_iota(jnp.int32, (rows, 128), 1)
    return lane // HEAD_DIM == head


def allowed_bias(facts_ref, keys_ref, causal):
    key = keys_ref[...]
    query = facts_ref[...]
    allowed = (key[:, 0:1] == query[0:1, :]) & (key[:, 2:3] > 0)
    if causal:
        allowed = allowed & (key[:, 1:2] <= query[1:2, :])
    return jnp.where(allowed, 0.0, MASKED)


class Attend(Extra):
    def __init__(self, call, queries, key_value, facts, keys, causal):
        self.call, self.causal = call, causal
        self.queries, self.key_value = call.fetch(queries), call.fetch(key_value)
        self.facts, self.keys = call.take(facts), call.take(keys)
        self.mixed = call.keep((4, 128, 256), BF16)
        self.total = call.give((8, 512), F32)
        self.bias = call.hold((1024, 512), F32)

    def late(self, get, at):
        mask = get(self.bias)
        mask[...] = allowed_bias(get(self.facts), get(self.keys), self.causal)
        q_ref, kv_ref = get(self.queries), get(self.key_value)
        mixed_ref, total_ref = get(self.mixed), get(self.total)

        def pair_step(pair, carry):
            lanes = pl.ds(pl.multiple_of(pair * 128, 128), 128)
            value_lanes = pl.ds(pl.multiple_of(256 + pair * 128, 128), 128)
            keys = kv_ref[:, :, :, lanes].reshape(1024, 128)
            values = kv_ref[:, :, :, value_lanes].reshape(1024, 128)
            for block in range(2):
                span = slice(block * 256, block * 256 + 256)
                queries = q_ref[2 * block : 2 * block + 2, :, lanes].reshape(256, 128)
                mixed = []
                for head in range(2):
                    picked = jnp.where(lanes_of(head, 256), queries * 0.125, 0.0).astype(BF16)
                    scores = nt(keys, picked) + mask[:, span]
                    top = jnp.max(scores, 0, keepdims=True)
                    raised = jnp.exp(scores - top)
                    total = jnp.sum(raised, 0, keepdims=True)
                    probs = (raised * (1.0 / total)).astype(BF16)
                    mixed.append(tn(values, probs)[head * HEAD_DIM : (head + 1) * HEAD_DIM])
                    total_ref[pl.ds(pair * 2 + head, 1), span] = top + jnp.log(total)
                mixed = jnp.concatenate(mixed, 0).T.astype(BF16)
                mixed_ref[2 * block : 2 * block + 2, :, lanes] = mixed.reshape(2, 128, 128)
            return carry

        lax.fori_loop(0, 2, pair_step, 0)
        self.call.save(get, self.mixed)


class AttendBack(Extra):
    def __init__(self, call, queries, key_value, grad_mixed, total, facts, keys, causal):
        self.call, self.causal = call, causal
        self.queries, self.key_value = call.fetch(queries), call.fetch(key_value)
        self.grad_mixed, self.total = call.fetch(grad_mixed), call.take(total)
        self.facts, self.keys = call.take(facts), call.take(keys)
        self.out = call.keep((4, 128, 768), BF16)
        self.bias, self.sums = call.hold((1024, 512), F32), call.hold((1024, 512), F32)
        self.away, self.landed = call.hold((2, 512, 256), BF16), call.hold((2, 512, 256), BF16)
        self.send_sem, self.recv_sem = call.sems(2), call.sems(2)

    def partners(self, at):
        return [at["core"]]

    def late(self, get, at):
        out, mask, sums = get(self.out), get(self.bias), get(self.sums)
        away, here = get(self.away), get(self.landed)
        mask[...] = allowed_bias(get(self.facts), get(self.keys), self.causal)
        q_ref, kv_ref = get(self.queries), get(self.key_value)
        grad_ref, total_ref = get(self.grad_mixed), get(self.total)
        copies = []
        for pair in range(2):
            lanes = slice(pair * 128, pair * 128 + 128)
            keys_pair = kv_ref[:, :, :, lanes].reshape(1024, 128)
            values_pair = kv_ref[:, :, :, 256 + pair * 128 : 384 + pair * 128].reshape(1024, 128)
            key_sum = slice(pair * 256, pair * 256 + 128)
            value_sum = slice(pair * 256 + 128, pair * 256 + 256)
            for block in range(2):
                span = slice(block * 256, block * 256 + 256)
                two = slice(2 * block, 2 * block + 2)
                q_block = q_ref[two, :, lanes].reshape(256, 128)
                g_block = grad_ref[two, :, lanes].reshape(256, 128)
                grad_query = []
                for head in range(2):
                    inside = lanes_of(head, 256)
                    picked = jnp.where(inside, q_block * 1.0, 0.0).astype(BF16)
                    grads = jnp.where(inside, g_block * 1.0, 0.0).astype(BF16)
                    scores = nt(keys_pair, picked) * 0.125 + mask[:, span]
                    probs = jnp.exp(scores - total_ref[pair * 2 + head : pair * 2 + head + 1, span])
                    weighted = probs * nt(values_pair, grads)
                    inner = jnp.sum(weighted, 0, keepdims=True)
                    grad_raw = ((weighted - probs * inner) * 0.125).astype(BF16)
                    value_term = nn(probs.astype(BF16), grads)
                    key_term = nn(grad_raw, picked)
                    if block == 0 and head == 0:
                        sums[:, key_sum] = key_term
                        sums[:, value_sum] = value_term
                    else:
                        sums[:, key_sum] += key_term
                        sums[:, value_sum] += value_term
                    grad_query.append(tn(keys_pair, grad_raw)[head * HEAD_DIM : (head + 1) * HEAD_DIM])
                grad_query = jnp.concatenate(grad_query, 0).T.astype(BF16)
                out[two, :, lanes] = grad_query.reshape(2, 128, 128)
            away[pair] = sums[512:, pair * 256 : pair * 256 + 256].astype(BF16)
            copy = pltpu.make_async_remote_copy(
                src_ref=away.at[pair],
                dst_ref=here.at[pair],
                send_sem=get(self.send_sem).at[pair],
                recv_sem=get(self.recv_sem).at[pair],
                device_id=at["core"],
                device_id_type=MESH_ID,
            )
            copy.start()
            copies.append(copy)
        for pair in range(2):
            copies[pair].wait()
            both = sums[:512, pair * 256 : pair * 256 + 256] + here[pair].astype(F32)
            both = both.astype(BF16).reshape(4, 128, 256)
            out[:, :, 256 + pair * 128 : 384 + pair * 128] = both[:, :, :128]
            out[:, :, 512 + pair * 128 : 640 + pair * 128] = both[:, :, 128:]
        self.call.save(get, self.out)


class Shares(Extra):
    def __init__(self, call, pairs, count, out=None, base=0):
        self.call, self.count, self.base = call, count, base
        self.handles = [
            (call.fetch(left), column, call.fetch(by_owner(right)))
            for left, column, right in pairs
        ]
        shape = (4, 4, len(pairs) * count, 128)
        sends = len(pairs) * max(1, count // 64)
        self.made, self.landed = call.hold((2,) + shape, BF16), call.hold(shape, BF16)
        self.send_sem, self.recv_sem = call.sems(sends), call.sems(sends)
        self.rows = shape[2]
        self.out = call.give(shape, BF16, pltpu.HBM) if out is None else out
        self.room, self.save_sem = call.hold(shape, BF16), call.sems(1)

    def partners(self, at):
        return [at["core"]]

    def send(self, get, at, part):
        i = len(self.copies)
        copy = pltpu.make_async_remote_copy(
            src_ref=get(self.made).at[(1 - lax.axis_index("c"),) + part],
            dst_ref=get(self.landed).at[part],
            send_sem=get(self.send_sem).at[i],
            recv_sem=get(self.recv_sem).at[i],
            device_id=at["core"],
            device_id_type=MESH_ID,
        )
        copy.start()
        self.copies.append((part, copy))

    def middle(self, get, at):
        self.copies, every, count = [], slice(None), self.count
        made = get(self.made)
        for m, (left, column, right) in enumerate(self.handles):
            left, right = get(left), get(right)
            span = slice(m * count, (m + 1) * count)
            for first in range(0, 4 * count, 256):
                start = column + first
                product = tn(
                    left[:, :, start : start + 256].reshape(512, 256), right[...].reshape(512, 1024)
                )
                for inner in range(0, 256, count):
                    z = (first + inner) // count
                    for d in range(8):
                        made[d % 2, z, d // 2, span, :] = product[
                            inner : inner + count, d * 128 : d * 128 + 128
                        ].astype(BF16)
                if count == 256:
                    self.send(get, at, (first // 256, every, pl.ds(m * count, count)))
            if count < 256:
                self.send(get, at, (every, every, pl.ds(m * count, count)))

    def finish(self, get, at):
        core = lax.axis_index("c")
        for part, copy in self.copies:
            copy.wait()
            own = get(self.made)[(core,) + part].astype(F32)
            get(self.room)[part] = (own + get(self.landed)[part].astype(F32)).astype(BF16)
        target = get(self.out).at[:, :, pl.ds(self.base, self.rows)]
        copy = pltpu.make_async_copy(get(self.room), target, get(self.save_sem).at[0])
        copy.start()
        self.call.saves.append((None, copy))


class Carry(Extra):
    def __init__(self, call, array, out, base):
        self.call, self.array, self.out, self.base = call, call.take(array, pltpu.HBM), out, base
        self.rows, self.sem = array.shape[2], call.sems(1)

    def begin(self, get):
        target = get(self.out).at[:, :, pl.ds(self.base, self.rows)]
        copy = pltpu.make_async_copy(get(self.array), target, get(self.sem).at[0])
        copy.start()
        self.call.saves.append((None, copy))


class Swap(Extra):
    def __init__(self, call, packs):
        self.packs = [call.take(pack) for pack in packs]
        self.outs = [call.give(pack.shape, pack.dtype) for pack in packs]
        count = max(1, 3 * len(packs))
        self.send_sem, self.recv_sem = call.sems(count), call.sems(count)

    def start(self, get, at):
        hi, k, y, c, z = at["mesh"]
        own = hi * 2 + y
        self.copies = []
        for pack, out in zip(self.packs, self.outs, strict=True):
            pack, out = get(pack), get(out)
            for name, q in (
                ("d", (1 - hi) * 2 + 1 - y),
                ("x", (1 - hi) * 2 + y),
                ("y", hi * 2 + 1 - y),
            ):
                i = len(self.copies)
                copy = pltpu.make_async_remote_copy(
                    src_ref=pack.at[q],
                    dst_ref=out.at[own],
                    send_sem=get(self.send_sem).at[i],
                    recv_sem=get(self.recv_sem).at[i],
                    device_id=at[name],
                    device_id_type=MESH_ID,
                )
                copy.start()
                self.copies.append(copy)
            out[own] = pack[own]

    def partners(self, at):
        return [at["x"], at["y"], at["d"]]

    def finish(self, get, at):
        for copy in self.copies:
            copy.wait()


class Local(Extra):
    def __init__(self, work):
        self.late = work


class Slots(Extra):
    def __init__(self, call, arrays, inward):
        self.inward = inward
        self.arrays = [call.take(array) for array in arrays]
        shape = (128, 1024) if inward else (2, 64, 1024)
        self.outs = [call.give(shape, array.dtype) for array in arrays]
        self.send_sem, self.recv_sem = call.sems(2 * len(arrays)), call.sems(2 * len(arrays))

    def ends(self, get, at, j, step):
        z = at["mesh"][4]
        low = lax.div(z, 2)
        other = low if step == 0 else 1 - low
        array, out = get(self.arrays[j]), get(self.outs[j])
        if self.inward:
            return array.at[other], out.at[pl.ds(pl.multiple_of(low * 64, 64), 64)]
        return array.at[pl.ds(pl.multiple_of(other * 64, 64), 64)], out.at[low]

    def partners(self, at):
        return all_partners(at)[1]

    def stays(self, at):
        hi, z = at["mesh"][0], at["mesh"][4]
        return lax.rem(z, 2) == hi

    def copy(self, get, at, j, step):
        hi, k, y, c, z = at["mesh"]
        low = lax.div(z, 2)
        partner = (lax.rem(z, 2), k, y, c, 2 * (low if step == 0 else 1 - low) + hi)
        source, target = self.ends(get, at, j, step)
        return pltpu.make_async_remote_copy(
            src_ref=source,
            dst_ref=target,
            send_sem=get(self.send_sem).at[2 * j + step],
            recv_sem=get(self.recv_sem).at[2 * j + step],
            device_id=partner,
            device_id_type=MESH_ID,
        )

    def start(self, get, at):
        stays = self.stays(at)
        for j in range(len(self.arrays)):
            self.copy(get, at, j, 1).start()

        @pl.when(jnp.logical_not(stays))
        def _():
            for j in range(len(self.arrays)):
                self.copy(get, at, j, 0).start()

        @pl.when(stays)
        def _():
            for j in range(len(self.arrays)):
                source, target = self.ends(get, at, j, 0)
                target[...] = source[...]

    def finish(self, get, at):
        for j in range(len(self.arrays)):
            self.copy(get, at, j, 1).wait()

        @pl.when(jnp.logical_not(self.stays(at)))
        def _():
            for j in range(len(self.arrays)):
                self.copy(get, at, j, 0).wait()


def all_partners(at):
    hi, k, y, c, z = at["mesh"]
    plane = [
        ((hi + i) % 2, k, (y + j) % 2, (c + n) % 2, z)
        for i in range(2)
        for j in range(2)
        for n in range(2)
        if i + j + n > 0
    ]
    ways = [((hi + i) % 2, k, y, c, (z + n) % 4) for i in range(2) for n in range(1, 4)]
    return plane, ways


def meet(at):
    plane, ways = all_partners(at)
    greet(plane + ways)
    return plane


def open_program(rows, vectors, facts, packs):
    call = Call()
    slots, swap = Slots(call, rows, True), Swap(call, packs)
    vec_in, fact_in = call.take(vectors), call.take(facts)
    vec_out, fact_out = call.give((16, 1024), F32), call.give((2,) + facts.shape, facts.dtype)
    landed, whole = call.hold((3, 16, 128), F32), call.hold((16, 128), F32)
    vec_send, vec_recv = call.sems(11), call.sems(11)

    def body(get):
        at = place()
        plane = meet(at)
        hi, k, y, c, z = at["mesh"]
        send, recv = get(vec_send), get(vec_recv)

        def push(i, source, target, partner):
            copy = pltpu.make_async_remote_copy(
                src_ref=source,
                dst_ref=target,
                send_sem=send.at[i],
                recv_sem=recv.at[i],
                device_id=partner,
                device_id_type=MESH_ID,
            )
            copy.start()
            return copy

        first = [
            push(n - 1, get(vec_in), get(landed).at[n - 1], (hi, k, y, c, (z + n) % 4))
            for n in range(1, 4)
        ]
        fact_copy = push(10, get(fact_in), get(fact_out).at[1], at["x"])
        slots.start(get, at)
        swap.start(get, at)
        get(fact_out)[0] = get(fact_in)[...]
        for copy in first:
            copy.wait()
        parts = get(landed)
        get(whole)[...] = get(vec_in)[...] + parts[0] + parts[1] + parts[2]
        block = pl.ds(pl.multiple_of(((hi * 2 + y) * 2 + c) * 128, 128), 128)
        second = [
            push(3 + i, get(whole), get(vec_out).at[:, block], partner)
            for i, partner in enumerate(plane)
        ]
        get(vec_out)[:, block] = get(whole)[...]
        for copy in second:
            copy.wait()
        fact_copy.wait()
        slots.finish(get, at)
        swap.finish(get, at)

    outs = call.run(body, "open_program", 13, 12 * MICROSECOND)
    n, m = len(rows), len(packs)
    return outs[:n], outs[n : n + m], outs[n + m], outs[n + m + 1]


def close_program(rows, vectors, packs):
    call = Call()
    slots, swap = Slots(call, rows, False), Swap(call, packs)
    vec_in = call.take(vectors)
    vec_out = call.give((16, 128), F32)
    landed, block_sum = call.hold((7, 16, 128), F32), call.hold((16, 128), F32)
    blocks, along = call.hold((8, 16, 128), F32), call.hold((3, 16, 128), F32)
    vec_send, vec_recv = call.sems(10), call.sems(10)

    def body(get):
        at = place()
        plane = meet(at)
        hi, k, y, c, z = at["mesh"]
        send, recv = get(vec_send), get(vec_recv)
        split = get(blocks)
        for d in range(8):
            split[d] = get(vec_in)[:, d * 128 : d * 128 + 128]

        def push(i, source, target, partner):
            copy = pltpu.make_async_remote_copy(
                src_ref=source,
                dst_ref=target,
                send_sem=send.at[i],
                recv_sem=recv.at[i],
                device_id=partner,
                device_id_type=MESH_ID,
            )
            copy.start()
            return copy

        first = [
            push(
                i,
                split.at[(partner[0] * 2 + partner[2]) * 2 + partner[3]],
                get(landed).at[i],
                partner,
            )
            for i, partner in enumerate(plane)
        ]
        slots.start(get, at)
        swap.start(get, at)
        for copy in first:
            copy.wait()
        total = split[(hi * 2 + y) * 2 + c]
        for i in range(7):
            total = total + get(landed)[i]
        get(block_sum)[...] = total
        second = [
            push(6 + n, get(block_sum), get(along).at[n - 1], (hi, k, y, c, (z + n) % 4))
            for n in range(1, 4)
        ]
        for copy in second:
            copy.wait()
        get(vec_out)[...] = get(block_sum)[...] + get(along)[0] + get(along)[1] + get(along)[2]
        slots.finish(get, at)
        swap.finish(get, at)

    outs = call.run(body, "close_program", 14, 16 * MICROSECOND)
    n, m = len(rows), len(packs)
    return outs[:n], outs[n : n + m], outs[n + m]


def swap_packs(packs, collective):
    call = Call()
    swap = Swap(call, packs)

    def body(get):
        at = place()
        greet([at["x"], at["y"], at["d"]])
        swap.start(get, at)
        swap.finish(get, at)

    return call.run(body, "swap_packs", collective, 5 * MICROSECOND)


def transposed(qkv):
    return [qkv[i].T for i in range(3)]


def pack_rows(matrices):
    stacked = jnp.stack(matrices)
    count, units, width = stacked.shape
    return jnp.swapaxes(stacked.reshape(count, 4, units // 4, width), 0, 1).reshape(4, -1, width)


def over_slots(shares):
    return lax.psum_scatter(shares, "mp", scatter_dimension=0)


def widen(packed):
    return packed if lax.axis_size("k") == 1 else lax.all_gather(packed, "k", axis=2, tiled=True)


def gather_weights(packed):
    copies = lax.axis_size("k")
    rows, width = packed.shape[1], 128 // copies
    packed = lax.all_gather(packed, ("c", "mp")).reshape(2, 4, 4, rows, 128)
    if copies > 1:
        packed = packed.reshape(2, 4, 2, 2, rows, copies, width)
        packed = packed.transpose(1, 4, 2, 5, 3, 0, 6).reshape(4, rows, 4, 2, 128)
        packed = packed.transpose(3, 0, 2, 1, 4)
    return packed


def by_owner(rights):
    copies = lax.axis_size("k")
    if copies == 1 or isinstance(rights, tuple):
        return rights
    shape = rights.shape
    rights = rights.reshape(-1, 2, copies, 2, 2, 128 // copies).transpose(0, 1, 3, 4, 2, 5)
    return rights.reshape(shape)


def narrow(shares):
    shares = shares.astype(F32)
    if lax.axis_size("k") > 1:
        shares = lax.psum_scatter(shares, "k", scatter_dimension=2, tiled=True)
    return shares


def unpack(packed, count):
    parts, rows, width = packed.shape
    unpacked = packed.reshape(parts, count, rows // count, width)
    return jnp.swapaxes(unpacked, 0, 1).reshape(count, parts * rows // count, width)


def row_order(values):
    c = lax.axis_index("c")
    split = values.reshape(2, 2, 2, 2, values.shape[0] // 16).swapaxes(2, 3)
    own = jnp.where(c == 0, split[:, 0], split[:, 1]).reshape(-1)
    other = jnp.where(c == 0, split[:, 1], split[:, 0]).reshape(-1)
    return own, jnp.concatenate([own, other])


def local(
    source,
    target,
    cotangent,
    source_len,
    target_len,
    source_seg,
    target_seg,
    enc_qkv,
    enc_proj,
    enc_up,
    enc_down,
    enc_gain,
    enc_shift,
    dec_qkv,
    dec_proj,
    cross_qkv,
    cross_proj,
    dec_up,
    dec_down,
    dec_gain,
    dec_shift,
):
    copies, z = lax.axis_size("k"), lax.axis_index("mp")
    vectors = jnp.concatenate([enc_gain, enc_shift, dec_gain, dec_shift, dec_shift[:2]], 0)
    if copies > 1:
        vectors = lax.all_gather(vectors, "k", axis=1, tiled=True)
    lane = jnp.arange(128)[None]
    vectors = jnp.where(lane // 32 == z, jnp.tile(vectors, (1, 4)), 0.0)
    facts = jnp.concatenate(
        [
            jnp.concatenate([segments, jnp.broadcast_to(lengths[:, None], (2, 128))], 1)
            for lengths, segments in ((source_len, source_seg), (target_len, target_seg))
        ],
        0,
    )
    facts = jnp.concatenate([facts.reshape(-1, 128), jnp.zeros((4, 128), jnp.int32)], 0)
    first_p = widen(
        pack_rows([*transposed(enc_qkv), enc_proj, *transposed(dec_qkv), dec_proj])
    )
    second_p = jnp.concatenate(
        [pack_rows([*transposed(cross_qkv), cross_proj]), pack_rows([enc_up.T, enc_down])], 1
    )
    second_p, third_p = widen(second_p), widen(pack_rows([dec_up.T, dec_down]))

    (stream_in, target_in), (first_p,), vectors, facts = open_program(
        [source, target], vectors, facts, [first_p]
    )
    if copies > 1:
        vectors = vectors.reshape(16, 2, 2, 2, 4, copies, 32 // copies)
        vectors = vectors.transpose(0, 1, 5, 2, 3, 4, 6).reshape(16, 1024)
    first_w = gather_weights(first_p)
    near = jnp.where(lax.axis_index("hi") == z % 2, facts[0], facts[1])[:36].reshape(2, 2, 1152)
    near = jnp.where(z < 2, near[:, 0], near[:, 1])
    source_length, source_ids = near[0, 1024], near[0, :1024]
    target_length, target_ids = near[1, 1024], near[1, :1024]
    place_own, place_all = row_order(jnp.arange(source_ids.shape[0]))
    source_own, source_all = row_order(source_ids)
    target_own, target_all = row_order(target_ids)
    zero = jnp.zeros_like(place_own)
    source_facts = jnp.stack([source_own, place_own] + [zero] * 6)
    target_facts = jnp.stack([target_own, place_own] + [zero] * 6)

    def key_facts(ids, length):
        live = (place_all < length).astype(jnp.int32)
        blank = jnp.zeros_like(live)
        return jnp.stack([ids, place_all, live] + [blank] * 5, 1)

    source_keys = key_facts(source_all, source_length)
    target_keys = key_facts(target_all, target_length)

    ENC_G, ENC_B, DEC_G, DEC_B = 0, 3, 6, 10
    SELF, CROSS = 256, 0
    Q, QKV, KV, O = (0, 64), (0, 192), (64, 128), (192, 64)
    ENC_UP, ENC_DOWN, DEC_UP, DEC_DOWN = (256, 256), (512, 256), (0, 256), (256, 256)

    def pick(call, packed, span, base=0):
        return Weight(call, packed, base + span[0], span[1])

    def forward_mid(call, residual, gain, shift):
        vec, res = call.take(vectors), call.fetch(residual)
        kept = call.keep((128, 1024), F32)

        def mid(get, total):
            stream = get(res)[...].astype(F32) + total
            get(kept)[...] = stream
            call.save(get, kept)
            unit, scale = unit_of(stream)
            return (unit * get(vec)[gain : gain + 1] + get(vec)[shift : shift + 1]).astype(BF16)

        return mid

    def backward_mid(call, stream, gain, residual=None):
        vec, kept = call.take(vectors), call.fetch(stream)
        res = None if residual is None else call.fetch(residual)
        grad_out, share_out = call.keep((128, 1024), F32), call.give((2, 1024), F32)

        def mid(get, total):
            grad, shares = norm_back(get(kept)[...].astype(F32), get(vec)[gain : gain + 1], total)
            if res is not None:
                grad = grad + get(res)[...]
            get(grad_out)[...] = grad
            call.save(get, grad_out)
            get(share_out)[...] = shares
            return grad.astype(BF16)

        return mid

    def deactivated(call, slope):
        out = call.keep((4, 128, 1024), BF16, 4)

        def store(get, at, row, column, value):
            get(out)[row] = (value * get(slope)[row]).astype(BF16)
            call.save(get, out, row)

        return Kept(out, store)

    call = Call()

    def first_mid(stream, gain, shift):
        vec, res = call.take(vectors), call.fetch(stream)

        def mid(get, total):
            unit, scale = unit_of(get(res)[...].astype(F32))
            return (unit * get(vec)[gain : gain + 1] + get(vec)[shift : shift + 1]).astype(BF16)

        return mid

    jobs = []
    for stream, gain, shift in ((stream_in, ENC_G, ENC_B), (target_in, DEC_G, DEC_B)):
        jobs.append(Job(call, None, first_mid(stream, gain, shift), (None, None, None)))
    swap = Swap(call, [second_p])
    rows_a, rows_c, second_p = run_stage(
        call, jobs, [], "first_rows", 0, flops=24 * MICROSECOND, more=[swap]
    )
    second_w = gather_weights(second_p)

    call = Call()
    swap = Swap(call, [third_p])
    plans = []
    for rows, base in ((rows_a, 0), (rows_c, SELF)):
        query, shared = Plain(call, 256), Shared(call, 512, 256)
        plans.append((call.fetch(rows), pick(call, first_w, QKV, base), query, shared))
    enc_step = Attend(call, plans[0][2].out, plans[0][3].out, source_facts, source_keys, False)
    self_step = Attend(call, plans[1][2].out, plans[1][3].out, target_facts, target_keys, True)
    enc_o, self_o = pick(call, first_w, O), pick(call, first_w, O, SELF)
    mid = forward_mid(call, stream_in, ENC_G + 1, ENC_B + 1)
    job_b = Job(call, (enc_step.mixed, enc_o, [(0, 64)], 0), mid, (None, None, None))
    mid = forward_mid(call, target_in, DEC_G + 1, DEC_B + 1)
    job_d = Job(call, (self_step.mixed, self_o, [(0, 64)], 0), mid, (None, None, None))

    class Project(Extra):
        def partners(self, at):
            return [at["core"]] + swap.partners(at)

        def begin(self, get):
            for plan in plans:
                plan[1].start(get)

        def run(self, get, at):
            swap.start(get, at)
            for rows, weight, query, shared in plans:
                weight.wait(get)
                for row in range(4):
                    for m in range(3):
                        made = nt(get(rows)[row], weight.matrix(get, m * 64, 64))
                        (query if m == 0 else shared).store(get, at, row, m * 256, made)
            for plan in plans:
                plan[3].finish(get)
            swap.finish(get, at)

    (
        third_p,
        enc_q,
        enc_kv,
        self_q,
        self_kv,
        enc_mixed,
        enc_total,
        self_mixed,
        self_total,
        stream_mid,
        rows_b,
        target_mid,
        rows_d,
    ) = run_steps(
        call,
        [Project(), enc_step, self_step, Stage(call, [job_b, job_d], [enc_o, self_o])],
        "self_attention",
        1,
        58 * MICROSECOND,
    )
    third_w = gather_weights(third_p)

    call = Call()
    enc_u, enc_d = pick(call, second_w, ENC_UP), pick(call, second_w, ENC_DOWN)
    cross_a, cross_b = pick(call, second_w, Q), pick(call, second_w, KV)
    cross_o = pick(call, second_w, O)
    feed = Feed(call, rows_b, enc_u, enc_d)
    mid = forward_mid(call, stream_mid, ENC_G + 2, ENC_B + 2)
    shared, query, rows_in = Shared(call, 512), Plain(call, 256), call.fetch(rows_d)
    job_m = Job(call, feed, mid, (cross_b, [(0, 64), (64, 64)], shared.store))
    cross_step = Attend(call, query.out, shared.out, target_facts, source_keys, False)
    mid = forward_mid(call, target_mid, DEC_G + 2, DEC_B + 2)
    job_e = Job(call, (cross_step.mixed, cross_o, [(0, 64)], 0), mid, (None, None, None))
    slots = Slots(call, [cotangent], True)

    def queries(get, at):
        for row in range(4):
            query.store(get, at, row, 0, nt(get(rows_in)[row], cross_a.matrix(get, 0, 64)))

    (
        enc_hidden,
        enc_slope,
        stream_end,
        cross_kv,
        cross_q,
        memory,
        cross_mixed,
        cross_total,
        target_late,
        rows_e,
        grad_out,
    ) = run_steps(
        call,
        [
            Stage(
                call,
                [job_m],
                [enc_u, enc_d, cross_b, cross_a],
                shared.finish,
                True,
                [Local(queries)],
            ),
            cross_step,
            Stage(call, [job_e], [cross_o], more=[slots]),
        ],
        "cross_attention",
        3,
        52 * MICROSECOND,
    )

    call = Call()
    dec_u, dec_d = pick(call, third_w, DEC_UP), pick(call, third_w, DEC_DOWN)
    cross_o = pick(call, second_w, O)
    feed = Feed(call, rows_e, dec_u, dec_d)
    vec, res, cot = call.take(vectors), call.fetch(target_late), call.fetch(grad_out)
    decoded_out, grad_end = call.keep((128, 1024), BF16), call.hold((128, 1024), F32)
    share_out = call.give((2, 1024), F32)

    def last_mid(get, total):
        stream = get(res)[...] + total
        gain, shift = get(vec)[DEC_G + 3 : DEC_G + 4], get(vec)[DEC_B + 3 : DEC_B + 4]
        unit, unused = unit_of(stream)
        get(decoded_out)[...] = (unit * gain + shift).astype(BF16)
        grad, shares = norm_back(stream, gain, get(cot)[...].astype(F32))
        get(grad_end)[...] = grad
        get(share_out)[...] = shares
        call.save(get, decoded_out)
        return grad.astype(BF16)

    active = deactivated(call, feed.slope)
    job_t = Job(call, feed, last_mid, (dec_d, [(0, 256)], active.store))
    mid = backward_mid(call, target_late, DEC_G + 2, grad_end)
    query = Plain(call, 256)
    job_c = Job(call, (active.out, dec_u, [(0, 256)], 0), mid, (cross_o, [(0, 64)], query.store))
    dec_shares = Shares(
        call, [(active.out, 0, feed.rows), (feed.hidden, 0, job_t.gathered)], 256
    )
    back = AttendBack(
        call, cross_q, cross_kv, query.out, cross_total, target_facts, source_keys, False
    )
    cross_shares = Shares(
        call,
        [
            (back.out, 0, rows_d),
            (back.out, 256, memory),
            (back.out, 512, memory),
            (cross_mixed, 0, job_c.gathered),
        ],
        64,
    )
    (
        dec_hidden,
        dec_slope,
        decoded,
        norm_3,
        dec_grad_act,
        grad_rows_e,
        grad_late,
        norm_2,
        cross_grad_mixed,
        grad_rows_d,
        dec_s,
        cross_grads,
        cross_s,
    ) = run_steps(
        call,
        [
            Stage(call, [job_t], [dec_u, dec_d]),
            Stage(call, [job_c], [cross_o], more=[dec_shares]),
            back,
            cross_shares,
        ],
        "back_cross",
        5,
        60 * MICROSECOND,
    )
    dec_g = over_slots(dec_s)

    call = Call()
    cross_a, cross_b = pick(call, second_w, Q), pick(call, second_w, KV)
    self_o, enc_d = pick(call, first_w, O, SELF), pick(call, second_w, ENC_DOWN)
    slots = Slots(call, [decoded], False)
    mid = backward_mid(call, target_mid, DEC_G + 1, grad_late)
    query = Plain(call, 256)
    job_t = Job(call, (cross_grads, cross_a, [(0, 64)], 0), mid, (self_o, [(0, 64)], query.store))
    mid = backward_mid(call, stream_end, ENC_G + 2)
    active = deactivated(call, call.fetch(enc_slope))
    job_s = Job(
        call,
        (cross_grads, cross_b, [(0, 64), (64, 64)], 256),
        mid,
        (enc_d, [(0, 256)], active.store),
    )
    both = call.give((4, 4, 768, 128), BF16, pltpu.HBM)
    shares = Shares(
        call, [(active.out, 0, rows_b), (enc_hidden, 0, job_s.gathered)], 256, both, 256
    )
    (
        decoded,
        grad_mid,
        norm_1,
        self_grad_mixed,
        grad_rows_c,
        grad_stream,
        enc_norm_2,
        enc_grad_act,
        grad_rows_b,
        both_s,
    ) = run_steps(
        call,
        [
            Carry(call, cross_s, both, 0),
            Stage(call, [job_s, job_t], [cross_a, cross_b, self_o, enc_d], more=[slots]),
            shares,
        ],
        "back_both",
        8,
        46 * MICROSECOND,
    )
    both_g = over_slots(both_s)

    call = Call()
    call.take(both_s, pltpu.HBM)
    call.take(dec_g, pltpu.HBM)
    enc_u, enc_o = pick(call, second_w, ENC_UP), pick(call, first_w, O)
    self_a = pick(call, first_w, QKV, SELF)
    self_back = AttendBack(
        call, self_q, self_kv, self_grad_mixed, self_total, target_facts, target_keys, True
    )
    mid = backward_mid(call, stream_mid, ENC_G + 1, grad_stream)
    query = Plain(call, 256)
    job_s = Job(call, (enc_grad_act, enc_u, [(0, 256)], 0), mid, (enc_o, [(0, 64)], query.store))
    mid = backward_mid(call, target_in, DEC_G, grad_mid)
    job_t = Job(call, (self_back.out, self_a, [(0, 64), (64, 64), (128, 64)], 0), mid, None)
    last = call.give((4, 4, 512, 128), BF16, pltpu.HBM)
    self_shares = Shares(
        call,
        [
            (self_back.out, 0, rows_c),
            (self_back.out, 256, rows_c),
            (self_back.out, 512, rows_c),
            (self_mixed, 0, grad_rows_c),
        ],
        64,
        last,
        0,
    )
    enc_back = AttendBack(
        call, enc_q, enc_kv, query.out, enc_total, source_facts, source_keys, False
    )
    enc_shares = Shares(
        call,
        [
            (enc_back.out, 0, rows_a),
            (enc_back.out, 256, rows_a),
            (enc_back.out, 512, rows_a),
            (enc_mixed, 0, job_s.gathered),
        ],
        64,
        last,
        256,
    )
    (
        self_grads,
        grad_stream,
        enc_norm_1,
        enc_grad_mixed,
        grad_rows_a,
        target_grad,
        norm_0,
        last_s,
        enc_grads,
    ) = run_steps(
        call,
        [
            self_back,
            Stage(call, [job_s, job_t], [enc_u, self_a, enc_o], more=[self_shares]),
            enc_back,
            enc_shares,
        ],
        "back_self",
        10,
        58 * MICROSECOND,
    )
    last_g = over_slots(last_s)

    call = Call()
    call.take(last_s, pltpu.HBM)
    enc_a = pick(call, first_w, QKV)
    mid = backward_mid(call, stream_in, ENC_G, grad_stream)
    job = Job(call, (enc_grads, enc_a, [(0, 64), (64, 64), (128, 64)], 0), mid, None)
    swap = Swap(call, [dec_g, both_g])
    source_grad, enc_norm_0, dec_g, both_g = run_stage(
        call, [job], [enc_a], "back_first", 12, flops=14 * MICROSECOND, more=[swap]
    )

    norm_share = jnp.stack(
        [enc_norm_0, enc_norm_1, enc_norm_2], 1
    ).reshape(6, 1024)
    norm_share = jnp.concatenate(
        [
            norm_share,
            jnp.stack([norm_0, norm_1, norm_2, norm_3], 1).reshape(8, 1024),
            jnp.zeros((2, 1024), F32),
        ],
        0,
    )
    (source_grad, target_grad), unused, norm_grad = close_program(
        [source_grad.astype(BF16), target_grad.astype(BF16)],
        by_owner(norm_share),
        [],
    )
    norm_grad = norm_grad.reshape(16, copies, 4, 32 // copies)
    if copies > 1:
        norm_grad = lax.psum_scatter(norm_grad, "k", scatter_dimension=1)
    norm_grad = norm_grad.reshape(16, 4, -1)
    norm_grad = lax.dynamic_index_in_dim(norm_grad, z, 1, False)
    (last_g,) = swap_packs([last_g], 20)
    self_g, enc_g = last_g[:, :256], last_g[:, 256:]

    def attend_shares(packed):
        grads = unpack(narrow(packed), 4)
        return jnp.swapaxes(grads[:3], 1, 2), grads[3]

    def feed_shares(packed):
        grads = unpack(narrow(packed), 2)
        return grads[0].T, grads[1]

    dec_u, dec_d = feed_shares(dec_g)
    enc_u, enc_d = feed_shares(both_g[:, 256:])
    enc_a, enc_o = attend_shares(enc_g)
    cross_a, cross_o = attend_shares(both_g[:, :256])
    self_a, self_o = attend_shares(self_g)
    return (
        decoded,
        source_grad.astype(F32),
        target_grad.astype(F32),
        enc_a,
        enc_o,
        enc_u,
        enc_d,
        norm_grad[:3],
        norm_grad[3:6],
        self_a,
        self_o,
        cross_a,
        cross_o,
        dec_u,
        dec_d,
        norm_grad[6:10],
        norm_grad[10:14],
    )


def solution(mesh):
    dp, seq, mp = (mesh.shape[name] for name in ("dp", "seq", "mp"))
    assert dp % 2 == 0 and seq == 4 and mp == 4
    fine = Mesh(mesh.devices.reshape(2, dp // 2, 2, 2, 4), AXES)
    d, s = ("hi", "k"), ("y", "c")
    rows = P(d, s + ("mp",), None)
    three, flat = P(None, d + s, "mp"), P("mp", d + s)
    up, vector = P(d + s, "mp"), P(None, d + s + ("mp",))
    attention, feeding = (three, flat), (up, flat)
    return jax.shard_map(
        local,
        mesh=fine,
        in_specs=(rows,) * 3
        + (P(d), P(d), P(d, None), P(d, None))
        + attention
        + feeding
        + (vector, vector)
        + attention * 2
        + feeding
        + (vector, vector),
        out_specs=(rows,) * 3
        + attention
        + feeding
        + (vector, vector)
        + attention * 2
        + feeding
        + (vector, vector),
        check_vma=False,
    )
```

```python
import math

import jax
import jax.numpy as jnp
from jax import lax
from jax.experimental import pallas as pl
from jax.experimental.pallas import tpu as pltpu
from jax.sharding import Mesh, PartitionSpec as P

HEAD_DIM = 64
EPSILON = 1e-05
MASKED = -1000000000.0
PAIRS = 8
AXES = ("hi", "k", "y", "c", "mp")
MESH_ID = pl.DeviceIdType.MESH
F32 = jnp.float32
BF16 = jnp.bfloat16


class Call:
    def __init__(self):
        self.known, self.arrays, self.specs = [], [], []
        self.shapes, self.places, self.scratch = [], [], []
        self.fetched, self.kept, self.rows_of = [], [], {}

    def take(self, array, space=pltpu.VMEM):
        if isinstance(array, tuple):
            return array
        for i, known in enumerate(self.known):
            if known is array and self.specs[i].memory_space == space:
                return ("in", i)
        self.known.append(array)
        if space == pltpu.HBM:
            array = pltpu.with_memory_space_constraint(array, pltpu.HBM)
        self.arrays.append(array)
        self.specs.append(pl.BlockSpec(memory_space=space))
        return ("in", len(self.arrays) - 1)

    def fetch(self, array):
        if isinstance(array, tuple):
            return array
        source = self.take(array, pltpu.HBM)
        for i, (known, room, sem) in enumerate(self.fetched):
            if known == source:
                return ("fetch", i)
        self.fetched.append((source, self.hold(array.shape, array.dtype), self.sems(1)))
        return ("fetch", len(self.fetched) - 1)

    def give(self, shape, dtype, space=pltpu.VMEM):
        if space == pltpu.HBM:
            self.shapes.append(pltpu.HBM(shape, dtype))
        else:
            self.shapes.append(jax.ShapeDtypeStruct(shape, dtype))
        self.places.append(pl.BlockSpec(memory_space=space))
        return ("out", len(self.shapes) - 1)

    def keep(self, shape, dtype, parts=1):
        target = self.give(shape, dtype, pltpu.HBM)
        self.kept.append((target, self.hold(shape, dtype), self.sems(parts)))
        return ("keep", len(self.kept) - 1)

    def hold(self, shape, dtype):
        self.scratch.append(pltpu.VMEM(shape, dtype))
        return ("tmp", len(self.scratch) - 1)

    def sems(self, count):
        self.scratch.append(pltpu.SemaphoreType.DMA((count,)))
        return ("tmp", len(self.scratch) - 1)

    def save(self, get, handle, row=None):
        target, room, sems = (get(part) for part in self.kept[handle[1]])
        if row is not None:
            target, room = target.at[row], room.at[row]
        count = sum(1 for known, unused in self.saves if known == handle)
        copy = pltpu.make_async_copy(room, target, sems.at[count])
        copy.start()
        self.saves.append((handle, copy))

    def run(self, body, name, collective=None, flops=0):
        ins, outs = len(self.arrays), len(self.shapes)

        def kernel(*refs):
            parts = {"in": refs[:ins], "out": refs[ins : ins + outs], "tmp": refs[ins + outs :]}
            here, self.saves, self.waited = set(), [], []

            def get(handle):
                kind, i = handle
                if kind == "keep":
                    return get(self.kept[i][1])
                if kind != "fetch":
                    return parts[kind][i]
                source, room, sem = (get(part) for part in self.fetched[i])
                if i not in here:
                    here.add(i)
                    pltpu.make_async_copy(source, room, sem.at[0]).wait()
                return room

            for source, room, sem in self.fetched:
                pltpu.make_async_copy(get(source), get(room), get(sem).at[0]).start()
            body(get)
            for i in range(len(self.fetched)):
                get(("fetch", i))
            for handle, copy in self.saves:
                copy.wait()

        held = [a for a, spec in zip(self.arrays, self.specs) if spec.memory_space == pltpu.VMEM]
        held += [a for a, spec in zip(self.shapes, self.places) if spec.memory_space == pltpu.VMEM]
        held += [x for x in self.scratch if x.dtype in (BF16, F32)]
        room = sum(math.prod(x.shape) * jnp.dtype(x.dtype).itemsize for x in held)
        return pl.pallas_call(
            kernel,
            out_shape=tuple(self.shapes),
            in_specs=self.specs,
            out_specs=tuple(self.places),
            scratch_shapes=self.scratch,
            compiler_params=pltpu.CompilerParams(
                collective_id=collective,
                has_side_effects=collective is not None,
                vmem_limit_bytes=room + (8 << 20),
            ),
            cost_estimate=pl.CostEstimate(flops=flops, bytes_accessed=0, transcendentals=0),
            name=name,
        )(*self.arrays)


MICROSECOND = 1_000_000_000


def nt(left, right):
    return lax.dot_general(left, right, (((1,), (1,)), ((), ())), preferred_element_type=F32)


def nn(left, right):
    return lax.dot_general(left, right, (((1,), (0,)), ((), ())), preferred_element_type=F32)


def tn(left, right):
    return lax.dot_general(left, right, (((0,), (0,)), ((), ())), preferred_element_type=F32)


def unit_of(stream):
    average = jnp.mean(stream, -1, keepdims=True)
    centred = stream - average
    scale = lax.rsqrt(jnp.mean(centred * centred, -1, keepdims=True) + EPSILON)
    return centred * scale, scale


def norm_back(stream, gain, upstream):
    unit, scale = unit_of(stream)
    inner = upstream * gain
    grad = scale * (
        inner - jnp.mean(inner, -1, keepdims=True) - unit * jnp.mean(inner * unit, -1, keepdims=True)
    )
    shares = jnp.concatenate(
        [jnp.sum(upstream * unit, 0, keepdims=True), jnp.sum(upstream, 0, keepdims=True)], 0
    )
    return grad, shares


def gelu_pair(act):
    bell = 0.5 + 0.5 * lax.erf(act * 0.7071067811865476)
    slope = bell + act * (jnp.exp(act * act * -0.5) * 0.3989422804014327)
    return act * bell, slope


def place():
    hi, k, y, c, z = (lax.axis_index(name) for name in AXES)
    return {
        "x": (1 - hi, k, y, c, z),
        "y": (hi, k, 1 - y, c, z),
        "d": (1 - hi, k, 1 - y, c, z),
        "core": (hi, k, y, 1 - c, z),
        "mesh": (hi, k, y, c, z),
        "own_row": y * 2 + hi,
        "x_row": y * 2 + 1 - hi,
        "y_row": (1 - y) * 2 + hi,
        "d_row": (1 - y) * 2 + 1 - hi,
    }


def greet(partners):
    barrier = pltpu.get_barrier_semaphore()
    for partner in partners:
        pl.semaphore_signal(barrier, inc=1, device_id=partner, device_id_type=MESH_ID)
    pl.semaphore_wait(barrier, len(partners))


def along(at):
    hi, k, y, c, z = at["mesh"]
    return [(hi, k, y, c, lax.rem(z + n, 4)) for n in range(1, 4)]


class Weight:
    def __init__(self, call, packed, first, count):
        self.call, self.source = call, call.take(packed, pltpu.HBM)
        self.room = call.hold((4, count, 1024), BF16)
        self.sem = call.sems(1)
        self.first, self.count = first, count

    def start(self, get):
        source, room, sem = get(self.source), get(self.room), get(self.sem)
        for q in range(4):
            for c in range(2):
                pltpu.make_async_copy(
                    source.at[c, :, q, pl.ds(self.first, self.count), :],
                    room.at[:, :, pl.ds((q * 2 + c) * 128, 128)],
                    sem.at[0],
                ).start()

    def wait(self, get):
        if self in self.call.waited:
            return
        self.call.waited.append(self)
        room = get(self.room)
        pltpu.make_async_copy(room, room, get(self.sem).at[0]).wait()

    def matrix(self, get, first, count):
        return get(self.room)[:, first : first + count, :].reshape(4 * count, 1024)


def stack(blocks):
    return blocks[0] if len(blocks) == 1 else jnp.concatenate(blocks, 0)


class Feed:
    def __init__(self, call, rows, up, down):
        self.call, self.rows, self.weights = call, call.fetch(rows), [up, down]
        self.hidden = call.keep((4, 128, 1024), BF16, 4)
        self.slope = call.keep((4, 128, 1024), F32, 4)

    def part(self, get, *rows):
        up, down = self.weights
        whole = stack([get(self.rows)[row] for row in rows])
        made, slope = gelu_pair(nt(whole, up.matrix(get, 0, 256)))
        made = made.astype(BF16)
        for i, row in enumerate(rows):
            get(self.hidden)[row] = made[i * 128 : (i + 1) * 128]
            get(self.slope)[row] = slope[i * 128 : (i + 1) * 128]
            self.call.save(get, self.hidden, row)
            self.call.save(get, self.slope, row)
        return nn(made, down.matrix(get, 0, 256))


class Job:
    def __init__(self, call, left, mid, right):
        self.call, self.left, self.mid, self.right = call, left, mid, right
        self.kept, self.shares = getattr(mid, "kept", None), getattr(mid, "shares", None)
        if left is not None:
            self.rows_in = None if isinstance(left, Feed) else call.fetch(left[0])
            self.out_first = call.hold((2, 128, 1024), BF16)
            self.out_edge = call.hold((2, 64, 1024), BF16)
            self.out_late = call.hold((2, 64, 1024), BF16)
            self.keep = call.hold((2, 64, 1024), F32)
            self.own = call.hold((128, 1024), F32)
            self.landed = call.hold((6, 64, 1024), BF16)
            self.sum_send, self.sum_recv = call.sems(6), call.sems(6)
        self.gathered = None
        if right is not None:
            self.gathered = call.keep((4, 128, 1024), BF16, 4)
            self.row_send, self.row_recv = call.sems(6), call.sems(6)

    def lefts(self):
        return self.left.weights if isinstance(self.left, Feed) else [self.left[1]]

    def part(self, get, *rows):
        if isinstance(self.left, Feed):
            return self.left.part(get, *rows)
        unused, weight, picks, column = self.left
        total = None
        for first, count in picks:
            width = 4 * count
            left = stack([get(self.rows_in)[row, :, column : column + width] for row in rows])
            term = nn(left, weight.matrix(get, first, count))
            total = term if total is None else total + term
            column += width
        return total

    def send(self, get, i, source, target, partner):
        copy = pltpu.make_async_remote_copy(
            src_ref=source,
            dst_ref=target,
            send_sem=get(self.sum_send).at[i],
            recv_sem=get(self.sum_recv).at[i],
            device_id=partner,
            device_id_type=MESH_ID,
        )
        copy.start()
        return copy

    def sum_start(self, get, at):
        first, edge, landed = get(self.out_first), get(self.out_edge), get(self.landed)
        keep = get(self.keep)
        self.copies = [None] * 6
        first[0] = self.part(get, at["d_row"]).astype(BF16)
        self.copies[0] = self.send(
            get, 0, first.at[0, pl.ds(0, 64)], landed.at[0], at["x"]
        )
        self.copies[1] = self.send(
            get, 1, first.at[0, pl.ds(64, 64)], landed.at[1], at["y"]
        )
        part = self.part(get, at["x_row"], at["y_row"])
        edge[0] = part[:64].astype(BF16)
        keep[0] = part[64:128]
        self.copies[2] = self.send(get, 2, edge.at[0], landed.at[2], at["x"])
        edge[1] = part[192:].astype(BF16)
        keep[1] = part[128:192]
        self.copies[3] = self.send(get, 3, edge.at[1], landed.at[3], at["y"])

    def sum_forward(self, get, at):
        late, landed, keep = get(self.out_late), get(self.landed), get(self.keep)
        self.copies[0].wait_recv()
        late[1] = (keep[1] + landed[0].astype(F32)).astype(BF16)
        self.copies[4] = self.send(get, 4, late.at[1], landed.at[4], at["y"])
        self.copies[1].wait_recv()
        late[0] = (keep[0] + landed[1].astype(F32)).astype(BF16)
        self.copies[5] = self.send(get, 5, late.at[0], landed.at[5], at["x"])

    def sum_own(self, get, at):
        get(self.own)[...] = self.part(get, at["own_row"])

    def sum_end(self, get):
        landed, own = get(self.landed), get(self.own)
        for i in (2, 3, 4, 5):
            self.copies[i].wait_recv()
        upper = own[:64] + landed[2].astype(F32) + landed[4].astype(F32)
        lower = own[64:] + landed[5].astype(F32) + landed[3].astype(F32)
        return jnp.concatenate([upper, lower], 0)

    def row_copy(self, get, i, row, half, partner):
        block = get(self.gathered).at[row, pl.ds(half * 64, 64)]
        copy = pltpu.make_async_remote_copy(
            src_ref=block,
            dst_ref=block,
            send_sem=get(self.row_send).at[i],
            recv_sem=get(self.row_recv).at[i],
            device_id=partner,
            device_id_type=MESH_ID,
        )
        copy.start()
        return copy

    def rows_start(self, get, at, normed):
        get(self.gathered)[at["own_row"]] = normed
        self.call.save(get, self.gathered, at["own_row"])
        self.moves = [
            self.row_copy(get, 0, at["own_row"], 0, at["y"]),
            self.row_copy(get, 1, at["own_row"], 1, at["x"]),
            self.row_copy(get, 2, at["own_row"], 1, at["y"]),
            self.row_copy(get, 3, at["own_row"], 0, at["x"]),
        ]

    def rows_forward(self, get, at):
        self.moves[0].wait_recv()
        self.moves.append(self.row_copy(get, 4, at["y_row"], 0, at["x"]))
        self.moves[1].wait_recv()
        self.moves.append(self.row_copy(get, 5, at["x_row"], 1, at["y"]))

    def product(self, get, at, row):
        weight, picks, store = self.right
        if weight is None:
            return
        weight.wait(get)
        rows = get(self.gathered)[row]
        column = 0
        for first, count in picks:
            store(get, at, row, column, nt(rows, weight.matrix(get, first, count)))
            column += 4 * count

    def sums(self, get, at):
        for weight in self.lefts():
            weight.wait(get)
        self.sum_start(get, at)

    def settle(self, get, at):
        normed = self.mid(get, self.sum_end(get) if self.left is not None else None)
        if self.right is not None:
            self.rows_start(get, at, normed)

    def collect(self, get, at, sides=True, far=True):
        for moves, row in (((3,), "x_row"), ((2,), "y_row"), ((4, 5), "d_row")):
            if far if row == "d_row" else sides:
                for i in moves:
                    self.moves[i].wait_recv()
                self.call.save(get, self.gathered, at[row])
                self.product(get, at, at[row])

    def drain(self):
        if self.left is not None:
            for copy in self.copies:
                copy.wait_send()
        if self.right is not None:
            for copy in self.moves:
                copy.wait_send()


def run_body(call, work, names, name, collective, flops):
    groups = {"all": meeting, "z": along, "ways": lambda at: all_partners(at)[1]}

    def body(get):
        at = place()
        partners = []
        for group in names:
            partners += groups[group](at) if group in groups else [at[group]]
        greet(partners)
        work(get, at)

    return call.run(body, name, collective, flops)


class Kept:
    def __init__(self, out, store):
        self.out, self.store = out, store


class Plain:
    def __init__(self, call, width):
        self.call, self.width = call, width
        self.out = call.keep((4, 128, width), BF16, 4)

    def store(self, get, at, row, column, value):
        get(self.out)[row, :, column : column + value.shape[1]] = value.astype(BF16)
        if column + value.shape[1] == self.width:
            self.call.save(get, self.out, row)


class Shared:
    def __init__(self, call, width, skip=0):
        self.call, self.out = call, call.keep((2, 4, 128, width), BF16, 2)
        self.send_sem, self.recv_sem = call.sems(4), call.sems(4)
        self.width, self.skip, self.copies, self.blocks = width, skip, [], 0

    def store(self, get, at, row, column, value):
        out = get(self.out)
        column = column - self.skip
        out[0, row, :, column : column + value.shape[1]] = value.astype(BF16)
        if column + value.shape[1] == self.width:
            i = len(self.copies)
            copy = pltpu.make_async_remote_copy(
                src_ref=out.at[0, row],
                dst_ref=out.at[1, row],
                send_sem=get(self.send_sem).at[i],
                recv_sem=get(self.recv_sem).at[i],
                device_id=at["core"],
                device_id_type=MESH_ID,
            )
            copy.start()
            self.copies.append(copy)

    def finish(self, get):
        self.call.save(get, self.out, 0)
        for copy in self.copies:
            copy.wait()
        self.call.save(get, self.out, 1)


def query_and_shared(call, width):
    query, shared = Plain(call, width), Shared(call, 2 * width, skip=width)

    def store(get, at, row, column, value):
        if column < width:
            query.store(get, at, row, column, value)
        else:
            shared.store(get, at, row, column, value)

    return store, shared.finish


def lanes_of(head, rows):
    lane = lax.broadcasted_iota(jnp.int32, (rows, 128), 1)
    return lane // HEAD_DIM == head


SOURCE, TARGET, PLACE, LIVE = 0, 1, 2, 3


def allowed_bias(rows, columns, query_kind, key_kind, causal):
    allowed = columns[:, key_kind : key_kind + 1] == rows[query_kind : query_kind + 1, :512]
    allowed = allowed & (columns[:, LIVE + key_kind : LIVE + key_kind + 1] > 0.5)
    if causal:
        allowed = allowed & (columns[:, PLACE : PLACE + 1] <= rows[PLACE : PLACE + 1, :512])
    return jnp.where(allowed, 0.0, MASKED)


class Attend:
    def __init__(self, call, queries, key_value, rows, columns, kinds):
        self.call, self.kinds = call, kinds
        self.queries, self.key_value = call.fetch(queries), call.fetch(key_value)
        self.rows, self.columns = call.take(rows), call.fetch(columns)
        self.mixed = call.keep((4, 128, 256), BF16)
        self.total = call.give((8, 512), F32)
        self.bias = call.hold((1024, 512), F32)

    def late(self, get, at):
        self.prepare(get)
        self.pairs(get, 0, 2)
        self.call.save(get, self.mixed)

    def prepare(self, get):
        mask = get(self.bias)
        mask[...] = allowed_bias(get(self.rows), get(self.columns), *self.kinds)

    def pairs(self, get, first, last):
        mask = get(self.bias)
        q_ref, kv_ref = get(self.queries), get(self.key_value)
        mixed_ref, total_ref = get(self.mixed), get(self.total)

        def pair_step(pair, carry):
            lanes = pl.ds(pl.multiple_of(pair * 128, 128), 128)
            value_lanes = pl.ds(pl.multiple_of(256 + pair * 128, 128), 128)
            keys = kv_ref[:, :, :, lanes].reshape(1024, 128)
            values = kv_ref[:, :, :, value_lanes].reshape(1024, 128)
            for block in range(2):
                span = slice(block * 256, block * 256 + 256)
                queries = q_ref[2 * block : 2 * block + 2, :, lanes].reshape(256, 128)
                mixed = []
                for head in range(2):
                    picked = jnp.where(lanes_of(head, 256), queries * 0.125, 0.0).astype(BF16)
                    scores = nt(keys, picked) + mask[:, span]
                    top = jnp.max(scores, 0, keepdims=True)
                    raised = jnp.exp(scores - top)
                    total = jnp.sum(raised, 0, keepdims=True)
                    probs = (raised * (1.0 / total)).astype(BF16)
                    mixed.append(tn(values, probs)[head * HEAD_DIM : (head + 1) * HEAD_DIM])
                    total_ref[pl.ds(pair * 2 + head, 1), span] = top + jnp.log(total)
                mixed = jnp.concatenate(mixed, 0).T.astype(BF16)
                mixed_ref[2 * block : 2 * block + 2, :, lanes] = mixed.reshape(2, 128, 128)
            return carry

        lax.fori_loop(first, last, pair_step, 0)


class AttendBack:
    def __init__(self, call, queries, key_value, grad_mixed, total, rows, columns, kinds):
        self.call, self.kinds = call, kinds
        self.queries, self.key_value = call.fetch(queries), call.fetch(key_value)
        self.grad_mixed, self.total = call.fetch(grad_mixed), call.take(total)
        self.rows, self.columns = call.take(rows), call.fetch(columns)
        self.out = call.keep((4, 128, 768), BF16)
        self.bias, self.sums = call.hold((1024, 512), F32), call.hold((1024, 512), F32)
        self.away, self.landed = call.hold((2, 512, 256), BF16), call.hold((2, 512, 256), BF16)
        self.send_sem, self.recv_sem = call.sems(2), call.sems(2)

    def partners(self, at):
        return [at["core"]]

    def late(self, get, at):
        self.prepare(get)
        for pair in range(2):
            self.pair(get, at, pair)
        self.end(get)

    def prepare(self, get):
        mask = get(self.bias)
        mask[...] = allowed_bias(get(self.rows), get(self.columns), *self.kinds)
        self.copies = []

    def pair(self, get, at, pair):
        out, mask, sums = get(self.out), get(self.bias), get(self.sums)
        away, here = get(self.away), get(self.landed)
        q_ref, kv_ref = get(self.queries), get(self.key_value)
        grad_ref, total_ref = get(self.grad_mixed), get(self.total)
        lanes = slice(pair * 128, pair * 128 + 128)
        keys_pair = kv_ref[:, :, :, lanes].reshape(1024, 128)
        values_pair = kv_ref[:, :, :, 256 + pair * 128 : 384 + pair * 128].reshape(1024, 128)
        key_sum = slice(pair * 256, pair * 256 + 128)
        value_sum = slice(pair * 256 + 128, pair * 256 + 256)
        for block in range(2):
            span = slice(block * 256, block * 256 + 256)
            two = slice(2 * block, 2 * block + 2)
            q_block = q_ref[two, :, lanes].reshape(256, 128)
            g_block = grad_ref[two, :, lanes].reshape(256, 128)
            grad_query = []
            for head in range(2):
                inside = lanes_of(head, 256)
                picked = jnp.where(inside, q_block * 1.0, 0.0).astype(BF16)
                grads = jnp.where(inside, g_block * 1.0, 0.0).astype(BF16)
                scores = nt(keys_pair, picked) * 0.125 + mask[:, span]
                probs = jnp.exp(scores - total_ref[pair * 2 + head : pair * 2 + head + 1, span])
                weighted = probs * nt(values_pair, grads)
                inner = jnp.sum(weighted, 0, keepdims=True)
                grad_raw = ((weighted - probs * inner) * 0.125).astype(BF16)
                value_term = nn(probs.astype(BF16), grads)
                key_term = nn(grad_raw, picked)
                if block == 0 and head == 0:
                    sums[:, key_sum] = key_term
                    sums[:, value_sum] = value_term
                else:
                    sums[:, key_sum] += key_term
                    sums[:, value_sum] += value_term
                grad_query.append(tn(keys_pair, grad_raw)[head * HEAD_DIM : (head + 1) * HEAD_DIM])
            grad_query = jnp.concatenate(grad_query, 0).T.astype(BF16)
            out[two, :, lanes] = grad_query.reshape(2, 128, 128)
        away[pair] = sums[512:, pair * 256 : pair * 256 + 256].astype(BF16)
        copy = pltpu.make_async_remote_copy(
            src_ref=away.at[pair],
            dst_ref=here.at[pair],
            send_sem=get(self.send_sem).at[pair],
            recv_sem=get(self.recv_sem).at[pair],
            device_id=at["core"],
            device_id_type=MESH_ID,
        )
        copy.start()
        self.copies.append(copy)

    def end(self, get):
        out, sums, here = get(self.out), get(self.sums), get(self.landed)
        for pair in range(2):
            self.copies[pair].wait()
            both = sums[:512, pair * 256 : pair * 256 + 256] + here[pair].astype(F32)
            both = both.astype(BF16).reshape(4, 128, 256)
            out[:, :, 256 + pair * 128 : 384 + pair * 128] = both[:, :, :128]
            out[:, :, 512 + pair * 128 : 640 + pair * 128] = both[:, :, 128:]
        self.call.save(get, self.out)


class Shares:
    def __init__(self, call, pairs, count, out=None, base=0):
        self.call, self.count, self.base = call, count, base
        self.handles = [
            (call.fetch(left), column, call.fetch(right))
            for left, column, right in pairs
        ]
        shape = (4, 4, len(pairs) * count, 128)
        sends = len(pairs) * max(1, count // 64)
        self.made, self.landed = call.hold((2,) + shape, BF16), call.hold(shape, BF16)
        self.send_sem, self.recv_sem = call.sems(sends), call.sems(sends)
        self.rows = shape[2]
        self.out = call.give(shape, BF16, pltpu.HBM) if out is None else out
        self.saved = out is not False
        self.room, self.save_sem = call.hold(shape, BF16), call.sems(1)

    def partners(self, at):
        return [at["core"]]

    def send(self, get, at, part):
        i = len(self.copies)
        copy = pltpu.make_async_remote_copy(
            src_ref=get(self.made).at[(1 - lax.axis_index("c"),) + part],
            dst_ref=get(self.landed).at[part],
            send_sem=get(self.send_sem).at[i],
            recv_sem=get(self.recv_sem).at[i],
            device_id=at["core"],
            device_id_type=MESH_ID,
        )
        copy.start()
        self.copies.append((part, copy))

    def middle(self, get, at):
        self.copies, every, count = [], slice(None), self.count
        made = get(self.made)
        for m, (left, column, right) in enumerate(self.handles):
            left, right = get(left), get(right)
            span = slice(m * count, (m + 1) * count)
            for first in range(0, 4 * count, 256):
                start = column + first
                product = tn(
                    left[:, :, start : start + 256].reshape(512, 256), right[...].reshape(512, 1024)
                )
                for inner in range(0, 256, count):
                    z = (first + inner) // count
                    for d in range(8):
                        made[d % 2, z, d // 2, span, :] = product[
                            inner : inner + count, d * 128 : d * 128 + 128
                        ].astype(BF16)
                if count == 256:
                    self.send(get, at, (first // 256, every, pl.ds(m * count, count)))
            if count < 256:
                self.send(get, at, (every, every, pl.ds(m * count, count)))

    def finish(self, get, at):
        core = lax.axis_index("c")
        for part, copy in self.copies:
            copy.wait()
            own = get(self.made)[(core,) + part].astype(F32)
            get(self.room)[part] = (own + get(self.landed)[part].astype(F32)).astype(BF16)
        if not self.saved:
            return
        target = get(self.out).at[:, :, pl.ds(self.base, self.rows)]
        copy = pltpu.make_async_copy(get(self.room), target, get(self.save_sem).at[0])
        copy.start()
        self.call.saves.append((None, copy))


def push(source, target, send_sem, recv_sem, partner):
    return pltpu.make_async_remote_copy(
        src_ref=source,
        dst_ref=target,
        send_sem=send_sem,
        recv_sem=recv_sem,
        device_id=partner,
        device_id_type=MESH_ID,
    )


class Spread:
    def __init__(self, call, pack):
        rows = pack.shape if not isinstance(pack, tuple) else (4, call.rows_of[pack], 128)
        self.pack = call.take(pack, pltpu.HBM)
        self.out = call.give((2, 4) + tuple(rows), BF16, pltpu.HBM)
        self.send_sem, self.recv_sem = call.sems(3), call.sems(3)
        self.core_send, self.core_recv, self.own_sem = call.sems(4), call.sems(4), call.sems(1)

    def block(self, get, at, n):
        c, z = at["mesh"][3:]
        return get(self.out).at[c, lax.rem(z + 4 - n, 4)]

    def move(self, get, at, n):
        return push(
            get(self.pack),
            self.block(get, at, 0),
            get(self.send_sem).at[n - 1],
            get(self.recv_sem).at[n - 1],
            along(at)[n - 1],
        )

    def to_core(self, get, at, n):
        target = self.block(get, at, n)
        return push(
            get(self.pack) if n == 0 else target,
            target,
            get(self.core_send).at[n],
            get(self.core_recv).at[n],
            at["core"],
        )

    def own(self, get, at):
        return pltpu.make_async_copy(
            get(self.pack), self.block(get, at, 0), get(self.own_sem).at[0]
        )

    def launch(self, get, at):
        for n in (2, 1, 3):
            self.move(get, at, n).start()
        self.to_core(get, at, 0).start()
        self.own(get, at).start()

    def pass_on(self, get, at):
        for n in (1, 3, 2):
            self.move(get, at, n).wait_recv()
            self.to_core(get, at, n).start()

    def finish(self, get, at):
        self.own(get, at).wait()
        for n in range(4):
            self.to_core(get, at, n).wait()
        for n in range(1, 4):
            self.move(get, at, n).wait_send()


class Gather:
    def __init__(self, call, shares, rows, first=0):
        self.call, self.shares, self.rows, self.first = call, call.take(shares, pltpu.HBM), rows, first
        self.landed, self.own = call.hold((3, 4, rows, 128), BF16), call.hold((4, rows, 128), BF16)
        self.out = call.keep((4, rows, 128), BF16)
        self.send_sem, self.recv_sem, self.own_sem = call.sems(3), call.sems(3), call.sems(1)

    def share(self, get, plane):
        return get(self.shares).at[plane, :, pl.ds(self.first, self.rows)]

    def move(self, get, at, n):
        return push(
            self.share(get, lax.rem(at["mesh"][4] + n, 4)),
            get(self.landed).at[n - 1],
            get(self.send_sem).at[n - 1],
            get(self.recv_sem).at[n - 1],
            along(at)[n - 1],
        )

    def mine(self, get, at):
        return pltpu.make_async_copy(
            self.share(get, at["mesh"][4]), get(self.own), get(self.own_sem).at[0]
        )

    def launch(self, get, at):
        for n in (2, 1, 3):
            self.move(get, at, n).start()
        self.mine(get, at).start()

    def finish(self, get, at):
        self.mine(get, at).wait()
        for n in range(1, 4):
            self.move(get, at, n).wait()
        landed, own, out = get(self.landed), get(self.own), get(self.out)
        for q in range(4):
            total = own[q].astype(F32) + landed[0, q].astype(F32)
            out[q] = (total + landed[1, q].astype(F32) + landed[2, q].astype(F32)).astype(BF16)
        self.call.save(get, self.out)


class Swap:
    def __init__(self, call, pack):
        self.pack = call.take(pack, pltpu.HBM)
        rows = call.rows_of[pack] if isinstance(pack, tuple) else pack.shape[1]
        self.out = call.give((4, rows, 128), BF16, pltpu.HBM)
        call.rows_of[self.out] = rows
        self.send_sem, self.recv_sem, self.own_sem = call.sems(3), call.sems(3), call.sems(1)

    def start(self, get, at):
        hi, k, y, c, z = at["mesh"]
        own = hi * 2 + y
        pack, out = get(self.pack), get(self.out)
        self.copies = [pltpu.make_async_copy(pack.at[own], out.at[own], get(self.own_sem).at[0])]
        for i, (name, q) in enumerate(
            (("d", (1 - hi) * 2 + 1 - y), ("x", (1 - hi) * 2 + y), ("y", hi * 2 + 1 - y))
        ):
            send, recv = get(self.send_sem).at[i], get(self.recv_sem).at[i]
            self.copies.append(push(pack.at[q], out.at[own], send, recv, at[name]))
        for copy in self.copies:
            copy.start()

    def finish(self, get, at):
        for copy in self.copies:
            copy.wait()


class Slots:
    def __init__(self, call, arrays, inward):
        self.inward = inward
        self.call, self.arrays = call, [call.fetch(array) for array in arrays]
        shape = (128, 1024) if inward else (2, 64, 1024)
        self.outs = [call.keep(shape, BF16) for array in arrays]
        self.send_sem, self.recv_sem = call.sems(2 * len(arrays)), call.sems(2 * len(arrays))

    def ends(self, get, at, j, step):
        z = at["mesh"][4]
        low = lax.div(z, 2)
        other = low if step == 0 else 1 - low
        array, out = get(self.arrays[j]), get(self.outs[j])
        if self.inward:
            return array.at[other], out.at[pl.ds(pl.multiple_of(low * 64, 64), 64)]
        return array.at[pl.ds(pl.multiple_of(other * 64, 64), 64)], out.at[low]

    def stays(self, at):
        hi, z = at["mesh"][0], at["mesh"][4]
        return lax.rem(z, 2) == hi

    def copy(self, get, at, j, step):
        hi, k, y, c, z = at["mesh"]
        low = lax.div(z, 2)
        partner = (lax.rem(z, 2), k, y, c, 2 * (low if step == 0 else 1 - low) + hi)
        source, target = self.ends(get, at, j, step)
        return pltpu.make_async_remote_copy(
            src_ref=source,
            dst_ref=target,
            send_sem=get(self.send_sem).at[2 * j + step],
            recv_sem=get(self.recv_sem).at[2 * j + step],
            device_id=partner,
            device_id_type=MESH_ID,
        )

    def start(self, get, at):
        stays = self.stays(at)
        for j in range(len(self.arrays)):
            self.copy(get, at, j, 1).start()

        @pl.when(jnp.logical_not(stays))
        def _():
            for j in range(len(self.arrays)):
                self.copy(get, at, j, 0).start()

        @pl.when(stays)
        def _():
            for j in range(len(self.arrays)):
                source, target = self.ends(get, at, j, 0)
                target[...] = source[...]

    def finish(self, get, at):
        for j in range(len(self.arrays)):
            self.copy(get, at, j, 1).wait()

        @pl.when(jnp.logical_not(self.stays(at)))
        def _():
            for j in range(len(self.arrays)):
                self.copy(get, at, j, 0).wait()

        for out in self.outs:
            self.call.save(get, out)


def all_partners(at):
    hi, k, y, c, z = at["mesh"]
    plane = [
        ((hi + i) % 2, k, (y + j) % 2, (c + n) % 2, z)
        for i in range(2)
        for j in range(2)
        for n in range(2)
        if i + j + n > 0
    ]
    ways = [((hi + i) % 2, k, y, c, (z + n) % 4) for i in range(2) for n in range(1, 4)]
    return plane, ways


def meeting(at):
    plane, ways = all_partners(at)
    return plane + ways


class Vectors:
    def __init__(self, call, vectors, inward):
        self.inward = inward
        self.source = call.take(vectors)
        self.out = call.give((16, 1024) if inward else (16, 128), F32)
        self.landed, self.whole = call.hold((7, 16, 128), F32), call.hold((16, 128), F32)
        self.split, self.along = call.hold((8, 16, 128), F32), call.hold((3, 16, 128), F32)
        self.send_sem, self.recv_sem = call.sems(10), call.sems(10)

    def move(self, get, i, source, target, partner):
        return push(source, target, get(self.send_sem).at[i], get(self.recv_sem).at[i], partner)

    def planes(self, get, at, source):
        return [
            self.move(get, n, source, get(self.along).at[n], partner)
            for n, partner in enumerate(along(at))
        ]

    def block(self, at):
        hi, k, y, c, z = at["mesh"]
        return (hi * 2 + y) * 2 + c

    def start(self, get, at):
        plane = all_partners(at)[0]
        if self.inward:
            self.copies = self.planes(get, at, get(self.source))
        else:
            split = get(self.split)
            for d in range(8):
                split[d] = get(self.source)[:, d * 128 : d * 128 + 128]
            self.copies = [
                self.move(
                    get,
                    3 + i,
                    split.at[(partner[0] * 2 + partner[2]) * 2 + partner[3]],
                    get(self.landed).at[i],
                    partner,
                )
                for i, partner in enumerate(plane)
            ]
        for copy in self.copies:
            copy.start()

    def second(self, get, at):
        plane = all_partners(at)[0]
        for copy in self.copies:
            copy.wait()
        whole, out = get(self.whole), get(self.out)
        if self.inward:
            whole[...] = get(self.source)[...] + jnp.sum(get(self.along)[...], 0)
            block = pl.ds(pl.multiple_of(self.block(at) * 128, 128), 128)
            out[:, block] = whole[...]
            self.copies = [
                self.move(get, 3 + i, whole, out.at[:, block], partner)
                for i, partner in enumerate(plane)
            ]
        else:
            whole[...] = get(self.split)[self.block(at)] + jnp.sum(get(self.landed)[...], 0)
            self.copies = self.planes(get, at, whole)
        for copy in self.copies:
            copy.start()

    def finish(self, get, at):
        for copy in self.copies:
            copy.wait()
        if not self.inward:
            get(self.out)[...] = get(self.whole)[...] + jnp.sum(get(self.along)[...], 0)


class Pack:
    def __init__(self, call, matrices):
        self.parts = [(call.fetch(array), index, across) for array, index, across in matrices]
        counts = [
            (array.shape[-1] if across else array.shape[-2]) // 4
            for array, index, across in matrices
        ]
        self.counts = counts
        self.out = call.hold((4, sum(counts), 128), BF16)
        call.rows_of[self.out] = sum(counts)

    def make(self, get):
        out, base = get(self.out), 0
        for (part, index, across), count in zip(self.parts, self.counts, strict=True):
            part = get(part)
            whole = part[...] if index is None else part[index]
            if across:
                whole = whole.astype(F32).T.astype(BF16)
            out[:, base : base + count, :] = whole.reshape(4, count, 128)
            base += count


def by_owner(rows, back=False):
    copies = lax.axis_size("k")
    if copies == 1:
        return rows
    shape, width = rows.shape, 128 // copies
    if back:
        rows = rows.reshape(-1, 2, 2, 2, copies, width).transpose(0, 1, 4, 2, 3, 5)
    else:
        rows = rows.reshape(-1, 2, copies, 2, 2, width).transpose(0, 1, 3, 4, 2, 5)
    return rows.reshape(shape)


def unpacked(packs, rows, wide):
    call = Call()
    rows_in = [call.fetch(array) for array in rows]
    ins = [call.fetch(array) for array in packs]
    plans = []
    for handle, array, kinds in zip(ins, packs, wide, strict=True):
        base = 0
        for kind in kinds:
            count = 256 if kind in ("up", "down") else 64
            if kind == "q":
                out = call.give((3, 128, 256), F32)
                plans += [(handle, base + i * 64, 64, out, i, True) for i in range(3)]
                base += 192
                continue
            shape = (128, 4 * count) if kind == "up" else (4 * count, 128)
            plans.append((handle, base, count, call.give(shape, F32), None, kind == "up"))
            base += count
    outs = [call.give(array.shape, F32) for array in rows]

    def body(get):
        for handle, base, count, out, index, across in plans:
            whole = get(handle)[:, base : base + count, :].astype(F32).reshape(4 * count, 128)
            whole = whole.T if across else whole
            if index is None:
                get(out)[...] = whole
            else:
                get(out)[index] = whole
        for source, out in zip(rows_in, outs, strict=True):
            get(out)[...] = get(source)[...].astype(F32)

    return call.run(body, "unpacked", None, 4 * MICROSECOND)


def local(
    source,
    target,
    cotangent,
    source_len,
    target_len,
    source_seg,
    target_seg,
    enc_qkv,
    enc_proj,
    enc_up,
    enc_down,
    enc_gain,
    enc_shift,
    dec_qkv,
    dec_proj,
    cross_qkv,
    cross_proj,
    dec_up,
    dec_down,
    dec_gain,
    dec_shift,
):
    copies, z = lax.axis_size("k"), lax.axis_index("mp")
    vectors = jnp.concatenate([enc_gain, enc_shift, dec_gain, dec_shift, dec_shift[:2]], 0)
    if copies > 1:
        vectors = lax.all_gather(vectors, "k", axis=1, tiled=True)
    vectors = vectors.reshape(16, copies, 1, 32 // copies)
    vectors = jnp.where(jnp.arange(4)[:, None] == z, vectors, 0.0).reshape(16, 128)
    facts = jnp.concatenate([source_seg, target_seg], 0)
    lengths = jnp.concatenate([source_len, target_len], 0)
    facts = jnp.concatenate([facts, jnp.broadcast_to(lengths[:, None], (4, 128))], 1)

    def widen(array, axis):
        return array if copies == 1 else lax.all_gather(array, "k", axis=axis, tiled=True)

    enc_qkv, dec_qkv, cross_qkv = (widen(array, 1) for array in (enc_qkv, dec_qkv, cross_qkv))
    enc_proj, dec_proj, cross_proj = (widen(array, 1) for array in (enc_proj, dec_proj, cross_proj))
    enc_up, dec_up = widen(enc_up, 0), widen(dec_up, 0)
    enc_down, dec_down = widen(enc_down, 1), widen(dec_down, 1)

    ENC_G, ENC_B, DEC_G, DEC_B = 0, 3, 6, 10
    SELF, SELF_O = 192, 64
    Q, QKV, KV, O, FIRST_O = (0, 64), (0, 192), (64, 128), (192, 64), (0, 64)
    UP, DOWN = (0, 256), (256, 256)

    def pick(call, packed, span, base=0):
        return Weight(call, packed, base + span[0], span[1])

    def forward_mid(call, residual, gain, shift, normed=None):
        vec, res = call.take(vectors), call.fetch(residual)
        kept = call.keep((128, 1024), F32)

        def mid(get, total):
            stream = get(res)[...].astype(F32) + total
            get(kept)[...] = stream
            call.save(get, kept)
            unit, scale = unit_of(stream)
            made = (unit * get(vec)[gain : gain + 1] + get(vec)[shift : shift + 1]).astype(BF16)
            if normed is not None:
                get(normed)[...] = made
                call.save(get, normed)
            return made

        mid.kept = kept
        return mid

    def backward_mid(call, stream, gain, residual=None, dtype=F32):
        vec, kept = call.take(vectors), call.fetch(stream)
        res = None if residual is None else call.fetch(residual)
        grad_out, share_out = call.keep((128, 1024), dtype), call.give((2, 1024), F32)

        def mid(get, total):
            grad, shares = norm_back(get(kept)[...].astype(F32), get(vec)[gain : gain + 1], total)
            if res is not None:
                grad = grad + get(res)[...]
            get(grad_out)[...] = grad.astype(dtype)
            call.save(get, grad_out)
            get(share_out)[...] = shares
            return grad.astype(BF16)

        mid.kept, mid.shares = grad_out, share_out
        return mid

    def deactivated(call, slope):
        out = call.keep((4, 128, 1024), BF16, 4)

        def store(get, at, row, column, value):
            get(out)[row] = (value * get(slope)[row]).astype(BF16)
            call.save(get, out, row)

        return Kept(out, store)

    call = Call()
    slots = Slots(call, [by_owner(source), by_owner(target)], True)
    stream_h, target_h = slots.outs
    first_vectors = Vectors(call, vectors, True)
    fact_in = call.take(facts)
    fact_own, fact_room = call.hold((2, 8, 128), F32), call.hold((2, 8, 128), F32)
    fact_rows, fact_columns = call.give((8, 1024), F32), call.keep((1024, 128), F32)
    fact_send, fact_recv = call.sems(1), call.sems(1)

    def three(array):
        return [(array, i, True) for i in range(3)]

    pack_1 = Pack(call, three(enc_qkv) + three(dec_qkv))
    pack_o = Pack(call, [(enc_proj, None, False), (dec_proj, None, False)])
    pack_2 = Pack(call, [(enc_up, None, True), (enc_down, None, False)])
    pack_3 = Pack(call, three(cross_qkv) + [(cross_proj, None, False)])
    pack_4 = Pack(call, [(dec_up, None, True), (dec_down, None, False)])
    swap_1, swap_o, swap_2, swap_3, swap_4 = (
        Swap(call, pack.out) for pack in (pack_1, pack_o, pack_2, pack_3, pack_4)
    )
    spread_1, spread_o, spread_2, spread_3, spread_4 = (
        Spread(call, swap.out) for swap in (swap_1, swap_o, swap_2, swap_3, swap_4)
    )

    def count_facts(get):
        given = get(fact_in)[...]
        lane = lax.broadcasted_iota(jnp.int32, (4, 128), 1)
        table = jnp.where(lane == 0, given[:, 1024:].astype(F32), 0.0)
        for p in range(1, PAIRS):
            before = jnp.sum((given[:, :1024] < p).astype(F32), 1, keepdims=True)
            table = table + jnp.where(lane == p, before, 0.0)
        own = get(fact_own)
        own[...] = jnp.zeros_like(own)
        for slot in range(2):
            own[slot, 0:1] = table[slot : slot + 1]
            own[slot, 1:2] = table[2 + slot : 3 + slot]

    def place_facts(get, at):
        hi, k, y, c, z = at["mesh"]
        slot = lax.div(z, 2)
        table = jnp.where(lax.rem(z, 2) == hi, get(fact_own)[slot], get(fact_room)[slot])

        def kinds(index):
            core = jnp.where(index < 512, c, 1 - c)
            part = index % 512
            place = (part // 256) * 512 + core * 256 + ((part // 64) % 2) * 128
            place = (place + ((part // 128) % 2) * 64 + part % 64).astype(F32)
            found = []
            for row in range(2):
                ids = jnp.zeros_like(place)
                for p in range(1, PAIRS):
                    ids = ids + jnp.where(place >= table[row : row + 1, p : p + 1], 1.0, 0.0)
                found.append(ids)
            live = [jnp.where(place < table[row : row + 1, 0:1], 1.0, 0.0) for row in range(2)]
            return found + [place] + live

        across = kinds(lax.broadcasted_iota(jnp.int32, (1, 1024), 1))
        down = kinds(lax.broadcasted_iota(jnp.int32, (1024, 128), 0))
        rows, columns = get(fact_rows), get(fact_columns)
        rows[...] = jnp.zeros_like(rows)
        lane = lax.broadcasted_iota(jnp.int32, (1024, 128), 1)
        wide = jnp.zeros((1024, 128), F32)
        for i in range(5):
            rows[i : i + 1] = across[i]
            wide = jnp.where(lane == i, down[i], wide)
        columns[...] = wide
        call.save(get, fact_columns)

    def first_mid(stream, gain, shift):
        def mid(get, total):
            unit, scale = unit_of(get(stream)[...].astype(F32))
            vec = get(first_vectors.out)
            return (unit * vec[gain : gain + 1] + vec[shift : shift + 1]).astype(BF16)

        return mid

    job_a = Job(call, None, first_mid(stream_h, ENC_G, ENC_B), (None, None, None))
    job_c = Job(call, None, first_mid(target_h, DEC_G, DEC_B), (None, None, None))
    vectors = first_vectors.out

    plans = []
    for rows, base in ((job_a.gathered, 0), (job_c.gathered, SELF)):
        query, shared = Plain(call, 256), Shared(call, 512, 256)
        plans.append((call.fetch(rows), pick(call, spread_1.out, QKV, base), query, shared))
    enc_step = Attend(
        call, plans[0][2].out, plans[0][3].out, fact_rows, fact_columns, (SOURCE, SOURCE, False)
    )
    self_step = Attend(
        call, plans[1][2].out, plans[1][3].out, fact_rows, fact_columns, (TARGET, TARGET, True)
    )
    enc_o, self_o = pick(call, spread_o.out, FIRST_O), pick(call, spread_o.out, FIRST_O, SELF_O)
    mid = forward_mid(call, stream_h, ENC_G + 1, ENC_B + 1)
    job_b = Job(call, (enc_step.mixed, enc_o, [(0, 64)], 0), mid, (None, None, None))
    mid = forward_mid(call, target_h, DEC_G + 1, DEC_B + 1)
    cross_a, cross_b = pick(call, spread_3.out, Q), pick(call, spread_3.out, KV)
    cross_o = pick(call, spread_3.out, O)
    query, shared = Plain(call, 256), Shared(call, 512)
    job_d = Job(call, (self_step.mixed, self_o, [(0, 64)], 0), mid, (cross_a, [(0, 64)], query.store))
    enc_u, enc_d = pick(call, spread_2.out, UP), pick(call, spread_2.out, DOWN)
    feed = Feed(call, job_b.gathered, enc_u, enc_d)
    mid = forward_mid(call, job_b.kept, ENC_G + 2, ENC_B + 2)
    job_m = Job(call, feed, mid, (cross_b, [(0, 64), (64, 64)], shared.store))
    cross_step = Attend(
        call, query.out, shared.out, fact_rows, fact_columns, (TARGET, SOURCE, False)
    )
    mid = forward_mid(call, job_d.kept, DEC_G + 2, DEC_B + 2)
    job_e = Job(call, (cross_step.mixed, cross_o, [(0, 64)], 0), mid, (None, None, None))

    def onward(get, at):
        first_vectors.start(get, at)
        slots.start(get, at)
        pack_1.make(get)
        swap_1.start(get, at)
        count_facts(get)
        fact_copy = push(
            get(fact_own), get(fact_room), get(fact_send).at[0], get(fact_recv).at[0], at["x"]
        )
        fact_copy.start()
        first_vectors.second(get, at)
        swap_1.finish(get, at)
        spread_1.launch(get, at)
        for pack in (pack_o, pack_2):
            pack.make(get)
        first_vectors.finish(get, at)
        slots.finish(get, at)
        job_a.settle(get, at)
        job_c.settle(get, at)
        fact_copy.wait()
        place_facts(get, at)
        job_a.rows_forward(get, at)
        job_c.rows_forward(get, at)
        swap_o.start(get, at)
        swap_2.start(get, at)
        for pack in (pack_3, pack_4):
            pack.make(get)
        job_a.collect(get, at)
        job_c.collect(get, at)
        enc_step.prepare(get)
        swap_o.finish(get, at)
        swap_2.finish(get, at)
        job_a.drain()
        job_c.drain()
        spread_1.pass_on(get, at)
        spread_o.launch(get, at)
        spread_2.launch(get, at)
        swap_3.start(get, at)
        swap_4.start(get, at)
        spread_1.finish(get, at)
        for plan in plans:
            plan[1].start(get)
        for rows, weight, queries, keys in plans:
            weight.wait(get)
            for row in range(4):
                for m in range(3):
                    made = nt(get(rows)[row], weight.matrix(get, m * 64, 64))
                    (queries if m == 0 else keys).store(get, at, row, m * 256, made)
        for plan in plans:
            plan[3].finish(get)
        enc_step.pairs(get, 0, 2)
        call.save(get, enc_step.mixed)
        spread_o.pass_on(get, at)
        swap_3.finish(get, at)
        swap_4.finish(get, at)
        spread_o.finish(get, at)
        enc_o.start(get)
        self_o.start(get)
        job_b.sums(get, at)
        self_step.prepare(get)
        self_step.pairs(get, 0, 1)
        job_b.sum_forward(get, at)
        self_step.pairs(get, 1, 2)
        call.save(get, self_step.mixed)
        job_b.sum_own(get, at)
        job_d.sums(get, at)
        job_b.settle(get, at)
        job_d.sum_forward(get, at)
        job_d.sum_own(get, at)
        job_b.rows_forward(get, at)
        spread_2.pass_on(get, at)
        spread_3.launch(get, at)
        job_d.settle(get, at)
        spread_2.finish(get, at)
        enc_u.start(get)
        enc_d.start(get)
        job_b.collect(get, at)
        job_m.sums(get, at)
        job_d.rows_forward(get, at)
        job_m.sum_forward(get, at)
        job_m.sum_own(get, at)
        spread_3.pass_on(get, at)
        spread_4.launch(get, at)
        job_m.settle(get, at)
        spread_3.finish(get, at)
        for weight in (cross_a, cross_b, cross_o):
            weight.start(get)
        job_m.rows_forward(get, at)
        job_d.product(get, at, at["own_row"])
        job_d.collect(get, at)
        job_m.product(get, at, at["own_row"])
        job_m.collect(get, at)
        for job in (job_b, job_d, job_m):
            job.drain()
        shared.finish(get)
        cross_step.late(get, at)
        job_e.sums(get, at)
        job_e.sum_forward(get, at)
        job_e.sum_own(get, at)
        job_e.settle(get, at)
        spread_4.pass_on(get, at)
        job_e.rows_forward(get, at)
        job_e.collect(get, at)
        job_e.drain()
        spread_4.finish(get, at)

    (
        stream_in,
        target_in,
        vectors,
        fact_rows,
        fact_columns,
        unused,
        unused,
        unused,
        unused,
        unused,
        first_w,
        first_o,
        second_w,
        cross_w,
        third_w,
        rows_a,
        rows_c,
        enc_q,
        enc_kv,
        self_q,
        self_kv,
        enc_mixed,
        enc_total,
        self_mixed,
        self_total,
        stream_mid,
        rows_b,
        target_mid,
        cross_q,
        cross_kv,
        rows_d,
        enc_hidden,
        enc_slope,
        stream_end,
        memory,
        cross_mixed,
        cross_total,
        target_late,
        rows_e,
    ) = run_body(call, onward, ["all"], "onward", 0, 170 * MICROSECOND)

    call = Call()
    dec_u, dec_d = pick(call, third_w, UP), pick(call, third_w, DOWN)
    cross_o = pick(call, cross_w, O)
    feed = Feed(call, rows_e, dec_u, dec_d)
    slots = Slots(call, [by_owner(cotangent)], True)
    vec, res, cot = call.take(vectors), call.fetch(target_late), slots.outs[0]
    decoded_out, grad_end = call.keep((128, 1024), BF16), call.hold((128, 1024), F32)
    share_out = call.give((2, 1024), F32)

    def last_mid(get, total):
        stream = get(res)[...] + total
        gain, shift = get(vec)[DEC_G + 3 : DEC_G + 4], get(vec)[DEC_B + 3 : DEC_B + 4]
        unit, unused = unit_of(stream)
        get(decoded_out)[...] = (unit * gain + shift).astype(BF16)
        grad, shares = norm_back(stream, gain, get(cot)[...].astype(F32))
        get(grad_end)[...] = grad
        get(share_out)[...] = shares
        call.save(get, decoded_out)
        return grad.astype(BF16)

    active = deactivated(call, feed.slope)
    job_t = Job(call, feed, last_mid, (dec_d, [(0, 256)], active.store))
    mid = backward_mid(call, target_late, DEC_G + 2, grad_end)
    query = Plain(call, 256)
    job_c = Job(call, (active.out, dec_u, [(0, 256)], 0), mid, (cross_o, [(0, 64)], query.store))
    down_shares = Shares(call, [(feed.hidden, 0, job_t.gathered)], 256, False)
    joined = call.give((4, 4, 512, 128), BF16, pltpu.HBM)
    up_shares = Shares(call, [(active.out, 0, feed.rows)], 256, joined, 0)
    back = AttendBack(
        call,
        cross_q,
        cross_kv,
        query.out,
        cross_total,
        fact_rows,
        fact_columns,
        (TARGET, SOURCE, False),
    )
    cross_shares = Shares(
        call,
        [
            (back.out, 0, rows_d),
            (back.out, 256, memory),
            (back.out, 512, memory),
            (cross_mixed, 0, job_c.gathered),
        ],
        64,
        joined,
        256,
    )
    gather = Gather(call, down_shares.room, 256)

    def turning(get, at):
        for weight in (dec_u, dec_d, cross_o):
            weight.start(get)
        slots.start(get, at)
        job_t.sums(get, at)
        job_t.sum_forward(get, at)
        job_t.sum_own(get, at)
        slots.finish(get, at)
        job_t.settle(get, at)
        job_t.product(get, at, at["own_row"])
        job_t.rows_forward(get, at)
        job_t.collect(get, at)
        job_c.sums(get, at)
        job_c.sum_forward(get, at)
        job_c.sum_own(get, at)
        down_shares.middle(get, at)
        down_shares.finish(get, at)
        job_c.settle(get, at)
        gather.launch(get, at)
        job_c.product(get, at, at["own_row"])
        job_c.rows_forward(get, at)
        up_shares.middle(get, at)
        job_c.collect(get, at)
        up_shares.finish(get, at)
        job_t.drain()
        job_c.drain()
        back.late(get, at)
        cross_shares.middle(get, at)
        cross_shares.finish(get, at)
        gather.finish(get, at)

    (
        dec_hidden,
        dec_slope,
        unused,
        decoded,
        norm_3,
        dec_grad_act,
        grad_rows_e,
        grad_late,
        norm_2,
        cross_grad_mixed,
        grad_rows_d,
        joined_s,
        cross_grads,
        down_g,
    ) = run_body(call, turning, ["all"], "turning", 1, 62 * MICROSECOND)

    call = Call()
    cross_a, cross_b = pick(call, cross_w, Q), pick(call, cross_w, KV)
    self_o, enc_d = pick(call, first_o, FIRST_O, SELF_O), pick(call, second_w, DOWN)
    slots = Slots(call, [decoded], False)
    mid = backward_mid(call, target_mid, DEC_G + 1, grad_late)
    query = Plain(call, 256)
    job_t = Job(call, (cross_grads, cross_a, [(0, 64)], 0), mid, (self_o, [(0, 64)], query.store))
    mid = backward_mid(call, stream_end, ENC_G + 2)
    active = deactivated(call, call.fetch(enc_slope))
    job_s = Job(
        call,
        (cross_grads, cross_b, [(0, 64), (64, 64)], 256),
        mid,
        (enc_d, [(0, 256)], active.store),
    )
    shares = Shares(
        call, [(active.out, 0, rows_b), (enc_hidden, 0, job_s.gathered)], 256
    )
    gather, swap = Gather(call, joined_s, 512), Swap(call, down_g)

    def backing(get, at):
        gather.launch(get, at)
        for weight in (cross_b, cross_a, enc_d, self_o):
            weight.start(get)
        job_s.sums(get, at)
        job_t.sums(get, at)
        job_s.sum_forward(get, at)
        job_t.sum_forward(get, at)
        job_s.sum_own(get, at)
        job_s.settle(get, at)
        job_t.sum_own(get, at)
        job_t.settle(get, at)
        slots.start(get, at)
        job_s.product(get, at, at["own_row"])
        job_s.rows_forward(get, at)
        job_t.product(get, at, at["own_row"])
        job_t.rows_forward(get, at)
        swap.start(get, at)
        job_s.collect(get, at)
        shares.middle(get, at)
        job_t.collect(get, at)
        shares.finish(get, at)
        job_s.drain()
        job_t.drain()
        slots.finish(get, at)
        swap.finish(get, at)
        gather.finish(get, at)

    (
        decoded,
        grad_mid,
        norm_1,
        self_grad_mixed,
        grad_rows_c,
        grad_stream,
        enc_norm_2,
        enc_grad_act,
        grad_rows_b,
        feed_s,
        up_cross_g,
        down_g,
    ) = run_body(call, backing, ["x", "y", "core", "d", "ways"], "backing", 2, 46 * MICROSECOND)

    call = Call()
    enc_u, enc_o = pick(call, second_w, UP), pick(call, first_o, FIRST_O)
    self_a = pick(call, first_w, QKV, SELF)
    self_back = AttendBack(
        call,
        self_q,
        self_kv,
        self_grad_mixed,
        self_total,
        fact_rows,
        fact_columns,
        (TARGET, TARGET, True),
    )
    mid = backward_mid(call, stream_mid, ENC_G + 1, grad_stream)
    query = Plain(call, 256)
    job_s = Job(call, (enc_grad_act, enc_u, [(0, 256)], 0), mid, (enc_o, [(0, 64)], query.store))
    mid = backward_mid(call, target_in, DEC_G, grad_mid, BF16)
    job_t = Job(call, (self_back.out, self_a, [(0, 64), (64, 64), (128, 64)], 0), mid, None)
    self_shares = Shares(
        call,
        [
            (self_back.out, 0, rows_c),
            (self_back.out, 256, rows_c),
            (self_back.out, 512, rows_c),
            (self_mixed, 0, grad_rows_c),
        ],
        64,
        False,
    )
    enc_back = AttendBack(
        call,
        enc_q,
        enc_kv,
        query.out,
        enc_total,
        fact_rows,
        fact_columns,
        (SOURCE, SOURCE, False),
    )
    enc_shares = Shares(
        call,
        [
            (enc_back.out, 0, rows_a),
            (enc_back.out, 256, rows_a),
            (enc_back.out, 512, rows_a),
            (enc_mixed, 0, job_s.gathered),
        ],
        64,
        False,
    )
    enc_a = pick(call, first_w, QKV)
    mid = backward_mid(call, stream_in, ENC_G, job_s.kept, BF16)
    job_f = Job(call, (enc_back.out, enc_a, [(0, 64), (64, 64), (128, 64)], 0), mid, None)
    gather_f, gather_s = Gather(call, feed_s, 512), Gather(call, self_shares.room, 256)
    gather_e = Gather(call, enc_shares.room, 256)
    for gather, rows in ((gather_f, 512), (gather_s, 256), (gather_e, 256)):
        call.rows_of[gather.out] = rows
    swap, swap_f = Swap(call, up_cross_g), Swap(call, gather_f.out)
    swap_s, swap_e = Swap(call, gather_s.out), Swap(call, gather_e.out)
    target_slots, source_slots = Slots(call, [job_t.kept], False), Slots(call, [job_f.kept], False)
    others = [call.take(norm) for norm in (norm_1, norm_2, norm_3, enc_norm_2)]
    norm_sum = call.hold((16, 1024), F32)
    sums = Vectors(call, norm_sum, False)

    def selfward(get, at):
        gather_f.launch(get, at)
        for weight in (enc_u, self_a, enc_o, enc_a):
            weight.start(get)
        self_back.prepare(get)
        job_s.sums(get, at)
        self_back.pair(get, at, 0)
        job_s.sum_forward(get, at)
        self_back.pair(get, at, 1)
        self_back.end(get)
        job_s.sum_own(get, at)
        job_t.sums(get, at)
        job_s.settle(get, at)
        job_t.sum_forward(get, at)
        job_t.sum_own(get, at)
        self_shares.middle(get, at)
        self_shares.finish(get, at)
        gather_s.launch(get, at)
        job_s.product(get, at, at["own_row"])
        job_s.rows_forward(get, at)
        job_t.settle(get, at)
        target_slots.start(get, at)
        swap.start(get, at)
        job_s.collect(get, at)
        job_s.drain()
        job_t.drain()
        enc_back.late(get, at)
        enc_shares.middle(get, at)
        enc_shares.finish(get, at)
        gather_e.launch(get, at)
        job_f.sums(get, at)
        job_f.sum_forward(get, at)
        job_f.sum_own(get, at)
        job_f.settle(get, at)
        source_slots.start(get, at)
        total = get(norm_sum)
        for row, shares in (
            (0, get(job_f.shares)),
            (1, get(job_s.shares)),
            (2, get(others[3])),
            (6, get(job_t.shares)),
            (7, get(others[0])),
            (8, get(others[1])),
            (9, get(others[2])),
        ):
            below = row + (3 if row < 6 else 4)
            total[row : row + 1] = shares[0:1]
            total[below : below + 1] = shares[1:2]
        total[14:16] = jnp.zeros((2, 1024), F32)
        sums.start(get, at)
        job_f.drain()
        gather_f.finish(get, at)
        swap_f.start(get, at)
        sums.second(get, at)
        target_slots.finish(get, at)
        gather_s.finish(get, at)
        swap_s.start(get, at)
        sums.finish(get, at)
        source_slots.finish(get, at)
        swap.finish(get, at)
        swap_f.finish(get, at)
        gather_e.finish(get, at)
        swap_e.start(get, at)
        swap_s.finish(get, at)
        swap_e.finish(get, at)

    made = run_body(call, selfward, ["all"], "selfward", 3, 105 * MICROSECOND)
    up_cross_g, feed_g, self_g, enc_g, target_grad, source_grad, norm_grad = made[-7:]
    norm_grad = norm_grad.reshape(16, copies, 4, 32 // copies)
    if copies > 1:
        norm_grad = lax.psum_scatter(norm_grad, "k", scatter_dimension=1)
    norm_grad = norm_grad.reshape(16, 4, -1)
    norm_grad = lax.dynamic_index_in_dim(norm_grad, z, 1, False)

    (
        dec_d,
        dec_u,
        cross_a,
        cross_o,
        enc_u,
        enc_d,
        self_a,
        self_o,
        enc_a,
        enc_o,
        source_grad,
        target_grad,
    ) = unpacked(
        [down_g, up_cross_g, feed_g, self_g, enc_g],
        [source_grad, target_grad],
        [("down",), ("up", "q", "o"), ("up", "down"), ("q", "o"), ("q", "o")],
    )

    def narrow(array, axis):
        if copies == 1:
            return array
        return lax.psum_scatter(array, "k", scatter_dimension=axis, tiled=True)

    enc_a, self_a, cross_a = (narrow(array, 1) for array in (enc_a, self_a, cross_a))
    enc_o, self_o, cross_o = (narrow(array, 1) for array in (enc_o, self_o, cross_o))
    enc_u, dec_u = narrow(enc_u, 0), narrow(dec_u, 0)
    enc_d, dec_d = narrow(enc_d, 1), narrow(dec_d, 1)
    return (
        by_owner(decoded, True),
        by_owner(source_grad, True),
        by_owner(target_grad, True),
        enc_a,
        enc_o,
        enc_u,
        enc_d,
        norm_grad[:3],
        norm_grad[3:6],
        self_a,
        self_o,
        cross_a,
        cross_o,
        dec_u,
        dec_d,
        norm_grad[6:10],
        norm_grad[10:14],
    )


def solution(mesh):
    dp, seq, mp = (mesh.shape[name] for name in ("dp", "seq", "mp"))
    assert dp % 2 == 0 and seq == 4 and mp == 4
    fine = Mesh(mesh.devices.reshape(2, dp // 2, 2, 2, 4), AXES)
    d, s = ("hi", "k"), ("y", "c")
    rows = P(d, s + ("mp",), None)
    three, flat = P(None, d + s, "mp"), P("mp", d + s)
    up, vector = P(d + s, "mp"), P(None, d + s + ("mp",))
    attention, feeding = (three, flat), (up, flat)
    return jax.shard_map(
        local,
        mesh=fine,
        in_specs=(rows,) * 3
        + (P(d), P(d), P(d, None), P(d, None))
        + attention
        + feeding
        + (vector, vector)
        + attention * 2
        + feeding
        + (vector, vector),
        out_specs=(rows,) * 3
        + attention
        + feeding
        + (vector, vector)
        + attention * 2
        + feeding
        + (vector, vector),
        check_vma=False,
    )
```

```python
import math

import jax
import jax.numpy as jnp
from jax import lax
from jax.experimental import pallas as pl
from jax.experimental.pallas import tpu as pltpu
from jax.sharding import Mesh, PartitionSpec as P

HEAD_DIM = 64
EPSILON = 1e-05
MASKED = -1000000000.0
PAIRS = 8
AXES = ("hi", "k", "y", "c", "mp")
MESH_ID = pl.DeviceIdType.MESH
F32 = jnp.float32
BF16 = jnp.bfloat16


class Call:
    def __init__(self):
        self.known, self.arrays, self.specs = [], [], []
        self.shapes, self.places, self.scratch = [], [], []
        self.fetched, self.kept, self.rows_of = [], [], {}

    def take(self, array, space=pltpu.VMEM):
        if isinstance(array, tuple):
            return array
        for i, known in enumerate(self.known):
            if known is array and self.specs[i].memory_space == space:
                return ("in", i)
        self.known.append(array)
        if space == pltpu.HBM:
            array = pltpu.with_memory_space_constraint(array, pltpu.HBM)
        self.arrays.append(array)
        self.specs.append(pl.BlockSpec(memory_space=space))
        return ("in", len(self.arrays) - 1)

    def fetch(self, array):
        if isinstance(array, tuple):
            return array
        source = self.take(array, pltpu.HBM)
        for i, (known, room, sem) in enumerate(self.fetched):
            if known == source:
                return ("fetch", i)
        self.fetched.append((source, self.hold(array.shape, array.dtype), self.sems(1)))
        return ("fetch", len(self.fetched) - 1)

    def give(self, shape, dtype, space=pltpu.VMEM):
        if space == pltpu.HBM:
            self.shapes.append(pltpu.HBM(shape, dtype))
        else:
            self.shapes.append(jax.ShapeDtypeStruct(shape, dtype))
        self.places.append(pl.BlockSpec(memory_space=space))
        return ("out", len(self.shapes) - 1)

    def keep(self, shape, dtype, parts=1):
        target = self.give(shape, dtype, pltpu.HBM)
        self.kept.append((target, self.hold(shape, dtype), self.sems(parts)))
        return ("keep", len(self.kept) - 1)

    def hold(self, shape, dtype):
        self.scratch.append(pltpu.VMEM(shape, dtype))
        return ("tmp", len(self.scratch) - 1)

    def sems(self, count):
        self.scratch.append(pltpu.SemaphoreType.DMA((count,)))
        return ("tmp", len(self.scratch) - 1)

    def save(self, get, handle, row=None):
        target, room, sems = (get(part) for part in self.kept[handle[1]])
        if row is not None:
            target, room = target.at[row], room.at[row]
        count = sum(1 for known, unused in self.saves if known == handle)
        copy = pltpu.make_async_copy(room, target, sems.at[count])
        copy.start()
        self.saves.append((handle, copy))

    def run(self, body, name, collective=None, flops=0):
        ins, outs = len(self.arrays), len(self.shapes)

        def kernel(*refs):
            parts = {"in": refs[:ins], "out": refs[ins : ins + outs], "tmp": refs[ins + outs :]}
            here, self.saves, self.waited = set(), [], []

            def get(handle):
                kind, i = handle
                if kind == "keep":
                    return get(self.kept[i][1])
                if kind != "fetch":
                    return parts[kind][i]
                source, room, sem = (get(part) for part in self.fetched[i])
                if i not in here:
                    here.add(i)
                    pltpu.make_async_copy(source, room, sem.at[0]).wait()
                return room

            for source, room, sem in self.fetched:
                pltpu.make_async_copy(get(source), get(room), get(sem).at[0]).start()
            body(get)
            for i in range(len(self.fetched)):
                get(("fetch", i))
            for handle, copy in self.saves:
                copy.wait()

        held = [a for a, spec in zip(self.arrays, self.specs) if spec.memory_space == pltpu.VMEM]
        held += [a for a, spec in zip(self.shapes, self.places) if spec.memory_space == pltpu.VMEM]
        held += [x for x in self.scratch if x.dtype in (BF16, F32)]
        room = sum(math.prod(x.shape) * jnp.dtype(x.dtype).itemsize for x in held)
        return pl.pallas_call(
            kernel,
            out_shape=tuple(self.shapes),
            in_specs=self.specs,
            out_specs=tuple(self.places),
            scratch_shapes=self.scratch,
            compiler_params=pltpu.CompilerParams(
                collective_id=collective,
                has_side_effects=collective is not None,
                vmem_limit_bytes=room + (8 << 20),
            ),
            cost_estimate=pl.CostEstimate(flops=flops, bytes_accessed=0, transcendentals=0),
            name=name,
        )(*self.arrays)


MICROSECOND = 1_000_000_000


def nt(left, right):
    return lax.dot_general(left, right, (((1,), (1,)), ((), ())), preferred_element_type=F32)


def nn(left, right):
    return lax.dot_general(left, right, (((1,), (0,)), ((), ())), preferred_element_type=F32)


def tn(left, right):
    return lax.dot_general(left, right, (((0,), (0,)), ((), ())), preferred_element_type=F32)


def unit_of(stream):
    average = jnp.mean(stream, -1, keepdims=True)
    centred = stream - average
    scale = lax.rsqrt(jnp.mean(centred * centred, -1, keepdims=True) + EPSILON)
    return centred * scale, scale


def norm_back(stream, gain, upstream):
    unit, scale = unit_of(stream)
    inner = upstream * gain
    grad = scale * (
        inner - jnp.mean(inner, -1, keepdims=True) - unit * jnp.mean(inner * unit, -1, keepdims=True)
    )
    shares = jnp.concatenate(
        [jnp.sum(upstream * unit, 0, keepdims=True), jnp.sum(upstream, 0, keepdims=True)], 0
    )
    return grad, shares


def gelu_pair(act):
    bell = 0.5 + 0.5 * lax.erf(act * 0.7071067811865476)
    slope = bell + act * (jnp.exp(act * act * -0.5) * 0.3989422804014327)
    return act * bell, slope


def place():
    hi, k, y, c, z = (lax.axis_index(name) for name in AXES)
    return {
        "x": (1 - hi, k, y, c, z),
        "y": (hi, k, 1 - y, c, z),
        "d": (1 - hi, k, 1 - y, c, z),
        "core": (hi, k, y, 1 - c, z),
        "mesh": (hi, k, y, c, z),
        "own_row": y * 2 + hi,
        "x_row": y * 2 + 1 - hi,
        "y_row": (1 - y) * 2 + hi,
        "d_row": (1 - y) * 2 + 1 - hi,
    }


def greet(partners):
    barrier = pltpu.get_barrier_semaphore()
    for partner in partners:
        pl.semaphore_signal(barrier, inc=1, device_id=partner, device_id_type=MESH_ID)
    pl.semaphore_wait(barrier, len(partners))


def along(at):
    hi, k, y, c, z = at["mesh"]
    return [(hi, k, y, c, lax.rem(z + n, 4)) for n in range(1, 4)]


class Weight:
    def __init__(self, call, packed, first, count):
        self.call, self.source = call, call.take(packed, pltpu.HBM)
        self.room = call.hold((4, count, 1024), BF16)
        self.sem = call.sems(1)
        self.first, self.count = first, count

    def start(self, get):
        source, room, sem = get(self.source), get(self.room), get(self.sem)
        for q in range(4):
            for c in range(2):
                pltpu.make_async_copy(
                    source.at[c, :, q, pl.ds(self.first, self.count), :],
                    room.at[:, :, pl.ds((q * 2 + c) * 128, 128)],
                    sem.at[0],
                ).start()

    def wait(self, get):
        if self in self.call.waited:
            return
        self.call.waited.append(self)
        room = get(self.room)
        pltpu.make_async_copy(room, room, get(self.sem).at[0]).wait()

    def matrix(self, get, first, count):
        return get(self.room)[:, first : first + count, :].reshape(4 * count, 1024)


def stack(blocks):
    return blocks[0] if len(blocks) == 1 else jnp.concatenate(blocks, 0)


class Feed:
    def __init__(self, call, rows, up, down):
        self.call, self.rows, self.weights = call, call.fetch(rows), [up, down]
        self.hidden = call.keep((4, 128, 1024), BF16, 4)
        self.slope = call.keep((4, 128, 1024), F32, 4)

    def part(self, get, *rows):
        up, down = self.weights
        whole = stack([get(self.rows)[row] for row in rows])
        made, slope = gelu_pair(nt(whole, up.matrix(get, 0, 256)))
        made = made.astype(BF16)
        for i, row in enumerate(rows):
            get(self.hidden)[row] = made[i * 128 : (i + 1) * 128]
            get(self.slope)[row] = slope[i * 128 : (i + 1) * 128]
            self.call.save(get, self.hidden, row)
            self.call.save(get, self.slope, row)
        return nn(made, down.matrix(get, 0, 256))


class Job:
    def __init__(self, call, left, mid, right):
        self.call, self.left, self.mid, self.right = call, left, mid, right
        self.kept, self.shares = getattr(mid, "kept", None), getattr(mid, "shares", None)
        if left is not None:
            self.rows_in = None if isinstance(left, Feed) else call.fetch(left[0])
            self.out_first = call.hold((2, 128, 1024), BF16)
            self.out_edge = call.hold((2, 64, 1024), BF16)
            self.out_late = call.hold((2, 64, 1024), BF16)
            self.keep = call.hold((2, 64, 1024), F32)
            self.own = call.hold((128, 1024), F32)
            self.landed = call.hold((6, 64, 1024), BF16)
            self.sum_send, self.sum_recv = call.sems(6), call.sems(6)
        self.gathered = None
        if right is not None:
            self.gathered = call.keep((4, 128, 1024), BF16, 4)
            self.row_send, self.row_recv = call.sems(6), call.sems(6)

    def lefts(self):
        return self.left.weights if isinstance(self.left, Feed) else [self.left[1]]

    def part(self, get, *rows):
        if isinstance(self.left, Feed):
            return self.left.part(get, *rows)
        unused, weight, picks, column = self.left
        total = None
        for first, count in picks:
            width = 4 * count
            left = stack([get(self.rows_in)[row, :, column : column + width] for row in rows])
            term = nn(left, weight.matrix(get, first, count))
            total = term if total is None else total + term
            column += width
        return total

    def send(self, get, i, source, target, partner):
        copy = pltpu.make_async_remote_copy(
            src_ref=source,
            dst_ref=target,
            send_sem=get(self.sum_send).at[i],
            recv_sem=get(self.sum_recv).at[i],
            device_id=partner,
            device_id_type=MESH_ID,
        )
        copy.start()
        return copy

    def sum_start(self, get, at):
        first, edge, landed = get(self.out_first), get(self.out_edge), get(self.landed)
        keep = get(self.keep)
        self.copies = [None] * 6
        first[0] = self.part(get, at["d_row"]).astype(BF16)
        self.copies[0] = self.send(
            get, 0, first.at[0, pl.ds(0, 64)], landed.at[0], at["x"]
        )
        self.copies[1] = self.send(
            get, 1, first.at[0, pl.ds(64, 64)], landed.at[1], at["y"]
        )
        part = self.part(get, at["x_row"], at["y_row"])
        edge[0] = part[:64].astype(BF16)
        keep[0] = part[64:128]
        self.copies[2] = self.send(get, 2, edge.at[0], landed.at[2], at["x"])
        edge[1] = part[192:].astype(BF16)
        keep[1] = part[128:192]
        self.copies[3] = self.send(get, 3, edge.at[1], landed.at[3], at["y"])

    def sum_forward(self, get, at):
        late, landed, keep = get(self.out_late), get(self.landed), get(self.keep)
        self.copies[0].wait_recv()
        late[1] = (keep[1] + landed[0].astype(F32)).astype(BF16)
        self.copies[4] = self.send(get, 4, late.at[1], landed.at[4], at["y"])
        self.copies[1].wait_recv()
        late[0] = (keep[0] + landed[1].astype(F32)).astype(BF16)
        self.copies[5] = self.send(get, 5, late.at[0], landed.at[5], at["x"])

    def sum_own(self, get, at):
        get(self.own)[...] = self.part(get, at["own_row"])

    def sum_end(self, get):
        landed, own = get(self.landed), get(self.own)
        for i in (2, 3, 4, 5):
            self.copies[i].wait_recv()
        upper = own[:64] + landed[2].astype(F32) + landed[4].astype(F32)
        lower = own[64:] + landed[5].astype(F32) + landed[3].astype(F32)
        return jnp.concatenate([upper, lower], 0)

    def row_copy(self, get, i, row, half, partner):
        block = get(self.gathered).at[row, pl.ds(half * 64, 64)]
        copy = pltpu.make_async_remote_copy(
            src_ref=block,
            dst_ref=block,
            send_sem=get(self.row_send).at[i],
            recv_sem=get(self.row_recv).at[i],
            device_id=partner,
            device_id_type=MESH_ID,
        )
        copy.start()
        return copy

    def rows_start(self, get, at, normed):
        get(self.gathered)[at["own_row"]] = normed
        self.call.save(get, self.gathered, at["own_row"])
        self.moves = [
            self.row_copy(get, 0, at["own_row"], 0, at["y"]),
            self.row_copy(get, 1, at["own_row"], 1, at["x"]),
            self.row_copy(get, 2, at["own_row"], 1, at["y"]),
            self.row_copy(get, 3, at["own_row"], 0, at["x"]),
        ]

    def rows_forward(self, get, at):
        self.moves[0].wait_recv()
        self.moves.append(self.row_copy(get, 4, at["y_row"], 0, at["x"]))
        self.moves[1].wait_recv()
        self.moves.append(self.row_copy(get, 5, at["x_row"], 1, at["y"]))

    def product(self, get, at, row):
        weight, picks, store = self.right
        if weight is None:
            return
        weight.wait(get)
        rows = get(self.gathered)[row]
        column = 0
        for first, count in picks:
            store(get, at, row, column, nt(rows, weight.matrix(get, first, count)))
            column += 4 * count

    def sums(self, get, at):
        for weight in self.lefts():
            weight.wait(get)
        self.sum_start(get, at)

    def settle(self, get, at):
        normed = self.mid(get, self.sum_end(get) if self.left is not None else None)
        if self.right is not None:
            self.rows_start(get, at, normed)

    def collect(self, get, at, sides=True, far=True):
        for moves, row in (((3,), "x_row"), ((2,), "y_row"), ((4, 5), "d_row")):
            if far if row == "d_row" else sides:
                for i in moves:
                    self.moves[i].wait_recv()
                self.call.save(get, self.gathered, at[row])
                self.product(get, at, at[row])

    def drain(self):
        if self.left is not None:
            for copy in self.copies:
                copy.wait_send()
        if self.right is not None:
            for copy in self.moves:
                copy.wait_send()


def run_body(call, work, names, name, collective, flops):
    groups = {"all": meeting, "z": along, "ways": lambda at: all_partners(at)[1]}

    def body(get):
        at = place()
        partners = []
        for group in names:
            partners += groups[group](at) if group in groups else [at[group]]
        greet(partners)
        work(get, at)

    return call.run(body, name, collective, flops)


class Kept:
    def __init__(self, out, store):
        self.out, self.store = out, store


class Plain:
    def __init__(self, call, width):
        self.call, self.width = call, width
        self.out = call.keep((4, 128, width), BF16, 4)

    def store(self, get, at, row, column, value):
        get(self.out)[row, :, column : column + value.shape[1]] = value.astype(BF16)
        if column + value.shape[1] == self.width:
            self.call.save(get, self.out, row)


class Shared:
    def __init__(self, call, width, skip=0):
        self.call, self.out = call, call.keep((2, 4, 128, width), BF16, 2)
        self.send_sem, self.recv_sem = call.sems(4), call.sems(4)
        self.width, self.skip, self.copies, self.blocks = width, skip, [], 0

    def store(self, get, at, row, column, value):
        out = get(self.out)
        column = column - self.skip
        out[0, row, :, column : column + value.shape[1]] = value.astype(BF16)
        if column + value.shape[1] == self.width:
            i = len(self.copies)
            copy = pltpu.make_async_remote_copy(
                src_ref=out.at[0, row],
                dst_ref=out.at[1, row],
                send_sem=get(self.send_sem).at[i],
                recv_sem=get(self.recv_sem).at[i],
                device_id=at["core"],
                device_id_type=MESH_ID,
            )
            copy.start()
            self.copies.append(copy)

    def finish(self, get):
        self.call.save(get, self.out, 0)
        for copy in self.copies:
            copy.wait()
        self.call.save(get, self.out, 1)


def query_and_shared(call, width):
    query, shared = Plain(call, width), Shared(call, 2 * width, skip=width)

    def store(get, at, row, column, value):
        if column < width:
            query.store(get, at, row, column, value)
        else:
            shared.store(get, at, row, column, value)

    return store, shared.finish


def lanes_of(head, rows):
    lane = lax.broadcasted_iota(jnp.int32, (rows, 128), 1)
    return lane // HEAD_DIM == head


SOURCE, TARGET, PLACE, LIVE = 0, 1, 2, 3


def allowed_bias(rows, columns, query_kind, key_kind, causal):
    allowed = columns[:, key_kind : key_kind + 1] == rows[query_kind : query_kind + 1, :512]
    allowed = allowed & (columns[:, LIVE + key_kind : LIVE + key_kind + 1] > 0.5)
    if causal:
        allowed = allowed & (columns[:, PLACE : PLACE + 1] <= rows[PLACE : PLACE + 1, :512])
    return jnp.where(allowed, 0.0, MASKED)


class Attend:
    def __init__(self, call, queries, key_value, rows, columns, kinds):
        self.call, self.kinds = call, kinds
        self.queries, self.key_value = call.fetch(queries), call.fetch(key_value)
        self.rows, self.columns = call.take(rows), call.fetch(columns)
        self.mixed = call.keep((4, 128, 256), BF16)
        self.total = call.give((8, 512), F32)
        self.bias = call.hold((1024, 512), F32)

    def late(self, get, at):
        self.prepare(get)
        self.pairs(get, 0, 2)
        self.call.save(get, self.mixed)

    def prepare(self, get):
        mask = get(self.bias)
        mask[...] = allowed_bias(get(self.rows), get(self.columns), *self.kinds)

    def pairs(self, get, first, last):
        mask = get(self.bias)
        q_ref, kv_ref = get(self.queries), get(self.key_value)
        mixed_ref, total_ref = get(self.mixed), get(self.total)

        def pair_step(pair, carry):
            lanes = pl.ds(pl.multiple_of(pair * 128, 128), 128)
            value_lanes = pl.ds(pl.multiple_of(256 + pair * 128, 128), 128)
            keys = kv_ref[:, :, :, lanes].reshape(1024, 128)
            values = kv_ref[:, :, :, value_lanes].reshape(1024, 128)
            for block in range(2):
                span = slice(block * 256, block * 256 + 256)
                queries = q_ref[2 * block : 2 * block + 2, :, lanes].reshape(256, 128)
                mixed = []
                for head in range(2):
                    picked = jnp.where(lanes_of(head, 256), queries * 0.125, 0.0).astype(BF16)
                    scores = nt(keys, picked) + mask[:, span]
                    top = jnp.max(scores, 0, keepdims=True)
                    raised = jnp.exp(scores - top)
                    total = jnp.sum(raised, 0, keepdims=True)
                    probs = (raised * (1.0 / total)).astype(BF16)
                    mixed.append(tn(values, probs)[head * HEAD_DIM : (head + 1) * HEAD_DIM])
                    total_ref[pl.ds(pair * 2 + head, 1), span] = top + jnp.log(total)
                mixed = jnp.concatenate(mixed, 0).T.astype(BF16)
                mixed_ref[2 * block : 2 * block + 2, :, lanes] = mixed.reshape(2, 128, 128)
            return carry

        lax.fori_loop(first, last, pair_step, 0)


class AttendBack:
    def __init__(self, call, queries, key_value, grad_mixed, total, rows, columns, kinds):
        self.call, self.kinds = call, kinds
        self.queries, self.key_value = call.fetch(queries), call.fetch(key_value)
        self.grad_mixed, self.total = call.fetch(grad_mixed), call.take(total)
        self.rows, self.columns = call.take(rows), call.fetch(columns)
        self.out = call.keep((4, 128, 768), BF16)
        self.bias, self.sums = call.hold((1024, 512), F32), call.hold((1024, 512), F32)
        self.away, self.landed = call.hold((2, 512, 256), BF16), call.hold((2, 512, 256), BF16)
        self.send_sem, self.recv_sem = call.sems(2), call.sems(2)

    def partners(self, at):
        return [at["core"]]

    def late(self, get, at):
        self.prepare(get)
        for pair in range(2):
            self.pair(get, at, pair)
        self.end(get)

    def prepare(self, get):
        mask = get(self.bias)
        mask[...] = allowed_bias(get(self.rows), get(self.columns), *self.kinds)
        self.copies = []

    def pair(self, get, at, pair):
        out, mask, sums = get(self.out), get(self.bias), get(self.sums)
        away, here = get(self.away), get(self.landed)
        q_ref, kv_ref = get(self.queries), get(self.key_value)
        grad_ref, total_ref = get(self.grad_mixed), get(self.total)
        lanes = slice(pair * 128, pair * 128 + 128)
        keys_pair = kv_ref[:, :, :, lanes].reshape(1024, 128)
        values_pair = kv_ref[:, :, :, 256 + pair * 128 : 384 + pair * 128].reshape(1024, 128)
        key_sum = slice(pair * 256, pair * 256 + 128)
        value_sum = slice(pair * 256 + 128, pair * 256 + 256)
        for block in range(2):
            span = slice(block * 256, block * 256 + 256)
            two = slice(2 * block, 2 * block + 2)
            q_block = q_ref[two, :, lanes].reshape(256, 128)
            g_block = grad_ref[two, :, lanes].reshape(256, 128)
            grad_query = []
            for head in range(2):
                inside = lanes_of(head, 256)
                picked = jnp.where(inside, q_block * 1.0, 0.0).astype(BF16)
                grads = jnp.where(inside, g_block * 1.0, 0.0).astype(BF16)
                scores = nt(keys_pair, picked) * 0.125 + mask[:, span]
                probs = jnp.exp(scores - total_ref[pair * 2 + head : pair * 2 + head + 1, span])
                weighted = probs * nt(values_pair, grads)
                inner = jnp.sum(weighted, 0, keepdims=True)
                grad_raw = ((weighted - probs * inner) * 0.125).astype(BF16)
                value_term = nn(probs.astype(BF16), grads)
                key_term = nn(grad_raw, picked)
                if block == 0 and head == 0:
                    sums[:, key_sum] = key_term
                    sums[:, value_sum] = value_term
                else:
                    sums[:, key_sum] += key_term
                    sums[:, value_sum] += value_term
                grad_query.append(tn(keys_pair, grad_raw)[head * HEAD_DIM : (head + 1) * HEAD_DIM])
            grad_query = jnp.concatenate(grad_query, 0).T.astype(BF16)
            out[two, :, lanes] = grad_query.reshape(2, 128, 128)
        away[pair] = sums[512:, pair * 256 : pair * 256 + 256].astype(BF16)
        copy = pltpu.make_async_remote_copy(
            src_ref=away.at[pair],
            dst_ref=here.at[pair],
            send_sem=get(self.send_sem).at[pair],
            recv_sem=get(self.recv_sem).at[pair],
            device_id=at["core"],
            device_id_type=MESH_ID,
        )
        copy.start()
        self.copies.append(copy)

    def end(self, get):
        out, sums, here = get(self.out), get(self.sums), get(self.landed)
        for pair in range(2):
            self.copies[pair].wait()
            both = sums[:512, pair * 256 : pair * 256 + 256] + here[pair].astype(F32)
            both = both.astype(BF16).reshape(4, 128, 256)
            out[:, :, 256 + pair * 128 : 384 + pair * 128] = both[:, :, :128]
            out[:, :, 512 + pair * 128 : 640 + pair * 128] = both[:, :, 128:]
        self.call.save(get, self.out)


class Shares:
    def __init__(self, call, pairs, count, out=None, base=0):
        self.call, self.count, self.base = call, count, base
        self.handles = [
            (call.fetch(left), column, call.fetch(right))
            for left, column, right in pairs
        ]
        shape = (4, 4, len(pairs) * count, 128)
        sends = len(pairs) * max(1, count // 64)
        self.made, self.landed = call.hold((2,) + shape, BF16), call.hold(shape, BF16)
        self.send_sem, self.recv_sem = call.sems(sends), call.sems(sends)
        self.rows = shape[2]
        self.out = call.give(shape, BF16, pltpu.HBM) if out is None else out
        self.saved = out is not False
        self.room, self.save_sem = call.hold(shape, BF16), call.sems(1)

    def partners(self, at):
        return [at["core"]]

    def send(self, get, at, part):
        i = len(self.copies)
        copy = pltpu.make_async_remote_copy(
            src_ref=get(self.made).at[(1 - lax.axis_index("c"),) + part],
            dst_ref=get(self.landed).at[part],
            send_sem=get(self.send_sem).at[i],
            recv_sem=get(self.recv_sem).at[i],
            device_id=at["core"],
            device_id_type=MESH_ID,
        )
        copy.start()
        self.copies.append((part, copy))

    def middle(self, get, at):
        self.copies, every, count = [], slice(None), self.count
        made = get(self.made)
        for m, (left, column, right) in enumerate(self.handles):
            left, right = get(left), get(right)
            span = slice(m * count, (m + 1) * count)
            for first in range(0, 4 * count, 256):
                start = column + first
                product = tn(
                    left[:, :, start : start + 256].reshape(512, 256), right[...].reshape(512, 1024)
                )
                for inner in range(0, 256, count):
                    z = (first + inner) // count
                    for d in range(8):
                        made[d % 2, z, d // 2, span, :] = product[
                            inner : inner + count, d * 128 : d * 128 + 128
                        ].astype(BF16)
                if count == 256:
                    self.send(get, at, (first // 256, every, pl.ds(m * count, count)))
            if count < 256:
                self.send(get, at, (every, every, pl.ds(m * count, count)))

    def finish(self, get, at):
        core = lax.axis_index("c")
        for part, copy in self.copies:
            copy.wait()
            own = get(self.made)[(core,) + part].astype(F32)
            get(self.room)[part] = (own + get(self.landed)[part].astype(F32)).astype(BF16)
        if not self.saved:
            return
        target = get(self.out).at[:, :, pl.ds(self.base, self.rows)]
        copy = pltpu.make_async_copy(get(self.room), target, get(self.save_sem).at[0])
        copy.start()
        self.call.saves.append((None, copy))


def push(source, target, send_sem, recv_sem, partner):
    return pltpu.make_async_remote_copy(
        src_ref=source,
        dst_ref=target,
        send_sem=send_sem,
        recv_sem=recv_sem,
        device_id=partner,
        device_id_type=MESH_ID,
    )


class Spread:
    def __init__(self, call, pack):
        rows = pack.shape if not isinstance(pack, tuple) else (4, call.rows_of[pack], 128)
        self.pack = call.take(pack, pltpu.HBM)
        self.out = call.give((2, 4) + tuple(rows), BF16, pltpu.HBM)
        self.send_sem, self.recv_sem = call.sems(5), call.sems(5)
        self.core_send, self.core_recv, self.own_sem = call.sems(6), call.sems(6), call.sems(1)

    def block(self, get, at, origin):
        return get(self.out).at[at["mesh"][3], origin]

    def move(self, get, at, way):
        hi, k, y, c, z = at["mesh"]
        step = {0: 1, 1: -1, 2: 2, 3: -2, 4: jnp.where(z == 2, 1, -1)}[way]
        origin = jnp.where(z == 2, 0, 3) if way == 4 else z
        target = self.block(get, at, origin)
        return push(
            target if way == 4 else get(self.pack),
            target,
            get(self.send_sem).at[way],
            get(self.recv_sem).at[way],
            (hi, k, y, c, lax.rem(z + step + 4, 4)),
        )

    def sends(self, at, way):
        z = at["mesh"][4]
        middle = (z == 1) | (z == 2)
        return {0: z < 3, 1: z > 0, 2: z < 2, 3: z > 1, 4: middle}[way]

    def comes(self, at, way):
        z = at["mesh"][4]
        return {0: z > 0, 1: z < 3, 2: z > 1, 3: z < 2, 4: (z == 0) | (z == 3)}[way]

    def to_core(self, get, at, way):
        z = at["mesh"][4]
        origin = {0: z - 1, 1: z + 1, 2: z - 2, 3: z + 2, 4: 3 - z, 5: z}[way]
        target = self.block(get, at, origin)
        return push(
            get(self.pack) if way == 5 else target,
            target,
            get(self.core_send).at[way],
            get(self.core_recv).at[way],
            at["core"],
        )

    def own(self, get, at):
        return pltpu.make_async_copy(
            get(self.pack), self.block(get, at, at["mesh"][4]), get(self.own_sem).at[0]
        )

    def launch(self, get, at):
        for way in (2, 3, 0, 1):

            @pl.when(self.sends(at, way))
            def _():
                self.move(get, at, way).start()

        self.to_core(get, at, 5).start()
        self.own(get, at).start()

    def relay(self, get, at):
        for plane, way in ((2, 2), (1, 3)):

            @pl.when(at["mesh"][4] == plane)
            def _():
                self.move(get, at, way).wait_recv()
                self.move(get, at, 4).start()
                self.to_core(get, at, way).start()

    def pass_on(self, get, at):
        z = at["mesh"][4]
        for way in (0, 1, 2, 3, 4):
            taken = {2: z == 2, 3: z == 1}.get(way, z < 0)

            @pl.when(self.comes(at, way) & jnp.logical_not(taken))
            def _():
                self.move(get, at, way).wait_recv()
                self.to_core(get, at, way).start()

    def finish(self, get, at):
        self.own(get, at).wait()
        self.to_core(get, at, 5).wait()
        for way in range(5):

            @pl.when(self.comes(at, way))
            def _():
                self.to_core(get, at, way).wait()

            @pl.when(self.sends(at, way))
            def _():
                self.move(get, at, way).wait_send()


class Gather:
    def __init__(self, call, shares, rows, first=0):
        self.call, self.shares, self.rows, self.first = call, call.take(shares, pltpu.HBM), rows, first
        self.landed, self.own = call.hold((3, 4, rows, 128), BF16), call.hold((4, rows, 128), BF16)
        self.far, self.room = call.hold((4, rows, 128), BF16), call.hold((4, rows, 128), BF16)
        self.out = call.keep((4, rows, 128), BF16)
        self.send_sem, self.recv_sem, self.own_sem = call.sems(4), call.sems(4), call.sems(2)

    def share(self, get, plane):
        return get(self.shares).at[plane, :, pl.ds(self.first, self.rows)]

    def move(self, get, at, way, summed=False):
        hi, k, y, c, z = at["mesh"]
        step = {0: 1, 1: 3, 2: 2, 3: jnp.where(z == 0, 1, 3)}[way]
        partner = lax.rem(z + step, 4)
        source = self.share(get, 3 - z if way == 3 else partner)
        return push(
            get(self.room) if summed else source,
            get(self.room) if way == 3 else get(self.landed).at[way],
            get(self.send_sem).at[way],
            get(self.recv_sem).at[way],
            (hi, k, y, c, partner),
        )

    def local(self, get, at, far):
        z = at["mesh"][4]
        return pltpu.make_async_copy(
            self.share(get, lax.rem(z + 2, 4) if far else z),
            get(self.far if far else self.own),
            get(self.own_sem).at[1 if far else 0],
        )

    def launch(self, get, at):
        z = at["mesh"][4]
        outer = (z == 0) | (z == 3)
        for way, when in ((3, outer), (2, outer), (0, z < 3), (1, z > 0)):

            @pl.when(when)
            def _():
                self.move(get, at, way).start()

        for far in (False, True):
            self.local(get, at, far).start()

    def relay(self, get, at):
        z = at["mesh"][4]

        @pl.when((z == 1) | (z == 2))
        def _():
            self.move(get, at, 3).wait_recv()
            self.local(get, at, True).wait()
            room = get(self.room)
            room[...] = (room[...].astype(F32) + get(self.far)[...].astype(F32)).astype(BF16)
            self.move(get, at, 2, True).start()

        @pl.when((z == 0) | (z == 3))
        def _():
            self.local(get, at, True).wait()

    def finish(self, get, at):
        z = at["mesh"][4]
        landed, own, out = get(self.landed), get(self.own), get(self.out)
        self.local(get, at, False).wait()
        self.move(get, at, 2).wait()
        for which, ways in ((z == 0, (1,)), (z == 3, (0,)), ((z == 1) | (z == 2), (0, 1))):

            @pl.when(which)
            def _():
                for way in ways:
                    self.move(get, at, way).wait_recv()
                for q in range(4):
                    total = own[q].astype(F32) + landed[2, q].astype(F32)
                    for way in ways:
                        total = total + landed[way, q].astype(F32)
                    out[q] = total.astype(BF16)

        self.call.save(get, self.out)
        for way, when in ((3, (z == 0) | (z == 3)), (0, z < 3), (1, z > 0)):

            @pl.when(when)
            def _():
                self.move(get, at, way).wait_send()


class Swap:
    def __init__(self, call, pack):
        self.pack = call.take(pack, pltpu.HBM)
        rows = call.rows_of[pack] if isinstance(pack, tuple) else pack.shape[1]
        self.out = call.give((4, rows, 128), BF16, pltpu.HBM)
        call.rows_of[self.out] = rows
        self.send_sem, self.recv_sem, self.own_sem = call.sems(3), call.sems(3), call.sems(1)

    def start(self, get, at):
        hi, k, y, c, z = at["mesh"]
        own = hi * 2 + y
        pack, out = get(self.pack), get(self.out)
        self.copies = [pltpu.make_async_copy(pack.at[own], out.at[own], get(self.own_sem).at[0])]
        for i, (name, q) in enumerate(
            (("d", (1 - hi) * 2 + 1 - y), ("x", (1 - hi) * 2 + y), ("y", hi * 2 + 1 - y))
        ):
            send, recv = get(self.send_sem).at[i], get(self.recv_sem).at[i]
            self.copies.append(push(pack.at[q], out.at[own], send, recv, at[name]))
        for copy in self.copies:
            copy.start()

    def finish(self, get, at):
        for copy in self.copies:
            copy.wait()


class Slots:
    def __init__(self, call, arrays, inward):
        self.inward = inward
        self.call, self.arrays = call, [call.fetch(array) for array in arrays]
        shape = (128, 1024) if inward else (2, 64, 1024)
        self.outs = [call.keep(shape, BF16) for array in arrays]
        self.send_sem, self.recv_sem = call.sems(2 * len(arrays)), call.sems(2 * len(arrays))

    def ends(self, get, at, j, step):
        z = at["mesh"][4]
        low = lax.div(z, 2)
        other = low if step == 0 else 1 - low
        array, out = get(self.arrays[j]), get(self.outs[j])
        if self.inward:
            return array.at[other], out.at[pl.ds(pl.multiple_of(low * 64, 64), 64)]
        return array.at[pl.ds(pl.multiple_of(other * 64, 64), 64)], out.at[low]

    def stays(self, at):
        hi, z = at["mesh"][0], at["mesh"][4]
        return lax.rem(z, 2) == hi

    def copy(self, get, at, j, step):
        hi, k, y, c, z = at["mesh"]
        low = lax.div(z, 2)
        partner = (lax.rem(z, 2), k, y, c, 2 * (low if step == 0 else 1 - low) + hi)
        source, target = self.ends(get, at, j, step)
        return pltpu.make_async_remote_copy(
            src_ref=source,
            dst_ref=target,
            send_sem=get(self.send_sem).at[2 * j + step],
            recv_sem=get(self.recv_sem).at[2 * j + step],
            device_id=partner,
            device_id_type=MESH_ID,
        )

    def start(self, get, at):
        stays = self.stays(at)
        for j in range(len(self.arrays)):
            self.copy(get, at, j, 1).start()

        @pl.when(jnp.logical_not(stays))
        def _():
            for j in range(len(self.arrays)):
                self.copy(get, at, j, 0).start()

        @pl.when(stays)
        def _():
            for j in range(len(self.arrays)):
                source, target = self.ends(get, at, j, 0)
                target[...] = source[...]

    def finish(self, get, at):
        for j in range(len(self.arrays)):
            self.copy(get, at, j, 1).wait()

        @pl.when(jnp.logical_not(self.stays(at)))
        def _():
            for j in range(len(self.arrays)):
                self.copy(get, at, j, 0).wait()

        for out in self.outs:
            self.call.save(get, out)


def all_partners(at):
    hi, k, y, c, z = at["mesh"]
    plane = [
        ((hi + i) % 2, k, (y + j) % 2, (c + n) % 2, z)
        for i in range(2)
        for j in range(2)
        for n in range(2)
        if i + j + n > 0
    ]
    ways = [((hi + i) % 2, k, y, c, (z + n) % 4) for i in range(2) for n in range(1, 4)]
    return plane, ways


def meeting(at):
    plane, ways = all_partners(at)
    return plane + ways


class Vectors:
    def __init__(self, call, vectors, inward):
        self.inward = inward
        self.source = call.take(vectors)
        self.out = call.give((16, 1024) if inward else (16, 128), F32)
        self.landed, self.whole = call.hold((7, 16, 128), F32), call.hold((16, 128), F32)
        self.split, self.along = call.hold((8, 16, 128), F32), call.hold((3, 16, 128), F32)
        self.send_sem, self.recv_sem = call.sems(10), call.sems(10)

    def move(self, get, i, source, target, partner):
        return push(source, target, get(self.send_sem).at[i], get(self.recv_sem).at[i], partner)

    def planes(self, get, at, source):
        return [
            self.move(get, n, source, get(self.along).at[n], partner)
            for n, partner in enumerate(along(at))
        ]

    def block(self, at):
        hi, k, y, c, z = at["mesh"]
        return (hi * 2 + y) * 2 + c

    def start(self, get, at):
        plane = all_partners(at)[0]
        if self.inward:
            self.copies = self.planes(get, at, get(self.source))
        else:
            split = get(self.split)
            for d in range(8):
                split[d] = get(self.source)[:, d * 128 : d * 128 + 128]
            self.copies = [
                self.move(
                    get,
                    3 + i,
                    split.at[(partner[0] * 2 + partner[2]) * 2 + partner[3]],
                    get(self.landed).at[i],
                    partner,
                )
                for i, partner in enumerate(plane)
            ]
        for copy in self.copies:
            copy.start()

    def second(self, get, at):
        plane = all_partners(at)[0]
        for copy in self.copies:
            copy.wait()
        whole, out = get(self.whole), get(self.out)
        if self.inward:
            whole[...] = get(self.source)[...] + jnp.sum(get(self.along)[...], 0)
            block = pl.ds(pl.multiple_of(self.block(at) * 128, 128), 128)
            out[:, block] = whole[...]
            self.copies = [
                self.move(get, 3 + i, whole, out.at[:, block], partner)
                for i, partner in enumerate(plane)
            ]
        else:
            whole[...] = get(self.split)[self.block(at)] + jnp.sum(get(self.landed)[...], 0)
            self.copies = self.planes(get, at, whole)
        for copy in self.copies:
            copy.start()

    def finish(self, get, at):
        for copy in self.copies:
            copy.wait()
        if not self.inward:
            get(self.out)[...] = get(self.whole)[...] + jnp.sum(get(self.along)[...], 0)


class Pack:
    def __init__(self, call, matrices):
        self.parts = [(call.fetch(array), index, across) for array, index, across in matrices]
        counts = [
            (array.shape[-1] if across else array.shape[-2]) // 4
            for array, index, across in matrices
        ]
        self.counts = counts
        self.out = call.hold((4, sum(counts), 128), BF16)
        call.rows_of[self.out] = sum(counts)

    def make(self, get):
        out, base = get(self.out), 0
        for (part, index, across), count in zip(self.parts, self.counts, strict=True):
            part = get(part)
            whole = part[...] if index is None else part[index]
            if across:
                whole = whole.astype(F32).T.astype(BF16)
            out[:, base : base + count, :] = whole.reshape(4, count, 128)
            base += count


def by_owner(rows, back=False):
    copies = lax.axis_size("k")
    if copies == 1:
        return rows
    shape, width = rows.shape, 128 // copies
    if back:
        rows = rows.reshape(-1, 2, 2, 2, copies, width).transpose(0, 1, 4, 2, 3, 5)
    else:
        rows = rows.reshape(-1, 2, copies, 2, 2, width).transpose(0, 1, 3, 4, 2, 5)
    return rows.reshape(shape)


def unpacked(packs, rows, wide):
    call = Call()
    rows_in = [call.fetch(array) for array in rows]
    ins = [call.fetch(array) for array in packs]
    plans = []
    for handle, array, kinds in zip(ins, packs, wide, strict=True):
        base = 0
        for kind in kinds:
            count = 256 if kind in ("up", "down") else 64
            if kind == "q":
                out = call.give((3, 128, 256), F32)
                plans += [(handle, base + i * 64, 64, out, i, True) for i in range(3)]
                base += 192
                continue
            shape = (128, 4 * count) if kind == "up" else (4 * count, 128)
            plans.append((handle, base, count, call.give(shape, F32), None, kind == "up"))
            base += count
    outs = [call.give(array.shape, F32) for array in rows]

    def body(get):
        for handle, base, count, out, index, across in plans:
            whole = get(handle)[:, base : base + count, :].astype(F32).reshape(4 * count, 128)
            whole = whole.T if across else whole
            if index is None:
                get(out)[...] = whole
            else:
                get(out)[index] = whole
        for source, out in zip(rows_in, outs, strict=True):
            get(out)[...] = get(source)[...].astype(F32)

    return call.run(body, "unpacked", None, 4 * MICROSECOND)


def local(
    source,
    target,
    cotangent,
    source_len,
    target_len,
    source_seg,
    target_seg,
    enc_qkv,
    enc_proj,
    enc_up,
    enc_down,
    enc_gain,
    enc_shift,
    dec_qkv,
    dec_proj,
    cross_qkv,
    cross_proj,
    dec_up,
    dec_down,
    dec_gain,
    dec_shift,
):
    copies, z = lax.axis_size("k"), lax.axis_index("mp")
    vectors = jnp.concatenate([enc_gain, enc_shift, dec_gain, dec_shift, dec_shift[:2]], 0)
    if copies > 1:
        vectors = lax.all_gather(vectors, "k", axis=1, tiled=True)
    vectors = vectors.reshape(16, copies, 1, 32 // copies)
    vectors = jnp.where(jnp.arange(4)[:, None] == z, vectors, 0.0).reshape(16, 128)
    facts = jnp.concatenate([source_seg, target_seg], 0)
    lengths = jnp.concatenate([source_len, target_len], 0)
    facts = jnp.concatenate([facts, jnp.broadcast_to(lengths[:, None], (4, 128))], 1)

    def widen(array, axis):
        return array if copies == 1 else lax.all_gather(array, "k", axis=axis, tiled=True)

    enc_qkv, dec_qkv, cross_qkv = (widen(array, 1) for array in (enc_qkv, dec_qkv, cross_qkv))
    enc_proj, dec_proj, cross_proj = (widen(array, 1) for array in (enc_proj, dec_proj, cross_proj))
    enc_up, dec_up = widen(enc_up, 0), widen(dec_up, 0)
    enc_down, dec_down = widen(enc_down, 1), widen(dec_down, 1)

    ENC_G, ENC_B, DEC_G, DEC_B = 0, 3, 6, 10
    SELF, SELF_O = 192, 64
    Q, QKV, KV, O, FIRST_O = (0, 64), (0, 192), (64, 128), (192, 64), (0, 64)
    UP, DOWN = (0, 256), (256, 256)

    def pick(call, packed, span, base=0):
        return Weight(call, packed, base + span[0], span[1])

    def forward_mid(call, residual, gain, shift, normed=None):
        vec, res = call.take(vectors), call.fetch(residual)
        kept = call.keep((128, 1024), F32)

        def mid(get, total):
            stream = get(res)[...].astype(F32) + total
            get(kept)[...] = stream
            call.save(get, kept)
            unit, scale = unit_of(stream)
            made = (unit * get(vec)[gain : gain + 1] + get(vec)[shift : shift + 1]).astype(BF16)
            if normed is not None:
                get(normed)[...] = made
                call.save(get, normed)
            return made

        mid.kept = kept
        return mid

    def backward_mid(call, stream, gain, residual=None, dtype=F32):
        vec, kept = call.take(vectors), call.fetch(stream)
        res = None if residual is None else call.fetch(residual)
        grad_out, share_out = call.keep((128, 1024), dtype), call.give((2, 1024), F32)

        def mid(get, total):
            grad, shares = norm_back(get(kept)[...].astype(F32), get(vec)[gain : gain + 1], total)
            if res is not None:
                grad = grad + get(res)[...]
            get(grad_out)[...] = grad.astype(dtype)
            call.save(get, grad_out)
            get(share_out)[...] = shares
            return grad.astype(BF16)

        mid.kept, mid.shares = grad_out, share_out
        return mid

    def deactivated(call, slope):
        out = call.keep((4, 128, 1024), BF16, 4)

        def store(get, at, row, column, value):
            get(out)[row] = (value * get(slope)[row]).astype(BF16)
            call.save(get, out, row)

        return Kept(out, store)

    call = Call()
    slots = Slots(call, [by_owner(source), by_owner(target)], True)
    stream_h, target_h = slots.outs
    first_vectors = Vectors(call, vectors, True)
    fact_in = call.take(facts)
    fact_own, fact_room = call.hold((2, 8, 128), F32), call.hold((2, 8, 128), F32)
    fact_rows, fact_columns = call.give((8, 1024), F32), call.keep((1024, 128), F32)
    fact_send, fact_recv = call.sems(1), call.sems(1)

    def three(array):
        return [(array, i, True) for i in range(3)]

    pack_1 = Pack(call, three(enc_qkv) + three(dec_qkv))
    pack_o = Pack(call, [(enc_proj, None, False), (dec_proj, None, False)])
    pack_2 = Pack(call, [(enc_up, None, True), (enc_down, None, False)])
    pack_3 = Pack(call, three(cross_qkv) + [(cross_proj, None, False)])
    pack_4 = Pack(call, [(dec_up, None, True), (dec_down, None, False)])
    swap_1, swap_o, swap_2, swap_3, swap_4 = (
        Swap(call, pack.out) for pack in (pack_1, pack_o, pack_2, pack_3, pack_4)
    )
    spread_1, spread_o, spread_2, spread_3, spread_4 = (
        Spread(call, swap.out) for swap in (swap_1, swap_o, swap_2, swap_3, swap_4)
    )

    def count_facts(get):
        given = get(fact_in)[...]
        lane = lax.broadcasted_iota(jnp.int32, (4, 128), 1)
        table = jnp.where(lane == 0, given[:, 1024:].astype(F32), 0.0)
        for p in range(1, PAIRS):
            before = jnp.sum((given[:, :1024] < p).astype(F32), 1, keepdims=True)
            table = table + jnp.where(lane == p, before, 0.0)
        own = get(fact_own)
        own[...] = jnp.zeros_like(own)
        for slot in range(2):
            own[slot, 0:1] = table[slot : slot + 1]
            own[slot, 1:2] = table[2 + slot : 3 + slot]

    def place_facts(get, at):
        hi, k, y, c, z = at["mesh"]
        slot = lax.div(z, 2)
        table = jnp.where(lax.rem(z, 2) == hi, get(fact_own)[slot], get(fact_room)[slot])

        def kinds(index):
            core = jnp.where(index < 512, c, 1 - c)
            part = index % 512
            place = (part // 256) * 512 + core * 256 + ((part // 64) % 2) * 128
            place = (place + ((part // 128) % 2) * 64 + part % 64).astype(F32)
            found = []
            for row in range(2):
                ids = jnp.zeros_like(place)
                for p in range(1, PAIRS):
                    ids = ids + jnp.where(place >= table[row : row + 1, p : p + 1], 1.0, 0.0)
                found.append(ids)
            live = [jnp.where(place < table[row : row + 1, 0:1], 1.0, 0.0) for row in range(2)]
            return found + [place] + live

        across = kinds(lax.broadcasted_iota(jnp.int32, (1, 1024), 1))
        down = kinds(lax.broadcasted_iota(jnp.int32, (1024, 128), 0))
        rows, columns = get(fact_rows), get(fact_columns)
        rows[...] = jnp.zeros_like(rows)
        lane = lax.broadcasted_iota(jnp.int32, (1024, 128), 1)
        wide = jnp.zeros((1024, 128), F32)
        for i in range(5):
            rows[i : i + 1] = across[i]
            wide = jnp.where(lane == i, down[i], wide)
        columns[...] = wide
        call.save(get, fact_columns)

    def first_mid(stream, gain, shift):
        def mid(get, total):
            unit, scale = unit_of(get(stream)[...].astype(F32))
            vec = get(first_vectors.out)
            return (unit * vec[gain : gain + 1] + vec[shift : shift + 1]).astype(BF16)

        return mid

    job_a = Job(call, None, first_mid(stream_h, ENC_G, ENC_B), (None, None, None))
    job_c = Job(call, None, first_mid(target_h, DEC_G, DEC_B), (None, None, None))
    vectors = first_vectors.out

    plans = []
    for rows, base in ((job_a.gathered, 0), (job_c.gathered, SELF)):
        query, shared = Plain(call, 256), Shared(call, 512, 256)
        plans.append((call.fetch(rows), pick(call, spread_1.out, QKV, base), query, shared))
    enc_step = Attend(
        call, plans[0][2].out, plans[0][3].out, fact_rows, fact_columns, (SOURCE, SOURCE, False)
    )
    self_step = Attend(
        call, plans[1][2].out, plans[1][3].out, fact_rows, fact_columns, (TARGET, TARGET, True)
    )
    enc_o, self_o = pick(call, spread_o.out, FIRST_O), pick(call, spread_o.out, FIRST_O, SELF_O)
    mid = forward_mid(call, stream_h, ENC_G + 1, ENC_B + 1)
    job_b = Job(call, (enc_step.mixed, enc_o, [(0, 64)], 0), mid, (None, None, None))
    mid = forward_mid(call, target_h, DEC_G + 1, DEC_B + 1)
    cross_a, cross_b = pick(call, spread_3.out, Q), pick(call, spread_3.out, KV)
    cross_o = pick(call, spread_3.out, O)
    query, shared = Plain(call, 256), Shared(call, 512)
    job_d = Job(call, (self_step.mixed, self_o, [(0, 64)], 0), mid, (cross_a, [(0, 64)], query.store))
    enc_u, enc_d = pick(call, spread_2.out, UP), pick(call, spread_2.out, DOWN)
    feed = Feed(call, job_b.gathered, enc_u, enc_d)
    mid = forward_mid(call, job_b.kept, ENC_G + 2, ENC_B + 2)
    job_m = Job(call, feed, mid, (cross_b, [(0, 64), (64, 64)], shared.store))
    cross_step = Attend(
        call, query.out, shared.out, fact_rows, fact_columns, (TARGET, SOURCE, False)
    )
    mid = forward_mid(call, job_d.kept, DEC_G + 2, DEC_B + 2)
    job_e = Job(call, (cross_step.mixed, cross_o, [(0, 64)], 0), mid, (None, None, None))

    def onward(get, at):
        first_vectors.start(get, at)
        slots.start(get, at)
        pack_1.make(get)
        swap_1.start(get, at)
        count_facts(get)
        fact_copy = push(
            get(fact_own), get(fact_room), get(fact_send).at[0], get(fact_recv).at[0], at["x"]
        )
        fact_copy.start()
        first_vectors.second(get, at)
        swap_1.finish(get, at)
        spread_1.launch(get, at)
        for pack in (pack_o, pack_2):
            pack.make(get)
        first_vectors.finish(get, at)
        slots.finish(get, at)
        job_a.settle(get, at)
        job_c.settle(get, at)
        fact_copy.wait()
        place_facts(get, at)
        job_a.rows_forward(get, at)
        job_c.rows_forward(get, at)
        spread_1.relay(get, at)
        swap_o.start(get, at)
        swap_2.start(get, at)
        for pack in (pack_3, pack_4):
            pack.make(get)
        job_a.collect(get, at)
        job_c.collect(get, at)
        enc_step.prepare(get)
        swap_o.finish(get, at)
        swap_2.finish(get, at)
        job_a.drain()
        job_c.drain()
        spread_1.pass_on(get, at)
        spread_o.launch(get, at)
        spread_2.launch(get, at)
        swap_3.start(get, at)
        swap_4.start(get, at)
        spread_1.finish(get, at)
        for plan in plans:
            plan[1].start(get)
        for rows, weight, queries, keys in plans:
            weight.wait(get)
            for row in range(4):
                for m in range(3):
                    made = nt(get(rows)[row], weight.matrix(get, m * 64, 64))
                    (queries if m == 0 else keys).store(get, at, row, m * 256, made)
        for plan in plans:
            plan[3].finish(get)
        spread_o.relay(get, at)
        enc_step.pairs(get, 0, 2)
        call.save(get, enc_step.mixed)
        spread_o.pass_on(get, at)
        swap_3.finish(get, at)
        swap_4.finish(get, at)
        spread_o.finish(get, at)
        enc_o.start(get)
        self_o.start(get)
        job_b.sums(get, at)
        self_step.prepare(get)
        self_step.pairs(get, 0, 1)
        job_b.sum_forward(get, at)
        self_step.pairs(get, 1, 2)
        call.save(get, self_step.mixed)
        job_b.sum_own(get, at)
        job_d.sums(get, at)
        job_b.settle(get, at)
        spread_2.relay(get, at)
        spread_3.launch(get, at)
        job_d.sum_forward(get, at)
        job_d.sum_own(get, at)
        job_b.rows_forward(get, at)
        job_d.settle(get, at)
        spread_2.pass_on(get, at)
        spread_2.finish(get, at)
        enc_u.start(get)
        enc_d.start(get)
        job_b.collect(get, at)
        job_m.sums(get, at)
        job_d.rows_forward(get, at)
        job_m.sum_forward(get, at)
        job_m.sum_own(get, at)
        spread_3.relay(get, at)
        spread_4.launch(get, at)
        job_m.settle(get, at)
        spread_3.pass_on(get, at)
        spread_3.finish(get, at)
        for weight in (cross_a, cross_b, cross_o):
            weight.start(get)
        job_m.rows_forward(get, at)
        job_d.product(get, at, at["own_row"])
        job_d.collect(get, at)
        job_m.product(get, at, at["own_row"])
        job_m.collect(get, at)
        for job in (job_b, job_d, job_m):
            job.drain()
        shared.finish(get)
        cross_step.prepare(get)
        cross_step.pairs(get, 0, 1)
        spread_4.relay(get, at)
        cross_step.pairs(get, 1, 2)
        call.save(get, cross_step.mixed)
        job_e.sums(get, at)
        job_e.sum_forward(get, at)
        job_e.sum_own(get, at)
        job_e.settle(get, at)
        spread_4.pass_on(get, at)
        job_e.rows_forward(get, at)
        job_e.collect(get, at)
        job_e.drain()
        spread_4.finish(get, at)

    (
        stream_in,
        target_in,
        vectors,
        fact_rows,
        fact_columns,
        unused,
        unused,
        unused,
        unused,
        unused,
        first_w,
        first_o,
        second_w,
        cross_w,
        third_w,
        rows_a,
        rows_c,
        enc_q,
        enc_kv,
        self_q,
        self_kv,
        enc_mixed,
        enc_total,
        self_mixed,
        self_total,
        stream_mid,
        rows_b,
        target_mid,
        cross_q,
        cross_kv,
        rows_d,
        enc_hidden,
        enc_slope,
        stream_end,
        memory,
        cross_mixed,
        cross_total,
        target_late,
        rows_e,
    ) = run_body(call, onward, ["all"], "onward", 0, 170 * MICROSECOND)

    call = Call()
    dec_u, dec_d = pick(call, third_w, UP), pick(call, third_w, DOWN)
    cross_o = pick(call, cross_w, O)
    feed = Feed(call, rows_e, dec_u, dec_d)
    slots = Slots(call, [by_owner(cotangent)], True)
    vec, res, cot = call.take(vectors), call.fetch(target_late), slots.outs[0]
    decoded_out, grad_end = call.keep((128, 1024), BF16), call.hold((128, 1024), F32)
    share_out = call.give((2, 1024), F32)

    def last_mid(get, total):
        stream = get(res)[...] + total
        gain, shift = get(vec)[DEC_G + 3 : DEC_G + 4], get(vec)[DEC_B + 3 : DEC_B + 4]
        unit, unused = unit_of(stream)
        get(decoded_out)[...] = (unit * gain + shift).astype(BF16)
        grad, shares = norm_back(stream, gain, get(cot)[...].astype(F32))
        get(grad_end)[...] = grad
        get(share_out)[...] = shares
        call.save(get, decoded_out)
        return grad.astype(BF16)

    active = deactivated(call, feed.slope)
    job_t = Job(call, feed, last_mid, (dec_d, [(0, 256)], active.store))
    mid = backward_mid(call, target_late, DEC_G + 2, grad_end)
    query = Plain(call, 256)
    job_c = Job(call, (active.out, dec_u, [(0, 256)], 0), mid, (cross_o, [(0, 64)], query.store))
    down_shares = Shares(call, [(feed.hidden, 0, job_t.gathered)], 256, False)
    joined = call.give((4, 4, 512, 128), BF16, pltpu.HBM)
    up_shares = Shares(call, [(active.out, 0, feed.rows)], 256, joined, 0)
    back = AttendBack(
        call,
        cross_q,
        cross_kv,
        query.out,
        cross_total,
        fact_rows,
        fact_columns,
        (TARGET, SOURCE, False),
    )
    cross_shares = Shares(
        call,
        [
            (back.out, 0, rows_d),
            (back.out, 256, memory),
            (back.out, 512, memory),
            (cross_mixed, 0, job_c.gathered),
        ],
        64,
        joined,
        256,
    )
    gather = Gather(call, down_shares.room, 256)

    def turning(get, at):
        for weight in (dec_u, dec_d, cross_o):
            weight.start(get)
        slots.start(get, at)
        job_t.sums(get, at)
        job_t.sum_forward(get, at)
        job_t.sum_own(get, at)
        slots.finish(get, at)
        job_t.settle(get, at)
        job_t.product(get, at, at["own_row"])
        job_t.rows_forward(get, at)
        job_t.collect(get, at)
        job_c.sums(get, at)
        job_c.sum_forward(get, at)
        job_c.sum_own(get, at)
        down_shares.middle(get, at)
        down_shares.finish(get, at)
        job_c.settle(get, at)
        gather.launch(get, at)
        job_c.product(get, at, at["own_row"])
        job_c.rows_forward(get, at)
        up_shares.middle(get, at)
        job_c.collect(get, at)
        up_shares.finish(get, at)
        gather.relay(get, at)
        job_t.drain()
        job_c.drain()
        back.late(get, at)
        cross_shares.middle(get, at)
        cross_shares.finish(get, at)
        gather.finish(get, at)

    (
        dec_hidden,
        dec_slope,
        unused,
        decoded,
        norm_3,
        dec_grad_act,
        grad_rows_e,
        grad_late,
        norm_2,
        cross_grad_mixed,
        grad_rows_d,
        joined_s,
        cross_grads,
        down_g,
    ) = run_body(call, turning, ["all"], "turning", 1, 62 * MICROSECOND)

    call = Call()
    cross_a, cross_b = pick(call, cross_w, Q), pick(call, cross_w, KV)
    self_o, enc_d = pick(call, first_o, FIRST_O, SELF_O), pick(call, second_w, DOWN)
    slots = Slots(call, [decoded], False)
    mid = backward_mid(call, target_mid, DEC_G + 1, grad_late)
    query = Plain(call, 256)
    job_t = Job(call, (cross_grads, cross_a, [(0, 64)], 0), mid, (self_o, [(0, 64)], query.store))
    mid = backward_mid(call, stream_end, ENC_G + 2)
    active = deactivated(call, call.fetch(enc_slope))
    job_s = Job(
        call,
        (cross_grads, cross_b, [(0, 64), (64, 64)], 256),
        mid,
        (enc_d, [(0, 256)], active.store),
    )
    shares = Shares(
        call, [(active.out, 0, rows_b), (enc_hidden, 0, job_s.gathered)], 256
    )
    gather, swap = Gather(call, joined_s, 512), Swap(call, down_g)

    def backing(get, at):
        gather.launch(get, at)
        for weight in (cross_b, cross_a, enc_d, self_o):
            weight.start(get)
        job_s.sums(get, at)
        job_t.sums(get, at)
        job_s.sum_forward(get, at)
        job_t.sum_forward(get, at)
        job_s.sum_own(get, at)
        job_s.settle(get, at)
        job_t.sum_own(get, at)
        job_t.settle(get, at)
        slots.start(get, at)
        job_s.product(get, at, at["own_row"])
        job_s.rows_forward(get, at)
        job_t.product(get, at, at["own_row"])
        job_t.rows_forward(get, at)
        swap.start(get, at)
        job_s.collect(get, at)
        gather.relay(get, at)
        shares.middle(get, at)
        job_t.collect(get, at)
        shares.finish(get, at)
        job_s.drain()
        job_t.drain()
        slots.finish(get, at)
        swap.finish(get, at)
        gather.finish(get, at)

    (
        decoded,
        grad_mid,
        norm_1,
        self_grad_mixed,
        grad_rows_c,
        grad_stream,
        enc_norm_2,
        enc_grad_act,
        grad_rows_b,
        feed_s,
        up_cross_g,
        down_g,
    ) = run_body(call, backing, ["x", "y", "core", "d", "ways"], "backing", 2, 46 * MICROSECOND)

    call = Call()
    enc_u, enc_o = pick(call, second_w, UP), pick(call, first_o, FIRST_O)
    self_a = pick(call, first_w, QKV, SELF)
    self_back = AttendBack(
        call,
        self_q,
        self_kv,
        self_grad_mixed,
        self_total,
        fact_rows,
        fact_columns,
        (TARGET, TARGET, True),
    )
    mid = backward_mid(call, stream_mid, ENC_G + 1, grad_stream)
    query = Plain(call, 256)
    job_s = Job(call, (enc_grad_act, enc_u, [(0, 256)], 0), mid, (enc_o, [(0, 64)], query.store))
    mid = backward_mid(call, target_in, DEC_G, grad_mid, BF16)
    job_t = Job(call, (self_back.out, self_a, [(0, 64), (64, 64), (128, 64)], 0), mid, None)
    self_shares = Shares(
        call,
        [
            (self_back.out, 0, rows_c),
            (self_back.out, 256, rows_c),
            (self_back.out, 512, rows_c),
            (self_mixed, 0, grad_rows_c),
        ],
        64,
        False,
    )
    enc_back = AttendBack(
        call,
        enc_q,
        enc_kv,
        query.out,
        enc_total,
        fact_rows,
        fact_columns,
        (SOURCE, SOURCE, False),
    )
    enc_shares = Shares(
        call,
        [
            (enc_back.out, 0, rows_a),
            (enc_back.out, 256, rows_a),
            (enc_back.out, 512, rows_a),
            (enc_mixed, 0, job_s.gathered),
        ],
        64,
        False,
    )
    enc_a = pick(call, first_w, QKV)
    mid = backward_mid(call, stream_in, ENC_G, job_s.kept, BF16)
    job_f = Job(call, (enc_back.out, enc_a, [(0, 64), (64, 64), (128, 64)], 0), mid, None)
    gather_f, gather_s = Gather(call, feed_s, 512), Gather(call, self_shares.room, 256)
    gather_e = Gather(call, enc_shares.room, 256)
    for gather, rows in ((gather_f, 512), (gather_s, 256), (gather_e, 256)):
        call.rows_of[gather.out] = rows
    swap, swap_f = Swap(call, up_cross_g), Swap(call, gather_f.out)
    swap_s, swap_e = Swap(call, gather_s.out), Swap(call, gather_e.out)
    target_slots, source_slots = Slots(call, [job_t.kept], False), Slots(call, [job_f.kept], False)
    others = [call.take(norm) for norm in (norm_1, norm_2, norm_3, enc_norm_2)]
    norm_sum = call.hold((16, 1024), F32)
    sums = Vectors(call, norm_sum, False)

    def selfward(get, at):
        gather_f.launch(get, at)
        for weight in (enc_u, self_a, enc_o, enc_a):
            weight.start(get)
        self_back.prepare(get)
        job_s.sums(get, at)
        self_back.pair(get, at, 0)
        job_s.sum_forward(get, at)
        self_back.pair(get, at, 1)
        self_back.end(get)
        job_s.sum_own(get, at)
        job_t.sums(get, at)
        job_s.settle(get, at)
        job_t.sum_forward(get, at)
        job_t.sum_own(get, at)
        self_shares.middle(get, at)
        self_shares.finish(get, at)
        gather_s.launch(get, at)
        job_s.product(get, at, at["own_row"])
        job_s.rows_forward(get, at)
        job_t.settle(get, at)
        gather_f.relay(get, at)
        target_slots.start(get, at)
        swap.start(get, at)
        job_s.collect(get, at)
        job_s.drain()
        job_t.drain()
        enc_back.late(get, at)
        enc_shares.middle(get, at)
        enc_shares.finish(get, at)
        gather_e.launch(get, at)
        gather_s.relay(get, at)
        job_f.sums(get, at)
        job_f.sum_forward(get, at)
        job_f.sum_own(get, at)
        job_f.settle(get, at)
        gather_e.relay(get, at)
        source_slots.start(get, at)
        total = get(norm_sum)
        for row, shares in (
            (0, get(job_f.shares)),
            (1, get(job_s.shares)),
            (2, get(others[3])),
            (6, get(job_t.shares)),
            (7, get(others[0])),
            (8, get(others[1])),
            (9, get(others[2])),
        ):
            below = row + (3 if row < 6 else 4)
            total[row : row + 1] = shares[0:1]
            total[below : below + 1] = shares[1:2]
        total[14:16] = jnp.zeros((2, 1024), F32)
        sums.start(get, at)
        job_f.drain()
        gather_f.finish(get, at)
        swap_f.start(get, at)
        sums.second(get, at)
        target_slots.finish(get, at)
        gather_s.finish(get, at)
        swap_s.start(get, at)
        sums.finish(get, at)
        source_slots.finish(get, at)
        swap.finish(get, at)
        swap_f.finish(get, at)
        gather_e.finish(get, at)
        swap_e.start(get, at)
        swap_s.finish(get, at)
        swap_e.finish(get, at)

    made = run_body(call, selfward, ["all"], "selfward", 3, 105 * MICROSECOND)
    up_cross_g, feed_g, self_g, enc_g, target_grad, source_grad, norm_grad = made[-7:]
    norm_grad = norm_grad.reshape(16, copies, 4, 32 // copies)
    if copies > 1:
        norm_grad = lax.psum_scatter(norm_grad, "k", scatter_dimension=1)
    norm_grad = norm_grad.reshape(16, 4, -1)
    norm_grad = lax.dynamic_index_in_dim(norm_grad, z, 1, False)

    (
        dec_d,
        dec_u,
        cross_a,
        cross_o,
        enc_u,
        enc_d,
        self_a,
        self_o,
        enc_a,
        enc_o,
        source_grad,
        target_grad,
    ) = unpacked(
        [down_g, up_cross_g, feed_g, self_g, enc_g],
        [source_grad, target_grad],
        [("down",), ("up", "q", "o"), ("up", "down"), ("q", "o"), ("q", "o")],
    )

    def narrow(array, axis):
        if copies == 1:
            return array
        return lax.psum_scatter(array, "k", scatter_dimension=axis, tiled=True)

    enc_a, self_a, cross_a = (narrow(array, 1) for array in (enc_a, self_a, cross_a))
    enc_o, self_o, cross_o = (narrow(array, 1) for array in (enc_o, self_o, cross_o))
    enc_u, dec_u = narrow(enc_u, 0), narrow(dec_u, 0)
    enc_d, dec_d = narrow(enc_d, 1), narrow(dec_d, 1)
    return (
        by_owner(decoded, True),
        by_owner(source_grad, True),
        by_owner(target_grad, True),
        enc_a,
        enc_o,
        enc_u,
        enc_d,
        norm_grad[:3],
        norm_grad[3:6],
        self_a,
        self_o,
        cross_a,
        cross_o,
        dec_u,
        dec_d,
        norm_grad[6:10],
        norm_grad[10:14],
    )


def solution(mesh):
    dp, seq, mp = (mesh.shape[name] for name in ("dp", "seq", "mp"))
    assert dp % 2 == 0 and seq == 4 and mp == 4
    fine = Mesh(mesh.devices.reshape(2, dp // 2, 2, 2, 4), AXES)
    d, s = ("hi", "k"), ("y", "c")
    rows = P(d, s + ("mp",), None)
    three, flat = P(None, d + s, "mp"), P("mp", d + s)
    up, vector = P(d + s, "mp"), P(None, d + s + ("mp",))
    attention, feeding = (three, flat), (up, flat)
    return jax.shard_map(
        local,
        mesh=fine,
        in_specs=(rows,) * 3
        + (P(d), P(d), P(d, None), P(d, None))
        + attention
        + feeding
        + (vector, vector)
        + attention * 2
        + feeding
        + (vector, vector),
        out_specs=(rows,) * 3
        + attention
        + feeding
        + (vector, vector)
        + attention * 2
        + feeding
        + (vector, vector),
        check_vma=False,
    )
```

```python
import math

import jax
import jax.numpy as jnp
from jax import lax
from jax.experimental import pallas as pl
from jax.experimental.pallas import tpu as pltpu
from jax.sharding import Mesh, PartitionSpec as P

HEAD_DIM = 64
EPSILON = 1e-05
MASKED = -1000000000.0
PAIRS = 8
AXES = ("hi", "k", "y", "c", "mp")
MESH_ID = pl.DeviceIdType.MESH
F32 = jnp.float32
BF16 = jnp.bfloat16


class Call:
    def __init__(self):
        self.known, self.arrays, self.specs = [], [], []
        self.shapes, self.places, self.scratch = [], [], []
        self.fetched, self.kept, self.rows_of = [], [], {}

    def take(self, array, space=pltpu.VMEM):
        if isinstance(array, tuple):
            return array
        for i, known in enumerate(self.known):
            if known is array and self.specs[i].memory_space == space:
                return ("in", i)
        self.known.append(array)
        if space == pltpu.HBM:
            array = pltpu.with_memory_space_constraint(array, pltpu.HBM)
        self.arrays.append(array)
        self.specs.append(pl.BlockSpec(memory_space=space))
        return ("in", len(self.arrays) - 1)

    def fetch(self, array):
        if isinstance(array, tuple):
            return array
        source = self.take(array, pltpu.HBM)
        for i, (known, room, sem) in enumerate(self.fetched):
            if known == source:
                return ("fetch", i)
        self.fetched.append((source, self.hold(array.shape, array.dtype), self.sems(1)))
        return ("fetch", len(self.fetched) - 1)

    def give(self, shape, dtype, space=pltpu.VMEM):
        if space == pltpu.HBM:
            self.shapes.append(pltpu.HBM(shape, dtype))
        else:
            self.shapes.append(jax.ShapeDtypeStruct(shape, dtype))
        self.places.append(pl.BlockSpec(memory_space=space))
        return ("out", len(self.shapes) - 1)

    def keep(self, shape, dtype, parts=1):
        target = self.give(shape, dtype, pltpu.HBM)
        self.kept.append((target, self.hold(shape, dtype), self.sems(parts)))
        return ("keep", len(self.kept) - 1)

    def hold(self, shape, dtype):
        self.scratch.append(pltpu.VMEM(shape, dtype))
        return ("tmp", len(self.scratch) - 1)

    def sems(self, count):
        self.scratch.append(pltpu.SemaphoreType.DMA((count,)))
        return ("tmp", len(self.scratch) - 1)

    def save(self, get, handle, row=None):
        target, room, sems = (get(part) for part in self.kept[handle[1]])
        if row is not None:
            target, room = target.at[row], room.at[row]
        count = sum(1 for known, unused in self.saves if known == handle)
        copy = pltpu.make_async_copy(room, target, sems.at[count])
        copy.start()
        self.saves.append((handle, copy))

    def run(self, body, name, collective=None, flops=0):
        ins, outs = len(self.arrays), len(self.shapes)

        def kernel(*refs):
            parts = {"in": refs[:ins], "out": refs[ins : ins + outs], "tmp": refs[ins + outs :]}
            here, self.saves, self.waited = set(), [], []

            def get(handle):
                kind, i = handle
                if kind == "keep":
                    return get(self.kept[i][1])
                if kind != "fetch":
                    return parts[kind][i]
                source, room, sem = (get(part) for part in self.fetched[i])
                if i not in here:
                    here.add(i)
                    pltpu.make_async_copy(source, room, sem.at[0]).wait()
                return room

            for source, room, sem in self.fetched:
                pltpu.make_async_copy(get(source), get(room), get(sem).at[0]).start()
            body(get)
            for i in range(len(self.fetched)):
                get(("fetch", i))
            for handle, copy in self.saves:
                copy.wait()

        held = [a for a, spec in zip(self.arrays, self.specs) if spec.memory_space == pltpu.VMEM]
        held += [a for a, spec in zip(self.shapes, self.places) if spec.memory_space == pltpu.VMEM]
        held += [x for x in self.scratch if x.dtype in (BF16, F32)]
        room = sum(math.prod(x.shape) * jnp.dtype(x.dtype).itemsize for x in held)
        return pl.pallas_call(
            kernel,
            out_shape=tuple(self.shapes),
            in_specs=self.specs,
            out_specs=tuple(self.places),
            scratch_shapes=self.scratch,
            compiler_params=pltpu.CompilerParams(
                collective_id=collective,
                has_side_effects=collective is not None,
                vmem_limit_bytes=room + (8 << 20),
            ),
            cost_estimate=pl.CostEstimate(flops=flops, bytes_accessed=0, transcendentals=0),
            name=name,
        )(*self.arrays)


MICROSECOND = 1_000_000_000


def nt(left, right):
    return lax.dot_general(left, right, (((1,), (1,)), ((), ())), preferred_element_type=F32)


def nn(left, right):
    return lax.dot_general(left, right, (((1,), (0,)), ((), ())), preferred_element_type=F32)


def tn(left, right):
    return lax.dot_general(left, right, (((0,), (0,)), ((), ())), preferred_element_type=F32)


def unit_of(stream):
    average = jnp.mean(stream, -1, keepdims=True)
    centred = stream - average
    scale = lax.rsqrt(jnp.mean(centred * centred, -1, keepdims=True) + EPSILON)
    return centred * scale, scale


def norm_back(stream, gain, upstream):
    unit, scale = unit_of(stream)
    inner = upstream * gain
    grad = scale * (
        inner - jnp.mean(inner, -1, keepdims=True) - unit * jnp.mean(inner * unit, -1, keepdims=True)
    )
    shares = jnp.concatenate(
        [jnp.sum(upstream * unit, 0, keepdims=True), jnp.sum(upstream, 0, keepdims=True)], 0
    )
    return grad, shares


def gelu_pair(act):
    bell = 0.5 + 0.5 * lax.erf(act * 0.7071067811865476)
    slope = bell + act * (jnp.exp(act * act * -0.5) * 0.3989422804014327)
    return act * bell, slope


def place():
    hi, k, y, c, z = (lax.axis_index(name) for name in AXES)
    return {
        "x": (1 - hi, k, y, c, z),
        "y": (hi, k, 1 - y, c, z),
        "d": (1 - hi, k, 1 - y, c, z),
        "core": (hi, k, y, 1 - c, z),
        "mesh": (hi, k, y, c, z),
        "own_row": y * 2 + hi,
        "x_row": y * 2 + 1 - hi,
        "y_row": (1 - y) * 2 + hi,
        "d_row": (1 - y) * 2 + 1 - hi,
    }


def greet(partners):
    barrier = pltpu.get_barrier_semaphore()
    for partner in partners:
        pl.semaphore_signal(barrier, inc=1, device_id=partner, device_id_type=MESH_ID)
    pl.semaphore_wait(barrier, len(partners))


def along(at):
    hi, k, y, c, z = at["mesh"]
    return [(hi, k, y, c, lax.rem(z + n, 4)) for n in range(1, 4)]


class Weight:
    def __init__(self, call, packed, first, count):
        self.call, self.source = call, call.take(packed, pltpu.HBM)
        self.room = call.hold((4, count, 1024), BF16)
        self.sem = call.sems(1)
        self.first, self.count = first, count

    def start(self, get):
        source, room, sem = get(self.source), get(self.room), get(self.sem)
        for q in range(4):
            for c in range(2):
                pltpu.make_async_copy(
                    source.at[c, :, q, pl.ds(self.first, self.count), :],
                    room.at[:, :, pl.ds((q * 2 + c) * 128, 128)],
                    sem.at[0],
                ).start()

    def wait(self, get):
        if self in self.call.waited:
            return
        self.call.waited.append(self)
        room = get(self.room)
        pltpu.make_async_copy(room, room, get(self.sem).at[0]).wait()

    def matrix(self, get, first, count):
        return get(self.room)[:, first : first + count, :].reshape(4 * count, 1024)


def stack(blocks):
    return blocks[0] if len(blocks) == 1 else jnp.concatenate(blocks, 0)


class Feed:
    def __init__(self, call, rows, up, down):
        self.call, self.rows, self.weights = call, call.fetch(rows), [up, down]
        self.hidden = call.keep((4, 128, 1024), BF16, 4)
        self.slope = call.keep((4, 128, 1024), F32, 4)

    def part(self, get, *rows):
        up, down = self.weights
        whole = stack([get(self.rows)[row] for row in rows])
        made, slope = gelu_pair(nt(whole, up.matrix(get, 0, 256)))
        made = made.astype(BF16)
        for i, row in enumerate(rows):
            get(self.hidden)[row] = made[i * 128 : (i + 1) * 128]
            get(self.slope)[row] = slope[i * 128 : (i + 1) * 128]
            self.call.save(get, self.hidden, row)
            self.call.save(get, self.slope, row)
        return nn(made, down.matrix(get, 0, 256))


class Job:
    def __init__(self, call, left, mid, right):
        self.call, self.left, self.mid, self.right = call, left, mid, right
        self.kept, self.shares = getattr(mid, "kept", None), getattr(mid, "shares", None)
        if left is not None:
            self.rows_in = None if isinstance(left, Feed) else call.fetch(left[0])
            self.out_first = call.hold((2, 128, 1024), BF16)
            self.out_edge = call.hold((2, 64, 1024), BF16)
            self.out_late = call.hold((2, 64, 1024), BF16)
            self.keep = call.hold((2, 64, 1024), F32)
            self.own = call.hold((128, 1024), F32)
            self.landed = call.hold((6, 64, 1024), BF16)
            self.sum_send, self.sum_recv = call.sems(6), call.sems(6)
        self.gathered = None
        if right is not None:
            self.gathered = call.keep((4, 128, 1024), BF16, 4)
            self.row_send, self.row_recv = call.sems(6), call.sems(6)

    def lefts(self):
        return self.left.weights if isinstance(self.left, Feed) else [self.left[1]]

    def part(self, get, *rows):
        if isinstance(self.left, Feed):
            return self.left.part(get, *rows)
        unused, weight, picks, column = self.left
        total = None
        for first, count in picks:
            width = 4 * count
            left = stack([get(self.rows_in)[row, :, column : column + width] for row in rows])
            term = nn(left, weight.matrix(get, first, count))
            total = term if total is None else total + term
            column += width
        return total

    def send(self, get, i, source, target, partner):
        copy = pltpu.make_async_remote_copy(
            src_ref=source,
            dst_ref=target,
            send_sem=get(self.sum_send).at[i],
            recv_sem=get(self.sum_recv).at[i],
            device_id=partner,
            device_id_type=MESH_ID,
        )
        copy.start()
        return copy

    def sum_start(self, get, at):
        first, edge, landed = get(self.out_first), get(self.out_edge), get(self.landed)
        keep = get(self.keep)
        self.copies = [None] * 6
        first[0] = self.part(get, at["d_row"]).astype(BF16)
        self.copies[0] = self.send(
            get, 0, first.at[0, pl.ds(0, 64)], landed.at[0], at["x"]
        )
        self.copies[1] = self.send(
            get, 1, first.at[0, pl.ds(64, 64)], landed.at[1], at["y"]
        )
        part = self.part(get, at["x_row"], at["y_row"])
        edge[0] = part[:64].astype(BF16)
        keep[0] = part[64:128]
        self.copies[2] = self.send(get, 2, edge.at[0], landed.at[2], at["x"])
        edge[1] = part[192:].astype(BF16)
        keep[1] = part[128:192]
        self.copies[3] = self.send(get, 3, edge.at[1], landed.at[3], at["y"])

    def sum_forward(self, get, at):
        late, landed, keep = get(self.out_late), get(self.landed), get(self.keep)
        self.copies[0].wait_recv()
        late[1] = (keep[1] + landed[0].astype(F32)).astype(BF16)
        self.copies[4] = self.send(get, 4, late.at[1], landed.at[4], at["y"])
        self.copies[1].wait_recv()
        late[0] = (keep[0] + landed[1].astype(F32)).astype(BF16)
        self.copies[5] = self.send(get, 5, late.at[0], landed.at[5], at["x"])

    def sum_own(self, get, at):
        get(self.own)[...] = self.part(get, at["own_row"])

    def sum_end(self, get):
        landed, own = get(self.landed), get(self.own)
        for i in (2, 3, 4, 5):
            self.copies[i].wait_recv()
        upper = own[:64] + landed[2].astype(F32) + landed[4].astype(F32)
        lower = own[64:] + landed[5].astype(F32) + landed[3].astype(F32)
        return jnp.concatenate([upper, lower], 0)

    def row_copy(self, get, i, row, half, partner):
        block = get(self.gathered).at[row, pl.ds(half * 64, 64)]
        copy = pltpu.make_async_remote_copy(
            src_ref=block,
            dst_ref=block,
            send_sem=get(self.row_send).at[i],
            recv_sem=get(self.row_recv).at[i],
            device_id=partner,
            device_id_type=MESH_ID,
        )
        copy.start()
        return copy

    def rows_start(self, get, at, normed):
        get(self.gathered)[at["own_row"]] = normed
        self.call.save(get, self.gathered, at["own_row"])
        self.moves = [
            self.row_copy(get, 0, at["own_row"], 0, at["y"]),
            self.row_copy(get, 1, at["own_row"], 1, at["x"]),
            self.row_copy(get, 2, at["own_row"], 1, at["y"]),
            self.row_copy(get, 3, at["own_row"], 0, at["x"]),
        ]

    def rows_forward(self, get, at):
        self.moves[0].wait_recv()
        self.moves.append(self.row_copy(get, 4, at["y_row"], 0, at["x"]))
        self.moves[1].wait_recv()
        self.moves.append(self.row_copy(get, 5, at["x_row"], 1, at["y"]))

    def product(self, get, at, row):
        weight, picks, store = self.right
        if weight is None:
            return
        weight.wait(get)
        rows = get(self.gathered)[row]
        column = 0
        for first, count in picks:
            store(get, at, row, column, nt(rows, weight.matrix(get, first, count)))
            column += 4 * count

    def sums(self, get, at):
        for weight in self.lefts():
            weight.wait(get)
        self.sum_start(get, at)

    def settle(self, get, at):
        normed = self.mid(get, self.sum_end(get) if self.left is not None else None)
        if self.right is not None:
            self.rows_start(get, at, normed)

    def collect(self, get, at, sides=True, far=True):
        for moves, row in (((3,), "x_row"), ((2,), "y_row"), ((4, 5), "d_row")):
            if far if row == "d_row" else sides:
                for i in moves:
                    self.moves[i].wait_recv()
                self.call.save(get, self.gathered, at[row])
                self.product(get, at, at[row])

    def drain(self):
        if self.left is not None:
            for copy in self.copies:
                copy.wait_send()
        if self.right is not None:
            for copy in self.moves:
                copy.wait_send()


def run_body(call, work, names, name, collective, flops):
    groups = {"all": meeting, "z": along, "ways": lambda at: all_partners(at)[1]}

    def body(get):
        at = place()
        partners = []
        for group in names:
            partners += groups[group](at) if group in groups else [at[group]]
        greet(partners)
        work(get, at)

    return call.run(body, name, collective, flops)


class Kept:
    def __init__(self, out, store):
        self.out, self.store = out, store


class Plain:
    def __init__(self, call, width):
        self.call, self.width = call, width
        self.out = call.keep((4, 128, width), BF16, 4)

    def store(self, get, at, row, column, value):
        get(self.out)[row, :, column : column + value.shape[1]] = value.astype(BF16)
        if column + value.shape[1] == self.width:
            self.call.save(get, self.out, row)


class Shared:
    def __init__(self, call, width, skip=0):
        self.call, self.out = call, call.keep((2, 4, 128, width), BF16, 2)
        self.send_sem, self.recv_sem = call.sems(4), call.sems(4)
        self.width, self.skip, self.copies, self.blocks = width, skip, [], 0

    def store(self, get, at, row, column, value):
        out = get(self.out)
        column = column - self.skip
        out[0, row, :, column : column + value.shape[1]] = value.astype(BF16)
        if column + value.shape[1] == self.width:
            i = len(self.copies)
            copy = pltpu.make_async_remote_copy(
                src_ref=out.at[0, row],
                dst_ref=out.at[1, row],
                send_sem=get(self.send_sem).at[i],
                recv_sem=get(self.recv_sem).at[i],
                device_id=at["core"],
                device_id_type=MESH_ID,
            )
            copy.start()
            self.copies.append(copy)

    def finish(self, get):
        self.call.save(get, self.out, 0)
        for copy in self.copies:
            copy.wait()
        self.call.save(get, self.out, 1)


def query_and_shared(call, width):
    query, shared = Plain(call, width), Shared(call, 2 * width, skip=width)

    def store(get, at, row, column, value):
        if column < width:
            query.store(get, at, row, column, value)
        else:
            shared.store(get, at, row, column, value)

    return store, shared.finish


def lanes_of(head, rows):
    lane = lax.broadcasted_iota(jnp.int32, (rows, 128), 1)
    return lane // HEAD_DIM == head


SOURCE, TARGET, PLACE, LIVE = 0, 1, 2, 3


def allowed_bias(rows, columns, query_kind, key_kind, causal):
    allowed = columns[:, key_kind : key_kind + 1] == rows[query_kind : query_kind + 1, :512]
    allowed = allowed & (columns[:, LIVE + key_kind : LIVE + key_kind + 1] > 0.5)
    if causal:
        allowed = allowed & (columns[:, PLACE : PLACE + 1] <= rows[PLACE : PLACE + 1, :512])
    return jnp.where(allowed, 0.0, MASKED)


def masked(mask, span, count):
    if count == 4:
        return mask[:, span]
    return jnp.concatenate([mask[: count * 128, span], mask[512 : 512 + count * 128, span]], 0)


class Attend:
    def __init__(self, call, queries, key_value, rows, columns, kinds):
        self.call, self.kinds = call, kinds
        self.queries, self.key_value = call.fetch(queries), call.fetch(key_value)
        self.rows, self.columns = call.take(rows), call.fetch(columns)
        self.mixed = call.keep((4, 128, 256), BF16)
        self.total = call.give((8, 512), F32)
        self.bias = call.hold((1024, 512), F32)

    def late(self, get, at):
        self.prepare(get)
        self.pairs(get, 0, 2)
        self.call.save(get, self.mixed)

    def visible(self, block):
        return 2 if self.kinds[2] and block == 0 else 4

    def prepare(self, get):
        mask = get(self.bias)
        mask[...] = allowed_bias(get(self.rows), get(self.columns), *self.kinds)

    def pairs(self, get, first, last):
        mask = get(self.bias)
        q_ref, kv_ref = get(self.queries), get(self.key_value)
        mixed_ref, total_ref = get(self.mixed), get(self.total)

        def pair_step(pair, carry):
            lanes = pl.ds(pl.multiple_of(pair * 128, 128), 128)
            value_lanes = pl.ds(pl.multiple_of(256 + pair * 128, 128), 128)
            for block in range(2):
                count = self.visible(block)
                keys = kv_ref[:, :count, :, lanes].reshape(count * 256, 128)
                values = kv_ref[:, :count, :, value_lanes].reshape(count * 256, 128)
                span = slice(block * 256, block * 256 + 256)
                queries = q_ref[2 * block : 2 * block + 2, :, lanes].reshape(256, 128)
                mixed = []
                for head in range(2):
                    picked = jnp.where(lanes_of(head, 256), queries * 0.125, 0.0).astype(BF16)
                    scores = nt(keys, picked) + masked(mask, span, count)
                    top = jnp.max(scores, 0, keepdims=True)
                    raised = jnp.exp(scores - top)
                    total = jnp.sum(raised, 0, keepdims=True)
                    probs = (raised * (1.0 / total)).astype(BF16)
                    mixed.append(tn(values, probs)[head * HEAD_DIM : (head + 1) * HEAD_DIM])
                    total_ref[pl.ds(pair * 2 + head, 1), span] = top + jnp.log(total)
                mixed = jnp.concatenate(mixed, 0).T.astype(BF16)
                mixed_ref[2 * block : 2 * block + 2, :, lanes] = mixed.reshape(2, 128, 128)
            return carry

        lax.fori_loop(first, last, pair_step, 0)


class AttendBack:
    def __init__(self, call, queries, key_value, grad_mixed, total, rows, columns, kinds):
        self.call, self.kinds = call, kinds
        self.queries, self.key_value = call.fetch(queries), call.fetch(key_value)
        self.grad_mixed, self.total = call.fetch(grad_mixed), call.take(total)
        self.rows, self.columns = call.take(rows), call.fetch(columns)
        self.out = call.keep((4, 128, 768), BF16)
        self.bias, self.sums = call.hold((1024, 512), F32), call.hold((1024, 512), F32)
        self.away, self.landed = call.hold((2, 512, 256), BF16), call.hold((2, 512, 256), BF16)
        self.send_sem, self.recv_sem = call.sems(2), call.sems(2)

    def partners(self, at):
        return [at["core"]]

    def late(self, get, at):
        self.prepare(get)
        for pair in range(2):
            self.pair(get, at, pair)
        self.end(get)

    def prepare(self, get):
        mask = get(self.bias)
        mask[...] = allowed_bias(get(self.rows), get(self.columns), *self.kinds)
        self.copies = []

    def pair(self, get, at, pair):
        out, mask, sums = get(self.out), get(self.bias), get(self.sums)
        away, here = get(self.away), get(self.landed)
        q_ref, kv_ref = get(self.queries), get(self.key_value)
        grad_ref, total_ref = get(self.grad_mixed), get(self.total)
        lanes = slice(pair * 128, pair * 128 + 128)
        key_sum = slice(pair * 256, pair * 256 + 128)
        value_sum = slice(pair * 256 + 128, pair * 256 + 256)
        for block in (1, 0):
            count = 2 if self.kinds[2] and block == 0 else 4
            keys_pair = kv_ref[:, :count, :, lanes].reshape(count * 256, 128)
            values_pair = kv_ref[:, :count, :, 256 + pair * 128 : 384 + pair * 128]
            values_pair = values_pair.reshape(count * 256, 128)
            span = slice(block * 256, block * 256 + 256)
            two = slice(2 * block, 2 * block + 2)
            q_block = q_ref[two, :, lanes].reshape(256, 128)
            g_block = grad_ref[two, :, lanes].reshape(256, 128)
            grad_query = []
            for head in range(2):
                inside = lanes_of(head, 256)
                picked = jnp.where(inside, q_block * 1.0, 0.0).astype(BF16)
                grads = jnp.where(inside, g_block * 1.0, 0.0).astype(BF16)
                scores = nt(keys_pair, picked) * 0.125 + masked(mask, span, count)
                probs = jnp.exp(scores - total_ref[pair * 2 + head : pair * 2 + head + 1, span])
                weighted = probs * nt(values_pair, grads)
                inner = jnp.sum(weighted, 0, keepdims=True)
                grad_raw = ((weighted - probs * inner) * 0.125).astype(BF16)
                value_term = nn(probs.astype(BF16), grads)
                key_term = nn(grad_raw, picked)
                if block == 1 and head == 0:
                    sums[:, key_sum] = key_term
                    sums[:, value_sum] = value_term
                else:
                    for half in range(2 if count < 4 else 1):
                        size = count * 128 if count < 4 else 1024
                        rows = slice(half * 512, half * 512 + size)
                        terms = slice(half * size, half * size + size)
                        sums[rows, key_sum] += key_term[terms]
                        sums[rows, value_sum] += value_term[terms]
                grad_query.append(tn(keys_pair, grad_raw)[head * HEAD_DIM : (head + 1) * HEAD_DIM])
            grad_query = jnp.concatenate(grad_query, 0).T.astype(BF16)
            out[two, :, lanes] = grad_query.reshape(2, 128, 128)
        away[pair] = sums[512:, pair * 256 : pair * 256 + 256].astype(BF16)
        copy = pltpu.make_async_remote_copy(
            src_ref=away.at[pair],
            dst_ref=here.at[pair],
            send_sem=get(self.send_sem).at[pair],
            recv_sem=get(self.recv_sem).at[pair],
            device_id=at["core"],
            device_id_type=MESH_ID,
        )
        copy.start()
        self.copies.append(copy)

    def end(self, get):
        out, sums, here = get(self.out), get(self.sums), get(self.landed)
        for pair in range(2):
            self.copies[pair].wait()
            both = sums[:512, pair * 256 : pair * 256 + 256] + here[pair].astype(F32)
            both = both.astype(BF16).reshape(4, 128, 256)
            out[:, :, 256 + pair * 128 : 384 + pair * 128] = both[:, :, :128]
            out[:, :, 512 + pair * 128 : 640 + pair * 128] = both[:, :, 128:]
        self.call.save(get, self.out)


class Shares:
    def __init__(self, call, pairs, count, out=None, base=0):
        self.call, self.count, self.base = call, count, base
        self.handles = [
            (call.fetch(left), column, call.fetch(right))
            for left, column, right in pairs
        ]
        shape = (4, 4, len(pairs) * count, 128)
        sends = len(pairs) * max(1, count // 64)
        self.made, self.landed = call.hold((2,) + shape, BF16), call.hold(shape, BF16)
        self.send_sem, self.recv_sem = call.sems(sends), call.sems(sends)
        self.rows = shape[2]
        self.out = call.give(shape, BF16, pltpu.HBM) if out is None else out
        self.saved = out is not False
        self.room, self.save_sem = call.hold(shape, BF16), call.sems(1)

    def partners(self, at):
        return [at["core"]]

    def send(self, get, at, part):
        i = len(self.copies)
        copy = pltpu.make_async_remote_copy(
            src_ref=get(self.made).at[(1 - lax.axis_index("c"),) + part],
            dst_ref=get(self.landed).at[part],
            send_sem=get(self.send_sem).at[i],
            recv_sem=get(self.recv_sem).at[i],
            device_id=at["core"],
            device_id_type=MESH_ID,
        )
        copy.start()
        self.copies.append((part, copy))

    def middle(self, get, at):
        self.copies, every, count = [], slice(None), self.count
        made = get(self.made)
        for m, (left, column, right) in enumerate(self.handles):
            left, right = get(left), get(right)
            span = slice(m * count, (m + 1) * count)
            for first in range(0, 4 * count, 256):
                start = column + first
                product = tn(
                    left[:, :, start : start + 256].reshape(512, 256), right[...].reshape(512, 1024)
                )
                for inner in range(0, 256, count):
                    z = (first + inner) // count
                    for d in range(8):
                        made[d % 2, z, d // 2, span, :] = product[
                            inner : inner + count, d * 128 : d * 128 + 128
                        ].astype(BF16)
                if count == 256:
                    self.send(get, at, (first // 256, every, pl.ds(m * count, count)))
            if count < 256:
                self.send(get, at, (every, every, pl.ds(m * count, count)))

    def finish(self, get, at):
        core = lax.axis_index("c")
        for part, copy in self.copies:
            copy.wait()
            own = get(self.made)[(core,) + part].astype(F32)
            get(self.room)[part] = (own + get(self.landed)[part].astype(F32)).astype(BF16)
        if not self.saved:
            return
        target = get(self.out).at[:, :, pl.ds(self.base, self.rows)]
        copy = pltpu.make_async_copy(get(self.room), target, get(self.save_sem).at[0])
        copy.start()
        self.call.saves.append((None, copy))


def push(source, target, send_sem, recv_sem, partner):
    return pltpu.make_async_remote_copy(
        src_ref=source,
        dst_ref=target,
        send_sem=send_sem,
        recv_sem=recv_sem,
        device_id=partner,
        device_id_type=MESH_ID,
    )


class Spread:
    def __init__(self, call, pack):
        rows = pack.shape if not isinstance(pack, tuple) else (4, call.rows_of[pack], 128)
        self.pack = call.take(pack, pltpu.HBM)
        self.out = call.give((2, 4) + tuple(rows), BF16, pltpu.HBM)
        self.send_sem, self.recv_sem = call.sems(5), call.sems(5)
        self.core_send, self.core_recv, self.own_sem = call.sems(6), call.sems(6), call.sems(1)

    def block(self, get, at, origin):
        return get(self.out).at[at["mesh"][3], origin]

    def move(self, get, at, way):
        hi, k, y, c, z = at["mesh"]
        step = {0: 1, 1: -1, 2: 2, 3: -2, 4: jnp.where(z == 2, 1, -1)}[way]
        origin = jnp.where(z == 2, 0, 3) if way == 4 else z
        target = self.block(get, at, origin)
        return push(
            target if way == 4 else get(self.pack),
            target,
            get(self.send_sem).at[way],
            get(self.recv_sem).at[way],
            (hi, k, y, c, lax.rem(z + step + 4, 4)),
        )

    def sends(self, at, way):
        z = at["mesh"][4]
        middle = (z == 1) | (z == 2)
        return {0: z < 3, 1: z > 0, 2: z < 2, 3: z > 1, 4: middle}[way]

    def comes(self, at, way):
        z = at["mesh"][4]
        return {0: z > 0, 1: z < 3, 2: z > 1, 3: z < 2, 4: (z == 0) | (z == 3)}[way]

    def to_core(self, get, at, way):
        z = at["mesh"][4]
        origin = {0: z - 1, 1: z + 1, 2: z - 2, 3: z + 2, 4: 3 - z, 5: z}[way]
        target = self.block(get, at, origin)
        return push(
            get(self.pack) if way == 5 else target,
            target,
            get(self.core_send).at[way],
            get(self.core_recv).at[way],
            at["core"],
        )

    def own(self, get, at):
        return pltpu.make_async_copy(
            get(self.pack), self.block(get, at, at["mesh"][4]), get(self.own_sem).at[0]
        )

    def launch(self, get, at):
        for way in (2, 3, 0, 1):

            @pl.when(self.sends(at, way))
            def _():
                self.move(get, at, way).start()

        self.to_core(get, at, 5).start()
        self.own(get, at).start()

    def relay(self, get, at):
        for plane, way in ((2, 2), (1, 3)):

            @pl.when(at["mesh"][4] == plane)
            def _():
                self.move(get, at, way).wait_recv()
                self.move(get, at, 4).start()
                self.to_core(get, at, way).start()

    def pass_on(self, get, at):
        z = at["mesh"][4]
        for way in (0, 1, 2, 3, 4):
            taken = {2: z == 2, 3: z == 1}.get(way, z < 0)

            @pl.when(self.comes(at, way) & jnp.logical_not(taken))
            def _():
                self.move(get, at, way).wait_recv()
                self.to_core(get, at, way).start()

    def finish(self, get, at):
        self.own(get, at).wait()
        self.to_core(get, at, 5).wait()
        for way in range(5):

            @pl.when(self.comes(at, way))
            def _():
                self.to_core(get, at, way).wait()

            @pl.when(self.sends(at, way))
            def _():
                self.move(get, at, way).wait_send()


class Gather:
    def __init__(self, call, shares, rows, first=0):
        self.call, self.shares, self.rows, self.first = call, call.take(shares, pltpu.HBM), rows, first
        self.landed, self.own = call.hold((3, 4, rows, 128), BF16), call.hold((4, rows, 128), BF16)
        self.far, self.room = call.hold((4, rows, 128), BF16), call.hold((4, rows, 128), BF16)
        self.out = call.keep((4, rows, 128), BF16)
        self.send_sem, self.recv_sem, self.own_sem = call.sems(4), call.sems(4), call.sems(2)

    def share(self, get, plane):
        return get(self.shares).at[plane, :, pl.ds(self.first, self.rows)]

    def move(self, get, at, way, summed=False):
        hi, k, y, c, z = at["mesh"]
        step = {0: 1, 1: 3, 2: 2, 3: jnp.where(z == 0, 1, 3)}[way]
        partner = lax.rem(z + step, 4)
        source = self.share(get, 3 - z if way == 3 else partner)
        return push(
            get(self.room) if summed else source,
            get(self.room) if way == 3 else get(self.landed).at[way],
            get(self.send_sem).at[way],
            get(self.recv_sem).at[way],
            (hi, k, y, c, partner),
        )

    def local(self, get, at, far):
        z = at["mesh"][4]
        return pltpu.make_async_copy(
            self.share(get, lax.rem(z + 2, 4) if far else z),
            get(self.far if far else self.own),
            get(self.own_sem).at[1 if far else 0],
        )

    def launch(self, get, at):
        z = at["mesh"][4]
        outer = (z == 0) | (z == 3)
        for way, when in ((3, outer), (2, outer), (0, z < 3), (1, z > 0)):

            @pl.when(when)
            def _():
                self.move(get, at, way).start()

        for far in (False, True):
            self.local(get, at, far).start()

    def relay(self, get, at):
        z = at["mesh"][4]

        @pl.when((z == 1) | (z == 2))
        def _():
            self.move(get, at, 3).wait_recv()
            self.local(get, at, True).wait()
            room = get(self.room)
            room[...] = (room[...].astype(F32) + get(self.far)[...].astype(F32)).astype(BF16)
            self.move(get, at, 2, True).start()

        @pl.when((z == 0) | (z == 3))
        def _():
            self.local(get, at, True).wait()

    def finish(self, get, at):
        z = at["mesh"][4]
        landed, own, out = get(self.landed), get(self.own), get(self.out)
        self.local(get, at, False).wait()
        self.move(get, at, 2).wait()
        for which, ways in ((z == 0, (1,)), (z == 3, (0,)), ((z == 1) | (z == 2), (0, 1))):

            @pl.when(which)
            def _():
                for way in ways:
                    self.move(get, at, way).wait_recv()
                for q in range(4):
                    total = own[q].astype(F32) + landed[2, q].astype(F32)
                    for way in ways:
                        total = total + landed[way, q].astype(F32)
                    out[q] = total.astype(BF16)

        self.call.save(get, self.out)
        for way, when in ((3, (z == 0) | (z == 3)), (0, z < 3), (1, z > 0)):

            @pl.when(when)
            def _():
                self.move(get, at, way).wait_send()


class Swap:
    def __init__(self, call, pack):
        self.pack = call.take(pack, pltpu.HBM)
        rows = call.rows_of[pack] if isinstance(pack, tuple) else pack.shape[1]
        self.out = call.give((4, rows, 128), BF16, pltpu.HBM)
        call.rows_of[self.out] = rows
        self.send_sem, self.recv_sem, self.own_sem = call.sems(3), call.sems(3), call.sems(1)

    def start(self, get, at):
        hi, k, y, c, z = at["mesh"]
        own = hi * 2 + y
        pack, out = get(self.pack), get(self.out)
        self.copies = [pltpu.make_async_copy(pack.at[own], out.at[own], get(self.own_sem).at[0])]
        for i, (name, q) in enumerate(
            (("d", (1 - hi) * 2 + 1 - y), ("x", (1 - hi) * 2 + y), ("y", hi * 2 + 1 - y))
        ):
            send, recv = get(self.send_sem).at[i], get(self.recv_sem).at[i]
            self.copies.append(push(pack.at[q], out.at[own], send, recv, at[name]))
        for copy in self.copies:
            copy.start()

    def finish(self, get, at):
        for copy in self.copies:
            copy.wait()


class Slots:
    def __init__(self, call, arrays, inward):
        self.inward = inward
        self.call, self.arrays = call, [call.fetch(array) for array in arrays]
        shape = (128, 1024) if inward else (2, 64, 1024)
        self.outs = [call.keep(shape, BF16) for array in arrays]
        self.send_sem, self.recv_sem = call.sems(2 * len(arrays)), call.sems(2 * len(arrays))

    def ends(self, get, at, j, step):
        z = at["mesh"][4]
        low = lax.div(z, 2)
        other = low if step == 0 else 1 - low
        array, out = get(self.arrays[j]), get(self.outs[j])
        if self.inward:
            return array.at[other], out.at[pl.ds(pl.multiple_of(low * 64, 64), 64)]
        return array.at[pl.ds(pl.multiple_of(other * 64, 64), 64)], out.at[low]

    def stays(self, at):
        hi, z = at["mesh"][0], at["mesh"][4]
        return lax.rem(z, 2) == hi

    def copy(self, get, at, j, step):
        hi, k, y, c, z = at["mesh"]
        low = lax.div(z, 2)
        partner = (lax.rem(z, 2), k, y, c, 2 * (low if step == 0 else 1 - low) + hi)
        source, target = self.ends(get, at, j, step)
        return pltpu.make_async_remote_copy(
            src_ref=source,
            dst_ref=target,
            send_sem=get(self.send_sem).at[2 * j + step],
            recv_sem=get(self.recv_sem).at[2 * j + step],
            device_id=partner,
            device_id_type=MESH_ID,
        )

    def start(self, get, at):
        stays = self.stays(at)
        for j in range(len(self.arrays)):
            self.copy(get, at, j, 1).start()

        @pl.when(jnp.logical_not(stays))
        def _():
            for j in range(len(self.arrays)):
                self.copy(get, at, j, 0).start()

        @pl.when(stays)
        def _():
            for j in range(len(self.arrays)):
                source, target = self.ends(get, at, j, 0)
                target[...] = source[...]

    def finish(self, get, at):
        for j in range(len(self.arrays)):
            self.copy(get, at, j, 1).wait()

        @pl.when(jnp.logical_not(self.stays(at)))
        def _():
            for j in range(len(self.arrays)):
                self.copy(get, at, j, 0).wait()

        for out in self.outs:
            self.call.save(get, out)


def all_partners(at):
    hi, k, y, c, z = at["mesh"]
    plane = [
        ((hi + i) % 2, k, (y + j) % 2, (c + n) % 2, z)
        for i in range(2)
        for j in range(2)
        for n in range(2)
        if i + j + n > 0
    ]
    ways = [((hi + i) % 2, k, y, c, (z + n) % 4) for i in range(2) for n in range(1, 4)]
    return plane, ways


def meeting(at):
    plane, ways = all_partners(at)
    return plane + ways


class Vectors:
    def __init__(self, call, vectors, inward):
        self.inward = inward
        self.source = call.take(vectors)
        self.out = call.give((16, 1024) if inward else (16, 128), F32)
        self.landed, self.whole = call.hold((7, 16, 128), F32), call.hold((16, 128), F32)
        self.split, self.along = call.hold((8, 16, 128), F32), call.hold((3, 16, 128), F32)
        self.send_sem, self.recv_sem = call.sems(10), call.sems(10)

    def move(self, get, i, source, target, partner):
        return push(source, target, get(self.send_sem).at[i], get(self.recv_sem).at[i], partner)

    def planes(self, get, at, source):
        return [
            self.move(get, n, source, get(self.along).at[n], partner)
            for n, partner in enumerate(along(at))
        ]

    def block(self, at):
        hi, k, y, c, z = at["mesh"]
        return (hi * 2 + y) * 2 + c

    def start(self, get, at):
        plane = all_partners(at)[0]
        if self.inward:
            self.copies = self.planes(get, at, get(self.source))
        else:
            split = get(self.split)
            for d in range(8):
                split[d] = get(self.source)[:, d * 128 : d * 128 + 128]
            self.copies = [
                self.move(
                    get,
                    3 + i,
                    split.at[(partner[0] * 2 + partner[2]) * 2 + partner[3]],
                    get(self.landed).at[i],
                    partner,
                )
                for i, partner in enumerate(plane)
            ]
        for copy in self.copies:
            copy.start()

    def second(self, get, at):
        plane = all_partners(at)[0]
        for copy in self.copies:
            copy.wait()
        whole, out = get(self.whole), get(self.out)
        if self.inward:
            whole[...] = get(self.source)[...] + jnp.sum(get(self.along)[...], 0)
            block = pl.ds(pl.multiple_of(self.block(at) * 128, 128), 128)
            out[:, block] = whole[...]
            self.copies = [
                self.move(get, 3 + i, whole, out.at[:, block], partner)
                for i, partner in enumerate(plane)
            ]
        else:
            whole[...] = get(self.split)[self.block(at)] + jnp.sum(get(self.landed)[...], 0)
            self.copies = self.planes(get, at, whole)
        for copy in self.copies:
            copy.start()

    def finish(self, get, at):
        for copy in self.copies:
            copy.wait()
        if not self.inward:
            get(self.out)[...] = get(self.whole)[...] + jnp.sum(get(self.along)[...], 0)


class Pack:
    def __init__(self, call, matrices):
        self.parts = [(call.fetch(array), index, across) for array, index, across in matrices]
        counts = [
            (array.shape[-1] if across else array.shape[-2]) // 4
            for array, index, across in matrices
        ]
        self.counts = counts
        self.out = call.hold((4, sum(counts), 128), BF16)
        call.rows_of[self.out] = sum(counts)

    def make(self, get):
        out, base = get(self.out), 0
        for (part, index, across), count in zip(self.parts, self.counts, strict=True):
            part = get(part)
            whole = part[...] if index is None else part[index]
            if across:
                whole = whole.astype(F32).T.astype(BF16)
            out[:, base : base + count, :] = whole.reshape(4, count, 128)
            base += count


def by_owner(rows, back=False):
    copies = lax.axis_size("k")
    if copies == 1:
        return rows
    shape, width = rows.shape, 128 // copies
    if back:
        rows = rows.reshape(-1, 2, 2, 2, copies, width).transpose(0, 1, 4, 2, 3, 5)
    else:
        rows = rows.reshape(-1, 2, copies, 2, 2, width).transpose(0, 1, 3, 4, 2, 5)
    return rows.reshape(shape)


def unpacked(packs, rows, wide):
    call = Call()
    rows_in = [call.fetch(array) for array in rows]
    ins = [call.fetch(array) for array in packs]
    plans = []
    for handle, array, kinds in zip(ins, packs, wide, strict=True):
        base = 0
        for kind in kinds:
            count = 256 if kind in ("up", "down") else 64
            if kind == "q":
                out = call.give((3, 128, 256), F32)
                plans += [(handle, base + i * 64, 64, out, i, True) for i in range(3)]
                base += 192
                continue
            shape = (128, 4 * count) if kind == "up" else (4 * count, 128)
            plans.append((handle, base, count, call.give(shape, F32), None, kind == "up"))
            base += count
    outs = [call.give(array.shape, F32) for array in rows]

    def body(get):
        for handle, base, count, out, index, across in plans:
            whole = get(handle)[:, base : base + count, :].astype(F32).reshape(4 * count, 128)
            whole = whole.T if across else whole
            if index is None:
                get(out)[...] = whole
            else:
                get(out)[index] = whole
        for source, out in zip(rows_in, outs, strict=True):
            get(out)[...] = get(source)[...].astype(F32)

    return call.run(body, "unpacked", None, 4 * MICROSECOND)


def local(
    source,
    target,
    cotangent,
    source_len,
    target_len,
    source_seg,
    target_seg,
    enc_qkv,
    enc_proj,
    enc_up,
    enc_down,
    enc_gain,
    enc_shift,
    dec_qkv,
    dec_proj,
    cross_qkv,
    cross_proj,
    dec_up,
    dec_down,
    dec_gain,
    dec_shift,
):
    copies, z = lax.axis_size("k"), lax.axis_index("mp")
    norms = (enc_gain, enc_shift, dec_gain, dec_shift)
    if copies > 1:
        norms = [lax.all_gather(vector, "k", axis=1, tiled=True) for vector in norms]

    def widen(array, axis):
        return array if copies == 1 else lax.all_gather(array, "k", axis=axis, tiled=True)

    enc_qkv, dec_qkv, cross_qkv = (widen(array, 1) for array in (enc_qkv, dec_qkv, cross_qkv))
    enc_proj, dec_proj, cross_proj = (widen(array, 1) for array in (enc_proj, dec_proj, cross_proj))
    enc_up, dec_up = widen(enc_up, 0), widen(dec_up, 0)
    enc_down, dec_down = widen(enc_down, 1), widen(dec_down, 1)

    ENC_G, ENC_B, DEC_G, DEC_B = 0, 3, 6, 10
    SELF, SELF_O = 192, 64
    Q, QKV, KV, O, FIRST_O = (0, 64), (0, 192), (64, 128), (192, 64), (0, 64)
    UP, DOWN = (0, 256), (256, 256)

    def pick(call, packed, span, base=0):
        return Weight(call, packed, base + span[0], span[1])

    def forward_mid(call, residual, gain, shift, normed=None):
        vec, res = call.take(vectors), call.fetch(residual)
        kept = call.keep((128, 1024), F32)

        def mid(get, total):
            stream = get(res)[...].astype(F32) + total
            get(kept)[...] = stream
            call.save(get, kept)
            unit, scale = unit_of(stream)
            made = (unit * get(vec)[gain : gain + 1] + get(vec)[shift : shift + 1]).astype(BF16)
            if normed is not None:
                get(normed)[...] = made
                call.save(get, normed)
            return made

        mid.kept = kept
        return mid

    def backward_mid(call, stream, gain, residual=None, dtype=F32):
        vec, kept = call.take(vectors), call.fetch(stream)
        res = None if residual is None else call.fetch(residual)
        grad_out, share_out = call.keep((128, 1024), dtype), call.give((2, 1024), F32)

        def mid(get, total):
            grad, shares = norm_back(get(kept)[...].astype(F32), get(vec)[gain : gain + 1], total)
            if res is not None:
                grad = grad + get(res)[...]
            get(grad_out)[...] = grad.astype(dtype)
            call.save(get, grad_out)
            get(share_out)[...] = shares
            return grad.astype(BF16)

        mid.kept, mid.shares = grad_out, share_out
        return mid

    def deactivated(call, slope):
        out = call.keep((4, 128, 1024), BF16, 4)

        def store(get, at, row, column, value):
            get(out)[row] = (value * get(slope)[row]).astype(BF16)
            call.save(get, out, row)

        return Kept(out, store)

    call = Call()
    slots = Slots(call, [by_owner(source), by_owner(target)], True)
    stream_h, target_h = slots.outs
    norm_parts, norm_own = [call.take(vector) for vector in norms], call.hold((16, 128), F32)
    first_vectors = Vectors(call, norm_own, True)
    fact_ids = [call.take(source_seg), call.take(target_seg)]
    fact_lengths = [call.take(source_len, pltpu.SMEM), call.take(target_len, pltpu.SMEM)]
    fact_own, fact_room = call.hold((2, 8, 128), F32), call.hold((2, 8, 128), F32)
    fact_rows, fact_columns = call.give((8, 1024), F32), call.keep((1024, 128), F32)
    fact_send, fact_recv = call.sems(1), call.sems(1)

    def three(array):
        return [(array, i, True) for i in range(3)]

    pack_1 = Pack(call, three(enc_qkv) + three(dec_qkv))
    pack_o = Pack(call, [(enc_proj, None, False), (dec_proj, None, False)])
    pack_2 = Pack(call, [(enc_up, None, True), (enc_down, None, False)])
    pack_3 = Pack(call, three(cross_qkv) + [(cross_proj, None, False)])
    pack_4 = Pack(call, [(dec_up, None, True), (dec_down, None, False)])
    swap_1, swap_o, swap_2, swap_3, swap_4 = (
        Swap(call, pack.out) for pack in (pack_1, pack_o, pack_2, pack_3, pack_4)
    )
    spread_1, spread_o, spread_2, spread_3, spread_4 = (
        Spread(call, swap.out) for swap in (swap_1, swap_o, swap_2, swap_3, swap_4)
    )

    def count_facts(get):
        own = get(fact_own)
        own[...] = jnp.zeros_like(own)
        lane = lax.broadcasted_iota(jnp.int32, (2, 128), 1)
        for kind in range(2):
            ids, lengths = get(fact_ids[kind])[...], get(fact_lengths[kind])
            table = jnp.zeros((2, 128), F32)
            for p in range(1, PAIRS):
                before = jnp.sum((ids < p).astype(F32), 1, keepdims=True)
                table = table + jnp.where(lane == p, before, 0.0)
            for slot in range(2):
                length = lengths[slot].astype(F32)
                own[slot, kind : kind + 1] = jnp.where(
                    lane[:1] == 0, length, table[slot : slot + 1]
                )

    def place_norms(get, at):
        z, total, row = at["mesh"][4], get(norm_own), 0
        total[...] = jnp.zeros_like(total)
        lane = lax.broadcasted_iota(jnp.int32, (1, 128), 1)
        width = 32 // copies
        for part in norm_parts:
            given = get(part)[...]
            pieces = [given[:, i * width : (i + 1) * width] for i in range(copies) for _ in range(4)]
            wide = jnp.concatenate(pieces, 1)
            total[row : row + given.shape[0]] = jnp.where((lane // width) % 4 == z, wide, 0.0)
            row += given.shape[0]

    def place_facts(get, at):
        hi, k, y, c, z = at["mesh"]
        slot = lax.div(z, 2)
        table = jnp.where(lax.rem(z, 2) == hi, get(fact_own)[slot], get(fact_room)[slot])

        def kinds(index):
            core = jnp.where(index < 512, c, 1 - c)
            part = index % 512
            place = (part // 256) * 512 + core * 256 + ((part // 64) % 2) * 128
            place = (place + ((part // 128) % 2) * 64 + part % 64).astype(F32)
            found = []
            for row in range(2):
                ids = jnp.zeros_like(place)
                for p in range(1, PAIRS):
                    ids = ids + jnp.where(place >= table[row : row + 1, p : p + 1], 1.0, 0.0)
                found.append(ids)
            live = [jnp.where(place < table[row : row + 1, 0:1], 1.0, 0.0) for row in range(2)]
            return found + [place] + live

        across = kinds(lax.broadcasted_iota(jnp.int32, (1, 1024), 1))
        down = kinds(lax.broadcasted_iota(jnp.int32, (1024, 128), 0))
        rows, columns = get(fact_rows), get(fact_columns)
        rows[...] = jnp.zeros_like(rows)
        lane = lax.broadcasted_iota(jnp.int32, (1024, 128), 1)
        wide = jnp.zeros((1024, 128), F32)
        for i in range(5):
            rows[i : i + 1] = across[i]
            wide = jnp.where(lane == i, down[i], wide)
        columns[...] = wide
        call.save(get, fact_columns)

    def first_mid(stream, gain, shift):
        def mid(get, total):
            unit, scale = unit_of(get(stream)[...].astype(F32))
            vec = get(first_vectors.out)
            return (unit * vec[gain : gain + 1] + vec[shift : shift + 1]).astype(BF16)

        return mid

    job_a = Job(call, None, first_mid(stream_h, ENC_G, ENC_B), (None, None, None))
    job_c = Job(call, None, first_mid(target_h, DEC_G, DEC_B), (None, None, None))
    vectors = first_vectors.out

    plans = []
    for rows, base in ((job_a.gathered, 0), (job_c.gathered, SELF)):
        query, shared = Plain(call, 256), Shared(call, 512, 256)
        plans.append((call.fetch(rows), pick(call, spread_1.out, QKV, base), query, shared))
    enc_step = Attend(
        call, plans[0][2].out, plans[0][3].out, fact_rows, fact_columns, (SOURCE, SOURCE, False)
    )
    self_step = Attend(
        call, plans[1][2].out, plans[1][3].out, fact_rows, fact_columns, (TARGET, TARGET, True)
    )
    enc_o, self_o = pick(call, spread_o.out, FIRST_O), pick(call, spread_o.out, FIRST_O, SELF_O)
    mid = forward_mid(call, stream_h, ENC_G + 1, ENC_B + 1)
    job_b = Job(call, (enc_step.mixed, enc_o, [(0, 64)], 0), mid, (None, None, None))
    mid = forward_mid(call, target_h, DEC_G + 1, DEC_B + 1)
    cross_a, cross_b = pick(call, spread_3.out, Q), pick(call, spread_3.out, KV)
    cross_o = pick(call, spread_3.out, O)
    query, shared = Plain(call, 256), Shared(call, 512)
    job_d = Job(call, (self_step.mixed, self_o, [(0, 64)], 0), mid, (cross_a, [(0, 64)], query.store))
    enc_u, enc_d = pick(call, spread_2.out, UP), pick(call, spread_2.out, DOWN)
    feed = Feed(call, job_b.gathered, enc_u, enc_d)
    mid = forward_mid(call, job_b.kept, ENC_G + 2, ENC_B + 2)
    job_m = Job(call, feed, mid, (cross_b, [(0, 64), (64, 64)], shared.store))
    cross_step = Attend(
        call, query.out, shared.out, fact_rows, fact_columns, (TARGET, SOURCE, False)
    )
    mid = forward_mid(call, job_d.kept, DEC_G + 2, DEC_B + 2)
    job_e = Job(call, (cross_step.mixed, cross_o, [(0, 64)], 0), mid, (None, None, None))

    def onward(get, at):
        place_norms(get, at)
        first_vectors.start(get, at)
        slots.start(get, at)
        pack_1.make(get)
        swap_1.start(get, at)
        count_facts(get)
        fact_copy = push(
            get(fact_own), get(fact_room), get(fact_send).at[0], get(fact_recv).at[0], at["x"]
        )
        fact_copy.start()
        first_vectors.second(get, at)
        swap_1.finish(get, at)
        spread_1.launch(get, at)
        for pack in (pack_o, pack_2):
            pack.make(get)
        first_vectors.finish(get, at)
        slots.finish(get, at)
        job_a.settle(get, at)
        job_c.settle(get, at)
        fact_copy.wait()
        place_facts(get, at)
        job_a.rows_forward(get, at)
        job_c.rows_forward(get, at)
        spread_1.relay(get, at)
        swap_o.start(get, at)
        swap_2.start(get, at)
        for pack in (pack_3, pack_4):
            pack.make(get)
        job_a.collect(get, at)
        job_c.collect(get, at)
        enc_step.prepare(get)
        swap_o.finish(get, at)
        swap_2.finish(get, at)
        job_a.drain()
        job_c.drain()
        spread_1.pass_on(get, at)
        spread_o.launch(get, at)
        spread_2.launch(get, at)
        swap_3.start(get, at)
        swap_4.start(get, at)
        spread_1.finish(get, at)
        for plan in plans:
            plan[1].start(get)
        for rows, weight, queries, keys in plans:
            weight.wait(get)
            for row in range(4):
                for m in range(3):
                    made = nt(get(rows)[row], weight.matrix(get, m * 64, 64))
                    (queries if m == 0 else keys).store(get, at, row, m * 256, made)
        for plan in plans:
            plan[3].finish(get)
        spread_o.relay(get, at)
        enc_step.pairs(get, 0, 2)
        call.save(get, enc_step.mixed)
        spread_o.pass_on(get, at)
        swap_3.finish(get, at)
        swap_4.finish(get, at)
        spread_o.finish(get, at)
        enc_o.start(get)
        self_o.start(get)
        job_b.sums(get, at)
        self_step.prepare(get)
        self_step.pairs(get, 0, 1)
        job_b.sum_forward(get, at)
        self_step.pairs(get, 1, 2)
        call.save(get, self_step.mixed)
        job_b.sum_own(get, at)
        job_d.sums(get, at)
        job_b.settle(get, at)
        spread_2.relay(get, at)
        spread_3.launch(get, at)
        job_d.sum_forward(get, at)
        job_d.sum_own(get, at)
        job_b.rows_forward(get, at)
        job_d.settle(get, at)
        spread_2.pass_on(get, at)
        spread_2.finish(get, at)
        enc_u.start(get)
        enc_d.start(get)
        job_b.collect(get, at)
        job_m.sums(get, at)
        job_d.rows_forward(get, at)
        job_m.sum_forward(get, at)
        job_m.sum_own(get, at)
        spread_3.relay(get, at)
        spread_4.launch(get, at)
        job_m.settle(get, at)
        spread_3.pass_on(get, at)
        spread_3.finish(get, at)
        for weight in (cross_a, cross_b, cross_o):
            weight.start(get)
        job_m.rows_forward(get, at)
        job_d.product(get, at, at["own_row"])
        job_d.collect(get, at)
        job_m.product(get, at, at["own_row"])
        job_m.collect(get, at)
        for job in (job_b, job_d, job_m):
            job.drain()
        shared.finish(get)
        cross_step.prepare(get)
        cross_step.pairs(get, 0, 1)
        spread_4.relay(get, at)
        cross_step.pairs(get, 1, 2)
        call.save(get, cross_step.mixed)
        job_e.sums(get, at)
        job_e.sum_forward(get, at)
        job_e.sum_own(get, at)
        job_e.settle(get, at)
        spread_4.pass_on(get, at)
        job_e.rows_forward(get, at)
        job_e.collect(get, at)
        job_e.drain()
        spread_4.finish(get, at)

    (
        stream_in,
        target_in,
        vectors,
        fact_rows,
        fact_columns,
        unused,
        unused,
        unused,
        unused,
        unused,
        first_w,
        first_o,
        second_w,
        cross_w,
        third_w,
        rows_a,
        rows_c,
        enc_q,
        enc_kv,
        self_q,
        self_kv,
        enc_mixed,
        enc_total,
        self_mixed,
        self_total,
        stream_mid,
        rows_b,
        target_mid,
        cross_q,
        cross_kv,
        rows_d,
        enc_hidden,
        enc_slope,
        stream_end,
        memory,
        cross_mixed,
        cross_total,
        target_late,
        rows_e,
    ) = run_body(call, onward, ["all"], "onward", 0, 170 * MICROSECOND)

    call = Call()
    dec_u, dec_d = pick(call, third_w, UP), pick(call, third_w, DOWN)
    cross_o = pick(call, cross_w, O)
    feed = Feed(call, rows_e, dec_u, dec_d)
    slots = Slots(call, [by_owner(cotangent)], True)
    vec, res, cot = call.take(vectors), call.fetch(target_late), slots.outs[0]
    decoded_out, grad_end = call.keep((128, 1024), BF16), call.hold((128, 1024), F32)
    share_out = call.give((2, 1024), F32)

    def last_mid(get, total):
        stream = get(res)[...] + total
        gain, shift = get(vec)[DEC_G + 3 : DEC_G + 4], get(vec)[DEC_B + 3 : DEC_B + 4]
        unit, unused = unit_of(stream)
        get(decoded_out)[...] = (unit * gain + shift).astype(BF16)
        grad, shares = norm_back(stream, gain, get(cot)[...].astype(F32))
        get(grad_end)[...] = grad
        get(share_out)[...] = shares
        call.save(get, decoded_out)
        return grad.astype(BF16)

    active = deactivated(call, feed.slope)
    job_t = Job(call, feed, last_mid, (dec_d, [(0, 256)], active.store))
    mid = backward_mid(call, target_late, DEC_G + 2, grad_end)
    query = Plain(call, 256)
    job_c = Job(call, (active.out, dec_u, [(0, 256)], 0), mid, (cross_o, [(0, 64)], query.store))
    down_shares = Shares(call, [(feed.hidden, 0, job_t.gathered)], 256, False)
    joined = call.give((4, 4, 512, 128), BF16, pltpu.HBM)
    up_shares = Shares(call, [(active.out, 0, feed.rows)], 256, joined, 0)
    back = AttendBack(
        call,
        cross_q,
        cross_kv,
        query.out,
        cross_total,
        fact_rows,
        fact_columns,
        (TARGET, SOURCE, False),
    )
    cross_shares = Shares(
        call,
        [
            (back.out, 0, rows_d),
            (back.out, 256, memory),
            (back.out, 512, memory),
            (cross_mixed, 0, job_c.gathered),
        ],
        64,
        joined,
        256,
    )
    gather = Gather(call, down_shares.room, 256)

    def turning(get, at):
        for weight in (dec_u, dec_d, cross_o):
            weight.start(get)
        slots.start(get, at)
        job_t.sums(get, at)
        job_t.sum_forward(get, at)
        job_t.sum_own(get, at)
        slots.finish(get, at)
        job_t.settle(get, at)
        job_t.product(get, at, at["own_row"])
        job_t.rows_forward(get, at)
        job_t.collect(get, at)
        job_c.sums(get, at)
        job_c.sum_forward(get, at)
        job_c.sum_own(get, at)
        down_shares.middle(get, at)
        down_shares.finish(get, at)
        job_c.settle(get, at)
        gather.launch(get, at)
        job_c.product(get, at, at["own_row"])
        job_c.rows_forward(get, at)
        up_shares.middle(get, at)
        job_c.collect(get, at)
        up_shares.finish(get, at)
        gather.relay(get, at)
        job_t.drain()
        job_c.drain()
        back.late(get, at)
        cross_shares.middle(get, at)
        cross_shares.finish(get, at)
        gather.finish(get, at)

    (
        dec_hidden,
        dec_slope,
        unused,
        decoded,
        norm_3,
        dec_grad_act,
        grad_rows_e,
        grad_late,
        norm_2,
        cross_grad_mixed,
        grad_rows_d,
        joined_s,
        cross_grads,
        down_g,
    ) = run_body(call, turning, ["all"], "turning", 1, 62 * MICROSECOND)

    call = Call()
    cross_a, cross_b = pick(call, cross_w, Q), pick(call, cross_w, KV)
    self_o, enc_d = pick(call, first_o, FIRST_O, SELF_O), pick(call, second_w, DOWN)
    slots = Slots(call, [decoded], False)
    mid = backward_mid(call, target_mid, DEC_G + 1, grad_late)
    query = Plain(call, 256)
    job_t = Job(call, (cross_grads, cross_a, [(0, 64)], 0), mid, (self_o, [(0, 64)], query.store))
    mid = backward_mid(call, stream_end, ENC_G + 2)
    active = deactivated(call, call.fetch(enc_slope))
    job_s = Job(
        call,
        (cross_grads, cross_b, [(0, 64), (64, 64)], 256),
        mid,
        (enc_d, [(0, 256)], active.store),
    )
    shares = Shares(
        call, [(active.out, 0, rows_b), (enc_hidden, 0, job_s.gathered)], 256
    )
    gather, swap = Gather(call, joined_s, 512), Swap(call, down_g)

    def backing(get, at):
        gather.launch(get, at)
        for weight in (cross_b, cross_a, enc_d, self_o):
            weight.start(get)
        job_s.sums(get, at)
        job_t.sums(get, at)
        job_s.sum_forward(get, at)
        job_t.sum_forward(get, at)
        job_s.sum_own(get, at)
        job_s.settle(get, at)
        job_t.sum_own(get, at)
        job_t.settle(get, at)
        slots.start(get, at)
        job_s.product(get, at, at["own_row"])
        job_s.rows_forward(get, at)
        job_t.product(get, at, at["own_row"])
        job_t.rows_forward(get, at)
        swap.start(get, at)
        job_s.collect(get, at)
        gather.relay(get, at)
        shares.middle(get, at)
        job_t.collect(get, at)
        shares.finish(get, at)
        job_s.drain()
        job_t.drain()
        slots.finish(get, at)
        swap.finish(get, at)
        gather.finish(get, at)

    (
        decoded,
        grad_mid,
        norm_1,
        self_grad_mixed,
        grad_rows_c,
        grad_stream,
        enc_norm_2,
        enc_grad_act,
        grad_rows_b,
        feed_s,
        up_cross_g,
        down_g,
    ) = run_body(call, backing, ["x", "y", "core", "d", "ways"], "backing", 2, 46 * MICROSECOND)

    call = Call()
    enc_u, enc_o = pick(call, second_w, UP), pick(call, first_o, FIRST_O)
    self_a = pick(call, first_w, QKV, SELF)
    self_back = AttendBack(
        call,
        self_q,
        self_kv,
        self_grad_mixed,
        self_total,
        fact_rows,
        fact_columns,
        (TARGET, TARGET, True),
    )
    mid = backward_mid(call, stream_mid, ENC_G + 1, grad_stream)
    query = Plain(call, 256)
    job_s = Job(call, (enc_grad_act, enc_u, [(0, 256)], 0), mid, (enc_o, [(0, 64)], query.store))
    mid = backward_mid(call, target_in, DEC_G, grad_mid, BF16)
    job_t = Job(call, (self_back.out, self_a, [(0, 64), (64, 64), (128, 64)], 0), mid, None)
    self_shares = Shares(
        call,
        [
            (self_back.out, 0, rows_c),
            (self_back.out, 256, rows_c),
            (self_back.out, 512, rows_c),
            (self_mixed, 0, grad_rows_c),
        ],
        64,
        False,
    )
    enc_back = AttendBack(
        call,
        enc_q,
        enc_kv,
        query.out,
        enc_total,
        fact_rows,
        fact_columns,
        (SOURCE, SOURCE, False),
    )
    enc_shares = Shares(
        call,
        [
            (enc_back.out, 0, rows_a),
            (enc_back.out, 256, rows_a),
            (enc_back.out, 512, rows_a),
            (enc_mixed, 0, job_s.gathered),
        ],
        64,
        False,
    )
    enc_a = pick(call, first_w, QKV)
    mid = backward_mid(call, stream_in, ENC_G, job_s.kept, BF16)
    job_f = Job(call, (enc_back.out, enc_a, [(0, 64), (64, 64), (128, 64)], 0), mid, None)
    gather_f, gather_s = Gather(call, feed_s, 512), Gather(call, self_shares.room, 256)
    gather_e = Gather(call, enc_shares.room, 256)
    for gather, rows in ((gather_f, 512), (gather_s, 256), (gather_e, 256)):
        call.rows_of[gather.out] = rows
    swap, swap_f = Swap(call, up_cross_g), Swap(call, gather_f.out)
    swap_s, swap_e = Swap(call, gather_s.out), Swap(call, gather_e.out)
    target_slots, source_slots = Slots(call, [job_t.kept], False), Slots(call, [job_f.kept], False)
    others = [call.take(norm) for norm in (norm_1, norm_2, norm_3, enc_norm_2)]
    norm_sum = call.hold((16, 1024), F32)
    sums = Vectors(call, norm_sum, False)

    def selfward(get, at):
        gather_f.launch(get, at)
        for weight in (enc_u, self_a, enc_o, enc_a):
            weight.start(get)
        self_back.prepare(get)
        job_s.sums(get, at)
        self_back.pair(get, at, 0)
        job_s.sum_forward(get, at)
        self_back.pair(get, at, 1)
        self_back.end(get)
        job_s.sum_own(get, at)
        job_t.sums(get, at)
        job_s.settle(get, at)
        job_t.sum_forward(get, at)
        job_t.sum_own(get, at)
        self_shares.middle(get, at)
        self_shares.finish(get, at)
        gather_s.launch(get, at)
        job_s.product(get, at, at["own_row"])
        job_s.rows_forward(get, at)
        job_t.settle(get, at)
        gather_f.relay(get, at)
        target_slots.start(get, at)
        swap.start(get, at)
        job_s.collect(get, at)
        job_s.drain()
        job_t.drain()
        enc_back.late(get, at)
        enc_shares.middle(get, at)
        enc_shares.finish(get, at)
        gather_e.launch(get, at)
        gather_s.relay(get, at)
        job_f.sums(get, at)
        job_f.sum_forward(get, at)
        job_f.sum_own(get, at)
        job_f.settle(get, at)
        gather_e.relay(get, at)
        source_slots.start(get, at)
        total = get(norm_sum)
        for row, shares in (
            (0, get(job_f.shares)),
            (1, get(job_s.shares)),
            (2, get(others[3])),
            (6, get(job_t.shares)),
            (7, get(others[0])),
            (8, get(others[1])),
            (9, get(others[2])),
        ):
            below = row + (3 if row < 6 else 4)
            total[row : row + 1] = shares[0:1]
            total[below : below + 1] = shares[1:2]
        total[14:16] = jnp.zeros((2, 1024), F32)
        sums.start(get, at)
        job_f.drain()
        gather_f.finish(get, at)
        swap_f.start(get, at)
        sums.second(get, at)
        target_slots.finish(get, at)
        gather_s.finish(get, at)
        swap_s.start(get, at)
        sums.finish(get, at)
        source_slots.finish(get, at)
        swap.finish(get, at)
        swap_f.finish(get, at)
        gather_e.finish(get, at)
        swap_e.start(get, at)
        swap_s.finish(get, at)
        swap_e.finish(get, at)

    made = run_body(call, selfward, ["all"], "selfward", 3, 105 * MICROSECOND)
    up_cross_g, feed_g, self_g, enc_g, target_grad, source_grad, norm_grad = made[-7:]
    norm_grad = norm_grad.reshape(16, copies, 4, 32 // copies)
    if copies > 1:
        norm_grad = lax.psum_scatter(norm_grad, "k", scatter_dimension=1)
    norm_grad = norm_grad.reshape(16, 4, -1)
    norm_grad = lax.dynamic_index_in_dim(norm_grad, z, 1, False)

    (
        dec_d,
        dec_u,
        cross_a,
        cross_o,
        enc_u,
        enc_d,
        self_a,
        self_o,
        enc_a,
        enc_o,
        source_grad,
        target_grad,
    ) = unpacked(
        [down_g, up_cross_g, feed_g, self_g, enc_g],
        [source_grad, target_grad],
        [("down",), ("up", "q", "o"), ("up", "down"), ("q", "o"), ("q", "o")],
    )

    def narrow(array, axis):
        if copies == 1:
            return array
        return lax.psum_scatter(array, "k", scatter_dimension=axis, tiled=True)

    enc_a, self_a, cross_a = (narrow(array, 1) for array in (enc_a, self_a, cross_a))
    enc_o, self_o, cross_o = (narrow(array, 1) for array in (enc_o, self_o, cross_o))
    enc_u, dec_u = narrow(enc_u, 0), narrow(dec_u, 0)
    enc_d, dec_d = narrow(enc_d, 1), narrow(dec_d, 1)
    return (
        by_owner(decoded, True),
        by_owner(source_grad, True),
        by_owner(target_grad, True),
        enc_a,
        enc_o,
        enc_u,
        enc_d,
        norm_grad[:3],
        norm_grad[3:6],
        self_a,
        self_o,
        cross_a,
        cross_o,
        dec_u,
        dec_d,
        norm_grad[6:10],
        norm_grad[10:14],
    )


def solution(mesh):
    dp, seq, mp = (mesh.shape[name] for name in ("dp", "seq", "mp"))
    assert dp % 2 == 0 and seq == 4 and mp == 4
    fine = Mesh(mesh.devices.reshape(2, dp // 2, 2, 2, 4), AXES)
    d, s = ("hi", "k"), ("y", "c")
    rows = P(d, s + ("mp",), None)
    three, flat = P(None, d + s, "mp"), P("mp", d + s)
    up, vector = P(d + s, "mp"), P(None, d + s + ("mp",))
    attention, feeding = (three, flat), (up, flat)
    return jax.shard_map(
        local,
        mesh=fine,
        in_specs=(rows,) * 3
        + (P(d), P(d), P(d, None), P(d, None))
        + attention
        + feeding
        + (vector, vector)
        + attention * 2
        + feeding
        + (vector, vector),
        out_specs=(rows,) * 3
        + attention
        + feeding
        + (vector, vector)
        + attention * 2
        + feeding
        + (vector, vector),
        check_vma=False,
    )
```

```python
import math

import jax
import jax.numpy as jnp
from jax import lax
from jax.experimental import pallas as pl
from jax.experimental.pallas import tpu as pltpu
from jax.sharding import Mesh, PartitionSpec as P

HEAD_DIM = 64
EPSILON = 1e-05
MASKED = -1000000000.0
PAIRS = 8
AXES = ("hi", "k", "y", "c", "mp")
MESH_ID = pl.DeviceIdType.MESH
F32 = jnp.float32
BF16 = jnp.bfloat16


class Call:
    def __init__(self):
        self.known, self.arrays, self.specs = [], [], []
        self.shapes, self.places, self.scratch = [], [], []
        self.fetched, self.kept, self.rows_of = [], [], {}

    def take(self, array, space=pltpu.VMEM):
        if isinstance(array, tuple):
            return array
        for i, known in enumerate(self.known):
            if known is array and self.specs[i].memory_space == space:
                return ("in", i)
        self.known.append(array)
        if space == pltpu.HBM:
            array = pltpu.with_memory_space_constraint(array, pltpu.HBM)
        self.arrays.append(array)
        self.specs.append(pl.BlockSpec(memory_space=space))
        return ("in", len(self.arrays) - 1)

    def fetch(self, array):
        if isinstance(array, tuple):
            return array
        source = self.take(array, pltpu.HBM)
        for i, (known, room, sem) in enumerate(self.fetched):
            if known == source:
                return ("fetch", i)
        self.fetched.append((source, self.hold(array.shape, array.dtype), self.sems(1)))
        return ("fetch", len(self.fetched) - 1)

    def give(self, shape, dtype, space=pltpu.VMEM):
        if space == pltpu.HBM:
            self.shapes.append(pltpu.HBM(shape, dtype))
        else:
            self.shapes.append(jax.ShapeDtypeStruct(shape, dtype))
        self.places.append(pl.BlockSpec(memory_space=space))
        return ("out", len(self.shapes) - 1)

    def keep(self, shape, dtype, parts=1):
        target = self.give(shape, dtype, pltpu.HBM)
        self.kept.append((target, self.hold(shape, dtype), self.sems(parts)))
        return ("keep", len(self.kept) - 1)

    def hold(self, shape, dtype):
        self.scratch.append(pltpu.VMEM(shape, dtype))
        return ("tmp", len(self.scratch) - 1)

    def sems(self, count):
        self.scratch.append(pltpu.SemaphoreType.DMA((count,)))
        return ("tmp", len(self.scratch) - 1)

    def save(self, get, handle, row=None):
        target, room, sems = (get(part) for part in self.kept[handle[1]])
        if row is not None:
            target, room = target.at[row], room.at[row]
        count = sum(1 for known, unused in self.saves if known == handle)
        copy = pltpu.make_async_copy(room, target, sems.at[count])
        copy.start()
        self.saves.append((handle, copy))

    def run(self, body, name, collective=None, flops=0):
        ins, outs = len(self.arrays), len(self.shapes)

        def kernel(*refs):
            parts = {"in": refs[:ins], "out": refs[ins : ins + outs], "tmp": refs[ins + outs :]}
            here, self.saves, self.waited = set(), [], []

            def get(handle):
                kind, i = handle
                if kind == "keep":
                    return get(self.kept[i][1])
                if kind != "fetch":
                    return parts[kind][i]
                source, room, sem = (get(part) for part in self.fetched[i])
                if i not in here:
                    here.add(i)
                    pltpu.make_async_copy(source, room, sem.at[0]).wait()
                return room

            for source, room, sem in self.fetched:
                pltpu.make_async_copy(get(source), get(room), get(sem).at[0]).start()
            body(get)
            for i in range(len(self.fetched)):
                get(("fetch", i))
            for handle, copy in self.saves:
                copy.wait()

        held = [a for a, spec in zip(self.arrays, self.specs) if spec.memory_space == pltpu.VMEM]
        held += [a for a, spec in zip(self.shapes, self.places) if spec.memory_space == pltpu.VMEM]
        held += [x for x in self.scratch if x.dtype in (BF16, F32)]
        room = sum(math.prod(x.shape) * jnp.dtype(x.dtype).itemsize for x in held)
        return pl.pallas_call(
            kernel,
            out_shape=tuple(self.shapes),
            in_specs=self.specs,
            out_specs=tuple(self.places),
            scratch_shapes=self.scratch,
            compiler_params=pltpu.CompilerParams(
                collective_id=collective,
                has_side_effects=collective is not None,
                vmem_limit_bytes=room + (8 << 20),
            ),
            cost_estimate=pl.CostEstimate(flops=flops, bytes_accessed=0, transcendentals=0),
            name=name,
        )(*self.arrays)


MICROSECOND = 1_000_000_000


def nt(left, right):
    return lax.dot_general(left, right, (((1,), (1,)), ((), ())), preferred_element_type=F32)


def nn(left, right):
    return lax.dot_general(left, right, (((1,), (0,)), ((), ())), preferred_element_type=F32)


def tn(left, right):
    return lax.dot_general(left, right, (((0,), (0,)), ((), ())), preferred_element_type=F32)


def unit_of(stream):
    average = jnp.mean(stream, -1, keepdims=True)
    centred = stream - average
    scale = lax.rsqrt(jnp.mean(centred * centred, -1, keepdims=True) + EPSILON)
    return centred * scale, scale


def norm_back(stream, gain, upstream):
    unit, scale = unit_of(stream)
    inner = upstream * gain
    grad = scale * (
        inner - jnp.mean(inner, -1, keepdims=True) - unit * jnp.mean(inner * unit, -1, keepdims=True)
    )
    shares = jnp.concatenate(
        [jnp.sum(upstream * unit, 0, keepdims=True), jnp.sum(upstream, 0, keepdims=True)], 0
    )
    return grad, shares


def gelu_pair(act):
    bell = 0.5 + 0.5 * lax.erf(act * 0.7071067811865476)
    slope = bell + act * (jnp.exp(act * act * -0.5) * 0.3989422804014327)
    return act * bell, slope


def place():
    hi, k, y, c, z = (lax.axis_index(name) for name in AXES)
    return {
        "x": (1 - hi, k, y, c, z),
        "y": (hi, k, 1 - y, c, z),
        "d": (1 - hi, k, 1 - y, c, z),
        "core": (hi, k, y, 1 - c, z),
        "mesh": (hi, k, y, c, z),
        "own_row": y * 2 + hi,
        "x_row": y * 2 + 1 - hi,
        "y_row": (1 - y) * 2 + hi,
        "d_row": (1 - y) * 2 + 1 - hi,
    }


def greet(partners):
    barrier = pltpu.get_barrier_semaphore()
    for partner in partners:
        pl.semaphore_signal(barrier, inc=1, device_id=partner, device_id_type=MESH_ID)
    pl.semaphore_wait(barrier, len(partners))


def along(at):
    hi, k, y, c, z = at["mesh"]
    return [(hi, k, y, c, lax.rem(z + n, 4)) for n in range(1, 4)]


class Weight:
    def __init__(self, call, packed, first, count):
        self.call, self.source = call, call.take(packed, pltpu.HBM)
        self.room = call.hold((4, count, 1024), BF16)
        self.sem = call.sems(1)
        self.first, self.count = first, count

    def start(self, get):
        source, room, sem = get(self.source), get(self.room), get(self.sem)
        for q in range(4):
            for c in range(2):
                pltpu.make_async_copy(
                    source.at[c, :, q, pl.ds(self.first, self.count), :],
                    room.at[:, :, pl.ds((q * 2 + c) * 128, 128)],
                    sem.at[0],
                ).start()

    def wait(self, get):
        if self in self.call.waited:
            return
        self.call.waited.append(self)
        room = get(self.room)
        pltpu.make_async_copy(room, room, get(self.sem).at[0]).wait()

    def matrix(self, get, first, count):
        return get(self.room)[:, first : first + count, :].reshape(4 * count, 1024)


def stack(blocks):
    return blocks[0] if len(blocks) == 1 else jnp.concatenate(blocks, 0)


class Feed:
    def __init__(self, call, rows, up, down):
        self.call, self.rows, self.weights = call, call.fetch(rows), [up, down]
        self.hidden = call.keep((4, 128, 1024), BF16, 4)
        self.slope = call.keep((4, 128, 1024), F32, 4)

    def part(self, get, *rows):
        up, down = self.weights
        whole = stack([get(self.rows)[row] for row in rows])
        made, slope = gelu_pair(nt(whole, up.matrix(get, 0, 256)))
        made = made.astype(BF16)
        for i, row in enumerate(rows):
            get(self.hidden)[row] = made[i * 128 : (i + 1) * 128]
            get(self.slope)[row] = slope[i * 128 : (i + 1) * 128]
            self.call.save(get, self.hidden, row)
            self.call.save(get, self.slope, row)
        return nn(made, down.matrix(get, 0, 256))


class Job:
    def __init__(self, call, left, mid, right):
        self.call, self.left, self.mid, self.right = call, left, mid, right
        self.kept, self.shares = getattr(mid, "kept", None), getattr(mid, "shares", None)
        if left is not None:
            self.rows_in = None if isinstance(left, Feed) else call.fetch(left[0])
            self.out_first = call.hold((2, 128, 1024), BF16)
            self.out_edge = call.hold((2, 64, 1024), BF16)
            self.out_late = call.hold((2, 64, 1024), BF16)
            self.keep = call.hold((2, 64, 1024), F32)
            self.own = call.hold((128, 1024), F32)
            self.landed = call.hold((6, 64, 1024), BF16)
            self.sum_send, self.sum_recv = call.sems(6), call.sems(6)
        self.gathered = None
        if right is not None:
            self.gathered = call.keep((4, 128, 1024), BF16, 4)
            self.row_send, self.row_recv = call.sems(6), call.sems(6)

    def lefts(self):
        return self.left.weights if isinstance(self.left, Feed) else [self.left[1]]

    def part(self, get, *rows):
        if isinstance(self.left, Feed):
            return self.left.part(get, *rows)
        unused, weight, picks, column = self.left
        total = None
        for first, count in picks:
            width = 4 * count
            left = stack([get(self.rows_in)[row, :, column : column + width] for row in rows])
            term = nn(left, weight.matrix(get, first, count))
            total = term if total is None else total + term
            column += width
        return total

    def send(self, get, i, source, target, partner):
        copy = pltpu.make_async_remote_copy(
            src_ref=source,
            dst_ref=target,
            send_sem=get(self.sum_send).at[i],
            recv_sem=get(self.sum_recv).at[i],
            device_id=partner,
            device_id_type=MESH_ID,
        )
        copy.start()
        return copy

    def sum_start(self, get, at):
        first, edge, landed = get(self.out_first), get(self.out_edge), get(self.landed)
        keep = get(self.keep)
        self.copies = [None] * 6
        first[0] = self.part(get, at["d_row"]).astype(BF16)
        self.copies[0] = self.send(
            get, 0, first.at[0, pl.ds(0, 64)], landed.at[0], at["x"]
        )
        self.copies[1] = self.send(
            get, 1, first.at[0, pl.ds(64, 64)], landed.at[1], at["y"]
        )
        part = self.part(get, at["x_row"], at["y_row"])
        edge[0] = part[:64].astype(BF16)
        keep[0] = part[64:128]
        self.copies[2] = self.send(get, 2, edge.at[0], landed.at[2], at["x"])
        edge[1] = part[192:].astype(BF16)
        keep[1] = part[128:192]
        self.copies[3] = self.send(get, 3, edge.at[1], landed.at[3], at["y"])

    def sum_forward(self, get, at):
        late, landed, keep = get(self.out_late), get(self.landed), get(self.keep)
        self.copies[0].wait_recv()
        late[1] = (keep[1] + landed[0].astype(F32)).astype(BF16)
        self.copies[4] = self.send(get, 4, late.at[1], landed.at[4], at["y"])
        self.copies[1].wait_recv()
        late[0] = (keep[0] + landed[1].astype(F32)).astype(BF16)
        self.copies[5] = self.send(get, 5, late.at[0], landed.at[5], at["x"])

    def sum_own(self, get, at):
        get(self.own)[...] = self.part(get, at["own_row"])

    def sum_end(self, get):
        landed, own = get(self.landed), get(self.own)
        for i in (2, 3, 4, 5):
            self.copies[i].wait_recv()
        upper = own[:64] + landed[2].astype(F32) + landed[4].astype(F32)
        lower = own[64:] + landed[5].astype(F32) + landed[3].astype(F32)
        return jnp.concatenate([upper, lower], 0)

    def row_copy(self, get, i, row, half, partner):
        block = get(self.gathered).at[row, pl.ds(half * 64, 64)]
        copy = pltpu.make_async_remote_copy(
            src_ref=block,
            dst_ref=block,
            send_sem=get(self.row_send).at[i],
            recv_sem=get(self.row_recv).at[i],
            device_id=partner,
            device_id_type=MESH_ID,
        )
        copy.start()
        return copy

    def rows_start(self, get, at, normed):
        get(self.gathered)[at["own_row"]] = normed
        self.call.save(get, self.gathered, at["own_row"])
        self.moves = [
            self.row_copy(get, 0, at["own_row"], 0, at["y"]),
            self.row_copy(get, 1, at["own_row"], 1, at["x"]),
            self.row_copy(get, 2, at["own_row"], 1, at["y"]),
            self.row_copy(get, 3, at["own_row"], 0, at["x"]),
        ]

    def rows_forward(self, get, at):
        self.moves[0].wait_recv()
        self.moves.append(self.row_copy(get, 4, at["y_row"], 0, at["x"]))
        self.moves[1].wait_recv()
        self.moves.append(self.row_copy(get, 5, at["x_row"], 1, at["y"]))

    def product(self, get, at, row):
        weight, picks, store = self.right
        if weight is None:
            return
        weight.wait(get)
        rows = get(self.gathered)[row]
        column = 0
        for first, count in picks:
            store(get, at, row, column, nt(rows, weight.matrix(get, first, count)))
            column += 4 * count

    def sums(self, get, at):
        for weight in self.lefts():
            weight.wait(get)
        self.sum_start(get, at)

    def settle(self, get, at):
        normed = self.mid(get, self.sum_end(get) if self.left is not None else None)
        if self.right is not None:
            self.rows_start(get, at, normed)

    def collect(self, get, at, sides=True, far=True):
        for moves, row in (((3,), "x_row"), ((2,), "y_row"), ((4, 5), "d_row")):
            if far if row == "d_row" else sides:
                for i in moves:
                    self.moves[i].wait_recv()
                self.call.save(get, self.gathered, at[row])
                self.product(get, at, at[row])

    def drain(self):
        if self.left is not None:
            for copy in self.copies:
                copy.wait_send()
        if self.right is not None:
            for copy in self.moves:
                copy.wait_send()


def run_body(call, work, names, name, collective, flops):
    groups = {"all": meeting, "z": along, "ways": lambda at: all_partners(at)[1]}

    def body(get):
        at = place()
        partners = []
        for group in names:
            partners += groups[group](at) if group in groups else [at[group]]
        greet(partners)
        work(get, at)

    return call.run(body, name, collective, flops)


class Kept:
    def __init__(self, out, store):
        self.out, self.store = out, store


class Plain:
    def __init__(self, call, width):
        self.call, self.width = call, width
        self.out = call.keep((4, 128, width), BF16, 4)

    def store(self, get, at, row, column, value):
        get(self.out)[row, :, column : column + value.shape[1]] = value.astype(BF16)
        if column + value.shape[1] == self.width:
            self.call.save(get, self.out, row)


class Shared:
    def __init__(self, call, width, skip=0):
        self.call, self.out = call, call.keep((2, 4, 128, width), BF16, 2)
        self.send_sem, self.recv_sem = call.sems(4), call.sems(4)
        self.width, self.skip, self.copies, self.blocks = width, skip, [], 0

    def store(self, get, at, row, column, value):
        out = get(self.out)
        column = column - self.skip
        out[0, row, :, column : column + value.shape[1]] = value.astype(BF16)
        if column + value.shape[1] == self.width:
            i = len(self.copies)
            copy = pltpu.make_async_remote_copy(
                src_ref=out.at[0, row],
                dst_ref=out.at[1, row],
                send_sem=get(self.send_sem).at[i],
                recv_sem=get(self.recv_sem).at[i],
                device_id=at["core"],
                device_id_type=MESH_ID,
            )
            copy.start()
            self.copies.append(copy)

    def finish(self, get):
        self.call.save(get, self.out, 0)
        for copy in self.copies:
            copy.wait()
        self.call.save(get, self.out, 1)


def query_and_shared(call, width):
    query, shared = Plain(call, width), Shared(call, 2 * width, skip=width)

    def store(get, at, row, column, value):
        if column < width:
            query.store(get, at, row, column, value)
        else:
            shared.store(get, at, row, column, value)

    return store, shared.finish


def lanes_of(head, rows):
    lane = lax.broadcasted_iota(jnp.int32, (rows, 128), 1)
    return lane // HEAD_DIM == head


SOURCE, TARGET, PLACE, LIVE = 0, 1, 2, 3


def allowed_bias(rows, columns, query_kind, key_kind, causal):
    allowed = columns[:, key_kind : key_kind + 1] == rows[query_kind : query_kind + 1, :512]
    allowed = allowed & (columns[:, LIVE + key_kind : LIVE + key_kind + 1] > 0.5)
    if causal:
        allowed = allowed & (columns[:, PLACE : PLACE + 1] <= rows[PLACE : PLACE + 1, :512])
    return jnp.where(allowed, 0.0, MASKED)


def masked(mask, span, count):
    if count == 4:
        return mask[:, span]
    return jnp.concatenate([mask[: count * 128, span], mask[512 : 512 + count * 128, span]], 0)


class Attend:
    def __init__(self, call, queries, key_value, rows, columns, kinds):
        self.call, self.kinds = call, kinds
        self.queries, self.key_value = call.fetch(queries), call.fetch(key_value)
        self.rows, self.columns = call.fetch(rows), call.fetch(columns)
        self.mixed = call.keep((4, 128, 256), BF16)
        self.total = call.keep((8, 512), F32)
        self.bias = call.hold((1024, 512), F32)

    def late(self, get, at):
        self.prepare(get)
        self.pairs(get, 0, 2)
        self.save(get)

    def save(self, get):
        self.call.save(get, self.mixed)
        self.call.save(get, self.total)

    def visible(self, block):
        return 2 if self.kinds[2] and block == 0 else 4

    def prepare(self, get):
        mask, total = get(self.bias), get(self.total)
        total[4:8] = jnp.zeros((4, 512), F32)
        mask[...] = allowed_bias(get(self.rows), get(self.columns), *self.kinds)

    def pairs(self, get, first, last):
        mask = get(self.bias)
        q_ref, kv_ref = get(self.queries), get(self.key_value)
        mixed_ref, total_ref = get(self.mixed), get(self.total)

        def pair_step(pair, carry):
            lanes = pl.ds(pl.multiple_of(pair * 128, 128), 128)
            value_lanes = pl.ds(pl.multiple_of(256 + pair * 128, 128), 128)
            for block in range(2):
                count = self.visible(block)
                keys = kv_ref[:, :count, :, lanes].reshape(count * 256, 128)
                values = kv_ref[:, :count, :, value_lanes].reshape(count * 256, 128)
                span = slice(block * 256, block * 256 + 256)
                queries = q_ref[2 * block : 2 * block + 2, :, lanes].reshape(256, 128)
                mixed = []
                for head in range(2):
                    picked = jnp.where(lanes_of(head, 256), queries * 0.125, 0.0).astype(BF16)
                    scores = nt(keys, picked) + masked(mask, span, count)
                    top = jnp.max(scores, 0, keepdims=True)
                    raised = jnp.exp(scores - top)
                    total = jnp.sum(raised, 0, keepdims=True)
                    probs = (raised * (1.0 / total)).astype(BF16)
                    mixed.append(tn(values, probs)[head * HEAD_DIM : (head + 1) * HEAD_DIM])
                    total_ref[pl.ds(pair * 2 + head, 1), span] = top + jnp.log(total)
                mixed = jnp.concatenate(mixed, 0).T.astype(BF16)
                mixed_ref[2 * block : 2 * block + 2, :, lanes] = mixed.reshape(2, 128, 128)
            return carry

        lax.fori_loop(first, last, pair_step, 0)


class AttendBack:
    def __init__(self, call, queries, key_value, grad_mixed, total, rows, columns, kinds):
        self.call, self.kinds = call, kinds
        self.queries, self.key_value = call.fetch(queries), call.fetch(key_value)
        self.grad_mixed, self.total = call.fetch(grad_mixed), call.fetch(total)
        self.rows, self.columns = call.fetch(rows), call.fetch(columns)
        self.out = call.keep((4, 128, 768), BF16)
        self.bias, self.sums = call.hold((1024, 512), F32), call.hold((1024, 512), F32)
        self.away, self.landed = call.hold((2, 512, 256), BF16), call.hold((2, 512, 256), BF16)
        self.send_sem, self.recv_sem = call.sems(2), call.sems(2)

    def partners(self, at):
        return [at["core"]]

    def late(self, get, at):
        self.prepare(get)
        for pair in range(2):
            self.pair(get, at, pair)
        self.end(get)

    def prepare(self, get):
        mask = get(self.bias)
        mask[...] = allowed_bias(get(self.rows), get(self.columns), *self.kinds)
        self.copies = []

    def pair(self, get, at, pair):
        out, mask, sums = get(self.out), get(self.bias), get(self.sums)
        away, here = get(self.away), get(self.landed)
        q_ref, kv_ref = get(self.queries), get(self.key_value)
        grad_ref, total_ref = get(self.grad_mixed), get(self.total)
        lanes = slice(pair * 128, pair * 128 + 128)
        key_sum = slice(pair * 256, pair * 256 + 128)
        value_sum = slice(pair * 256 + 128, pair * 256 + 256)
        for block in (1, 0):
            count = 2 if self.kinds[2] and block == 0 else 4
            keys_pair = kv_ref[:, :count, :, lanes].reshape(count * 256, 128)
            values_pair = kv_ref[:, :count, :, 256 + pair * 128 : 384 + pair * 128]
            values_pair = values_pair.reshape(count * 256, 128)
            span = slice(block * 256, block * 256 + 256)
            two = slice(2 * block, 2 * block + 2)
            q_block = q_ref[two, :, lanes].reshape(256, 128)
            g_block = grad_ref[two, :, lanes].reshape(256, 128)
            grad_query = []
            for head in range(2):
                inside = lanes_of(head, 256)
                picked = jnp.where(inside, q_block * 1.0, 0.0).astype(BF16)
                grads = jnp.where(inside, g_block * 1.0, 0.0).astype(BF16)
                scores = nt(keys_pair, picked) * 0.125 + masked(mask, span, count)
                probs = jnp.exp(scores - total_ref[pair * 2 + head : pair * 2 + head + 1, span])
                weighted = probs * nt(values_pair, grads)
                inner = jnp.sum(weighted, 0, keepdims=True)
                grad_raw = ((weighted - probs * inner) * 0.125).astype(BF16)
                value_term = nn(probs.astype(BF16), grads)
                key_term = nn(grad_raw, picked)
                if block == 1 and head == 0:
                    sums[:, key_sum] = key_term
                    sums[:, value_sum] = value_term
                else:
                    for half in range(2 if count < 4 else 1):
                        size = count * 128 if count < 4 else 1024
                        rows = slice(half * 512, half * 512 + size)
                        terms = slice(half * size, half * size + size)
                        sums[rows, key_sum] += key_term[terms]
                        sums[rows, value_sum] += value_term[terms]
                grad_query.append(tn(keys_pair, grad_raw)[head * HEAD_DIM : (head + 1) * HEAD_DIM])
            grad_query = jnp.concatenate(grad_query, 0).T.astype(BF16)
            out[two, :, lanes] = grad_query.reshape(2, 128, 128)
        away[pair] = sums[512:, pair * 256 : pair * 256 + 256].astype(BF16)
        copy = pltpu.make_async_remote_copy(
            src_ref=away.at[pair],
            dst_ref=here.at[pair],
            send_sem=get(self.send_sem).at[pair],
            recv_sem=get(self.recv_sem).at[pair],
            device_id=at["core"],
            device_id_type=MESH_ID,
        )
        copy.start()
        self.copies.append(copy)

    def end(self, get):
        out, sums, here = get(self.out), get(self.sums), get(self.landed)
        for pair in range(2):
            self.copies[pair].wait()
            both = sums[:512, pair * 256 : pair * 256 + 256] + here[pair].astype(F32)
            both = both.astype(BF16).reshape(4, 128, 256)
            out[:, :, 256 + pair * 128 : 384 + pair * 128] = both[:, :, :128]
            out[:, :, 512 + pair * 128 : 640 + pair * 128] = both[:, :, 128:]
        self.call.save(get, self.out)


class Shares:
    def __init__(self, call, pairs, count, out=None, base=0):
        self.call, self.count, self.base = call, count, base
        self.handles = [
            (call.fetch(left), column, call.fetch(right))
            for left, column, right in pairs
        ]
        shape = (4, 4, len(pairs) * count, 128)
        sends = len(pairs) * max(1, count // 64)
        self.made, self.landed = call.hold((2,) + shape, BF16), call.hold(shape, BF16)
        self.send_sem, self.recv_sem = call.sems(sends), call.sems(sends)
        self.rows = shape[2]
        self.out = call.give(shape, BF16, pltpu.HBM) if out is None else out
        self.saved = out is not False
        self.room, self.save_sem = call.hold(shape, BF16), call.sems(1)

    def partners(self, at):
        return [at["core"]]

    def send(self, get, at, part):
        i = len(self.copies)
        copy = pltpu.make_async_remote_copy(
            src_ref=get(self.made).at[(1 - lax.axis_index("c"),) + part],
            dst_ref=get(self.landed).at[part],
            send_sem=get(self.send_sem).at[i],
            recv_sem=get(self.recv_sem).at[i],
            device_id=at["core"],
            device_id_type=MESH_ID,
        )
        copy.start()
        self.copies.append((part, copy))

    def middle(self, get, at):
        self.copies, every, count = [], slice(None), self.count
        made = get(self.made)
        for m, (left, column, right) in enumerate(self.handles):
            left, right = get(left), get(right)
            span = slice(m * count, (m + 1) * count)
            for first in range(0, 4 * count, 256):
                start = column + first
                product = tn(
                    left[:, :, start : start + 256].reshape(512, 256), right[...].reshape(512, 1024)
                )
                for inner in range(0, 256, count):
                    z = (first + inner) // count
                    for d in range(8):
                        made[d % 2, z, d // 2, span, :] = product[
                            inner : inner + count, d * 128 : d * 128 + 128
                        ].astype(BF16)
                if count == 256:
                    self.send(get, at, (first // 256, every, pl.ds(m * count, count)))
            if count < 256:
                self.send(get, at, (every, every, pl.ds(m * count, count)))

    def finish(self, get, at):
        core = lax.axis_index("c")
        for part, copy in self.copies:
            copy.wait()
            own = get(self.made)[(core,) + part].astype(F32)
            get(self.room)[part] = (own + get(self.landed)[part].astype(F32)).astype(BF16)
        if not self.saved:
            return
        target = get(self.out).at[:, :, pl.ds(self.base, self.rows)]
        copy = pltpu.make_async_copy(get(self.room), target, get(self.save_sem).at[0])
        copy.start()
        self.call.saves.append((None, copy))


def push(source, target, send_sem, recv_sem, partner):
    return pltpu.make_async_remote_copy(
        src_ref=source,
        dst_ref=target,
        send_sem=send_sem,
        recv_sem=recv_sem,
        device_id=partner,
        device_id_type=MESH_ID,
    )


class Spread:
    def __init__(self, call, pack):
        rows = pack.shape if not isinstance(pack, tuple) else (4, call.rows_of[pack], 128)
        self.pack = call.take(pack, pltpu.HBM)
        self.out = call.give((2, 4) + tuple(rows), BF16, pltpu.HBM)
        self.send_sem, self.recv_sem = call.sems(5), call.sems(5)
        self.core_send, self.core_recv, self.own_sem = call.sems(6), call.sems(6), call.sems(1)

    def block(self, get, at, origin):
        return get(self.out).at[at["mesh"][3], origin]

    def move(self, get, at, way):
        hi, k, y, c, z = at["mesh"]
        step = {0: 1, 1: -1, 2: 2, 3: -2, 4: jnp.where(z == 2, 1, -1)}[way]
        origin = jnp.where(z == 2, 0, 3) if way == 4 else z
        target = self.block(get, at, origin)
        return push(
            target if way == 4 else get(self.pack),
            target,
            get(self.send_sem).at[way],
            get(self.recv_sem).at[way],
            (hi, k, y, c, lax.rem(z + step + 4, 4)),
        )

    def sends(self, at, way):
        z = at["mesh"][4]
        middle = (z == 1) | (z == 2)
        return {0: z < 3, 1: z > 0, 2: z < 2, 3: z > 1, 4: middle}[way]

    def comes(self, at, way):
        z = at["mesh"][4]
        return {0: z > 0, 1: z < 3, 2: z > 1, 3: z < 2, 4: (z == 0) | (z == 3)}[way]

    def to_core(self, get, at, way):
        z = at["mesh"][4]
        origin = {0: z - 1, 1: z + 1, 2: z - 2, 3: z + 2, 4: 3 - z, 5: z}[way]
        target = self.block(get, at, origin)
        return push(
            get(self.pack) if way == 5 else target,
            target,
            get(self.core_send).at[way],
            get(self.core_recv).at[way],
            at["core"],
        )

    def own(self, get, at):
        return pltpu.make_async_copy(
            get(self.pack), self.block(get, at, at["mesh"][4]), get(self.own_sem).at[0]
        )

    def launch(self, get, at):
        for way in (2, 3, 0, 1):

            @pl.when(self.sends(at, way))
            def _():
                self.move(get, at, way).start()

        self.to_core(get, at, 5).start()
        self.own(get, at).start()

    def relay(self, get, at):
        for plane, way in ((2, 2), (1, 3)):

            @pl.when(at["mesh"][4] == plane)
            def _():
                self.move(get, at, way).wait_recv()
                self.move(get, at, 4).start()
                self.to_core(get, at, way).start()

    def pass_on(self, get, at):
        z = at["mesh"][4]
        for way in (0, 1, 2, 3, 4):
            taken = {2: z == 2, 3: z == 1}.get(way, z < 0)

            @pl.when(self.comes(at, way) & jnp.logical_not(taken))
            def _():
                self.move(get, at, way).wait_recv()
                self.to_core(get, at, way).start()

    def finish(self, get, at):
        self.own(get, at).wait()
        self.to_core(get, at, 5).wait()
        for way in range(5):

            @pl.when(self.comes(at, way))
            def _():
                self.to_core(get, at, way).wait()

            @pl.when(self.sends(at, way))
            def _():
                self.move(get, at, way).wait_send()


class Gather:
    def __init__(self, call, shares, rows, first=0):
        self.call, self.shares, self.rows, self.first = call, call.take(shares, pltpu.HBM), rows, first
        self.landed, self.own = call.hold((3, 4, rows, 128), BF16), call.hold((4, rows, 128), BF16)
        self.far, self.room = call.hold((4, rows, 128), BF16), call.hold((4, rows, 128), BF16)
        self.out = call.keep((4, rows, 128), BF16)
        self.send_sem, self.recv_sem, self.own_sem = call.sems(4), call.sems(4), call.sems(2)

    def share(self, get, plane):
        return get(self.shares).at[plane, :, pl.ds(self.first, self.rows)]

    def move(self, get, at, way, summed=False):
        hi, k, y, c, z = at["mesh"]
        step = {0: 1, 1: 3, 2: 2, 3: jnp.where(z == 0, 1, 3)}[way]
        partner = lax.rem(z + step, 4)
        source = self.share(get, 3 - z if way == 3 else partner)
        return push(
            get(self.room) if summed else source,
            get(self.room) if way == 3 else get(self.landed).at[way],
            get(self.send_sem).at[way],
            get(self.recv_sem).at[way],
            (hi, k, y, c, partner),
        )

    def local(self, get, at, far):
        z = at["mesh"][4]
        return pltpu.make_async_copy(
            self.share(get, lax.rem(z + 2, 4) if far else z),
            get(self.far if far else self.own),
            get(self.own_sem).at[1 if far else 0],
        )

    def launch(self, get, at):
        z = at["mesh"][4]
        outer = (z == 0) | (z == 3)
        for way, when in ((3, outer), (2, outer), (0, z < 3), (1, z > 0)):

            @pl.when(when)
            def _():
                self.move(get, at, way).start()

        for far in (False, True):
            self.local(get, at, far).start()

    def relay(self, get, at):
        z = at["mesh"][4]

        @pl.when((z == 1) | (z == 2))
        def _():
            self.move(get, at, 3).wait_recv()
            self.local(get, at, True).wait()
            room = get(self.room)
            room[...] = (room[...].astype(F32) + get(self.far)[...].astype(F32)).astype(BF16)
            self.move(get, at, 2, True).start()

        @pl.when((z == 0) | (z == 3))
        def _():
            self.local(get, at, True).wait()

    def finish(self, get, at):
        z = at["mesh"][4]
        landed, own, out = get(self.landed), get(self.own), get(self.out)
        self.local(get, at, False).wait()
        self.move(get, at, 2).wait()
        for which, ways in ((z == 0, (1,)), (z == 3, (0,)), ((z == 1) | (z == 2), (0, 1))):

            @pl.when(which)
            def _():
                for way in ways:
                    self.move(get, at, way).wait_recv()
                for q in range(4):
                    total = own[q].astype(F32) + landed[2, q].astype(F32)
                    for way in ways:
                        total = total + landed[way, q].astype(F32)
                    out[q] = total.astype(BF16)

        self.call.save(get, self.out)
        for way, when in ((3, (z == 0) | (z == 3)), (0, z < 3), (1, z > 0)):

            @pl.when(when)
            def _():
                self.move(get, at, way).wait_send()


class Swap:
    def __init__(self, call, pack):
        self.pack = call.take(pack, pltpu.HBM)
        rows = call.rows_of[pack] if isinstance(pack, tuple) else pack.shape[1]
        self.out = call.give((4, rows, 128), BF16, pltpu.HBM)
        call.rows_of[self.out] = rows
        self.send_sem, self.recv_sem, self.own_sem = call.sems(3), call.sems(3), call.sems(1)

    def start(self, get, at):
        hi, k, y, c, z = at["mesh"]
        own = hi * 2 + y
        pack, out = get(self.pack), get(self.out)
        self.copies = [pltpu.make_async_copy(pack.at[own], out.at[own], get(self.own_sem).at[0])]
        for i, (name, q) in enumerate(
            (("d", (1 - hi) * 2 + 1 - y), ("x", (1 - hi) * 2 + y), ("y", hi * 2 + 1 - y))
        ):
            send, recv = get(self.send_sem).at[i], get(self.recv_sem).at[i]
            self.copies.append(push(pack.at[q], out.at[own], send, recv, at[name]))
        for copy in self.copies:
            copy.start()

    def finish(self, get, at):
        for copy in self.copies:
            copy.wait()


class Slots:
    def __init__(self, call, arrays, inward):
        self.inward = inward
        self.call, self.arrays = call, [call.fetch(array) for array in arrays]
        shape = (128, 1024) if inward else (2, 64, 1024)
        self.outs = [call.keep(shape, BF16) for array in arrays]
        self.send_sem, self.recv_sem = call.sems(2 * len(arrays)), call.sems(2 * len(arrays))

    def ends(self, get, at, j, step):
        z = at["mesh"][4]
        low = lax.div(z, 2)
        other = low if step == 0 else 1 - low
        array, out = get(self.arrays[j]), get(self.outs[j])
        if self.inward:
            return array.at[other], out.at[pl.ds(pl.multiple_of(low * 64, 64), 64)]
        return array.at[pl.ds(pl.multiple_of(other * 64, 64), 64)], out.at[low]

    def stays(self, at):
        hi, z = at["mesh"][0], at["mesh"][4]
        return lax.rem(z, 2) == hi

    def copy(self, get, at, j, step):
        hi, k, y, c, z = at["mesh"]
        low = lax.div(z, 2)
        partner = (lax.rem(z, 2), k, y, c, 2 * (low if step == 0 else 1 - low) + hi)
        source, target = self.ends(get, at, j, step)
        return pltpu.make_async_remote_copy(
            src_ref=source,
            dst_ref=target,
            send_sem=get(self.send_sem).at[2 * j + step],
            recv_sem=get(self.recv_sem).at[2 * j + step],
            device_id=partner,
            device_id_type=MESH_ID,
        )

    def start(self, get, at):
        stays = self.stays(at)
        for j in range(len(self.arrays)):
            self.copy(get, at, j, 1).start()

        @pl.when(jnp.logical_not(stays))
        def _():
            for j in range(len(self.arrays)):
                self.copy(get, at, j, 0).start()

        @pl.when(stays)
        def _():
            for j in range(len(self.arrays)):
                source, target = self.ends(get, at, j, 0)
                target[...] = source[...]

    def finish(self, get, at):
        for j in range(len(self.arrays)):
            self.copy(get, at, j, 1).wait()

        @pl.when(jnp.logical_not(self.stays(at)))
        def _():
            for j in range(len(self.arrays)):
                self.copy(get, at, j, 0).wait()

        for out in self.outs:
            self.call.save(get, out)


def all_partners(at):
    hi, k, y, c, z = at["mesh"]
    plane = [
        ((hi + i) % 2, k, (y + j) % 2, (c + n) % 2, z)
        for i in range(2)
        for j in range(2)
        for n in range(2)
        if i + j + n > 0
    ]
    ways = [((hi + i) % 2, k, y, c, (z + n) % 4) for i in range(2) for n in range(1, 4)]
    return plane, ways


def meeting(at):
    plane, ways = all_partners(at)
    return plane + ways


class Vectors:
    def __init__(self, call, vectors, inward):
        self.inward = inward
        self.source = call.take(vectors)
        self.out = call.keep((16, 1024), F32) if inward else call.give((16, 128), F32)
        self.landed, self.whole = call.hold((7, 16, 128), F32), call.hold((16, 128), F32)
        self.split, self.along = call.hold((8, 16, 128), F32), call.hold((3, 16, 128), F32)
        self.send_sem, self.recv_sem = call.sems(10), call.sems(10)

    def move(self, get, i, source, target, partner):
        return push(source, target, get(self.send_sem).at[i], get(self.recv_sem).at[i], partner)

    def planes(self, get, at, source):
        return [
            self.move(get, n, source, get(self.along).at[n], partner)
            for n, partner in enumerate(along(at))
        ]

    def block(self, at):
        hi, k, y, c, z = at["mesh"]
        return (hi * 2 + y) * 2 + c

    def start(self, get, at):
        plane = all_partners(at)[0]
        if self.inward:
            self.copies = self.planes(get, at, get(self.source))
        else:
            split = get(self.split)
            for d in range(8):
                split[d] = get(self.source)[:, d * 128 : d * 128 + 128]
            self.copies = [
                self.move(
                    get,
                    3 + i,
                    split.at[(partner[0] * 2 + partner[2]) * 2 + partner[3]],
                    get(self.landed).at[i],
                    partner,
                )
                for i, partner in enumerate(plane)
            ]
        for copy in self.copies:
            copy.start()

    def second(self, get, at):
        plane = all_partners(at)[0]
        for copy in self.copies:
            copy.wait()
        whole, out = get(self.whole), get(self.out)
        if self.inward:
            whole[...] = get(self.source)[...] + jnp.sum(get(self.along)[...], 0)
            block = pl.ds(pl.multiple_of(self.block(at) * 128, 128), 128)
            out[:, block] = whole[...]
            self.copies = [
                self.move(get, 3 + i, whole, out.at[:, block], partner)
                for i, partner in enumerate(plane)
            ]
        else:
            whole[...] = get(self.split)[self.block(at)] + jnp.sum(get(self.landed)[...], 0)
            self.copies = self.planes(get, at, whole)
        for copy in self.copies:
            copy.start()

    def finish(self, get, at):
        for copy in self.copies:
            copy.wait()
        if not self.inward:
            get(self.out)[...] = get(self.whole)[...] + jnp.sum(get(self.along)[...], 0)


class Pack:
    def __init__(self, call, matrices):
        self.parts = [(call.fetch(array), index, across) for array, index, across in matrices]
        counts = [
            (array.shape[-1] if across else array.shape[-2]) // 4
            for array, index, across in matrices
        ]
        self.counts = counts
        self.out = call.hold((4, sum(counts), 128), BF16)
        call.rows_of[self.out] = sum(counts)

    def make(self, get):
        out, base = get(self.out), 0
        for (part, index, across), count in zip(self.parts, self.counts, strict=True):
            part = get(part)
            whole = part[...] if index is None else part[index]
            if across:
                whole = whole.astype(F32).T.astype(BF16)
            out[:, base : base + count, :] = whole.reshape(4, count, 128)
            base += count


def by_owner(rows, back=False):
    copies = lax.axis_size("k")
    if copies == 1:
        return rows
    shape, width = rows.shape, 128 // copies
    if back:
        rows = rows.reshape(-1, 2, 2, 2, copies, width).transpose(0, 1, 4, 2, 3, 5)
    else:
        rows = rows.reshape(-1, 2, copies, 2, 2, width).transpose(0, 1, 3, 4, 2, 5)
    return rows.reshape(shape)


def unpacked(packs, rows, wide):
    call = Call()
    rows_in = [call.fetch(array) for array in rows]
    ins = [call.fetch(array) for array in packs]
    plans = []
    for handle, array, kinds in zip(ins, packs, wide, strict=True):
        base = 0
        for kind in kinds:
            count = 256 if kind in ("up", "down") else 64
            if kind == "q":
                out = call.give((3, 128, 256), F32)
                plans += [(handle, base + i * 64, 64, out, i, True) for i in range(3)]
                base += 192
                continue
            shape = (128, 4 * count) if kind == "up" else (4 * count, 128)
            plans.append((handle, base, count, call.give(shape, F32), None, kind == "up"))
            base += count
    outs = [call.give(array.shape, F32) for array in rows]

    def body(get):
        for handle, base, count, out, index, across in plans:
            whole = get(handle)[:, base : base + count, :].astype(F32).reshape(4 * count, 128)
            whole = whole.T if across else whole
            if index is None:
                get(out)[...] = whole
            else:
                get(out)[index] = whole
        for source, out in zip(rows_in, outs, strict=True):
            get(out)[...] = get(source)[...].astype(F32)

    return call.run(body, "unpacked", None, 4 * MICROSECOND)


def local(
    source,
    target,
    cotangent,
    source_len,
    target_len,
    source_seg,
    target_seg,
    enc_qkv,
    enc_proj,
    enc_up,
    enc_down,
    enc_gain,
    enc_shift,
    dec_qkv,
    dec_proj,
    cross_qkv,
    cross_proj,
    dec_up,
    dec_down,
    dec_gain,
    dec_shift,
):
    copies, z = lax.axis_size("k"), lax.axis_index("mp")
    norms = (enc_gain, enc_shift, dec_gain, dec_shift)
    if copies > 1:
        norms = [lax.all_gather(vector, "k", axis=1, tiled=True) for vector in norms]

    def widen(array, axis):
        return array if copies == 1 else lax.all_gather(array, "k", axis=axis, tiled=True)

    enc_qkv, dec_qkv, cross_qkv = (widen(array, 1) for array in (enc_qkv, dec_qkv, cross_qkv))
    enc_proj, dec_proj, cross_proj = (widen(array, 1) for array in (enc_proj, dec_proj, cross_proj))
    enc_up, dec_up = widen(enc_up, 0), widen(dec_up, 0)
    enc_down, dec_down = widen(enc_down, 1), widen(dec_down, 1)

    ENC_G, ENC_B, DEC_G, DEC_B = 0, 3, 6, 10
    SELF, SELF_O = 192, 64
    Q, QKV, KV, O, FIRST_O = (0, 64), (0, 192), (64, 128), (192, 64), (0, 64)
    UP, DOWN = (0, 256), (256, 256)

    def pick(call, packed, span, base=0):
        return Weight(call, packed, base + span[0], span[1])

    def forward_mid(call, residual, gain, shift, normed=None):
        vec, res = call.fetch(vectors), call.fetch(residual)
        kept = call.keep((128, 1024), F32)

        def mid(get, total):
            stream = get(res)[...].astype(F32) + total
            get(kept)[...] = stream
            call.save(get, kept)
            unit, scale = unit_of(stream)
            made = (unit * get(vec)[gain : gain + 1] + get(vec)[shift : shift + 1]).astype(BF16)
            if normed is not None:
                get(normed)[...] = made
                call.save(get, normed)
            return made

        mid.kept = kept
        return mid

    def backward_mid(call, stream, gain, residual=None, dtype=F32):
        vec, kept = call.fetch(vectors), call.fetch(stream)
        res = None if residual is None else call.fetch(residual)
        grad_out, share_out = call.keep((128, 1024), dtype), call.keep((2, 1024), F32)

        def mid(get, total):
            grad, shares = norm_back(get(kept)[...].astype(F32), get(vec)[gain : gain + 1], total)
            if res is not None:
                grad = grad + get(res)[...]
            get(grad_out)[...] = grad.astype(dtype)
            call.save(get, grad_out)
            get(share_out)[...] = shares
            call.save(get, share_out)
            return grad.astype(BF16)

        mid.kept, mid.shares = grad_out, share_out
        return mid

    def deactivated(call, slope):
        out = call.keep((4, 128, 1024), BF16, 4)

        def store(get, at, row, column, value):
            get(out)[row] = (value * get(slope)[row]).astype(BF16)
            call.save(get, out, row)

        return Kept(out, store)

    call = Call()
    slots = Slots(call, [by_owner(source), by_owner(target)], True)
    stream_h, target_h = slots.outs
    norm_parts, norm_own = [call.take(vector) for vector in norms], call.hold((16, 128), F32)
    first_vectors = Vectors(call, norm_own, True)
    fact_ids = [call.take(source_seg), call.take(target_seg)]
    fact_lengths = [call.take(source_len, pltpu.SMEM), call.take(target_len, pltpu.SMEM)]
    fact_own, fact_room = call.hold((2, 8, 128), F32), call.hold((2, 8, 128), F32)
    fact_rows, fact_columns = call.keep((8, 1024), F32), call.keep((1024, 128), F32)
    fact_send, fact_recv = call.sems(1), call.sems(1)

    def three(array):
        return [(array, i, True) for i in range(3)]

    pack_1 = Pack(call, three(enc_qkv) + three(dec_qkv))
    pack_o = Pack(call, [(enc_proj, None, False), (dec_proj, None, False)])
    pack_2 = Pack(call, [(enc_up, None, True), (enc_down, None, False)])
    pack_3 = Pack(call, three(cross_qkv) + [(cross_proj, None, False)])
    pack_4 = Pack(call, [(dec_up, None, True), (dec_down, None, False)])
    swap_1, swap_o, swap_2, swap_3, swap_4 = (
        Swap(call, pack.out) for pack in (pack_1, pack_o, pack_2, pack_3, pack_4)
    )
    spread_1, spread_o, spread_2, spread_3, spread_4 = (
        Spread(call, swap.out) for swap in (swap_1, swap_o, swap_2, swap_3, swap_4)
    )

    def count_facts(get):
        own = get(fact_own)
        own[...] = jnp.zeros_like(own)
        lane = lax.broadcasted_iota(jnp.int32, (2, 128), 1)
        for kind in range(2):
            ids, lengths = get(fact_ids[kind])[...], get(fact_lengths[kind])
            table = jnp.zeros((2, 128), F32)
            for p in range(1, PAIRS):
                before = jnp.sum((ids < p).astype(F32), 1, keepdims=True)
                table = table + jnp.where(lane == p, before, 0.0)
            for slot in range(2):
                length = lengths[slot].astype(F32)
                own[slot, kind : kind + 1] = jnp.where(
                    lane[:1] == 0, length, table[slot : slot + 1]
                )

    def place_norms(get, at):
        z, total, row = at["mesh"][4], get(norm_own), 0
        total[...] = jnp.zeros_like(total)
        lane = lax.broadcasted_iota(jnp.int32, (1, 128), 1)
        width = 32 // copies
        for part in norm_parts:
            given = get(part)[...]
            pieces = [given[:, i * width : (i + 1) * width] for i in range(copies) for _ in range(4)]
            wide = jnp.concatenate(pieces, 1)
            total[row : row + given.shape[0]] = jnp.where((lane // width) % 4 == z, wide, 0.0)
            row += given.shape[0]

    def place_facts(get, at):
        hi, k, y, c, z = at["mesh"]
        slot = lax.div(z, 2)
        table = jnp.where(lax.rem(z, 2) == hi, get(fact_own)[slot], get(fact_room)[slot])

        def kinds(index):
            core = jnp.where(index < 512, c, 1 - c)
            part = index % 512
            place = (part // 256) * 512 + core * 256 + ((part // 64) % 2) * 128
            place = (place + ((part // 128) % 2) * 64 + part % 64).astype(F32)
            found = []
            for row in range(2):
                ids = jnp.zeros_like(place)
                for p in range(1, PAIRS):
                    ids = ids + jnp.where(place >= table[row : row + 1, p : p + 1], 1.0, 0.0)
                found.append(ids)
            live = [jnp.where(place < table[row : row + 1, 0:1], 1.0, 0.0) for row in range(2)]
            return found + [place] + live

        across = kinds(lax.broadcasted_iota(jnp.int32, (1, 1024), 1))
        down = kinds(lax.broadcasted_iota(jnp.int32, (1024, 128), 0))
        rows, columns = get(fact_rows), get(fact_columns)
        rows[...] = jnp.zeros_like(rows)
        lane = lax.broadcasted_iota(jnp.int32, (1024, 128), 1)
        wide = jnp.zeros((1024, 128), F32)
        for i in range(5):
            rows[i : i + 1] = across[i]
            wide = jnp.where(lane == i, down[i], wide)
        columns[...] = wide
        call.save(get, fact_columns)
        call.save(get, fact_rows)

    def first_mid(stream, gain, shift):
        def mid(get, total):
            unit, scale = unit_of(get(stream)[...].astype(F32))
            vec = get(first_vectors.out)
            return (unit * vec[gain : gain + 1] + vec[shift : shift + 1]).astype(BF16)

        return mid

    job_a = Job(call, None, first_mid(stream_h, ENC_G, ENC_B), (None, None, None))
    job_c = Job(call, None, first_mid(target_h, DEC_G, DEC_B), (None, None, None))
    vectors = first_vectors.out

    plans = []
    for rows, base in ((job_a.gathered, 0), (job_c.gathered, SELF)):
        query, shared = Plain(call, 256), Shared(call, 512, 256)
        plans.append((call.fetch(rows), pick(call, spread_1.out, QKV, base), query, shared))
    enc_step = Attend(
        call, plans[0][2].out, plans[0][3].out, fact_rows, fact_columns, (SOURCE, SOURCE, False)
    )
    self_step = Attend(
        call, plans[1][2].out, plans[1][3].out, fact_rows, fact_columns, (TARGET, TARGET, True)
    )
    enc_o, self_o = pick(call, spread_o.out, FIRST_O), pick(call, spread_o.out, FIRST_O, SELF_O)
    mid = forward_mid(call, stream_h, ENC_G + 1, ENC_B + 1)
    job_b = Job(call, (enc_step.mixed, enc_o, [(0, 64)], 0), mid, (None, None, None))
    mid = forward_mid(call, target_h, DEC_G + 1, DEC_B + 1)
    cross_a, cross_b = pick(call, spread_3.out, Q), pick(call, spread_3.out, KV)
    cross_o = pick(call, spread_3.out, O)
    query, shared = Plain(call, 256), Shared(call, 512)
    job_d = Job(call, (self_step.mixed, self_o, [(0, 64)], 0), mid, (cross_a, [(0, 64)], query.store))
    enc_u, enc_d = pick(call, spread_2.out, UP), pick(call, spread_2.out, DOWN)
    feed = Feed(call, job_b.gathered, enc_u, enc_d)
    mid = forward_mid(call, job_b.kept, ENC_G + 2, ENC_B + 2)
    job_m = Job(call, feed, mid, (cross_b, [(0, 64), (64, 64)], shared.store))
    cross_step = Attend(
        call, query.out, shared.out, fact_rows, fact_columns, (TARGET, SOURCE, False)
    )
    mid = forward_mid(call, job_d.kept, DEC_G + 2, DEC_B + 2)
    job_e = Job(call, (cross_step.mixed, cross_o, [(0, 64)], 0), mid, (None, None, None))

    def onward(get, at):
        place_norms(get, at)
        first_vectors.start(get, at)
        slots.start(get, at)
        pack_1.make(get)
        swap_1.start(get, at)
        count_facts(get)
        fact_copy = push(
            get(fact_own), get(fact_room), get(fact_send).at[0], get(fact_recv).at[0], at["x"]
        )
        fact_copy.start()
        first_vectors.second(get, at)
        swap_1.finish(get, at)
        spread_1.launch(get, at)
        for pack in (pack_o, pack_2):
            pack.make(get)
        first_vectors.finish(get, at)
        call.save(get, first_vectors.out)
        slots.finish(get, at)
        job_a.settle(get, at)
        job_c.settle(get, at)
        fact_copy.wait()
        place_facts(get, at)
        job_a.rows_forward(get, at)
        job_c.rows_forward(get, at)
        spread_1.relay(get, at)
        swap_o.start(get, at)
        swap_2.start(get, at)
        for pack in (pack_3, pack_4):
            pack.make(get)
        job_a.collect(get, at)
        job_c.collect(get, at)
        enc_step.prepare(get)
        swap_o.finish(get, at)
        swap_2.finish(get, at)
        job_a.drain()
        job_c.drain()
        spread_1.pass_on(get, at)
        spread_o.launch(get, at)
        spread_2.launch(get, at)
        swap_3.start(get, at)
        swap_4.start(get, at)
        spread_1.finish(get, at)
        for plan in plans:
            plan[1].start(get)
        for rows, weight, queries, keys in plans:
            weight.wait(get)
            for row in range(4):
                for m in range(3):
                    made = nt(get(rows)[row], weight.matrix(get, m * 64, 64))
                    (queries if m == 0 else keys).store(get, at, row, m * 256, made)
        for plan in plans:
            plan[3].finish(get)
        spread_o.relay(get, at)
        enc_step.pairs(get, 0, 2)
        enc_step.save(get)
        spread_o.pass_on(get, at)
        swap_3.finish(get, at)
        swap_4.finish(get, at)
        spread_o.finish(get, at)
        enc_o.start(get)
        self_o.start(get)
        job_b.sums(get, at)
        self_step.prepare(get)
        self_step.pairs(get, 0, 1)
        job_b.sum_forward(get, at)
        self_step.pairs(get, 1, 2)
        self_step.save(get)
        job_b.sum_own(get, at)
        job_d.sums(get, at)
        job_b.settle(get, at)
        spread_2.relay(get, at)
        spread_3.launch(get, at)
        job_d.sum_forward(get, at)
        job_d.sum_own(get, at)
        job_b.rows_forward(get, at)
        job_d.settle(get, at)
        spread_2.pass_on(get, at)
        spread_2.finish(get, at)
        enc_u.start(get)
        enc_d.start(get)
        job_b.collect(get, at)
        job_m.sums(get, at)
        job_d.rows_forward(get, at)
        job_m.sum_forward(get, at)
        job_m.sum_own(get, at)
        spread_3.relay(get, at)
        spread_4.launch(get, at)
        job_m.settle(get, at)
        spread_3.pass_on(get, at)
        spread_3.finish(get, at)
        for weight in (cross_a, cross_b, cross_o):
            weight.start(get)
        job_m.rows_forward(get, at)
        job_d.product(get, at, at["own_row"])
        job_d.collect(get, at)
        job_m.product(get, at, at["own_row"])
        job_m.collect(get, at)
        for job in (job_b, job_d, job_m):
            job.drain()
        shared.finish(get)
        cross_step.prepare(get)
        cross_step.pairs(get, 0, 1)
        spread_4.relay(get, at)
        cross_step.pairs(get, 1, 2)
        cross_step.save(get)
        job_e.sums(get, at)
        job_e.sum_forward(get, at)
        job_e.sum_own(get, at)
        job_e.settle(get, at)
        spread_4.pass_on(get, at)
        job_e.rows_forward(get, at)
        job_e.collect(get, at)
        job_e.drain()
        spread_4.finish(get, at)

    (
        stream_in,
        target_in,
        vectors,
        fact_rows,
        fact_columns,
        unused,
        unused,
        unused,
        unused,
        unused,
        first_w,
        first_o,
        second_w,
        cross_w,
        third_w,
        rows_a,
        rows_c,
        enc_q,
        enc_kv,
        self_q,
        self_kv,
        enc_mixed,
        enc_total,
        self_mixed,
        self_total,
        stream_mid,
        rows_b,
        target_mid,
        cross_q,
        cross_kv,
        rows_d,
        enc_hidden,
        enc_slope,
        stream_end,
        memory,
        cross_mixed,
        cross_total,
        target_late,
        rows_e,
    ) = run_body(call, onward, ["all"], "onward", 0, 170 * MICROSECOND)

    call = Call()
    dec_u, dec_d = pick(call, third_w, UP), pick(call, third_w, DOWN)
    cross_o = pick(call, cross_w, O)
    feed = Feed(call, rows_e, dec_u, dec_d)
    slots = Slots(call, [by_owner(cotangent)], True)
    vec, res, cot = call.fetch(vectors), call.fetch(target_late), slots.outs[0]
    decoded_out, grad_end = call.keep((128, 1024), BF16), call.hold((128, 1024), F32)
    share_out = call.keep((2, 1024), F32)

    def last_mid(get, total):
        stream = get(res)[...] + total
        gain, shift = get(vec)[DEC_G + 3 : DEC_G + 4], get(vec)[DEC_B + 3 : DEC_B + 4]
        unit, unused = unit_of(stream)
        get(decoded_out)[...] = (unit * gain + shift).astype(BF16)
        grad, shares = norm_back(stream, gain, get(cot)[...].astype(F32))
        get(grad_end)[...] = grad
        get(share_out)[...] = shares
        call.save(get, decoded_out)
        call.save(get, share_out)
        return grad.astype(BF16)

    active = deactivated(call, feed.slope)
    job_t = Job(call, feed, last_mid, (dec_d, [(0, 256)], active.store))
    mid = backward_mid(call, target_late, DEC_G + 2, grad_end)
    query = Plain(call, 256)
    job_c = Job(call, (active.out, dec_u, [(0, 256)], 0), mid, (cross_o, [(0, 64)], query.store))
    down_shares = Shares(call, [(feed.hidden, 0, job_t.gathered)], 256, False)
    joined = call.give((4, 4, 512, 128), BF16, pltpu.HBM)
    up_shares = Shares(call, [(active.out, 0, feed.rows)], 256, joined, 0)
    back = AttendBack(
        call,
        cross_q,
        cross_kv,
        query.out,
        cross_total,
        fact_rows,
        fact_columns,
        (TARGET, SOURCE, False),
    )
    cross_shares = Shares(
        call,
        [
            (back.out, 0, rows_d),
            (back.out, 256, memory),
            (back.out, 512, memory),
            (cross_mixed, 0, job_c.gathered),
        ],
        64,
        joined,
        256,
    )
    gather = Gather(call, down_shares.room, 256)

    def turning(get, at):
        for weight in (dec_u, dec_d, cross_o):
            weight.start(get)
        slots.start(get, at)
        job_t.sums(get, at)
        job_t.sum_forward(get, at)
        job_t.sum_own(get, at)
        slots.finish(get, at)
        job_t.settle(get, at)
        job_t.product(get, at, at["own_row"])
        job_t.rows_forward(get, at)
        job_t.collect(get, at)
        job_c.sums(get, at)
        job_c.sum_forward(get, at)
        job_c.sum_own(get, at)
        down_shares.middle(get, at)
        down_shares.finish(get, at)
        job_c.settle(get, at)
        gather.launch(get, at)
        job_c.product(get, at, at["own_row"])
        job_c.rows_forward(get, at)
        up_shares.middle(get, at)
        job_c.collect(get, at)
        up_shares.finish(get, at)
        gather.relay(get, at)
        job_t.drain()
        job_c.drain()
        back.late(get, at)
        cross_shares.middle(get, at)
        cross_shares.finish(get, at)
        gather.finish(get, at)

    (
        dec_hidden,
        dec_slope,
        unused,
        decoded,
        norm_3,
        dec_grad_act,
        grad_rows_e,
        grad_late,
        norm_2,
        cross_grad_mixed,
        grad_rows_d,
        joined_s,
        cross_grads,
        down_g,
    ) = run_body(call, turning, ["all"], "turning", 1, 62 * MICROSECOND)

    call = Call()
    cross_a, cross_b = pick(call, cross_w, Q), pick(call, cross_w, KV)
    self_o, enc_d = pick(call, first_o, FIRST_O, SELF_O), pick(call, second_w, DOWN)
    slots = Slots(call, [decoded], False)
    mid = backward_mid(call, target_mid, DEC_G + 1, grad_late)
    query = Plain(call, 256)
    job_t = Job(call, (cross_grads, cross_a, [(0, 64)], 0), mid, (self_o, [(0, 64)], query.store))
    mid = backward_mid(call, stream_end, ENC_G + 2)
    active = deactivated(call, call.fetch(enc_slope))
    job_s = Job(
        call,
        (cross_grads, cross_b, [(0, 64), (64, 64)], 256),
        mid,
        (enc_d, [(0, 256)], active.store),
    )
    shares = Shares(
        call, [(active.out, 0, rows_b), (enc_hidden, 0, job_s.gathered)], 256
    )
    gather, swap = Gather(call, joined_s, 512), Swap(call, down_g)

    def backing(get, at):
        gather.launch(get, at)
        for weight in (cross_b, cross_a, enc_d, self_o):
            weight.start(get)
        job_s.sums(get, at)
        job_t.sums(get, at)
        job_s.sum_forward(get, at)
        job_t.sum_forward(get, at)
        job_s.sum_own(get, at)
        job_s.settle(get, at)
        job_t.sum_own(get, at)
        job_t.settle(get, at)
        slots.start(get, at)
        job_s.product(get, at, at["own_row"])
        job_s.rows_forward(get, at)
        job_t.product(get, at, at["own_row"])
        job_t.rows_forward(get, at)
        swap.start(get, at)
        job_s.collect(get, at)
        gather.relay(get, at)
        shares.middle(get, at)
        job_t.collect(get, at)
        shares.finish(get, at)
        job_s.drain()
        job_t.drain()
        slots.finish(get, at)
        swap.finish(get, at)
        gather.finish(get, at)

    (
        decoded,
        grad_mid,
        norm_1,
        self_grad_mixed,
        grad_rows_c,
        grad_stream,
        enc_norm_2,
        enc_grad_act,
        grad_rows_b,
        feed_s,
        up_cross_g,
        down_g,
    ) = run_body(call, backing, ["x", "y", "core", "d", "ways"], "backing", 2, 46 * MICROSECOND)

    call = Call()
    enc_u, enc_o = pick(call, second_w, UP), pick(call, first_o, FIRST_O)
    self_a = pick(call, first_w, QKV, SELF)
    self_back = AttendBack(
        call,
        self_q,
        self_kv,
        self_grad_mixed,
        self_total,
        fact_rows,
        fact_columns,
        (TARGET, TARGET, True),
    )
    mid = backward_mid(call, stream_mid, ENC_G + 1, grad_stream)
    query = Plain(call, 256)
    job_s = Job(call, (enc_grad_act, enc_u, [(0, 256)], 0), mid, (enc_o, [(0, 64)], query.store))
    mid = backward_mid(call, target_in, DEC_G, grad_mid, BF16)
    job_t = Job(call, (self_back.out, self_a, [(0, 64), (64, 64), (128, 64)], 0), mid, None)
    self_shares = Shares(
        call,
        [
            (self_back.out, 0, rows_c),
            (self_back.out, 256, rows_c),
            (self_back.out, 512, rows_c),
            (self_mixed, 0, grad_rows_c),
        ],
        64,
        False,
    )
    enc_back = AttendBack(
        call,
        enc_q,
        enc_kv,
        query.out,
        enc_total,
        fact_rows,
        fact_columns,
        (SOURCE, SOURCE, False),
    )
    enc_shares = Shares(
        call,
        [
            (enc_back.out, 0, rows_a),
            (enc_back.out, 256, rows_a),
            (enc_back.out, 512, rows_a),
            (enc_mixed, 0, job_s.gathered),
        ],
        64,
        False,
    )
    enc_a = pick(call, first_w, QKV)
    mid = backward_mid(call, stream_in, ENC_G, job_s.kept, BF16)
    job_f = Job(call, (enc_back.out, enc_a, [(0, 64), (64, 64), (128, 64)], 0), mid, None)
    gather_f, gather_s = Gather(call, feed_s, 512), Gather(call, self_shares.room, 256)
    gather_e = Gather(call, enc_shares.room, 256)
    for gather, rows in ((gather_f, 512), (gather_s, 256), (gather_e, 256)):
        call.rows_of[gather.out] = rows
    swap, swap_f = Swap(call, up_cross_g), Swap(call, gather_f.out)
    swap_s, swap_e = Swap(call, gather_s.out), Swap(call, gather_e.out)
    target_slots, source_slots = Slots(call, [job_t.kept], False), Slots(call, [job_f.kept], False)
    others = [call.fetch(norm) for norm in (norm_1, norm_2, norm_3, enc_norm_2)]
    norm_sum = call.hold((16, 1024), F32)
    sums = Vectors(call, norm_sum, False)

    def selfward(get, at):
        gather_f.launch(get, at)
        for weight in (enc_u, self_a, enc_o, enc_a):
            weight.start(get)
        self_back.prepare(get)
        job_s.sums(get, at)
        self_back.pair(get, at, 0)
        job_s.sum_forward(get, at)
        self_back.pair(get, at, 1)
        self_back.end(get)
        job_s.sum_own(get, at)
        job_t.sums(get, at)
        job_s.settle(get, at)
        job_t.sum_forward(get, at)
        job_t.sum_own(get, at)
        self_shares.middle(get, at)
        self_shares.finish(get, at)
        gather_s.launch(get, at)
        job_s.product(get, at, at["own_row"])
        job_s.rows_forward(get, at)
        job_t.settle(get, at)
        gather_f.relay(get, at)
        target_slots.start(get, at)
        swap.start(get, at)
        job_s.collect(get, at)
        job_s.drain()
        job_t.drain()
        enc_back.late(get, at)
        enc_shares.middle(get, at)
        enc_shares.finish(get, at)
        gather_e.launch(get, at)
        gather_s.relay(get, at)
        job_f.sums(get, at)
        job_f.sum_forward(get, at)
        job_f.sum_own(get, at)
        job_f.settle(get, at)
        gather_e.relay(get, at)
        source_slots.start(get, at)
        total = get(norm_sum)
        for row, shares in (
            (0, get(job_f.shares)),
            (1, get(job_s.shares)),
            (2, get(others[3])),
            (6, get(job_t.shares)),
            (7, get(others[0])),
            (8, get(others[1])),
            (9, get(others[2])),
        ):
            below = row + (3 if row < 6 else 4)
            total[row : row + 1] = shares[0:1]
            total[below : below + 1] = shares[1:2]
        total[14:16] = jnp.zeros((2, 1024), F32)
        sums.start(get, at)
        job_f.drain()
        gather_f.finish(get, at)
        swap_f.start(get, at)
        sums.second(get, at)
        target_slots.finish(get, at)
        gather_s.finish(get, at)
        swap_s.start(get, at)
        sums.finish(get, at)
        source_slots.finish(get, at)
        swap.finish(get, at)
        swap_f.finish(get, at)
        gather_e.finish(get, at)
        swap_e.start(get, at)
        swap_s.finish(get, at)
        swap_e.finish(get, at)

    made = run_body(call, selfward, ["all"], "selfward", 3, 105 * MICROSECOND)
    up_cross_g, feed_g, self_g, enc_g, target_grad, source_grad, norm_grad = made[-7:]
    norm_grad = norm_grad.reshape(16, copies, 4, 32 // copies)
    if copies > 1:
        norm_grad = lax.psum_scatter(norm_grad, "k", scatter_dimension=1)
    norm_grad = norm_grad.reshape(16, 4, -1)
    norm_grad = lax.dynamic_index_in_dim(norm_grad, z, 1, False)

    (
        dec_d,
        dec_u,
        cross_a,
        cross_o,
        enc_u,
        enc_d,
        self_a,
        self_o,
        enc_a,
        enc_o,
        source_grad,
        target_grad,
    ) = unpacked(
        [down_g, up_cross_g, feed_g, self_g, enc_g],
        [source_grad, target_grad],
        [("down",), ("up", "q", "o"), ("up", "down"), ("q", "o"), ("q", "o")],
    )

    def narrow(array, axis):
        if copies == 1:
            return array
        return lax.psum_scatter(array, "k", scatter_dimension=axis, tiled=True)

    enc_a, self_a, cross_a = (narrow(array, 1) for array in (enc_a, self_a, cross_a))
    enc_o, self_o, cross_o = (narrow(array, 1) for array in (enc_o, self_o, cross_o))
    enc_u, dec_u = narrow(enc_u, 0), narrow(dec_u, 0)
    enc_d, dec_d = narrow(enc_d, 1), narrow(dec_d, 1)
    return (
        by_owner(decoded, True),
        by_owner(source_grad, True),
        by_owner(target_grad, True),
        enc_a,
        enc_o,
        enc_u,
        enc_d,
        norm_grad[:3],
        norm_grad[3:6],
        self_a,
        self_o,
        cross_a,
        cross_o,
        dec_u,
        dec_d,
        norm_grad[6:10],
        norm_grad[10:14],
    )


def solution(mesh):
    dp, seq, mp = (mesh.shape[name] for name in ("dp", "seq", "mp"))
    assert dp % 2 == 0 and seq == 4 and mp == 4
    fine = Mesh(mesh.devices.reshape(2, dp // 2, 2, 2, 4), AXES)
    d, s = ("hi", "k"), ("y", "c")
    rows = P(d, s + ("mp",), None)
    three, flat = P(None, d + s, "mp"), P("mp", d + s)
    up, vector = P(d + s, "mp"), P(None, d + s + ("mp",))
    attention, feeding = (three, flat), (up, flat)
    return jax.shard_map(
        local,
        mesh=fine,
        in_specs=(rows,) * 3
        + (P(d), P(d), P(d, None), P(d, None))
        + attention
        + feeding
        + (vector, vector)
        + attention * 2
        + feeding
        + (vector, vector),
        out_specs=(rows,) * 3
        + attention
        + feeding
        + (vector, vector)
        + attention * 2
        + feeding
        + (vector, vector),
        check_vma=False,
    )
```
